128 devices in a mesh: leaf: 8 (over x, core), grp: 16 (over y, z).
Axes of the slice: x: 4, y: 4, z: 4, core: 2. Of those that a mesh axis runs over, the one named last changes fastest.
Arguments:
- rhs_leaf: float32 [64, 262144], P(None, ('leaf', 'grp')), may hold values from -6 to 6
- rhs_sep: float32 [64, 32768], P(None, ('leaf', 'grp')), may hold values from -6 to 6
- rhs_top: float32 [64, 2048], replicated, may hold values from -6 to 6
- leaf_inverse: float32 [2048, 128, 128], P(('leaf', 'grp')), may hold values from -1.5 to 1.5, as said below
- leaf_coupling: bfloat16 [2048, 2, 256, 128], P(('leaf', 'grp')), may hold values from -0.09375 to 0.09375
- leaf_targets: int32 [2048, 2], P(('leaf', 'grp')), may hold values from 0 to 15, all different within a row
- sep_inverse: float32 [128, 256, 256], P(('leaf', 'grp')), may hold values from -1.5 to 1.5, as said below
- sep_blocks: bfloat16 [128, 16, 256, 256], P(('leaf', 'grp')), may hold values from -1 to 1, as said below
- top_coupling: bfloat16 [32768, 2048], P(('leaf', 'grp')), may hold values from -0.125 to 0.125
- top_inverse: float32 [16, 128, 128], replicated, may hold values from -1.5 to 1.5, as said below
- top_lower: bfloat16 [2048, 2048], replicated, may hold values from -1 to 1, as said below
- dest_map: int32 [2048, 1], P(('leaf', 'grp')), may hold values from 0 to 15; in each aligned block of 16 rows (0 to 15, 16 to 31, ...) at most 2 rows name the same one
- centers: float32 [2048, 3, 128], P(('leaf', 'grp')), may hold values from 0 to 1
- points: float32 [128, 3, 2048], P(('leaf', 'grp')), may hold values from 0 to 1
- eval_pattern: int32 [2048, 32], P(('leaf', 'grp')), may hold values 0 or 1
Outputs:
- coef_leaf: float32 [64, 262144], P(None, ('leaf', 'grp'))
- coef_sep: float32 [64, 32768], P(None, ('leaf', 'grp'))
- coef_top: float32 [64, 2048], replicated
- values: float32 [64, 262144], P(None, ('leaf', 'grp'))
The draws below stay inside these ranges and needn't reach their ends.
Inputs may be any that keep to these rules, and one draw needn't show every extreme that they name: `leaf_inverse`: each matrix is lower triangular with a diagonal between 0.5 and 1.5. `sep_inverse`: lower triangular with a diagonal between 0.5 and 1.5. `top_inverse`: lower triangular with a diagonal between 0.5 and 1.5. `sep_blocks`: slot q of device p of a group holds the factor block of separator blocks max(p, q) and min(p, q) of that group, the same on both devices; slot p is zero. `top_lower`: zero except in the 128 by 128 blocks strictly below the diagonal. `leaf_targets`: the 2 entries of a row differ. `dest_map`: of the 16 blocks of one device, at most 2 name the same device.
All inputs are finite; a program needn't handle non-finite values. No bound on the sum of `eval_pattern` on one device may be relied on, other than what follows from the above.
Results may differ from the reference program's by a relative error of at most 0.025.
Values may be sent and summed in bfloat16 or wider, within the bound.
A program may use at most 64 MiB of HBM per device.

```python
import math
import jax
import jax.numpy as jnp
import numpy as np
from jax import lax

R = 64
S = 128
B = 256
NL = 16
NC = 2
CAP = 2
NT = 16
PB = 16
TS = 2048
P_SIZE = 2048
LEAF_ROWS = 262144
SEP_ROWS = 32768
POINTS = 262144
N_LEAF = 8
N_GRP = 16
DEVICES = 128


def triangle(key, amount, span, low, high, spread):
    first_key, second_key = jax.random.split(key)
    diagonal = jax.random.uniform(first_key, (amount, span), jnp.float32, low, high)
    below = jax.random.truncated_normal(second_key, -3.0, 3.0, (amount, span, span), jnp.float32) * (spread / math.sqrt(span))
    row_ids = jnp.arange(span)[:, None]
    col_ids = jnp.arange(span)[None, :]
    lower_part = jnp.where(row_ids > col_ids, below, 0.0)
    return lower_part + diagonal[:, :, None] * (row_ids == col_ids).astype(jnp.float32)


def draw_leaf_inverse(key, part):
    return triangle(key, DEVICES * NL, S, 0.7, 1.3, 0.4)


def draw_sep_inverse(key, part):
    return triangle(key, DEVICES, B, 0.7, 1.3, 0.4)


def draw_top_inverse(key, part):
    return triangle(key, NT, S, 0.7, 1.3, 0.4)


def draw_sep_blocks(key, part):
    amount = DEVICES * N_GRP
    flat_ids = jnp.arange(amount)
    device_id = flat_ids // N_GRP
    slot_id = flat_ids % N_GRP
    group_id = device_id // N_GRP
    row_id = device_id % N_GRP
    upper_id = jnp.maximum(row_id, slot_id)
    lower_id = jnp.minimum(row_id, slot_id)
    ident = (group_id * N_GRP + upper_id) * N_GRP + lower_id
    blocks = jax.vmap(lambda item: jax.random.truncated_normal(jax.random.fold_in(key, item), -3.0, 3.0, (B, B), jnp.float32))(ident)
    blocks = blocks * (1.0 / math.sqrt(B * N_GRP))
    blocks = jnp.where((row_id == slot_id)[:, None, None], 0.0, blocks)
    return blocks.reshape(DEVICES, N_GRP, B, B).astype(jnp.bfloat16)


def draw_top_lower(key, part):
    entries = jax.random.truncated_normal(key, -3.0, 3.0, (TS, TS), jnp.float32)
    entries = entries * (1.0 / math.sqrt(TS))
    row_ids = jnp.arange(TS)[:, None] // S
    col_ids = jnp.arange(TS)[None, :] // S
    return jnp.where(row_ids > col_ids, entries, 0.0).astype(jnp.bfloat16)


def with_ends(result, key, smallest, top_value):
    longest = result.shape.index(max(result.shape))
    spots = []
    for shift in (0, 1):
        where = [jax.random.randint(jax.random.fold_in(key, axis), (), 0, length) for axis, length in enumerate(result.shape)]
        where[longest] = (where[longest] + shift) % result.shape[longest]
        spots.append(tuple(where))
    return result.at[spots[0]].set(smallest).at[spots[1]].set(top_value)


def strengthened(values, key, source, target, blocks, factor):
    def block_of(dim):
        return (jnp.arange(values.shape[dim]) // (values.shape[dim] // blocks)).reshape((-1,) + (1,) * (values.ndim - 1 - dim))

    near = jax.random.permutation(key, blocks)[block_of(target)]
    far = (block_of(target) + blocks // 2) % blocks
    return jnp.where((block_of(source) == near) | (block_of(source) == far), factor * values, values)


def block_levels(key, shape, pieces, smallest, largest):
    factor_of, own = 1.0, jax.random.fold_in(key, 6)
    for position, blocks in pieces:
        heights = jnp.exp(jax.random.uniform(jax.random.fold_in(own, position), (blocks,), jnp.float32, smallest / len(pieces), largest / len(pieces)))
        factor_of = factor_of * jnp.repeat(heights, shape[position] // blocks).reshape([-1 if axis == position else 1 for axis in range(len(shape))])
    return factor_of


def distinct(rng, rows, count, top, lift):
    sequence = jax.random.permutation(jax.random.fold_in(rng, 1), count)
    pull = sequence
    for power in range(3):
        pull = pull * pull // count
    pull = pull * lift // count
    lots = jax.random.randint(jax.random.fold_in(rng, 2), (rows, count), 0, 4096) + pull
    holders = jax.random.permutation(jax.random.fold_in(rng, 3), rows)[jnp.arange(count) % rows]
    lots = jnp.where(jnp.arange(rows)[:, None] == holders[None, :], 1 << 14, lots)
    priority = lots * count + jnp.arange(count)
    return lax.top_k(priority.astype(jnp.int32), top)[1].astype(jnp.int32)


def routed_block(key, own, number, rows, count, top, reach, lean):
    ranking = jax.random.permutation(key, count)
    crowded, usual = load_shares(count, rows * top, reach, lean, True), load_shares(count, rows * top, reach, lean, False)
    places = jnp.arange(count)

    def named(tallies, offset_by):
        used = int((tallies > 0).sum())
        fixed = max(1, used // 4)
        passed = fixed + (places - fixed + offset_by * (used - fixed)) % max(1, count - fixed)
        return jnp.zeros((count,), jnp.int32).at[ranking[jnp.where(places < fixed, places, passed)]].set(jnp.asarray(tallies, jnp.int32))

    tallies = jnp.where(number % 4 == 0, named(crowded, number // 4), named(usual, number - number // 4 - 1))
    mixed = jax.random.permutation(jax.random.fold_in(own, 3), count)
    giver, receiver = mixed[0:count // 2 * 2:2], mixed[1:count // 2 * 2:2]
    slack = jnp.minimum(tallies[giver] - 1, reach - tallies[receiver]) // 2
    slack = jnp.where((giver == ranking[0]) | (receiver == ranking[0]) | (tallies[receiver] == 0), 0, jnp.maximum(slack, 0))
    passed = jax.random.randint(jax.random.fold_in(own, 4), (count // 2,), 0, 1 << 20) % (slack + 1)
    tallies = tallies.at[giver].add(-passed).at[receiver].add(passed)
    members = jnp.searchsorted(jnp.cumsum(tallies), jnp.arange(rows * top), side="right").astype(jnp.int32)
    table = members.reshape(top, rows).T
    table = table[jax.random.permutation(jax.random.fold_in(own, 1), rows)]
    offset_by = jax.random.randint(jax.random.fold_in(own, 2), (rows, 1), 0, top)
    return jnp.take_along_axis(table, (jnp.arange(top)[None, :] + offset_by) % top, axis=1)


def load_shares(count, total, reach, skew, full):
    portions = [(1 << 20) // math.isqrt(grade ** skew) + 1 for grade in range(1, count + 1)]
    largest = reach if full else min(reach, max(-(-total // count), total * portions[0] // sum(portions)))
    least = 1 if total - largest >= count - 1 else 0
    counts, spare = [largest] + [least] * (count - 1), total - largest - least * (count - 1)
    while spare > 0:
        movable = [i for i in range(1, count) if counts[i] < largest] or [i for i in range(1, count) if counts[i] < reach]
        whole, left = sum([portions[i] for i in movable]), spare
        for i in movable:
            extra = min(reach - counts[i], max(1, left * portions[i] // whole), spare)
            counts[i] = counts[i] + extra
            spare = spare - extra
    return np.array(counts)


def scatter_about(own_key, extent, scale, bound, cuts=(), dtype=jnp.bfloat16):
    level = block_levels(own_key, extent, cuts, -0.22, 0.18) if cuts else 1.0
    result = jax.random.normal(own_key, extent, jnp.float32) * scale * level
    return jnp.minimum(jnp.maximum(result, -bound), bound).astype(dtype)


def noise_with(stream_key, extent, deviation, most, shards, heavy, held_as=jnp.bfloat16):
    drawn = deviation * jax.random.normal(stream_key, extent, jnp.float32)
    if shards:
        drawn = drawn * block_levels(stream_key, extent, shards, -0.22, 0.18)
    return jnp.clip(strengthened(drawn, jax.random.fold_in(stream_key, 3), *heavy), -most, most).astype(held_as)


def setup_inputs(seed: int = 0) -> dict:
    seeds = jax.random.split(jax.random.key(seed), 16)
    rhs_leaf = scatter_about(seeds[0], (R, LEAF_ROWS), 1.0, 6.0, ((1, 128),), jnp.float32)
    rhs_sep = scatter_about(seeds[1], (R, SEP_ROWS), 1.0, 6.0, ((1, 128),), jnp.float32)
    rhs_top = scatter_about(seeds[2], (R, TS), 1.0, 6.0, (), jnp.float32)
    leaf_inverse = draw_leaf_inverse(jax.random.fold_in(seeds[15], 71), 0)
    leaf_coupling = scatter_about(seeds[4], (DEVICES * NL, NC, B, S), (S * NL * NC) ** -0.5, 0.09375, ((0, 128),))
    leaf_targets = distinct(seeds[5], (DEVICES * NL), N_GRP, NC, 0)
    sep_inverse = draw_sep_inverse(jax.random.fold_in(seeds[15], 71), 0)
    sep_blocks = draw_sep_blocks(jax.random.fold_in(seeds[15], 71), 0)
    top_coupling = noise_with(seeds[8], (DEVICES * B, TS), (DEVICES * B) ** -0.5, 0.125, ((0, 128),), (0, 1, 128, 5.5))
    top_inverse = draw_top_inverse(jax.random.fold_in(seeds[15], 71), 0)
    top_lower = draw_top_lower(jax.random.fold_in(seeds[15], 71), 0)
    dest_map_keys = jax.random.split(jax.random.fold_in(seeds[11], 1), (DEVICES * NL) // NL)
    dest_map_turns = jax.random.permutation(jax.random.fold_in(seeds[11], 3), (DEVICES * NL) // NL)
    dest_map = jax.vmap(lambda own, number: routed_block(jax.random.fold_in(seeds[11], 2), own, number, NL, N_GRP, 1, CAP, 2))(dest_map_keys, dest_map_turns).reshape((DEVICES * NL, 1))
    centers = jnp.clip(1.0 * jax.random.uniform(seeds[12], (DEVICES * NL, 3, S), jnp.float32) ** block_levels(seeds[12], (DEVICES * NL, 3, S), ((0, 128),), -0.2, 0.2), 0.0, 1.0)
    points = jnp.clip(1.0 * jax.random.uniform(seeds[13], (DEVICES, 3, P_SIZE), jnp.float32) ** block_levels(seeds[13], (DEVICES, 3, P_SIZE), ((0, 128),), -0.2, 0.2), 0.0, 1.0)
    eval_pattern = with_ends((jax.random.randint(seeds[14], (DEVICES * PB, N_GRP * CAP), 0, 2) < 1).astype(jnp.int32), jax.random.fold_in(seeds[14], 1), 0, 1)
    return dict(rhs_leaf=rhs_leaf, rhs_sep=rhs_sep, rhs_top=rhs_top, leaf_inverse=leaf_inverse, leaf_coupling=leaf_coupling, leaf_targets=leaf_targets, sep_inverse=sep_inverse, sep_blocks=sep_blocks, top_coupling=top_coupling, top_inverse=top_inverse, top_lower=top_lower, dest_map=dest_map, centers=centers, points=points, eval_pattern=eval_pattern)


highest = lax.Precision.HIGHEST
support_sq = 0.25


def slot_ranks(dest_rows, grp_size):
    onehot = (dest_rows[..., None] == jnp.arange(grp_size).astype(jnp.int32)).astype(jnp.int32)
    before = jnp.cumsum(onehot, axis=-2) - onehot
    return jnp.sum(before * onehot, axis=-1)


def kernel_block(coef_all, centre_all, block_points, block_mask):
    dist = jnp.zeros((centre_all.shape[0], centre_all.shape[2], block_points.shape[1]), jnp.float32)
    for comp in range(3):
        delta = centre_all[:, comp, :, None] - block_points[None, comp, None, :]
        dist = dist + delta * delta
    weight = jnp.maximum(1.0 - dist / support_sq, 0.0) ** 3
    kernel = (weight * block_mask.astype(jnp.float32)[:, None, None]).astype(jnp.bfloat16)
    return jnp.einsum('krs,ksp->rp', coef_all.astype(jnp.float32), kernel.astype(jnp.float32), precision=highest)


def reference(rhs_leaf, rhs_sep, rhs_top, leaf_inverse, leaf_coupling, leaf_targets, sep_inverse, sep_blocks, top_coupling, top_inverse, top_lower, dest_map, centers, points, eval_pattern):
    groups = N_LEAF
    grp_size = N_GRP
    per_group = grp_size * NL
    leaf_rhs = rhs_leaf.reshape(R, groups, per_group, S).transpose(1, 2, 0, 3)
    leaf_inv = leaf_inverse.reshape(groups, per_group, S, S)
    couple = leaf_coupling.reshape(groups, per_group, NC, B, S)
    targets = leaf_targets.reshape(groups, per_group, NC)
    onehot = (targets[..., None] == jnp.arange(grp_size).astype(jnp.int32)).astype(jnp.float32)
    sep_rhs = rhs_sep.reshape(R, groups, grp_size, B).transpose(1, 2, 0, 3)
    sep_inv = sep_inverse.reshape(groups, grp_size, B, B)
    sep_blk = sep_blocks.reshape(groups, grp_size, grp_size, B, B)
    top_cpl = top_coupling.reshape(groups, grp_size, B, TS)
    dests = dest_map.reshape(groups, grp_size, NL)
    centres = centers.reshape(groups, grp_size, NL, 3, S)
    group_points = points.reshape(groups, grp_size, 3, P_SIZE)
    pattern = eval_pattern.reshape(groups, grp_size, PB, grp_size * CAP)

    def forward_group(item):
        brhs, linv, cpl, ohot, srhs, sinv, sblk, tcpl = item
        leaf_sol = jnp.einsum('nrs,nts->nrt', brhs, linv, precision=highest)
        leaf_half = leaf_sol.astype(jnp.bfloat16)
        partial_value = jnp.einsum('nrs,ncbs->ncrb', leaf_half.astype(jnp.float32), cpl.astype(jnp.float32), precision=highest)
        term = jnp.einsum('ncq,ncrb->qrb', ohot, partial_value, precision=highest)
        sep_start = srhs - term
        solved = []
        halves = []
        for target in range(grp_size):
            residue = sep_start[target]
            for source in range(target):
                residue = residue - jnp.dot(halves[source], sblk[target, source].T, preferred_element_type=jnp.float32)
            solved_block = jnp.dot(residue, sinv[target].T, precision=highest)
            solved.append(solved_block)
            halves.append(solved_block.astype(jnp.bfloat16))
        sep_sol = jnp.stack(solved)
        sep_half = jnp.stack(halves)
        top_term = jnp.einsum('qrb,qbt->rt', sep_half.astype(jnp.float32), tcpl.astype(jnp.float32), precision=highest)
        return leaf_sol, sep_sol, top_term

    leaf_all, sep_all, top_terms = lax.map(forward_group, (leaf_rhs, leaf_inv, couple, onehot, sep_rhs, sep_inv, sep_blk, top_cpl))
    top_start = rhs_top - jnp.sum(top_terms, axis=0)
    forward_half = jnp.zeros((R, TS), jnp.bfloat16)
    forward_full = []
    for block_id in range(NT):
        lower_rows = top_lower[block_id * S:(block_id + 1) * S, :]
        residue = top_start[:, block_id * S:(block_id + 1) * S] - jnp.dot(forward_half, lower_rows.T, preferred_element_type=jnp.float32)
        solved_block = jnp.dot(residue, top_inverse[block_id].T, precision=highest)
        forward_half = forward_half.at[:, block_id * S:(block_id + 1) * S].set(solved_block.astype(jnp.bfloat16))
        forward_full.append(solved_block)
    back_half = jnp.zeros((R, TS), jnp.bfloat16)
    back_full = [None] * NT
    for step_id in range(NT):
        block_id = NT - 1 - step_id
        lower_cols = top_lower[:, block_id * S:(block_id + 1) * S]
        residue = forward_full[block_id] - jnp.dot(back_half, lower_cols, preferred_element_type=jnp.float32)
        solved_block = jnp.dot(residue, top_inverse[block_id], precision=highest)
        back_half = back_half.at[:, block_id * S:(block_id + 1) * S].set(solved_block.astype(jnp.bfloat16))
        back_full[block_id] = solved_block
    coef_top = jnp.concatenate(back_full, axis=1)
    top_half = coef_top.astype(jnp.bfloat16)

    def backward_group(item):
        leaf_sol, sep_sol, linv, cpl, ohot, sinv, sblk, tcpl, dest_rows, cent, gpts, gpat = item
        back_start = sep_sol - jnp.einsum('rt,qbt->qrb', top_half.astype(jnp.float32), tcpl.astype(jnp.float32), precision=highest)
        solved = [None] * grp_size
        halves = [None] * grp_size
        for step_id in range(grp_size):
            target = grp_size - 1 - step_id
            residue = back_start[target]
            for source in range(target + 1, grp_size):
                residue = residue - jnp.dot(halves[source], sblk[target, source], preferred_element_type=jnp.float32)
            solved_block = jnp.dot(residue, sinv[target], precision=highest)
            solved[target] = solved_block
            halves[target] = solved_block.astype(jnp.bfloat16)
        sep_coef = jnp.stack(solved)
        sep_half = jnp.stack(halves)
        picked = jnp.einsum('ncq,qrb->ncrb', ohot, sep_half.astype(jnp.float32), precision=highest)
        reduced = jnp.einsum('ncrb,ncbs->nrs', picked, cpl.astype(jnp.float32), precision=highest)
        leaf_coef = jnp.einsum('nrs,nst->nrt', leaf_sol - reduced, linv, precision=highest)
        leaf_out = leaf_coef.astype(jnp.bfloat16).reshape(grp_size, NL, R, S)
        slot_rank = slot_ranks(dest_rows, grp_size)
        selector = (dest_rows[:, None, None, :] == jnp.arange(grp_size).astype(jnp.int32)[None, :, None, None]) & (slot_rank[:, None, None, :] == jnp.arange(CAP).astype(jnp.int32)[None, None, :, None])
        selector = selector.astype(jnp.float32)
        received = jnp.einsum('sdkj,sjrt->dskrt', selector, leaf_out.astype(jnp.float32), precision=highest)
        recv_centre = jnp.einsum('sdkj,sjct->dskct', selector, cent, precision=highest)

        def evaluate_device(dev_item):
            coef_dev, centre_dev, pts_dev, pat_dev = dev_item
            coef_all = coef_dev.reshape(grp_size * CAP, R, S)
            centre_all = centre_dev.reshape(grp_size * CAP, 3, S)
            pts_blocks = pts_dev.reshape(3, PB, S).transpose(1, 0, 2)

            def one_block(block_item):
                return kernel_block(coef_all, centre_all, block_item[0], block_item[1])

            blocks_out = lax.map(one_block, (pts_blocks, pat_dev))
            return blocks_out.transpose(1, 0, 2).reshape(R, P_SIZE)

        dev_values = lax.map(evaluate_device, (received, recv_centre, gpts, gpat))
        return leaf_coef, sep_coef, dev_values

    leaf_coefs, sep_coefs, all_values = lax.map(backward_group, (leaf_all, sep_all, leaf_inv, couple, onehot, sep_inv, sep_blk, top_cpl, dests, centres, group_points, pattern))
    coef_leaf = leaf_coefs.transpose(2, 0, 1, 3).reshape(R, LEAF_ROWS)
    coef_sep = sep_coefs.transpose(2, 0, 1, 3).reshape(R, SEP_ROWS)
    values = all_values.transpose(2, 0, 1, 3).reshape(R, POINTS)
    return (coef_leaf, coef_sep, coef_top, values)
```

```python
import functools

import jax
import jax.numpy as jnp
from jax import lax
from jax.sharding import PartitionSpec as P
from jax.experimental import pallas as pl
from jax.experimental.pallas import tpu as pltpu

MESH = pl.DeviceIdType.MESH

CAP = 2


highest = lax.Precision.HIGHEST
support_sq = 0.25


def split_up(shard, dim, peers):
    dims = shard.shape
    pieces = shard.reshape(*dims[:dim], peers, dims[dim] // peers, *dims[dim + 1 :])
    return jnp.moveaxis(pieces, dim, 0)


def sum_at_owner(shard, axis, dim):
    pieces = split_up(shard, dim, lax.axis_size(axis))
    arrived = lax.all_to_all(pieces, axis, split_axis=0, concat_axis=0, tiled=True)
    return arrived.astype(jnp.float32).sum(axis=0)


def from_root(shard, axis, root):
    return lax.dynamic_index_in_dim(lax.all_gather(shard, axis), root, 0, keepdims=False)


def copy_for_each(shard, axis):
    copies = jnp.broadcast_to(shard, (lax.axis_size(axis), *shard.shape))
    return lax.all_to_all(copies, axis, split_axis=0, concat_axis=0, tiled=True)


def over_copies(shard, axis):
    return copy_for_each(shard, axis).astype(jnp.float32).sum(axis=0)


def joined_along(pieces, dim):
    dims = list(pieces.shape[1:])
    dims[dim] *= pieces.shape[0]
    return jnp.moveaxis(pieces, 0, dim).reshape(dims)


def gather_directly(shard, axis, dim):
    pieces = copy_for_each(shard, axis)
    return joined_along(pieces, dim)


def _nt(a, b):
    return lax.dot_general(a, b, (((1,), (1,)), ((), ())), preferred_element_type=jnp.float32)


def _nn(a, b):
    return lax.dot_general(a, b, (((1,), (0,)), ((), ())), preferred_element_type=jnp.float32)


def _nt_exact(a, b):
    return lax.dot_general(
        a, b, (((1,), (1,)), ((), ())), precision=highest, preferred_element_type=jnp.float32
    )


def _nn_exact(a, b):
    return lax.dot_general(
        a, b, (((1,), (0,)), ((), ())), precision=highest, preferred_element_type=jnp.float32
    )


def _greet_group(n, leaf, me):
    barrier = pltpu.get_barrier_semaphore()
    for r in range(n):
        @pl.when(me != r)
        def _():
            pl.semaphore_signal(barrier, inc=1, device_id=(leaf, r), device_id_type=MESH)
    pl.semaphore_wait(barrier, n - 1)


def _block_copy(halves, q, dest, send_sem, recv_sem, leaf):
    return pltpu.make_async_remote_copy(
        src_ref=halves.at[q],
        dst_ref=halves.at[q],
        send_sem=send_sem,
        recv_sem=recv_sem.at[q],
        device_id=(leaf, dest),
        device_id_type=MESH,
    )


def sep_forward_kernel(n, start_ref, inv_ref, blocks_ref, sol_ref, halves, resid, send_sem, recv_sem):
    me = lax.axis_index("grp")
    leaf = lax.axis_index("leaf")
    _greet_group(n, leaf, me)
    resid[...] = start_ref[...]

    def step(q, carry):
        @pl.when(me == q)
        def _():
            solved = _nt_exact(resid[...], inv_ref[...])
            sol_ref[...] = solved
            halves[q] = solved.astype(jnp.bfloat16)
            for k in range(1, n):
                @pl.when(q + k < n)
                def _():
                    _block_copy(halves, q, q + k, send_sem.at[k], recv_sem, leaf).start()
            for k in range(1, n):
                @pl.when(q + k < n)
                def _():
                    _block_copy(halves, q, q + k, send_sem.at[k], recv_sem, leaf).wait_send()

        @pl.when(me > q)
        def _():
            _block_copy(halves, q, q, send_sem.at[0], recv_sem, leaf).wait_recv()
            resid[...] = resid[...] - _nt(halves[q], blocks_ref[q])

        return carry

    lax.fori_loop(0, n, step, 0)


def sep_backward_kernel(n, start_ref, inv_ref, blocks_ref, sol_ref, table_ref, halves, resid, send_sem, recv_sem):
    me = lax.axis_index("grp")
    leaf = lax.axis_index("leaf")
    _greet_group(n, leaf, me)
    resid[...] = start_ref[...]

    def step(s, carry):
        q = n - 1 - s

        @pl.when(me == q)
        def _():
            solved = _nn_exact(resid[...], inv_ref[...])
            sol_ref[...] = solved
            halves[q] = solved.astype(jnp.bfloat16)
            for k in range(1, n):
                dest = lax.rem(q - k + n, n)
                _block_copy(halves, q, dest, send_sem.at[k], recv_sem, leaf).start()
            for k in range(1, n):
                dest = lax.rem(q - k + n, n)
                _block_copy(halves, q, dest, send_sem.at[k], recv_sem, leaf).wait_send()

        @pl.when(me != q)
        def _():
            _block_copy(halves, q, q, send_sem.at[0], recv_sem, leaf).wait_recv()

        @pl.when(me < q)
        def _():
            resid[...] = resid[...] - _nn(halves[q], blocks_ref[q])

        return carry

    lax.fori_loop(0, n, step, 0)
    table_ref[...] = halves[...]


def sep_solve(kind, start, inv, blocks, n):
    rows, width = start.shape
    vmem = pl.BlockSpec(memory_space=pltpu.VMEM)
    scratch = [
        pltpu.VMEM((n, rows, width), jnp.bfloat16),
        pltpu.VMEM((rows, width), jnp.float32),
        pltpu.SemaphoreType.DMA((n,)),
        pltpu.SemaphoreType.DMA((n,)),
    ]
    sol_shape = jax.ShapeDtypeStruct((rows, width), jnp.float32)
    params = dict(has_side_effects=True, vmem_limit_bytes=48 * 1024 * 1024)
    if kind == "forward":
        return pl.pallas_call(
            functools.partial(sep_forward_kernel, n),
            out_shape=sol_shape,
            in_specs=[vmem] * 3,
            out_specs=vmem,
            scratch_shapes=scratch,
            compiler_params=pltpu.CompilerParams(collective_id=0, **params),
        )(start, inv, blocks)
    return pl.pallas_call(
        functools.partial(sep_backward_kernel, n),
        out_shape=(sol_shape, jax.ShapeDtypeStruct((n, rows, width), jnp.bfloat16)),
        in_specs=[vmem] * 3,
        out_specs=(vmem, vmem),
        scratch_shapes=scratch,
        compiler_params=pltpu.CompilerParams(collective_id=1, **params),
    )(start, inv, blocks)


def slot_ranks(dest_rows, grp_size):
    onehot = (dest_rows[..., None] == jnp.arange(grp_size)).astype(jnp.int32)
    before = jnp.cumsum(onehot, axis=-2) - onehot
    return jnp.sum(before * onehot, axis=-1)


def evaluate(coef_all, centre_all, block_points, block_mask):
    dist = jnp.zeros((centre_all.shape[0], centre_all.shape[2], block_points.shape[1]), jnp.float32)
    for comp in range(3):
        delta = centre_all[:, comp, :, None] - block_points[None, comp, None, :]
        dist = dist + delta * delta
    weight = jnp.maximum(1.0 - dist / support_sq, 0.0) ** 3
    kernel = (weight * block_mask.astype(jnp.float32)[:, None, None]).astype(jnp.bfloat16)
    return jnp.einsum("krs,ksp->rp", coef_all, kernel, preferred_element_type=jnp.float32)


def on_device(
    rhs_leaf,
    rhs_sep,
    rhs_top,
    leaf_inverse,
    leaf_coupling,
    leaf_targets,
    sep_inverse,
    sep_blocks,
    top_coupling,
    top_inverse,
    top_lower,
    dest_map,
    centers,
    points,
    eval_pattern,
):
    grp_size = lax.axis_size("grp")
    my_index = lax.axis_index("grp")
    blocks_here = leaf_inverse.shape[0]
    snapshots = rhs_leaf.shape[0]
    span = leaf_inverse.shape[1]
    slot_count = CAP
    leaf_rhs = rhs_leaf.reshape(snapshots, blocks_here, span).transpose(1, 0, 2)
    leaf_sol = jnp.einsum("nrs,nts->nrt", leaf_rhs, leaf_inverse, precision=highest)
    leaf_half = leaf_sol.astype(jnp.bfloat16)
    partial_value = jnp.einsum(
        "nrs,ncbs->ncrb", leaf_half, leaf_coupling, preferred_element_type=jnp.float32
    )
    onehot = (leaf_targets[:, :, None] == jnp.arange(grp_size)[None, None, :]).astype(jnp.float32)
    picked = onehot
    shared = sum_at_owner(
        jnp.einsum("ncq,ncrb->qrb", picked, partial_value, precision=highest).astype(jnp.bfloat16),
        "grp",
        0,
    )
    sep_start = rhs_sep - shared[0]
    inverse_own = sep_inverse[0]
    own_blocks = sep_blocks[0]

    sep_sol = sep_solve("forward", sep_start, inverse_own, own_blocks, grp_size)
    sep_half = sep_sol.astype(jnp.bfloat16)
    top_term = jnp.dot(sep_half, top_coupling, preferred_element_type=jnp.float32)
    top_part = sum_at_owner(top_term.astype(jnp.bfloat16), "grp", 1)
    top_part = over_copies(top_part.astype(jnp.bfloat16), "leaf").astype(jnp.float32)
    top_total = gather_directly(top_part.astype(jnp.bfloat16), "grp", 1).astype(top_part.dtype)
    top_start = rhs_top - top_total
    top_count = top_inverse.shape[0]
    top_span = top_inverse.shape[1]

    def top_forward(block_id, carry):
        half_all, full_all = carry
        lower_rows = lax.dynamic_slice_in_dim(top_lower, block_id * top_span, top_span, 0)
        residue = lax.dynamic_slice_in_dim(
            top_start, block_id * top_span, top_span, 1
        ) - lax.dot_general(
            half_all, lower_rows, (((1,), (1,)), ((), ())), preferred_element_type=jnp.float32
        )
        inverse_block = lax.dynamic_index_in_dim(top_inverse, block_id, 0, keepdims=False)
        solved_block = jnp.dot(residue, inverse_block.T, precision=highest)
        half_all = lax.dynamic_update_slice_in_dim(
            half_all, solved_block.astype(jnp.bfloat16), block_id * top_span, 1
        )
        full_all = lax.dynamic_update_slice_in_dim(full_all, solved_block, block_id * top_span, 1)
        return (half_all, full_all)

    empty_half = jnp.zeros(top_start.shape, jnp.bfloat16)
    empty_full = jnp.zeros(top_start.shape, jnp.float32)
    leftover_half, top_fwd = lax.fori_loop(0, top_count, top_forward, (empty_half, empty_full))

    def top_backward(step_id, carry):
        half_all, full_all = carry
        block_id = top_count - 1 - step_id
        lower_cols = lax.dynamic_slice_in_dim(top_lower, block_id * top_span, top_span, 1)
        residue = lax.dynamic_slice_in_dim(top_fwd, block_id * top_span, top_span, 1) - jnp.dot(
            half_all, lower_cols, preferred_element_type=jnp.float32
        )
        inverse_block = lax.dynamic_index_in_dim(top_inverse, block_id, 0, keepdims=False)
        solved_block = jnp.dot(residue, inverse_block, precision=highest)
        half_all = lax.dynamic_update_slice_in_dim(
            half_all, solved_block.astype(jnp.bfloat16), block_id * top_span, 1
        )
        full_all = lax.dynamic_update_slice_in_dim(full_all, solved_block, block_id * top_span, 1)
        return (half_all, full_all)

    top_half, coef_top = lax.fori_loop(0, top_count, top_backward, (empty_half, empty_full))
    back_start = sep_sol - lax.dot_general(
        top_half, top_coupling, (((1,), (1,)), ((), ())), preferred_element_type=jnp.float32
    )

    coef_sep, known_table = sep_solve("backward", back_start, inverse_own, own_blocks, grp_size)
    picked = jnp.einsum(
        "ncq,qrb->ncrb",
        onehot.astype(jnp.bfloat16),
        known_table,
        preferred_element_type=jnp.float32,
    ).astype(jnp.bfloat16)
    reduced = jnp.einsum(
        "ncrb,ncbs->nrs", picked, leaf_coupling, preferred_element_type=jnp.float32
    )
    leaf_coef = jnp.einsum("nrs,nst->nrt", leaf_sol - reduced, leaf_inverse, precision=highest)
    coef_leaf = leaf_coef.transpose(1, 0, 2).reshape(snapshots, blocks_here * span)
    leaf_out = leaf_coef.astype(jnp.bfloat16)
    slot_ids = jnp.arange(slot_count)
    grp_ids = jnp.arange(grp_size)
    own_dest = dest_map[:, 0]
    slot_rank = slot_ranks(own_dest[None, :], grp_size)[0]
    selector = (own_dest[None, None, :] == grp_ids[:, None, None]) & (
        slot_rank[None, None, :] == slot_ids[None, :, None]
    )
    send_coef = jnp.einsum(
        "dkj,jrt->dkrt", selector.astype(jnp.bfloat16), leaf_out, preferred_element_type=jnp.float32
    ).astype(jnp.bfloat16)
    send_centre = jnp.einsum(
        "dkj,jct->dkct", selector.astype(jnp.float32), centers, precision=highest
    )
    received, recv_centre = (
        lax.all_to_all(send_coef, "grp", split_axis=0, concat_axis=0, tiled=True),
        lax.all_to_all(
            send_centre.astype(jnp.bfloat16), "grp", split_axis=0, concat_axis=0, tiled=True
        ).astype(send_centre.dtype),
    )
    slot_total = grp_size * slot_count
    coef_all = received.reshape(slot_total, snapshots, span)
    centre_all = recv_centre.reshape(slot_total, 3, span)
    point_blocks = eval_pattern.shape[0]
    pts_blocks = points[0].reshape(3, point_blocks, span).transpose(1, 0, 2)

    def one_block(block_item):
        return evaluate(coef_all, centre_all, block_item[0], block_item[1])

    blocks_out = lax.map(one_block, (pts_blocks, eval_pattern))
    values = blocks_out.transpose(1, 0, 2).reshape(snapshots, point_blocks * span)
    return (coef_leaf, coef_sep, coef_top, values)


def solution(mesh):
    in_specs = (
        P(None, ("leaf", "grp")),
        P(None, ("leaf", "grp")),
        P(),
        P(("leaf", "grp"), None, None),
        P(("leaf", "grp"), None, None, None),
        P(("leaf", "grp"), None),
        P(("leaf", "grp"), None, None),
        P(("leaf", "grp"), None, None, None),
        P(("leaf", "grp"), None),
        P(),
        P(),
        P(("leaf", "grp"), None),
        P(("leaf", "grp"), None, None),
        P(("leaf", "grp"), None, None),
        P(("leaf", "grp"), None),
    )
    out_specs = (P(None, ("leaf", "grp")), P(None, ("leaf", "grp")), P(), P(None, ("leaf", "grp")))
    return jax.shard_map(
        on_device, mesh=mesh, in_specs=in_specs, out_specs=out_specs, check_vma=False
    )
```

```python
import functools

import jax
import jax.numpy as jnp
from jax import lax
from jax.sharding import PartitionSpec as P
from jax.experimental import pallas as pl
from jax.experimental.pallas import tpu as pltpu

MESH = pl.DeviceIdType.MESH

CAP = 2


highest = lax.Precision.HIGHEST
support_sq = 0.25


def split_up(shard, dim, peers):
    dims = shard.shape
    pieces = shard.reshape(*dims[:dim], peers, dims[dim] // peers, *dims[dim + 1 :])
    return jnp.moveaxis(pieces, dim, 0)


def sum_at_owner(shard, axis, dim):
    pieces = split_up(shard, dim, lax.axis_size(axis))
    arrived = lax.all_to_all(pieces, axis, split_axis=0, concat_axis=0, tiled=True)
    return arrived.astype(jnp.float32).sum(axis=0)


def from_root(shard, axis, root):
    return lax.dynamic_index_in_dim(lax.all_gather(shard, axis), root, 0, keepdims=False)


def copy_for_each(shard, axis):
    copies = jnp.broadcast_to(shard, (lax.axis_size(axis), *shard.shape))
    return lax.all_to_all(copies, axis, split_axis=0, concat_axis=0, tiled=True)


def over_copies(shard, axis):
    return copy_for_each(shard, axis).astype(jnp.float32).sum(axis=0)


def joined_along(pieces, dim):
    dims = list(pieces.shape[1:])
    dims[dim] *= pieces.shape[0]
    return jnp.moveaxis(pieces, 0, dim).reshape(dims)


def gather_directly(shard, axis, dim):
    pieces = copy_for_each(shard, axis)
    return joined_along(pieces, dim)


def _nt(a, b):
    return lax.dot_general(a, b, (((1,), (1,)), ((), ())), preferred_element_type=jnp.float32)


def _nn(a, b):
    return lax.dot_general(a, b, (((1,), (0,)), ((), ())), preferred_element_type=jnp.float32)


def _nt_exact(a, b):
    return lax.dot_general(
        a, b, (((1,), (1,)), ((), ())), precision=highest, preferred_element_type=jnp.float32
    )


def _nn_exact(a, b):
    return lax.dot_general(
        a, b, (((1,), (0,)), ((), ())), precision=highest, preferred_element_type=jnp.float32
    )


def _greet_group(n, leaf, me):
    barrier = pltpu.get_barrier_semaphore()
    for r in range(n):
        @pl.when(me != r)
        def _():
            pl.semaphore_signal(barrier, inc=1, device_id=(leaf, r), device_id_type=MESH)
    pl.semaphore_wait(barrier, n - 1)


def _block_copy(halves, q, dest, send_sem, recv_sem, leaf):
    return pltpu.make_async_remote_copy(
        src_ref=halves.at[q],
        dst_ref=halves.at[q],
        send_sem=send_sem,
        recv_sem=recv_sem.at[q],
        device_id=(leaf, dest),
        device_id_type=MESH,
    )


def sep_forward_kernel(n, start_ref, inv_ref, blocks_ref, sol_ref, halves, resid, send_sem, recv_sem):
    me = lax.axis_index("grp")
    leaf = lax.axis_index("leaf")
    _greet_group(n, leaf, me)
    resid[...] = start_ref[...]

    def step(q, carry):
        @pl.when(me == q)
        def _():
            solved = _nt_exact(resid[...], inv_ref[...])
            sol_ref[...] = solved
            halves[q] = solved.astype(jnp.bfloat16)
            for k in range(1, n):
                @pl.when(q + k < n)
                def _():
                    _block_copy(halves, q, q + k, send_sem.at[k], recv_sem, leaf).start()
            for k in range(1, n):
                @pl.when(q + k < n)
                def _():
                    _block_copy(halves, q, q + k, send_sem.at[k], recv_sem, leaf).wait_send()

        @pl.when(me > q)
        def _():
            _block_copy(halves, q, q, send_sem.at[0], recv_sem, leaf).wait_recv()
            resid[...] = resid[...] - _nt(halves[q], blocks_ref[q])

        return carry

    lax.fori_loop(0, n, step, 0)


def sep_backward_kernel(n, start_ref, inv_ref, blocks_ref, sol_ref, table_ref, halves, resid, send_sem, recv_sem):
    me = lax.axis_index("grp")
    leaf = lax.axis_index("leaf")
    _greet_group(n, leaf, me)
    resid[...] = start_ref[...]

    def step(s, carry):
        q = n - 1 - s

        @pl.when(me == q)
        def _():
            solved = _nn_exact(resid[...], inv_ref[...])
            sol_ref[...] = solved
            halves[q] = solved.astype(jnp.bfloat16)
            for k in range(1, n):
                dest = lax.rem(q - k + n, n)
                _block_copy(halves, q, dest, send_sem.at[k], recv_sem, leaf).start()
            for k in range(1, n):
                dest = lax.rem(q - k + n, n)
                _block_copy(halves, q, dest, send_sem.at[k], recv_sem, leaf).wait_send()

        @pl.when(me != q)
        def _():
            _block_copy(halves, q, q, send_sem.at[0], recv_sem, leaf).wait_recv()

        @pl.when(me < q)
        def _():
            resid[...] = resid[...] - _nn(halves[q], blocks_ref[q])

        return carry

    lax.fori_loop(0, n, step, 0)
    table_ref[...] = halves[...]


def sep_solve(kind, start, inv, blocks, n):
    rows, width = start.shape
    vmem = pl.BlockSpec(memory_space=pltpu.VMEM)
    scratch = [
        pltpu.VMEM((n, rows, width), jnp.bfloat16),
        pltpu.VMEM((rows, width), jnp.float32),
        pltpu.SemaphoreType.DMA((n,)),
        pltpu.SemaphoreType.DMA((n,)),
    ]
    sol_shape = jax.ShapeDtypeStruct((rows, width), jnp.float32)
    params = dict(has_side_effects=True, vmem_limit_bytes=48 * 1024 * 1024)
    if kind == "forward":
        return pl.pallas_call(
            functools.partial(sep_forward_kernel, n),
            out_shape=sol_shape,
            in_specs=[vmem] * 3,
            out_specs=vmem,
            scratch_shapes=scratch,
            compiler_params=pltpu.CompilerParams(collective_id=0, **params),
        )(start, inv, blocks)
    return pl.pallas_call(
        functools.partial(sep_backward_kernel, n),
        out_shape=(sol_shape, jax.ShapeDtypeStruct((n, rows, width), jnp.bfloat16)),
        in_specs=[vmem] * 3,
        out_specs=(vmem, vmem),
        scratch_shapes=scratch,
        compiler_params=pltpu.CompilerParams(collective_id=1, **params),
    )(start, inv, blocks)


def top_solve_kernel(nt, span, start_ref, inv_ref, lower_ref, coef_ref, half_ref, fwd_half, fwd_full):
    for t in range(nt):
        cols = slice(t * span, (t + 1) * span)
        residue = start_ref[:, cols]
        if t > 0:
            residue = residue - _nt(fwd_half[:, : t * span], lower_ref[cols, : t * span])
        solved = _nt_exact(residue, inv_ref[t])
        fwd_full[:, cols] = solved
        fwd_half[:, cols] = solved.astype(jnp.bfloat16)
    for t in reversed(range(nt)):
        cols = slice(t * span, (t + 1) * span)
        residue = fwd_full[:, cols]
        if t < nt - 1:
            residue = residue - _nn(half_ref[:, (t + 1) * span :], lower_ref[(t + 1) * span :, cols])
        solved = _nn_exact(residue, inv_ref[t])
        coef_ref[:, cols] = solved
        half_ref[:, cols] = solved.astype(jnp.bfloat16)


def top_solve(top_start, top_inverse, top_lower):
    nt, span = top_inverse.shape[0], top_inverse.shape[1]
    rows, width = top_start.shape
    vmem = pl.BlockSpec(memory_space=pltpu.VMEM)
    return pl.pallas_call(
        functools.partial(top_solve_kernel, nt, span),
        out_shape=(
            jax.ShapeDtypeStruct((rows, width), jnp.float32),
            jax.ShapeDtypeStruct((rows, width), jnp.bfloat16),
        ),
        in_specs=[vmem] * 3,
        out_specs=(vmem, vmem),
        scratch_shapes=[
            pltpu.VMEM((rows, width), jnp.bfloat16),
            pltpu.VMEM((rows, width), jnp.float32),
        ],
        compiler_params=pltpu.CompilerParams(vmem_limit_bytes=48 * 1024 * 1024),
    )(top_start, top_inverse, top_lower)


def slot_ranks(dest_rows, grp_size):
    onehot = (dest_rows[..., None] == jnp.arange(grp_size)).astype(jnp.int32)
    before = jnp.cumsum(onehot, axis=-2) - onehot
    return jnp.sum(before * onehot, axis=-1)


def evaluate(coef_all, centre_all, block_points, block_mask):
    dist = jnp.zeros((centre_all.shape[0], centre_all.shape[2], block_points.shape[1]), jnp.float32)
    for comp in range(3):
        delta = centre_all[:, comp, :, None] - block_points[None, comp, None, :]
        dist = dist + delta * delta
    weight = jnp.maximum(1.0 - dist / support_sq, 0.0) ** 3
    kernel = (weight * block_mask.astype(jnp.float32)[:, None, None]).astype(jnp.bfloat16)
    return jnp.einsum("krs,ksp->rp", coef_all, kernel, preferred_element_type=jnp.float32)


def on_device(
    rhs_leaf,
    rhs_sep,
    rhs_top,
    leaf_inverse,
    leaf_coupling,
    leaf_targets,
    sep_inverse,
    sep_blocks,
    top_coupling,
    top_inverse,
    top_lower,
    dest_map,
    centers,
    points,
    eval_pattern,
):
    grp_size = lax.axis_size("grp")
    my_index = lax.axis_index("grp")
    blocks_here = leaf_inverse.shape[0]
    snapshots = rhs_leaf.shape[0]
    span = leaf_inverse.shape[1]
    slot_count = CAP
    leaf_rhs = rhs_leaf.reshape(snapshots, blocks_here, span).transpose(1, 0, 2)
    leaf_sol = jnp.einsum("nrs,nts->nrt", leaf_rhs, leaf_inverse, precision=highest)
    leaf_half = leaf_sol.astype(jnp.bfloat16)
    partial_value = jnp.einsum(
        "nrs,ncbs->ncrb", leaf_half, leaf_coupling, preferred_element_type=jnp.float32
    )
    onehot = (leaf_targets[:, :, None] == jnp.arange(grp_size)[None, None, :]).astype(jnp.float32)
    picked = onehot
    shared = sum_at_owner(
        jnp.einsum("ncq,ncrb->qrb", picked, partial_value, precision=highest).astype(jnp.bfloat16),
        "grp",
        0,
    )
    sep_start = rhs_sep - shared[0]
    inverse_own = sep_inverse[0]
    own_blocks = sep_blocks[0]

    sep_sol = sep_solve("forward", sep_start, inverse_own, own_blocks, grp_size)
    sep_half = sep_sol.astype(jnp.bfloat16)
    top_term = jnp.dot(sep_half, top_coupling, preferred_element_type=jnp.float32)
    top_part = sum_at_owner(top_term.astype(jnp.bfloat16), "grp", 1)
    top_part = over_copies(top_part.astype(jnp.bfloat16), "leaf").astype(jnp.float32)
    top_total = gather_directly(top_part.astype(jnp.bfloat16), "grp", 1).astype(top_part.dtype)
    top_start = rhs_top - top_total
    coef_top, top_half = top_solve(top_start, top_inverse, top_lower)
    back_start = sep_sol - lax.dot_general(
        top_half, top_coupling, (((1,), (1,)), ((), ())), preferred_element_type=jnp.float32
    )

    coef_sep, known_table = sep_solve("backward", back_start, inverse_own, own_blocks, grp_size)
    picked = jnp.einsum(
        "ncq,qrb->ncrb",
        onehot.astype(jnp.bfloat16),
        known_table,
        preferred_element_type=jnp.float32,
    ).astype(jnp.bfloat16)
    reduced = jnp.einsum(
        "ncrb,ncbs->nrs", picked, leaf_coupling, preferred_element_type=jnp.float32
    )
    leaf_coef = jnp.einsum("nrs,nst->nrt", leaf_sol - reduced, leaf_inverse, precision=highest)
    coef_leaf = leaf_coef.transpose(1, 0, 2).reshape(snapshots, blocks_here * span)
    leaf_out = leaf_coef.astype(jnp.bfloat16)
    slot_ids = jnp.arange(slot_count)
    grp_ids = jnp.arange(grp_size)
    own_dest = dest_map[:, 0]
    slot_rank = slot_ranks(own_dest[None, :], grp_size)[0]
    selector = (own_dest[None, None, :] == grp_ids[:, None, None]) & (
        slot_rank[None, None, :] == slot_ids[None, :, None]
    )
    send_coef = jnp.einsum(
        "dkj,jrt->dkrt", selector.astype(jnp.bfloat16), leaf_out, preferred_element_type=jnp.float32
    ).astype(jnp.bfloat16)
    send_centre = jnp.einsum(
        "dkj,jct->dkct", selector.astype(jnp.float32), centers, precision=highest
    )
    received, recv_centre = (
        lax.all_to_all(send_coef, "grp", split_axis=0, concat_axis=0, tiled=True),
        lax.all_to_all(
            send_centre.astype(jnp.bfloat16), "grp", split_axis=0, concat_axis=0, tiled=True
        ).astype(send_centre.dtype),
    )
    slot_total = grp_size * slot_count
    coef_all = received.reshape(slot_total, snapshots, span)
    centre_all = recv_centre.reshape(slot_total, 3, span)
    point_blocks = eval_pattern.shape[0]
    pts_blocks = points[0].reshape(3, point_blocks, span).transpose(1, 0, 2)

    def one_block(block_item):
        return evaluate(coef_all, centre_all, block_item[0], block_item[1])

    blocks_out = lax.map(one_block, (pts_blocks, eval_pattern))
    values = blocks_out.transpose(1, 0, 2).reshape(snapshots, point_blocks * span)
    return (coef_leaf, coef_sep, coef_top, values)


def solution(mesh):
    in_specs = (
        P(None, ("leaf", "grp")),
        P(None, ("leaf", "grp")),
        P(),
        P(("leaf", "grp"), None, None),
        P(("leaf", "grp"), None, None, None),
        P(("leaf", "grp"), None),
        P(("leaf", "grp"), None, None),
        P(("leaf", "grp"), None, None, None),
        P(("leaf", "grp"), None),
        P(),
        P(),
        P(("leaf", "grp"), None),
        P(("leaf", "grp"), None, None),
        P(("leaf", "grp"), None, None),
        P(("leaf", "grp"), None),
    )
    out_specs = (P(None, ("leaf", "grp")), P(None, ("leaf", "grp")), P(), P(None, ("leaf", "grp")))
    return jax.shard_map(
        on_device, mesh=mesh, in_specs=in_specs, out_specs=out_specs, check_vma=False
    )
```

```python
import functools

import jax
import jax.numpy as jnp
from jax import lax
from jax.sharding import PartitionSpec as P
from jax.experimental import pallas as pl
from jax.experimental.pallas import tpu as pltpu

MESH = pl.DeviceIdType.MESH

CAP = 2


highest = lax.Precision.HIGHEST
support_sq = 0.25


def split_up(shard, dim, peers):
    dims = shard.shape
    pieces = shard.reshape(*dims[:dim], peers, dims[dim] // peers, *dims[dim + 1 :])
    return jnp.moveaxis(pieces, dim, 0)


def sum_at_owner(shard, axis, dim):
    pieces = split_up(shard, dim, lax.axis_size(axis))
    arrived = lax.all_to_all(pieces, axis, split_axis=0, concat_axis=0, tiled=True)
    return arrived.astype(jnp.float32).sum(axis=0)


def from_root(shard, axis, root):
    return lax.dynamic_index_in_dim(lax.all_gather(shard, axis), root, 0, keepdims=False)


def copy_for_each(shard, axis):
    copies = jnp.broadcast_to(shard, (lax.axis_size(axis), *shard.shape))
    return lax.all_to_all(copies, axis, split_axis=0, concat_axis=0, tiled=True)


def over_copies(shard, axis):
    return copy_for_each(shard, axis).astype(jnp.float32).sum(axis=0)


def joined_along(pieces, dim):
    dims = list(pieces.shape[1:])
    dims[dim] *= pieces.shape[0]
    return jnp.moveaxis(pieces, 0, dim).reshape(dims)


def gather_directly(shard, axis, dim):
    pieces = copy_for_each(shard, axis)
    return joined_along(pieces, dim)


def _nt(a, b):
    return lax.dot_general(a, b, (((1,), (1,)), ((), ())), preferred_element_type=jnp.float32)


def _nn(a, b):
    return lax.dot_general(a, b, (((1,), (0,)), ((), ())), preferred_element_type=jnp.float32)


def _nt_exact(a, b):
    return lax.dot_general(
        a, b, (((1,), (1,)), ((), ())), precision=highest, preferred_element_type=jnp.float32
    )


def _nn_exact(a, b):
    return lax.dot_general(
        a, b, (((1,), (0,)), ((), ())), precision=highest, preferred_element_type=jnp.float32
    )


def _greet_group(n, leaf, me):
    barrier = pltpu.get_barrier_semaphore()
    for r in range(n):
        @pl.when(me != r)
        def _():
            pl.semaphore_signal(barrier, inc=1, device_id=(leaf, r), device_id_type=MESH)
    pl.semaphore_wait(barrier, n - 1)


def _block_copy(halves, q, dest, send_sem, recv_sem, leaf):
    return pltpu.make_async_remote_copy(
        src_ref=halves.at[q],
        dst_ref=halves.at[q],
        send_sem=send_sem,
        recv_sem=recv_sem.at[q],
        device_id=(leaf, dest),
        device_id_type=MESH,
    )


def sep_forward_kernel(n, start_ref, inv_ref, blocks_ref, sol_ref, halves, resid, send_sem, recv_sem):
    me = lax.axis_index("grp")
    leaf = lax.axis_index("leaf")
    _greet_group(n, leaf, me)
    resid[...] = start_ref[...]

    def step(q, carry):
        @pl.when(me == q)
        def _():
            solved = _nt_exact(resid[...], inv_ref[...])
            sol_ref[...] = solved
            halves[q] = solved.astype(jnp.bfloat16)
            for k in range(1, n):
                @pl.when(q + k < n)
                def _():
                    _block_copy(halves, q, q + k, send_sem.at[k], recv_sem, leaf).start()
            for k in range(1, n):
                @pl.when(q + k < n)
                def _():
                    _block_copy(halves, q, q + k, send_sem.at[k], recv_sem, leaf).wait_send()

        @pl.when(me > q)
        def _():
            _block_copy(halves, q, q, send_sem.at[0], recv_sem, leaf).wait_recv()
            resid[...] = resid[...] - _nt(halves[q], blocks_ref[q])

        return carry

    lax.fori_loop(0, n, step, 0)


def sep_backward_kernel(n, start_ref, inv_ref, blocks_ref, sol_ref, table_ref, halves, resid, send_sem, recv_sem):
    me = lax.axis_index("grp")
    leaf = lax.axis_index("leaf")
    _greet_group(n, leaf, me)
    resid[...] = start_ref[...]

    def step(s, carry):
        q = n - 1 - s

        @pl.when(me == q)
        def _():
            solved = _nn_exact(resid[...], inv_ref[...])
            sol_ref[...] = solved
            halves[q] = solved.astype(jnp.bfloat16)
            for k in range(1, n):
                dest = lax.rem(q - k + n, n)
                _block_copy(halves, q, dest, send_sem.at[k], recv_sem, leaf).start()
            for k in range(1, n):
                dest = lax.rem(q - k + n, n)
                _block_copy(halves, q, dest, send_sem.at[k], recv_sem, leaf).wait_send()

        @pl.when(me != q)
        def _():
            _block_copy(halves, q, q, send_sem.at[0], recv_sem, leaf).wait_recv()

        @pl.when(me < q)
        def _():
            resid[...] = resid[...] - _nn(halves[q], blocks_ref[q])

        return carry

    lax.fori_loop(0, n, step, 0)
    table_ref[...] = halves[...]


def sep_solve(kind, start, inv, blocks, n):
    rows, width = start.shape
    vmem = pl.BlockSpec(memory_space=pltpu.VMEM)
    scratch = [
        pltpu.VMEM((n, rows, width), jnp.bfloat16),
        pltpu.VMEM((rows, width), jnp.float32),
        pltpu.SemaphoreType.DMA((n,)),
        pltpu.SemaphoreType.DMA((n,)),
    ]
    sol_shape = jax.ShapeDtypeStruct((rows, width), jnp.float32)
    params = dict(has_side_effects=True, vmem_limit_bytes=48 * 1024 * 1024)
    if kind == "forward":
        return pl.pallas_call(
            functools.partial(sep_forward_kernel, n),
            out_shape=sol_shape,
            in_specs=[vmem] * 3,
            out_specs=vmem,
            scratch_shapes=scratch,
            compiler_params=pltpu.CompilerParams(collective_id=0, **params),
        )(start, inv, blocks)
    return pl.pallas_call(
        functools.partial(sep_backward_kernel, n),
        out_shape=(sol_shape, jax.ShapeDtypeStruct((n, rows, width), jnp.bfloat16)),
        in_specs=[vmem] * 3,
        out_specs=(vmem, vmem),
        scratch_shapes=scratch,
        compiler_params=pltpu.CompilerParams(collective_id=1, **params),
    )(start, inv, blocks)


def top_solve_kernel(nt, span, start_ref, inv_ref, lower_ref, coef_ref, half_ref, fwd_half, fwd_full):
    for t in range(nt):
        cols = slice(t * span, (t + 1) * span)
        residue = start_ref[:, cols]
        if t > 0:
            residue = residue - _nt(fwd_half[:, : t * span], lower_ref[cols, : t * span])
        solved = _nt_exact(residue, inv_ref[t])
        fwd_full[:, cols] = solved
        fwd_half[:, cols] = solved.astype(jnp.bfloat16)
    for t in reversed(range(nt)):
        cols = slice(t * span, (t + 1) * span)
        residue = fwd_full[:, cols]
        if t < nt - 1:
            residue = residue - _nn(half_ref[:, (t + 1) * span :], lower_ref[(t + 1) * span :, cols])
        solved = _nn_exact(residue, inv_ref[t])
        coef_ref[:, cols] = solved
        half_ref[:, cols] = solved.astype(jnp.bfloat16)


def top_solve(top_start, top_inverse, top_lower):
    nt, span = top_inverse.shape[0], top_inverse.shape[1]
    rows, width = top_start.shape
    vmem = pl.BlockSpec(memory_space=pltpu.VMEM)
    return pl.pallas_call(
        functools.partial(top_solve_kernel, nt, span),
        out_shape=(
            jax.ShapeDtypeStruct((rows, width), jnp.float32),
            jax.ShapeDtypeStruct((rows, width), jnp.bfloat16),
        ),
        in_specs=[vmem] * 3,
        out_specs=(vmem, vmem),
        scratch_shapes=[
            pltpu.VMEM((rows, width), jnp.bfloat16),
            pltpu.VMEM((rows, width), jnp.float32),
        ],
        compiler_params=pltpu.CompilerParams(vmem_limit_bytes=48 * 1024 * 1024),
    )(top_start, top_inverse, top_lower)


def evaluate_kernel(slots, pattern_ref, coef_ref, centre_ref, column_ref, out_ref, acc):
    m = pl.program_id(0)
    acc[...] = jnp.zeros_like(acc)
    column = column_ref[0]

    def one_slot(s, carry):
        flag = pattern_ref[m, s]

        @pl.when(flag != 0)
        def _():
            centre = centre_ref[s]
            dist = jnp.zeros((column.shape[0], centre.shape[1]), jnp.float32)
            for comp in range(3):
                delta = centre[comp : comp + 1, :] - column[:, comp : comp + 1]
                dist = dist + delta * delta
            weight = jnp.maximum(1.0 - dist / support_sq, 0.0)
            weight = weight * weight * weight
            kernel = (weight * flag.astype(jnp.float32)).astype(jnp.bfloat16)
            acc[...] += _nt(coef_ref[s], kernel)

        return carry

    lax.fori_loop(0, slots, one_slot, 0)
    out_ref[...] = acc[...]


def evaluate_all(coef_all, centre_all, point_columns, pattern):
    slots, rows, span = coef_all.shape
    blocks = point_columns.shape[0]
    full = lambda shape: pl.BlockSpec(shape, lambda m, pat: (0,) * len(shape))
    grid_spec = pltpu.PrefetchScalarGridSpec(
        num_scalar_prefetch=1,
        grid=(blocks,),
        in_specs=[
            full(coef_all.shape),
            full(centre_all.shape),
            pl.BlockSpec((1, span, point_columns.shape[2]), lambda m, pat: (m, 0, 0)),
        ],
        out_specs=pl.BlockSpec((rows, span), lambda m, pat: (0, m)),
        scratch_shapes=[pltpu.VMEM((rows, span), jnp.float32)],
    )
    return pl.pallas_call(
        functools.partial(evaluate_kernel, slots),
        out_shape=jax.ShapeDtypeStruct((rows, blocks * span), jnp.float32),
        grid_spec=grid_spec,
    )(pattern, coef_all, centre_all, point_columns)


def slot_ranks(dest_rows, grp_size):
    onehot = (dest_rows[..., None] == jnp.arange(grp_size)).astype(jnp.int32)
    before = jnp.cumsum(onehot, axis=-2) - onehot
    return jnp.sum(before * onehot, axis=-1)


def evaluate(coef_all, centre_all, block_points, block_mask):
    dist = jnp.zeros((centre_all.shape[0], centre_all.shape[2], block_points.shape[1]), jnp.float32)
    for comp in range(3):
        delta = centre_all[:, comp, :, None] - block_points[None, comp, None, :]
        dist = dist + delta * delta
    weight = jnp.maximum(1.0 - dist / support_sq, 0.0) ** 3
    kernel = (weight * block_mask.astype(jnp.float32)[:, None, None]).astype(jnp.bfloat16)
    return jnp.einsum("krs,ksp->rp", coef_all, kernel, preferred_element_type=jnp.float32)


def on_device(
    rhs_leaf,
    rhs_sep,
    rhs_top,
    leaf_inverse,
    leaf_coupling,
    leaf_targets,
    sep_inverse,
    sep_blocks,
    top_coupling,
    top_inverse,
    top_lower,
    dest_map,
    centers,
    points,
    eval_pattern,
):
    grp_size = lax.axis_size("grp")
    my_index = lax.axis_index("grp")
    blocks_here = leaf_inverse.shape[0]
    snapshots = rhs_leaf.shape[0]
    span = leaf_inverse.shape[1]
    slot_count = CAP
    leaf_rhs = rhs_leaf.reshape(snapshots, blocks_here, span).transpose(1, 0, 2)
    leaf_sol = jnp.einsum("nrs,nts->nrt", leaf_rhs, leaf_inverse, precision=highest)
    leaf_half = leaf_sol.astype(jnp.bfloat16)
    partial_value = jnp.einsum(
        "nrs,ncbs->ncrb", leaf_half, leaf_coupling, preferred_element_type=jnp.float32
    )
    onehot = (leaf_targets[:, :, None] == jnp.arange(grp_size)[None, None, :]).astype(jnp.float32)
    picked = onehot
    shared = sum_at_owner(
        jnp.einsum("ncq,ncrb->qrb", picked, partial_value, precision=highest).astype(jnp.bfloat16),
        "grp",
        0,
    )
    sep_start = rhs_sep - shared[0]
    inverse_own = sep_inverse[0]
    own_blocks = sep_blocks[0]

    sep_sol = sep_solve("forward", sep_start, inverse_own, own_blocks, grp_size)
    sep_half = sep_sol.astype(jnp.bfloat16)
    top_term = jnp.dot(sep_half, top_coupling, preferred_element_type=jnp.float32)
    top_part = sum_at_owner(top_term.astype(jnp.bfloat16), "grp", 1)
    top_part = over_copies(top_part.astype(jnp.bfloat16), "leaf").astype(jnp.float32)
    top_total = gather_directly(top_part.astype(jnp.bfloat16), "grp", 1).astype(top_part.dtype)
    top_start = rhs_top - top_total
    coef_top, top_half = top_solve(top_start, top_inverse, top_lower)
    back_start = sep_sol - lax.dot_general(
        top_half, top_coupling, (((1,), (1,)), ((), ())), preferred_element_type=jnp.float32
    )

    coef_sep, known_table = sep_solve("backward", back_start, inverse_own, own_blocks, grp_size)
    picked = jnp.einsum(
        "ncq,qrb->ncrb",
        onehot.astype(jnp.bfloat16),
        known_table,
        preferred_element_type=jnp.float32,
    ).astype(jnp.bfloat16)
    reduced = jnp.einsum(
        "ncrb,ncbs->nrs", picked, leaf_coupling, preferred_element_type=jnp.float32
    )
    leaf_coef = jnp.einsum("nrs,nst->nrt", leaf_sol - reduced, leaf_inverse, precision=highest)
    coef_leaf = leaf_coef.transpose(1, 0, 2).reshape(snapshots, blocks_here * span)
    leaf_out = leaf_coef.astype(jnp.bfloat16)
    slot_ids = jnp.arange(slot_count)
    grp_ids = jnp.arange(grp_size)
    own_dest = dest_map[:, 0]
    slot_rank = slot_ranks(own_dest[None, :], grp_size)[0]
    selector = (own_dest[None, None, :] == grp_ids[:, None, None]) & (
        slot_rank[None, None, :] == slot_ids[None, :, None]
    )
    send_coef = jnp.einsum(
        "dkj,jrt->dkrt", selector.astype(jnp.bfloat16), leaf_out, preferred_element_type=jnp.float32
    ).astype(jnp.bfloat16)
    send_centre = jnp.einsum(
        "dkj,jct->dkct", selector.astype(jnp.float32), centers, precision=highest
    )
    received, recv_centre = (
        lax.all_to_all(send_coef, "grp", split_axis=0, concat_axis=0, tiled=True),
        lax.all_to_all(
            send_centre.astype(jnp.bfloat16), "grp", split_axis=0, concat_axis=0, tiled=True
        ).astype(send_centre.dtype),
    )
    slot_total = grp_size * slot_count
    coef_all = received.reshape(slot_total, snapshots, span)
    centre_all = recv_centre.reshape(slot_total, 3, span)
    point_blocks = eval_pattern.shape[0]
    point_columns = points[0].T.reshape(point_blocks, span, points.shape[1])
    values = evaluate_all(coef_all, centre_all, point_columns, eval_pattern)
    return (coef_leaf, coef_sep, coef_top, values)


def solution(mesh):
    in_specs = (
        P(None, ("leaf", "grp")),
        P(None, ("leaf", "grp")),
        P(),
        P(("leaf", "grp"), None, None),
        P(("leaf", "grp"), None, None, None),
        P(("leaf", "grp"), None),
        P(("leaf", "grp"), None, None),
        P(("leaf", "grp"), None, None, None),
        P(("leaf", "grp"), None),
        P(),
        P(),
        P(("leaf", "grp"), None),
        P(("leaf", "grp"), None, None),
        P(("leaf", "grp"), None, None),
        P(("leaf", "grp"), None),
    )
    out_specs = (P(None, ("leaf", "grp")), P(None, ("leaf", "grp")), P(), P(None, ("leaf", "grp")))
    return jax.shard_map(
        on_device, mesh=mesh, in_specs=in_specs, out_specs=out_specs, check_vma=False
    )
```

```python
import functools

import jax
import jax.numpy as jnp
from jax import lax
from jax.sharding import PartitionSpec as P
from jax.experimental import pallas as pl
from jax.experimental.pallas import tpu as pltpu

MESH = pl.DeviceIdType.MESH

CAP = 2


highest = lax.Precision.HIGHEST
support_sq = 0.25


def split_up(shard, dim, peers):
    dims = shard.shape
    pieces = shard.reshape(*dims[:dim], peers, dims[dim] // peers, *dims[dim + 1 :])
    return jnp.moveaxis(pieces, dim, 0)


def sum_at_owner(shard, axis, dim):
    pieces = split_up(shard, dim, lax.axis_size(axis))
    arrived = lax.all_to_all(pieces, axis, split_axis=0, concat_axis=0, tiled=True)
    return arrived.astype(jnp.float32).sum(axis=0)


def from_root(shard, axis, root):
    return lax.dynamic_index_in_dim(lax.all_gather(shard, axis), root, 0, keepdims=False)


def copy_for_each(shard, axis):
    copies = jnp.broadcast_to(shard, (lax.axis_size(axis), *shard.shape))
    return lax.all_to_all(copies, axis, split_axis=0, concat_axis=0, tiled=True)


def over_copies(shard, axis):
    return copy_for_each(shard, axis).astype(jnp.float32).sum(axis=0)


def joined_along(pieces, dim):
    dims = list(pieces.shape[1:])
    dims[dim] *= pieces.shape[0]
    return jnp.moveaxis(pieces, 0, dim).reshape(dims)


def gather_directly(shard, axis, dim):
    pieces = copy_for_each(shard, axis)
    return joined_along(pieces, dim)


def _nt(a, b):
    return lax.dot_general(a, b, (((1,), (1,)), ((), ())), preferred_element_type=jnp.float32)


def _nn(a, b):
    return lax.dot_general(a, b, (((1,), (0,)), ((), ())), preferred_element_type=jnp.float32)


def _nt_exact(a, b):
    return lax.dot_general(
        a, b, (((1,), (1,)), ((), ())), precision=highest, preferred_element_type=jnp.float32
    )


def _nn_exact(a, b):
    return lax.dot_general(
        a, b, (((1,), (0,)), ((), ())), precision=highest, preferred_element_type=jnp.float32
    )


def _greet_group(n, leaf, me):
    barrier = pltpu.get_barrier_semaphore()
    for r in range(n):
        @pl.when(me != r)
        def _():
            pl.semaphore_signal(barrier, inc=1, device_id=(leaf, r), device_id_type=MESH)
    pl.semaphore_wait(barrier, n - 1)


def _block_copy(halves, q, dest, send_sem, recv_sem, leaf):
    return pltpu.make_async_remote_copy(
        src_ref=halves.at[q],
        dst_ref=halves.at[q],
        send_sem=send_sem,
        recv_sem=recv_sem.at[q],
        device_id=(leaf, dest),
        device_id_type=MESH,
    )


def sep_forward_kernel(n, start_ref, inv_ref, blocks_ref, sol_ref, halves, resid, send_sem, recv_sem):
    me = lax.axis_index("grp")
    leaf = lax.axis_index("leaf")
    _greet_group(n, leaf, me)
    resid[...] = start_ref[...]

    def step(q, carry):
        @pl.when(me == q)
        def _():
            solved = _nt_exact(resid[...], inv_ref[...])
            sol_ref[...] = solved
            halves[q] = solved.astype(jnp.bfloat16)
            for k in range(1, n):
                @pl.when(q + k < n)
                def _():
                    _block_copy(halves, q, q + k, send_sem.at[k], recv_sem, leaf).start()
            for k in range(1, n):
                @pl.when(q + k < n)
                def _():
                    _block_copy(halves, q, q + k, send_sem.at[k], recv_sem, leaf).wait_send()

        @pl.when(me > q)
        def _():
            _block_copy(halves, q, q, send_sem.at[0], recv_sem, leaf).wait_recv()
            resid[...] = resid[...] - _nt(halves[q], blocks_ref[q])

        return carry

    lax.fori_loop(0, n, step, 0)


def sep_backward_kernel(n, start_ref, inv_ref, blocks_ref, sol_ref, table_ref, halves, resid, send_sem, recv_sem):
    me = lax.axis_index("grp")
    leaf = lax.axis_index("leaf")
    _greet_group(n, leaf, me)
    resid[...] = start_ref[...]

    def step(s, carry):
        q = n - 1 - s

        @pl.when(me == q)
        def _():
            solved = _nn_exact(resid[...], inv_ref[...])
            sol_ref[...] = solved
            halves[q] = solved.astype(jnp.bfloat16)
            for k in range(1, n):
                dest = lax.rem(q - k + n, n)
                _block_copy(halves, q, dest, send_sem.at[k], recv_sem, leaf).start()
            for k in range(1, n):
                dest = lax.rem(q - k + n, n)
                _block_copy(halves, q, dest, send_sem.at[k], recv_sem, leaf).wait_send()

        @pl.when(me != q)
        def _():
            _block_copy(halves, q, q, send_sem.at[0], recv_sem, leaf).wait_recv()

        @pl.when(me < q)
        def _():
            resid[...] = resid[...] - _nn(halves[q], blocks_ref[q])

        return carry

    lax.fori_loop(0, n, step, 0)
    table_ref[...] = halves[...]


def sep_solve(kind, start, inv, blocks, n):
    rows, width = start.shape
    vmem = pl.BlockSpec(memory_space=pltpu.VMEM)
    scratch = [
        pltpu.VMEM((n, rows, width), jnp.bfloat16),
        pltpu.VMEM((rows, width), jnp.float32),
        pltpu.SemaphoreType.DMA((n,)),
        pltpu.SemaphoreType.DMA((n,)),
    ]
    sol_shape = jax.ShapeDtypeStruct((rows, width), jnp.float32)
    params = dict(has_side_effects=True, vmem_limit_bytes=48 * 1024 * 1024)
    if kind == "forward":
        return pl.pallas_call(
            functools.partial(sep_forward_kernel, n),
            out_shape=sol_shape,
            in_specs=[vmem] * 3,
            out_specs=vmem,
            scratch_shapes=scratch,
            compiler_params=pltpu.CompilerParams(collective_id=0, **params),
        )(start, inv, blocks)
    return pl.pallas_call(
        functools.partial(sep_backward_kernel, n),
        out_shape=(sol_shape, jax.ShapeDtypeStruct((n, rows, width), jnp.bfloat16)),
        in_specs=[vmem] * 3,
        out_specs=(vmem, vmem),
        scratch_shapes=scratch,
        compiler_params=pltpu.CompilerParams(collective_id=1, **params),
    )(start, inv, blocks)


def top_solve_kernel(nt, span, start_ref, inv_ref, lower_ref, coef_ref, half_ref, fwd_half, fwd_full):
    for t in range(nt):
        cols = slice(t * span, (t + 1) * span)
        residue = start_ref[:, cols]
        if t > 0:
            residue = residue - _nt(fwd_half[:, : t * span], lower_ref[cols, : t * span])
        solved = _nt_exact(residue, inv_ref[t])
        fwd_full[:, cols] = solved
        fwd_half[:, cols] = solved.astype(jnp.bfloat16)
    for t in reversed(range(nt)):
        cols = slice(t * span, (t + 1) * span)
        residue = fwd_full[:, cols]
        if t < nt - 1:
            residue = residue - _nn(half_ref[:, (t + 1) * span :], lower_ref[(t + 1) * span :, cols])
        solved = _nn_exact(residue, inv_ref[t])
        coef_ref[:, cols] = solved
        half_ref[:, cols] = solved.astype(jnp.bfloat16)


def top_solve(top_start, top_inverse, top_lower):
    nt, span = top_inverse.shape[0], top_inverse.shape[1]
    rows, width = top_start.shape
    vmem = pl.BlockSpec(memory_space=pltpu.VMEM)
    return pl.pallas_call(
        functools.partial(top_solve_kernel, nt, span),
        out_shape=(
            jax.ShapeDtypeStruct((rows, width), jnp.float32),
            jax.ShapeDtypeStruct((rows, width), jnp.bfloat16),
        ),
        in_specs=[vmem] * 3,
        out_specs=(vmem, vmem),
        scratch_shapes=[
            pltpu.VMEM((rows, width), jnp.bfloat16),
            pltpu.VMEM((rows, width), jnp.float32),
        ],
        compiler_params=pltpu.CompilerParams(vmem_limit_bytes=48 * 1024 * 1024),
    )(top_start, top_inverse, top_lower)


def evaluate_kernel(slots, pattern_ref, coef_ref, centre_ref, column_ref, out_ref, acc, spread):
    m = pl.program_id(0)
    acc[...] = jnp.zeros_like(acc)
    column = column_ref[0]
    width = centre_ref.shape[2]
    for comp in range(3):
        spread[comp] = jnp.broadcast_to(column[:, comp : comp + 1], (column.shape[0], width))

    def one_slot(s, carry):
        @pl.when(pattern_ref[m, s] != 0)
        def _():
            centre = centre_ref[s]
            dist = None
            for comp in range(3):
                delta = centre[comp : comp + 1, :] - spread[comp]
                dist = delta * delta if dist is None else dist + delta * delta
            weight = jnp.maximum(1.0 - dist * (1.0 / support_sq), 0.0)
            kernel = (weight * weight * weight).astype(jnp.bfloat16)
            acc[...] += _nt(coef_ref[s], kernel)

        return carry

    lax.fori_loop(0, slots, one_slot, 0)
    out_ref[...] = acc[...]


def evaluate_all(coef_all, centre_all, point_columns, pattern):
    slots, rows, span = coef_all.shape
    blocks = point_columns.shape[0]
    full = lambda shape: pl.BlockSpec(shape, lambda m, pat: (0,) * len(shape))
    grid_spec = pltpu.PrefetchScalarGridSpec(
        num_scalar_prefetch=1,
        grid=(blocks,),
        in_specs=[
            full(coef_all.shape),
            full(centre_all.shape),
            pl.BlockSpec((1, span, point_columns.shape[2]), lambda m, pat: (m, 0, 0)),
        ],
        out_specs=pl.BlockSpec((rows, span), lambda m, pat: (0, m)),
        scratch_shapes=[
            pltpu.VMEM((rows, span), jnp.float32),
            pltpu.VMEM((3, span, centre_all.shape[2]), jnp.float32),
        ],
    )
    return pl.pallas_call(
        functools.partial(evaluate_kernel, slots),
        out_shape=jax.ShapeDtypeStruct((rows, blocks * span), jnp.float32),
        grid_spec=grid_spec,
    )(pattern, coef_all, centre_all, point_columns)


def slot_ranks(dest_rows, grp_size):
    onehot = (dest_rows[..., None] == jnp.arange(grp_size)).astype(jnp.int32)
    before = jnp.cumsum(onehot, axis=-2) - onehot
    return jnp.sum(before * onehot, axis=-1)


def evaluate(coef_all, centre_all, block_points, block_mask):
    dist = jnp.zeros((centre_all.shape[0], centre_all.shape[2], block_points.shape[1]), jnp.float32)
    for comp in range(3):
        delta = centre_all[:, comp, :, None] - block_points[None, comp, None, :]
        dist = dist + delta * delta
    weight = jnp.maximum(1.0 - dist / support_sq, 0.0) ** 3
    kernel = (weight * block_mask.astype(jnp.float32)[:, None, None]).astype(jnp.bfloat16)
    return jnp.einsum("krs,ksp->rp", coef_all, kernel, preferred_element_type=jnp.float32)


def on_device(
    rhs_leaf,
    rhs_sep,
    rhs_top,
    leaf_inverse,
    leaf_coupling,
    leaf_targets,
    sep_inverse,
    sep_blocks,
    top_coupling,
    top_inverse,
    top_lower,
    dest_map,
    centers,
    points,
    eval_pattern,
):
    grp_size = lax.axis_size("grp")
    my_index = lax.axis_index("grp")
    blocks_here = leaf_inverse.shape[0]
    snapshots = rhs_leaf.shape[0]
    span = leaf_inverse.shape[1]
    slot_count = CAP
    leaf_rhs = rhs_leaf.reshape(snapshots, blocks_here, span).transpose(1, 0, 2)
    leaf_sol = jnp.einsum("nrs,nts->nrt", leaf_rhs, leaf_inverse, precision=highest)
    leaf_half = leaf_sol.astype(jnp.bfloat16)
    partial_value = jnp.einsum(
        "nrs,ncbs->ncrb", leaf_half, leaf_coupling, preferred_element_type=jnp.float32
    )
    onehot = (leaf_targets[:, :, None] == jnp.arange(grp_size)[None, None, :]).astype(jnp.float32)
    picked = onehot
    shared = sum_at_owner(
        jnp.einsum("ncq,ncrb->qrb", picked, partial_value, precision=highest).astype(jnp.bfloat16),
        "grp",
        0,
    )
    sep_start = rhs_sep - shared[0]
    inverse_own = sep_inverse[0]
    own_blocks = sep_blocks[0]

    sep_sol = sep_solve("forward", sep_start, inverse_own, own_blocks, grp_size)
    sep_half = sep_sol.astype(jnp.bfloat16)
    top_term = jnp.dot(sep_half, top_coupling, preferred_element_type=jnp.float32)
    top_part = sum_at_owner(top_term.astype(jnp.bfloat16), "grp", 1)
    top_part = over_copies(top_part.astype(jnp.bfloat16), "leaf").astype(jnp.float32)
    top_total = gather_directly(top_part.astype(jnp.bfloat16), "grp", 1).astype(top_part.dtype)
    top_start = rhs_top - top_total
    coef_top, top_half = top_solve(top_start, top_inverse, top_lower)
    back_start = sep_sol - lax.dot_general(
        top_half, top_coupling, (((1,), (1,)), ((), ())), preferred_element_type=jnp.float32
    )

    coef_sep, known_table = sep_solve("backward", back_start, inverse_own, own_blocks, grp_size)
    picked = jnp.einsum(
        "ncq,qrb->ncrb",
        onehot.astype(jnp.bfloat16),
        known_table,
        preferred_element_type=jnp.float32,
    ).astype(jnp.bfloat16)
    reduced = jnp.einsum(
        "ncrb,ncbs->nrs", picked, leaf_coupling, preferred_element_type=jnp.float32
    )
    leaf_coef = jnp.einsum("nrs,nst->nrt", leaf_sol - reduced, leaf_inverse, precision=highest)
    coef_leaf = leaf_coef.transpose(1, 0, 2).reshape(snapshots, blocks_here * span)
    leaf_out = leaf_coef.astype(jnp.bfloat16)
    slot_ids = jnp.arange(slot_count)
    grp_ids = jnp.arange(grp_size)
    own_dest = dest_map[:, 0]
    slot_rank = slot_ranks(own_dest[None, :], grp_size)[0]
    selector = (own_dest[None, None, :] == grp_ids[:, None, None]) & (
        slot_rank[None, None, :] == slot_ids[None, :, None]
    )
    send_coef = jnp.einsum(
        "dkj,jrt->dkrt", selector.astype(jnp.bfloat16), leaf_out, preferred_element_type=jnp.float32
    ).astype(jnp.bfloat16)
    send_centre = jnp.einsum(
        "dkj,jct->dkct", selector.astype(jnp.float32), centers, precision=highest
    )
    received, recv_centre = (
        lax.all_to_all(send_coef, "grp", split_axis=0, concat_axis=0, tiled=True),
        lax.all_to_all(
            send_centre.astype(jnp.bfloat16), "grp", split_axis=0, concat_axis=0, tiled=True
        ).astype(send_centre.dtype),
    )
    slot_total = grp_size * slot_count
    coef_all = received.reshape(slot_total, snapshots, span)
    centre_all = recv_centre.reshape(slot_total, 3, span)
    point_blocks = eval_pattern.shape[0]
    point_columns = points[0].T.reshape(point_blocks, span, points.shape[1])
    values = evaluate_all(coef_all, centre_all, point_columns, eval_pattern)
    return (coef_leaf, coef_sep, coef_top, values)


def solution(mesh):
    in_specs = (
        P(None, ("leaf", "grp")),
        P(None, ("leaf", "grp")),
        P(),
        P(("leaf", "grp"), None, None),
        P(("leaf", "grp"), None, None, None),
        P(("leaf", "grp"), None),
        P(("leaf", "grp"), None, None),
        P(("leaf", "grp"), None, None, None),
        P(("leaf", "grp"), None),
        P(),
        P(),
        P(("leaf", "grp"), None),
        P(("leaf", "grp"), None, None),
        P(("leaf", "grp"), None, None),
        P(("leaf", "grp"), None),
    )
    out_specs = (P(None, ("leaf", "grp")), P(None, ("leaf", "grp")), P(), P(None, ("leaf", "grp")))
    return jax.shard_map(
        on_device, mesh=mesh, in_specs=in_specs, out_specs=out_specs, check_vma=False
    )
```

```python
import functools

import jax
import jax.numpy as jnp
from jax import lax
from jax.sharding import PartitionSpec as P
from jax.experimental import pallas as pl
from jax.experimental.pallas import tpu as pltpu

MESH = pl.DeviceIdType.MESH

CAP = 2


highest = lax.Precision.HIGHEST
support_sq = 0.25


def split_up(shard, dim, peers):
    dims = shard.shape
    pieces = shard.reshape(*dims[:dim], peers, dims[dim] // peers, *dims[dim + 1 :])
    return jnp.moveaxis(pieces, dim, 0)


def sum_at_owner(shard, axis, dim):
    pieces = split_up(shard, dim, lax.axis_size(axis))
    arrived = lax.all_to_all(pieces, axis, split_axis=0, concat_axis=0, tiled=True)
    return arrived.astype(jnp.float32).sum(axis=0)


def from_root(shard, axis, root):
    return lax.dynamic_index_in_dim(lax.all_gather(shard, axis), root, 0, keepdims=False)


def copy_for_each(shard, axis):
    copies = jnp.broadcast_to(shard, (lax.axis_size(axis), *shard.shape))
    return lax.all_to_all(copies, axis, split_axis=0, concat_axis=0, tiled=True)


def over_copies(shard, axis):
    return copy_for_each(shard, axis).astype(jnp.float32).sum(axis=0)


def joined_along(pieces, dim):
    dims = list(pieces.shape[1:])
    dims[dim] *= pieces.shape[0]
    return jnp.moveaxis(pieces, 0, dim).reshape(dims)


def gather_directly(shard, axis, dim):
    pieces = copy_for_each(shard, axis)
    return joined_along(pieces, dim)


def _nt(a, b):
    return lax.dot_general(a, b, (((1,), (1,)), ((), ())), preferred_element_type=jnp.float32)


def _nn(a, b):
    return lax.dot_general(a, b, (((1,), (0,)), ((), ())), preferred_element_type=jnp.float32)


def _nt_exact(a, b):
    return lax.dot_general(
        a, b, (((1,), (1,)), ((), ())), precision=highest, preferred_element_type=jnp.float32
    )


def _nn_exact(a, b):
    return lax.dot_general(
        a, b, (((1,), (0,)), ((), ())), precision=highest, preferred_element_type=jnp.float32
    )


def _greet_group(n, leaf, me):
    barrier = pltpu.get_barrier_semaphore()
    for r in range(n):
        @pl.when(me != r)
        def _():
            pl.semaphore_signal(barrier, inc=1, device_id=(leaf, r), device_id_type=MESH)
    pl.semaphore_wait(barrier, n - 1)


def _block_copy(halves, q, dest, send_sem, recv_sem, leaf):
    return pltpu.make_async_remote_copy(
        src_ref=halves.at[q],
        dst_ref=halves.at[q],
        send_sem=send_sem,
        recv_sem=recv_sem.at[q],
        device_id=(leaf, dest),
        device_id_type=MESH,
    )


def sep_forward_kernel(n, start_ref, inv_ref, blocks_ref, sol_ref, halves, resid, send_sem, recv_sem):
    me = lax.axis_index("grp")
    leaf = lax.axis_index("leaf")
    _greet_group(n, leaf, me)
    resid[...] = start_ref[...]

    def step(q, carry):
        @pl.when(me == q)
        def _():
            solved = _nt_exact(resid[...], inv_ref[...])
            sol_ref[...] = solved
            halves[q] = solved.astype(jnp.bfloat16)
            for k in range(1, n):
                @pl.when(q + k < n)
                def _():
                    _block_copy(halves, q, q + k, send_sem.at[k], recv_sem, leaf).start()
            for k in range(1, n):
                @pl.when(q + k < n)
                def _():
                    _block_copy(halves, q, q + k, send_sem.at[k], recv_sem, leaf).wait_send()

        @pl.when(me > q)
        def _():
            _block_copy(halves, q, q, send_sem.at[0], recv_sem, leaf).wait_recv()
            resid[...] = resid[...] - _nt(halves[q], blocks_ref[q])

        return carry

    lax.fori_loop(0, n, step, 0)


def sep_backward_kernel(n, start_ref, inv_ref, blocks_ref, sol_ref, table_ref, halves, resid, send_sem, recv_sem):
    me = lax.axis_index("grp")
    leaf = lax.axis_index("leaf")
    _greet_group(n, leaf, me)
    resid[...] = start_ref[...]

    def step(s, carry):
        q = n - 1 - s

        @pl.when(me == q)
        def _():
            solved = _nn_exact(resid[...], inv_ref[...])
            sol_ref[...] = solved
            halves[q] = solved.astype(jnp.bfloat16)
            for k in range(1, n):
                dest = lax.rem(q - k + n, n)
                _block_copy(halves, q, dest, send_sem.at[k], recv_sem, leaf).start()
            for k in range(1, n):
                dest = lax.rem(q - k + n, n)
                _block_copy(halves, q, dest, send_sem.at[k], recv_sem, leaf).wait_send()

        @pl.when(me != q)
        def _():
            _block_copy(halves, q, q, send_sem.at[0], recv_sem, leaf).wait_recv()

        @pl.when(me < q)
        def _():
            resid[...] = resid[...] - _nn(halves[q], blocks_ref[q])

        return carry

    lax.fori_loop(0, n, step, 0)
    table_ref[...] = halves[...]


def sep_solve(kind, start, inv, blocks, n):
    rows, width = start.shape
    vmem = pl.BlockSpec(memory_space=pltpu.VMEM)
    scratch = [
        pltpu.VMEM((n, rows, width), jnp.bfloat16),
        pltpu.VMEM((rows, width), jnp.float32),
        pltpu.SemaphoreType.DMA((n,)),
        pltpu.SemaphoreType.DMA((n,)),
    ]
    sol_shape = jax.ShapeDtypeStruct((rows, width), jnp.float32)
    params = dict(has_side_effects=True, vmem_limit_bytes=48 * 1024 * 1024)
    if kind == "forward":
        return pl.pallas_call(
            functools.partial(sep_forward_kernel, n),
            out_shape=sol_shape,
            in_specs=[vmem] * 3,
            out_specs=vmem,
            scratch_shapes=scratch,
            compiler_params=pltpu.CompilerParams(collective_id=0, **params),
        )(start, inv, blocks)
    return pl.pallas_call(
        functools.partial(sep_backward_kernel, n),
        out_shape=(sol_shape, jax.ShapeDtypeStruct((n, rows, width), jnp.bfloat16)),
        in_specs=[vmem] * 3,
        out_specs=(vmem, vmem),
        scratch_shapes=scratch,
        compiler_params=pltpu.CompilerParams(collective_id=1, **params),
    )(start, inv, blocks)


def top_solve_kernel(nt, span, start_ref, inv_ref, lower_ref, coef_ref, half_ref, fwd_half, fwd_full):
    for t in range(nt):
        cols = slice(t * span, (t + 1) * span)
        residue = start_ref[:, cols]
        if t > 0:
            residue = residue - _nt(fwd_half[:, : t * span], lower_ref[cols, : t * span])
        solved = _nt_exact(residue, inv_ref[t])
        fwd_full[:, cols] = solved
        fwd_half[:, cols] = solved.astype(jnp.bfloat16)
    for t in reversed(range(nt)):
        cols = slice(t * span, (t + 1) * span)
        residue = fwd_full[:, cols]
        if t < nt - 1:
            residue = residue - _nn(half_ref[:, (t + 1) * span :], lower_ref[(t + 1) * span :, cols])
        solved = _nn_exact(residue, inv_ref[t])
        coef_ref[:, cols] = solved
        half_ref[:, cols] = solved.astype(jnp.bfloat16)


def top_solve(top_start, top_inverse, top_lower):
    nt, span = top_inverse.shape[0], top_inverse.shape[1]
    rows, width = top_start.shape
    vmem = pl.BlockSpec(memory_space=pltpu.VMEM)
    return pl.pallas_call(
        functools.partial(top_solve_kernel, nt, span),
        out_shape=(
            jax.ShapeDtypeStruct((rows, width), jnp.float32),
            jax.ShapeDtypeStruct((rows, width), jnp.bfloat16),
        ),
        in_specs=[vmem] * 3,
        out_specs=(vmem, vmem),
        scratch_shapes=[
            pltpu.VMEM((rows, width), jnp.bfloat16),
            pltpu.VMEM((rows, width), jnp.float32),
        ],
        compiler_params=pltpu.CompilerParams(vmem_limit_bytes=48 * 1024 * 1024),
    )(top_start, top_inverse, top_lower)


def evaluate_kernel(slots, pattern_ref, coef_ref, centre_ref, column_ref, out_ref, acc, spread):
    m = pl.program_id(0)
    acc[...] = jnp.zeros_like(acc)
    column = column_ref[0]
    width = centre_ref.shape[2]
    for comp in range(3):
        spread[comp] = jnp.broadcast_to(column[:, comp : comp + 1], (column.shape[0], width))

    def one_slot(s, carry):
        @pl.when(pattern_ref[m, s] != 0)
        def _():
            centre = centre_ref[s]
            dist = None
            for comp in range(3):
                delta = centre[comp : comp + 1, :] - spread[comp]
                dist = delta * delta if dist is None else dist + delta * delta
            weight = jnp.maximum(1.0 - dist * (1.0 / support_sq), 0.0)
            kernel = (weight * weight * weight).astype(jnp.bfloat16)
            acc[...] += _nt(coef_ref[s], kernel)

        return carry

    lax.fori_loop(0, slots, one_slot, 0)
    out_ref[...] = acc[...]


def evaluate_all(coef_all, centre_all, point_columns, pattern):
    slots, rows, span = coef_all.shape
    blocks = point_columns.shape[0]
    full = lambda shape: pl.BlockSpec(shape, lambda m, pat: (0,) * len(shape))
    grid_spec = pltpu.PrefetchScalarGridSpec(
        num_scalar_prefetch=1,
        grid=(blocks,),
        in_specs=[
            full(coef_all.shape),
            full(centre_all.shape),
            pl.BlockSpec((1, span, point_columns.shape[2]), lambda m, pat: (m, 0, 0)),
        ],
        out_specs=pl.BlockSpec((rows, span), lambda m, pat: (0, m)),
        scratch_shapes=[
            pltpu.VMEM((rows, span), jnp.float32),
            pltpu.VMEM((3, span, centre_all.shape[2]), jnp.float32),
        ],
    )
    return pl.pallas_call(
        functools.partial(evaluate_kernel, slots),
        out_shape=jax.ShapeDtypeStruct((rows, blocks * span), jnp.float32),
        grid_spec=grid_spec,
    )(pattern, coef_all, centre_all, point_columns)


def slot_ranks(dest_rows, grp_size):
    onehot = (dest_rows[..., None] == jnp.arange(grp_size)).astype(jnp.int32)
    before = jnp.cumsum(onehot, axis=-2) - onehot
    return jnp.sum(before * onehot, axis=-1)


def evaluate(coef_all, centre_all, block_points, block_mask):
    dist = jnp.zeros((centre_all.shape[0], centre_all.shape[2], block_points.shape[1]), jnp.float32)
    for comp in range(3):
        delta = centre_all[:, comp, :, None] - block_points[None, comp, None, :]
        dist = dist + delta * delta
    weight = jnp.maximum(1.0 - dist / support_sq, 0.0) ** 3
    kernel = (weight * block_mask.astype(jnp.float32)[:, None, None]).astype(jnp.bfloat16)
    return jnp.einsum("krs,ksp->rp", coef_all, kernel, preferred_element_type=jnp.float32)


def on_device(
    rhs_leaf,
    rhs_sep,
    rhs_top,
    leaf_inverse,
    leaf_coupling,
    leaf_targets,
    sep_inverse,
    sep_blocks,
    top_coupling,
    top_inverse,
    top_lower,
    dest_map,
    centers,
    points,
    eval_pattern,
):
    grp_size = lax.axis_size("grp")
    my_index = lax.axis_index("grp")
    blocks_here = leaf_inverse.shape[0]
    snapshots = rhs_leaf.shape[0]
    span = leaf_inverse.shape[1]
    slot_count = CAP
    leaf_rhs = rhs_leaf.reshape(snapshots, blocks_here, span).transpose(1, 0, 2)
    leaf_sol = jnp.einsum("nrs,nts->nrt", leaf_rhs, leaf_inverse, precision=highest)
    leaf_half = leaf_sol.astype(jnp.bfloat16)
    partial_value = jnp.einsum(
        "nrs,ncbs->ncrb", leaf_half, leaf_coupling, preferred_element_type=jnp.float32
    )
    onehot = (leaf_targets[:, :, None] == jnp.arange(grp_size)[None, None, :]).astype(jnp.float32)
    picked = onehot
    shared = sum_at_owner(
        jnp.einsum("ncq,ncrb->qrb", picked, partial_value, precision=highest).astype(jnp.bfloat16),
        "grp",
        0,
    )
    sep_start = rhs_sep - shared[0]
    inverse_own = sep_inverse[0]
    own_blocks = sep_blocks[0]

    sep_sol = sep_solve("forward", sep_start, inverse_own, own_blocks, grp_size)
    sep_half = sep_sol.astype(jnp.bfloat16)
    top_term = jnp.dot(sep_half, top_coupling, preferred_element_type=jnp.float32)
    top_total = lax.psum(top_term, ("leaf", "grp"))
    top_start = rhs_top - top_total
    coef_top, top_half = top_solve(top_start, top_inverse, top_lower)
    back_start = sep_sol - lax.dot_general(
        top_half, top_coupling, (((1,), (1,)), ((), ())), preferred_element_type=jnp.float32
    )

    coef_sep, known_table = sep_solve("backward", back_start, inverse_own, own_blocks, grp_size)
    picked = jnp.einsum(
        "ncq,qrb->ncrb",
        onehot.astype(jnp.bfloat16),
        known_table,
        preferred_element_type=jnp.float32,
    ).astype(jnp.bfloat16)
    reduced = jnp.einsum(
        "ncrb,ncbs->nrs", picked, leaf_coupling, preferred_element_type=jnp.float32
    )
    leaf_coef = jnp.einsum("nrs,nst->nrt", leaf_sol - reduced, leaf_inverse, precision=highest)
    coef_leaf = leaf_coef.transpose(1, 0, 2).reshape(snapshots, blocks_here * span)
    leaf_out = leaf_coef.astype(jnp.bfloat16)
    slot_ids = jnp.arange(slot_count)
    grp_ids = jnp.arange(grp_size)
    own_dest = dest_map[:, 0]
    slot_rank = slot_ranks(own_dest[None, :], grp_size)[0]
    selector = (own_dest[None, None, :] == grp_ids[:, None, None]) & (
        slot_rank[None, None, :] == slot_ids[None, :, None]
    )
    send_coef = jnp.einsum(
        "dkj,jrt->dkrt", selector.astype(jnp.bfloat16), leaf_out, preferred_element_type=jnp.float32
    ).astype(jnp.bfloat16)
    send_centre = jnp.einsum(
        "dkj,jct->dkct", selector.astype(jnp.float32), centers, precision=highest
    )
    received, recv_centre = (
        lax.all_to_all(send_coef, "grp", split_axis=0, concat_axis=0, tiled=True),
        lax.all_to_all(
            send_centre.astype(jnp.bfloat16), "grp", split_axis=0, concat_axis=0, tiled=True
        ).astype(send_centre.dtype),
    )
    slot_total = grp_size * slot_count
    coef_all = received.reshape(slot_total, snapshots, span)
    centre_all = recv_centre.reshape(slot_total, 3, span)
    point_blocks = eval_pattern.shape[0]
    point_columns = points[0].T.reshape(point_blocks, span, points.shape[1])
    values = evaluate_all(coef_all, centre_all, point_columns, eval_pattern)
    return (coef_leaf, coef_sep, coef_top, values)


def solution(mesh):
    in_specs = (
        P(None, ("leaf", "grp")),
        P(None, ("leaf", "grp")),
        P(),
        P(("leaf", "grp"), None, None),
        P(("leaf", "grp"), None, None, None),
        P(("leaf", "grp"), None),
        P(("leaf", "grp"), None, None),
        P(("leaf", "grp"), None, None, None),
        P(("leaf", "grp"), None),
        P(),
        P(),
        P(("leaf", "grp"), None),
        P(("leaf", "grp"), None, None),
        P(("leaf", "grp"), None, None),
        P(("leaf", "grp"), None),
    )
    out_specs = (P(None, ("leaf", "grp")), P(None, ("leaf", "grp")), P(), P(None, ("leaf", "grp")))
    return jax.shard_map(
        on_device, mesh=mesh, in_specs=in_specs, out_specs=out_specs, check_vma=False
    )
```

```python
import functools

import jax
import jax.numpy as jnp
from jax import lax
from jax.sharding import PartitionSpec as P
from jax.experimental import pallas as pl
from jax.experimental.pallas import tpu as pltpu

MESH = pl.DeviceIdType.MESH

CAP = 2


highest = lax.Precision.HIGHEST
support_sq = 0.25


def split_up(shard, dim, peers):
    dims = shard.shape
    pieces = shard.reshape(*dims[:dim], peers, dims[dim] // peers, *dims[dim + 1 :])
    return jnp.moveaxis(pieces, dim, 0)


def sum_at_owner(shard, axis, dim):
    pieces = split_up(shard, dim, lax.axis_size(axis))
    arrived = lax.all_to_all(pieces, axis, split_axis=0, concat_axis=0, tiled=True)
    return arrived.astype(jnp.float32).sum(axis=0)


def from_root(shard, axis, root):
    return lax.dynamic_index_in_dim(lax.all_gather(shard, axis), root, 0, keepdims=False)


def copy_for_each(shard, axis):
    copies = jnp.broadcast_to(shard, (lax.axis_size(axis), *shard.shape))
    return lax.all_to_all(copies, axis, split_axis=0, concat_axis=0, tiled=True)


def over_copies(shard, axis):
    return copy_for_each(shard, axis).astype(jnp.float32).sum(axis=0)


def joined_along(pieces, dim):
    dims = list(pieces.shape[1:])
    dims[dim] *= pieces.shape[0]
    return jnp.moveaxis(pieces, 0, dim).reshape(dims)


def gather_directly(shard, axis, dim):
    pieces = copy_for_each(shard, axis)
    return joined_along(pieces, dim)


def _nt(a, b):
    return lax.dot_general(a, b, (((1,), (1,)), ((), ())), preferred_element_type=jnp.float32)


def _nn(a, b):
    return lax.dot_general(a, b, (((1,), (0,)), ((), ())), preferred_element_type=jnp.float32)


def _nt_exact(a, b):
    return lax.dot_general(
        a, b, (((1,), (1,)), ((), ())), precision=highest, preferred_element_type=jnp.float32
    )


def _nn_exact(a, b):
    return lax.dot_general(
        a, b, (((1,), (0,)), ((), ())), precision=highest, preferred_element_type=jnp.float32
    )


def _greet_group(n, leaf, me):
    barrier = pltpu.get_barrier_semaphore()
    for r in range(n):
        @pl.when(me != r)
        def _():
            pl.semaphore_signal(barrier, inc=1, device_id=(leaf, r), device_id_type=MESH)
    pl.semaphore_wait(barrier, n - 1)


def _block_copy(halves, q, dest, send_sem, recv_sem, leaf):
    return pltpu.make_async_remote_copy(
        src_ref=halves.at[q],
        dst_ref=halves.at[q],
        send_sem=send_sem,
        recv_sem=recv_sem.at[q],
        device_id=(leaf, dest),
        device_id_type=MESH,
    )


def sep_forward_kernel(n, start_ref, inv_ref, blocks_ref, sol_ref, halves, resid, send_sem, recv_sem):
    me = lax.axis_index("grp")
    leaf = lax.axis_index("leaf")
    _greet_group(n, leaf, me)
    resid[...] = start_ref[...]

    def step(q, carry):
        @pl.when(me == q)
        def _():
            solved = _nt_exact(resid[...], inv_ref[...])
            sol_ref[...] = solved
            halves[q] = solved.astype(jnp.bfloat16)
            for k in range(1, n):
                @pl.when(q + k < n)
                def _():
                    _block_copy(halves, q, q + k, send_sem.at[k], recv_sem, leaf).start()
            for k in range(1, n):
                @pl.when(q + k < n)
                def _():
                    _block_copy(halves, q, q + k, send_sem.at[k], recv_sem, leaf).wait_send()

        @pl.when(me > q)
        def _():
            _block_copy(halves, q, q, send_sem.at[0], recv_sem, leaf).wait_recv()
            resid[...] = resid[...] - _nt(halves[q], blocks_ref[q])

        return carry

    lax.fori_loop(0, n, step, 0)


def sep_backward_kernel(n, start_ref, inv_ref, blocks_ref, sol_ref, table_ref, halves, resid, send_sem, recv_sem):
    me = lax.axis_index("grp")
    leaf = lax.axis_index("leaf")
    _greet_group(n, leaf, me)
    resid[...] = start_ref[...]

    def step(s, carry):
        q = n - 1 - s

        @pl.when(me == q)
        def _():
            solved = _nn_exact(resid[...], inv_ref[...])
            sol_ref[...] = solved
            halves[q] = solved.astype(jnp.bfloat16)
            for k in range(1, n):
                dest = lax.rem(q - k + n, n)
                _block_copy(halves, q, dest, send_sem.at[k], recv_sem, leaf).start()
            for k in range(1, n):
                dest = lax.rem(q - k + n, n)
                _block_copy(halves, q, dest, send_sem.at[k], recv_sem, leaf).wait_send()

        @pl.when(me != q)
        def _():
            _block_copy(halves, q, q, send_sem.at[0], recv_sem, leaf).wait_recv()

        @pl.when(me < q)
        def _():
            resid[...] = resid[...] - _nn(halves[q], blocks_ref[q])

        return carry

    lax.fori_loop(0, n, step, 0)
    table_ref[...] = halves[...]


def sep_solve(kind, start, inv, blocks, n):
    rows, width = start.shape
    vmem = pl.BlockSpec(memory_space=pltpu.VMEM)
    scratch = [
        pltpu.VMEM((n, rows, width), jnp.bfloat16),
        pltpu.VMEM((rows, width), jnp.float32),
        pltpu.SemaphoreType.DMA((n,)),
        pltpu.SemaphoreType.DMA((n,)),
    ]
    sol_shape = jax.ShapeDtypeStruct((rows, width), jnp.float32)
    params = dict(has_side_effects=True, vmem_limit_bytes=48 * 1024 * 1024)
    if kind == "forward":
        return pl.pallas_call(
            functools.partial(sep_forward_kernel, n),
            out_shape=sol_shape,
            in_specs=[vmem] * 3,
            out_specs=vmem,
            scratch_shapes=scratch,
            compiler_params=pltpu.CompilerParams(collective_id=0, **params),
        )(start, inv, blocks)
    return pl.pallas_call(
        functools.partial(sep_backward_kernel, n),
        out_shape=(sol_shape, jax.ShapeDtypeStruct((n, rows, width), jnp.bfloat16)),
        in_specs=[vmem] * 3,
        out_specs=(vmem, vmem),
        scratch_shapes=scratch,
        compiler_params=pltpu.CompilerParams(collective_id=1, **params),
    )(start, inv, blocks)


def top_solve_kernel(nt, span, start_ref, inv_ref, lower_ref, coef_ref, half_ref, fwd_half, fwd_full):
    for t in range(nt):
        cols = slice(t * span, (t + 1) * span)
        residue = start_ref[:, cols]
        if t > 0:
            residue = residue - _nt(fwd_half[:, : t * span], lower_ref[cols, : t * span])
        solved = _nt_exact(residue, inv_ref[t])
        fwd_full[:, cols] = solved
        fwd_half[:, cols] = solved.astype(jnp.bfloat16)
    for t in reversed(range(nt)):
        cols = slice(t * span, (t + 1) * span)
        residue = fwd_full[:, cols]
        if t < nt - 1:
            residue = residue - _nn(half_ref[:, (t + 1) * span :], lower_ref[(t + 1) * span :, cols])
        solved = _nn_exact(residue, inv_ref[t])
        coef_ref[:, cols] = solved
        half_ref[:, cols] = solved.astype(jnp.bfloat16)


def top_solve(top_start, top_inverse, top_lower):
    nt, span = top_inverse.shape[0], top_inverse.shape[1]
    rows, width = top_start.shape
    vmem = pl.BlockSpec(memory_space=pltpu.VMEM)
    return pl.pallas_call(
        functools.partial(top_solve_kernel, nt, span),
        out_shape=(
            jax.ShapeDtypeStruct((rows, width), jnp.float32),
            jax.ShapeDtypeStruct((rows, width), jnp.bfloat16),
        ),
        in_specs=[vmem] * 3,
        out_specs=(vmem, vmem),
        scratch_shapes=[
            pltpu.VMEM((rows, width), jnp.bfloat16),
            pltpu.VMEM((rows, width), jnp.float32),
        ],
        compiler_params=pltpu.CompilerParams(vmem_limit_bytes=48 * 1024 * 1024),
    )(top_start, top_inverse, top_lower)


def evaluate_kernel(slots, pattern_ref, coef_ref, centre_ref, column_ref, out_ref, acc, spread):
    m = pl.program_id(0)
    acc[...] = jnp.zeros_like(acc)
    column = column_ref[0]
    width = centre_ref.shape[2]
    for comp in range(3):
        spread[comp] = jnp.broadcast_to(column[:, comp : comp + 1], (column.shape[0], width))

    def one_slot(s, carry):
        @pl.when(pattern_ref[m, s] != 0)
        def _():
            centre = centre_ref[s]
            dist = None
            for comp in range(3):
                delta = centre[comp : comp + 1, :] - spread[comp]
                dist = delta * delta if dist is None else dist + delta * delta
            weight = jnp.maximum(1.0 - dist * (1.0 / support_sq), 0.0)
            kernel = (weight * weight * weight).astype(jnp.bfloat16)
            acc[...] += _nt(coef_ref[s], kernel)

        return carry

    lax.fori_loop(0, slots, one_slot, 0)
    out_ref[...] = acc[...]


def evaluate_all(coef_all, centre_all, point_columns, pattern):
    slots, rows, span = coef_all.shape
    blocks = point_columns.shape[0]
    full = lambda shape: pl.BlockSpec(shape, lambda m, pat: (0,) * len(shape))
    grid_spec = pltpu.PrefetchScalarGridSpec(
        num_scalar_prefetch=1,
        grid=(blocks,),
        in_specs=[
            full(coef_all.shape),
            full(centre_all.shape),
            pl.BlockSpec((1, span, point_columns.shape[2]), lambda m, pat: (m, 0, 0)),
        ],
        out_specs=pl.BlockSpec((rows, span), lambda m, pat: (0, m)),
        scratch_shapes=[
            pltpu.VMEM((rows, span), jnp.float32),
            pltpu.VMEM((3, span, centre_all.shape[2]), jnp.float32),
        ],
    )
    return pl.pallas_call(
        functools.partial(evaluate_kernel, slots),
        out_shape=jax.ShapeDtypeStruct((rows, blocks * span), jnp.float32),
        grid_spec=grid_spec,
    )(pattern, coef_all, centre_all, point_columns)


def top_reduce_kernel(n, groups, span, term_ref, total_ref, parts_a, parts_b, gathered, local_sem, send_a, recv_a, send_b, recv_b, send_c, recv_c):
    me = lax.axis_index("grp")
    leaf = lax.axis_index("leaf")
    barrier = pltpu.get_barrier_semaphore()
    for r in range(n):
        @pl.when(me != r)
        def _():
            pl.semaphore_signal(barrier, inc=1, device_id=(leaf, r), device_id_type=MESH)
    for g in range(groups):
        @pl.when(leaf != g)
        def _():
            pl.semaphore_signal(barrier, inc=1, device_id=(g, me), device_id_type=MESH)
    pl.semaphore_wait(barrier, n - 1 + groups - 1)

    def column(q):
        return term_ref.at[:, pl.ds(pl.multiple_of(q * span, span), span)]

    def copy_a(k):
        dest = lax.rem(me + k, n)
        return pltpu.make_async_remote_copy(
            column(dest), parts_a.at[me], send_a.at[k], recv_a.at[me], device_id=(leaf, dest), device_id_type=MESH
        )

    def wait_a(k):
        src = lax.rem(me + n - k, n)
        pltpu.make_async_remote_copy(
            column(src), parts_a.at[src], send_a.at[0], recv_a.at[src], device_id=(leaf, src), device_id_type=MESH
        ).wait_recv()

    own = pltpu.make_async_copy(column(me), parts_a.at[me], local_sem.at[0])
    own.start()
    for k in range(1, n):
        copy_a(k).start()
    own.wait()
    for k in range(1, n):
        wait_a(k)
    for k in range(1, n):
        copy_a(k).wait_send()
    total = parts_a[0]
    for q in range(1, n):
        total = total + parts_a[q]
    parts_b[leaf] = total

    def copy_b(k):
        dest = lax.rem(leaf + k, groups)
        return pltpu.make_async_remote_copy(
            parts_b.at[leaf], parts_b.at[leaf], send_b.at[k], recv_b.at[leaf], device_id=(dest, me), device_id_type=MESH
        )

    for k in range(1, groups):
        copy_b(k).start()
    for k in range(1, groups):
        src = lax.rem(leaf + groups - k, groups)
        pltpu.make_async_remote_copy(
            parts_b.at[src], parts_b.at[src], send_b.at[0], recv_b.at[src], device_id=(src, me), device_id_type=MESH
        ).wait_recv()
    for k in range(1, groups):
        copy_b(k).wait_send()
    summed = parts_b[0]
    for g in range(1, groups):
        summed = summed + parts_b[g]
    gathered[me] = summed

    def copy_c(k):
        dest = lax.rem(me + k, n)
        return pltpu.make_async_remote_copy(
            gathered.at[me], gathered.at[me], send_c.at[k], recv_c.at[me], device_id=(leaf, dest), device_id_type=MESH
        )

    for k in range(1, n):
        copy_c(k).start()
    for k in range(1, n):
        src = lax.rem(me + n - k, n)
        pltpu.make_async_remote_copy(
            gathered.at[src], gathered.at[src], send_c.at[0], recv_c.at[src], device_id=(leaf, src), device_id_type=MESH
        ).wait_recv()
    for k in range(1, n):
        copy_c(k).wait_send()
    for q in range(n):
        total_ref[:, q * span : (q + 1) * span] = gathered[q]


def top_reduce(term, n, groups):
    rows, width = term.shape
    span = width // n
    vmem = pl.BlockSpec(memory_space=pltpu.VMEM)
    return pl.pallas_call(
        functools.partial(top_reduce_kernel, n, groups, span),
        out_shape=jax.ShapeDtypeStruct((rows, width), jnp.float32),
        in_specs=[vmem],
        out_specs=vmem,
        scratch_shapes=[
            pltpu.VMEM((n, rows, span), jnp.float32),
            pltpu.VMEM((groups, rows, span), jnp.float32),
            pltpu.VMEM((n, rows, span), jnp.float32),
            pltpu.SemaphoreType.DMA((1,)),
            pltpu.SemaphoreType.DMA((n,)),
            pltpu.SemaphoreType.DMA((n,)),
            pltpu.SemaphoreType.DMA((groups,)),
            pltpu.SemaphoreType.DMA((groups,)),
            pltpu.SemaphoreType.DMA((n,)),
            pltpu.SemaphoreType.DMA((n,)),
        ],
        compiler_params=pltpu.CompilerParams(collective_id=2, has_side_effects=True),
    )(term)


def slot_ranks(dest_rows, grp_size):
    onehot = (dest_rows[..., None] == jnp.arange(grp_size)).astype(jnp.int32)
    before = jnp.cumsum(onehot, axis=-2) - onehot
    return jnp.sum(before * onehot, axis=-1)


def evaluate(coef_all, centre_all, block_points, block_mask):
    dist = jnp.zeros((centre_all.shape[0], centre_all.shape[2], block_points.shape[1]), jnp.float32)
    for comp in range(3):
        delta = centre_all[:, comp, :, None] - block_points[None, comp, None, :]
        dist = dist + delta * delta
    weight = jnp.maximum(1.0 - dist / support_sq, 0.0) ** 3
    kernel = (weight * block_mask.astype(jnp.float32)[:, None, None]).astype(jnp.bfloat16)
    return jnp.einsum("krs,ksp->rp", coef_all, kernel, preferred_element_type=jnp.float32)


def on_device(
    rhs_leaf,
    rhs_sep,
    rhs_top,
    leaf_inverse,
    leaf_coupling,
    leaf_targets,
    sep_inverse,
    sep_blocks,
    top_coupling,
    top_inverse,
    top_lower,
    dest_map,
    centers,
    points,
    eval_pattern,
):
    grp_size = lax.axis_size("grp")
    my_index = lax.axis_index("grp")
    blocks_here = leaf_inverse.shape[0]
    snapshots = rhs_leaf.shape[0]
    span = leaf_inverse.shape[1]
    slot_count = CAP
    leaf_rhs = rhs_leaf.reshape(snapshots, blocks_here, span).transpose(1, 0, 2)
    leaf_sol = jnp.einsum("nrs,nts->nrt", leaf_rhs, leaf_inverse, precision=highest)
    leaf_half = leaf_sol.astype(jnp.bfloat16)
    partial_value = jnp.einsum(
        "nrs,ncbs->ncrb", leaf_half, leaf_coupling, preferred_element_type=jnp.float32
    )
    onehot = (leaf_targets[:, :, None] == jnp.arange(grp_size)[None, None, :]).astype(jnp.float32)
    picked = onehot
    shared = sum_at_owner(
        jnp.einsum("ncq,ncrb->qrb", picked, partial_value, precision=highest).astype(jnp.bfloat16),
        "grp",
        0,
    )
    sep_start = rhs_sep - shared[0]
    inverse_own = sep_inverse[0]
    own_blocks = sep_blocks[0]

    sep_sol = sep_solve("forward", sep_start, inverse_own, own_blocks, grp_size)
    sep_half = sep_sol.astype(jnp.bfloat16)
    top_term = jnp.dot(sep_half, top_coupling, preferred_element_type=jnp.float32)
    top_total = top_reduce(top_term, grp_size, lax.axis_size("leaf"))
    top_start = rhs_top - top_total
    coef_top, top_half = top_solve(top_start, top_inverse, top_lower)
    back_start = sep_sol - lax.dot_general(
        top_half, top_coupling, (((1,), (1,)), ((), ())), preferred_element_type=jnp.float32
    )

    coef_sep, known_table = sep_solve("backward", back_start, inverse_own, own_blocks, grp_size)
    picked = jnp.einsum(
        "ncq,qrb->ncrb",
        onehot.astype(jnp.bfloat16),
        known_table,
        preferred_element_type=jnp.float32,
    ).astype(jnp.bfloat16)
    reduced = jnp.einsum(
        "ncrb,ncbs->nrs", picked, leaf_coupling, preferred_element_type=jnp.float32
    )
    leaf_coef = jnp.einsum("nrs,nst->nrt", leaf_sol - reduced, leaf_inverse, precision=highest)
    coef_leaf = leaf_coef.transpose(1, 0, 2).reshape(snapshots, blocks_here * span)
    leaf_out = leaf_coef.astype(jnp.bfloat16)
    slot_ids = jnp.arange(slot_count)
    grp_ids = jnp.arange(grp_size)
    own_dest = dest_map[:, 0]
    slot_rank = slot_ranks(own_dest[None, :], grp_size)[0]
    selector = (own_dest[None, None, :] == grp_ids[:, None, None]) & (
        slot_rank[None, None, :] == slot_ids[None, :, None]
    )
    send_coef = jnp.einsum(
        "dkj,jrt->dkrt", selector.astype(jnp.bfloat16), leaf_out, preferred_element_type=jnp.float32
    ).astype(jnp.bfloat16)
    send_centre = jnp.einsum(
        "dkj,jct->dkct", selector.astype(jnp.float32), centers, precision=highest
    )
    received, recv_centre = (
        lax.all_to_all(send_coef, "grp", split_axis=0, concat_axis=0, tiled=True),
        lax.all_to_all(
            send_centre.astype(jnp.bfloat16), "grp", split_axis=0, concat_axis=0, tiled=True
        ).astype(send_centre.dtype),
    )
    slot_total = grp_size * slot_count
    coef_all = received.reshape(slot_total, snapshots, span)
    centre_all = recv_centre.reshape(slot_total, 3, span)
    point_blocks = eval_pattern.shape[0]
    point_columns = points[0].T.reshape(point_blocks, span, points.shape[1])
    values = evaluate_all(coef_all, centre_all, point_columns, eval_pattern)
    return (coef_leaf, coef_sep, coef_top, values)


def solution(mesh):
    in_specs = (
        P(None, ("leaf", "grp")),
        P(None, ("leaf", "grp")),
        P(),
        P(("leaf", "grp"), None, None),
        P(("leaf", "grp"), None, None, None),
        P(("leaf", "grp"), None),
        P(("leaf", "grp"), None, None),
        P(("leaf", "grp"), None, None, None),
        P(("leaf", "grp"), None),
        P(),
        P(),
        P(("leaf", "grp"), None),
        P(("leaf", "grp"), None, None),
        P(("leaf", "grp"), None, None),
        P(("leaf", "grp"), None),
    )
    out_specs = (P(None, ("leaf", "grp")), P(None, ("leaf", "grp")), P(), P(None, ("leaf", "grp")))
    return jax.shard_map(
        on_device, mesh=mesh, in_specs=in_specs, out_specs=out_specs, check_vma=False
    )
```

```python
import functools

import jax
import jax.numpy as jnp
from jax import lax
from jax.sharding import PartitionSpec as P
from jax.experimental import pallas as pl
from jax.experimental.pallas import tpu as pltpu

MESH = pl.DeviceIdType.MESH

CAP = 2


highest = lax.Precision.HIGHEST
support_sq = 0.25


def split_up(shard, dim, peers):
    dims = shard.shape
    pieces = shard.reshape(*dims[:dim], peers, dims[dim] // peers, *dims[dim + 1 :])
    return jnp.moveaxis(pieces, dim, 0)


def sum_at_owner(shard, axis, dim):
    pieces = split_up(shard, dim, lax.axis_size(axis))
    arrived = lax.all_to_all(pieces, axis, split_axis=0, concat_axis=0, tiled=True)
    return arrived.astype(jnp.float32).sum(axis=0)


def from_root(shard, axis, root):
    return lax.dynamic_index_in_dim(lax.all_gather(shard, axis), root, 0, keepdims=False)


def copy_for_each(shard, axis):
    copies = jnp.broadcast_to(shard, (lax.axis_size(axis), *shard.shape))
    return lax.all_to_all(copies, axis, split_axis=0, concat_axis=0, tiled=True)


def over_copies(shard, axis):
    return copy_for_each(shard, axis).astype(jnp.float32).sum(axis=0)


def joined_along(pieces, dim):
    dims = list(pieces.shape[1:])
    dims[dim] *= pieces.shape[0]
    return jnp.moveaxis(pieces, 0, dim).reshape(dims)


def gather_directly(shard, axis, dim):
    pieces = copy_for_each(shard, axis)
    return joined_along(pieces, dim)


def _nt(a, b):
    return lax.dot_general(a, b, (((1,), (1,)), ((), ())), preferred_element_type=jnp.float32)


def _nn(a, b):
    return lax.dot_general(a, b, (((1,), (0,)), ((), ())), preferred_element_type=jnp.float32)


def _nt_exact(a, b):
    return lax.dot_general(
        a, b, (((1,), (1,)), ((), ())), precision=highest, preferred_element_type=jnp.float32
    )


def _nn_exact(a, b):
    return lax.dot_general(
        a, b, (((1,), (0,)), ((), ())), precision=highest, preferred_element_type=jnp.float32
    )


def _greet_group(n, leaf, me):
    barrier = pltpu.get_barrier_semaphore()
    for r in range(n):
        @pl.when(me != r)
        def _():
            pl.semaphore_signal(barrier, inc=1, device_id=(leaf, r), device_id_type=MESH)
    pl.semaphore_wait(barrier, n - 1)


def _block_copy(halves, q, dest, send_sem, recv_sem, leaf):
    return pltpu.make_async_remote_copy(
        src_ref=halves.at[q],
        dst_ref=halves.at[q],
        send_sem=send_sem,
        recv_sem=recv_sem.at[q],
        device_id=(leaf, dest),
        device_id_type=MESH,
    )


def sep_forward_kernel(n, rhs_ref, part_ref, inv_ref, blocks_ref, sol_ref, halves, resid, send_sem, recv_sem, arrived, local_sem, give_sem, take_sem):
    me = lax.axis_index("grp")
    leaf = lax.axis_index("leaf")
    _greet_group(n, leaf, me)

    def give(dest):
        return pltpu.make_async_remote_copy(
            part_ref.at[dest], arrived.at[me], give_sem.at[dest], take_sem.at[me], device_id=(leaf, dest), device_id_type=MESH
        )

    own = pltpu.make_async_copy(part_ref.at[me], arrived.at[me], local_sem.at[0])
    own.start()
    for dest in range(n):
        @pl.when(me != dest)
        def _():
            give(dest).start()
    own.wait()
    for src in range(n):
        @pl.when(me != src)
        def _():
            pltpu.make_async_remote_copy(
                part_ref.at[src], arrived.at[src], give_sem.at[src], take_sem.at[src], device_id=(leaf, src), device_id_type=MESH
            ).wait_recv()
    total = arrived[0].astype(jnp.float32)
    for src in range(1, n):
        total = total + arrived[src].astype(jnp.float32)
    resid[...] = rhs_ref[...] - total
    for dest in range(n):
        @pl.when(me != dest)
        def _():
            give(dest).wait_send()

    def step(q, carry):
        @pl.when(me == q)
        def _():
            solved = _nt_exact(resid[...], inv_ref[...])
            sol_ref[...] = solved
            halves[q] = solved.astype(jnp.bfloat16)
            for k in range(1, n):
                @pl.when(q + k < n)
                def _():
                    _block_copy(halves, q, q + k, send_sem.at[k], recv_sem, leaf).start()
            for k in range(1, n):
                @pl.when(q + k < n)
                def _():
                    _block_copy(halves, q, q + k, send_sem.at[k], recv_sem, leaf).wait_send()

        @pl.when(me > q)
        def _():
            _block_copy(halves, q, q, send_sem.at[0], recv_sem, leaf).wait_recv()
            resid[...] = resid[...] - _nt(halves[q], blocks_ref[q])

        return carry

    lax.fori_loop(0, n, step, 0)


def sep_backward_kernel(n, start_ref, inv_ref, blocks_ref, sol_ref, table_ref, halves, resid, send_sem, recv_sem):
    me = lax.axis_index("grp")
    leaf = lax.axis_index("leaf")
    _greet_group(n, leaf, me)
    resid[...] = start_ref[...]

    def step(s, carry):
        q = n - 1 - s

        @pl.when(me == q)
        def _():
            solved = _nn_exact(resid[...], inv_ref[...])
            sol_ref[...] = solved
            halves[q] = solved.astype(jnp.bfloat16)
            for k in range(1, n):
                dest = lax.rem(q - k + n, n)
                _block_copy(halves, q, dest, send_sem.at[k], recv_sem, leaf).start()
            for k in range(1, n):
                dest = lax.rem(q - k + n, n)
                _block_copy(halves, q, dest, send_sem.at[k], recv_sem, leaf).wait_send()

        @pl.when(me != q)
        def _():
            _block_copy(halves, q, q, send_sem.at[0], recv_sem, leaf).wait_recv()

        @pl.when(me < q)
        def _():
            resid[...] = resid[...] - _nn(halves[q], blocks_ref[q])

        return carry

    lax.fori_loop(0, n, step, 0)
    table_ref[...] = halves[...]


def sep_solve(kind, start, inv, blocks, n):
    rows, width = (start[0] if kind == "forward" else start).shape
    vmem = pl.BlockSpec(memory_space=pltpu.VMEM)
    scratch = [
        pltpu.VMEM((n, rows, width), jnp.bfloat16),
        pltpu.VMEM((rows, width), jnp.float32),
        pltpu.SemaphoreType.DMA((n,)),
        pltpu.SemaphoreType.DMA((n,)),
    ]
    sol_shape = jax.ShapeDtypeStruct((rows, width), jnp.float32)
    params = dict(has_side_effects=True, vmem_limit_bytes=48 * 1024 * 1024)
    if kind == "forward":
        rhs, parts = start
        return pl.pallas_call(
            functools.partial(sep_forward_kernel, n),
            out_shape=sol_shape,
            in_specs=[vmem] * 4,
            out_specs=vmem,
            scratch_shapes=scratch
            + [
                pltpu.VMEM(parts.shape, parts.dtype),
                pltpu.SemaphoreType.DMA((1,)),
                pltpu.SemaphoreType.DMA((n,)),
                pltpu.SemaphoreType.DMA((n,)),
            ],
            compiler_params=pltpu.CompilerParams(collective_id=0, **params),
        )(rhs, parts, inv, blocks)
    return pl.pallas_call(
        functools.partial(sep_backward_kernel, n),
        out_shape=(sol_shape, jax.ShapeDtypeStruct((n, rows, width), jnp.bfloat16)),
        in_specs=[vmem] * 3,
        out_specs=(vmem, vmem),
        scratch_shapes=scratch,
        compiler_params=pltpu.CompilerParams(collective_id=1, **params),
    )(start, inv, blocks)


def top_solve_kernel(nt, span, start_ref, inv_ref, lower_ref, coef_ref, half_ref, fwd_half, fwd_full):
    for t in range(nt):
        cols = slice(t * span, (t + 1) * span)
        residue = start_ref[:, cols]
        if t > 0:
            residue = residue - _nt(fwd_half[:, : t * span], lower_ref[cols, : t * span])
        solved = _nt_exact(residue, inv_ref[t])
        fwd_full[:, cols] = solved
        fwd_half[:, cols] = solved.astype(jnp.bfloat16)
    for t in reversed(range(nt)):
        cols = slice(t * span, (t + 1) * span)
        residue = fwd_full[:, cols]
        if t < nt - 1:
            residue = residue - _nn(half_ref[:, (t + 1) * span :], lower_ref[(t + 1) * span :, cols])
        solved = _nn_exact(residue, inv_ref[t])
        coef_ref[:, cols] = solved
        half_ref[:, cols] = solved.astype(jnp.bfloat16)


def top_solve(top_start, top_inverse, top_lower):
    nt, span = top_inverse.shape[0], top_inverse.shape[1]
    rows, width = top_start.shape
    vmem = pl.BlockSpec(memory_space=pltpu.VMEM)
    return pl.pallas_call(
        functools.partial(top_solve_kernel, nt, span),
        out_shape=(
            jax.ShapeDtypeStruct((rows, width), jnp.float32),
            jax.ShapeDtypeStruct((rows, width), jnp.bfloat16),
        ),
        in_specs=[vmem] * 3,
        out_specs=(vmem, vmem),
        scratch_shapes=[
            pltpu.VMEM((rows, width), jnp.bfloat16),
            pltpu.VMEM((rows, width), jnp.float32),
        ],
        compiler_params=pltpu.CompilerParams(vmem_limit_bytes=48 * 1024 * 1024),
    )(top_start, top_inverse, top_lower)


def evaluate_kernel(slots, pattern_ref, coef_ref, centre_ref, column_ref, out_ref, acc, spread):
    m = pl.program_id(0)
    acc[...] = jnp.zeros_like(acc)
    column = column_ref[0]
    width = centre_ref.shape[2]
    for comp in range(3):
        spread[comp] = jnp.broadcast_to(column[:, comp : comp + 1], (column.shape[0], width))

    def one_slot(s, carry):
        @pl.when(pattern_ref[m, s] != 0)
        def _():
            centre = centre_ref[s]
            dist = None
            for comp in range(3):
                delta = centre[comp : comp + 1, :] - spread[comp]
                dist = delta * delta if dist is None else dist + delta * delta
            weight = jnp.maximum(1.0 - dist * (1.0 / support_sq), 0.0)
            kernel = (weight * weight * weight).astype(jnp.bfloat16)
            acc[...] += _nt(coef_ref[s], kernel)

        return carry

    lax.fori_loop(0, slots, one_slot, 0)
    out_ref[...] = acc[...]


def evaluate_all(coef_all, centre_all, point_columns, pattern):
    slots, rows, span = coef_all.shape
    blocks = point_columns.shape[0]
    full = lambda shape: pl.BlockSpec(shape, lambda m, pat: (0,) * len(shape))
    grid_spec = pltpu.PrefetchScalarGridSpec(
        num_scalar_prefetch=1,
        grid=(blocks,),
        in_specs=[
            full(coef_all.shape),
            full(centre_all.shape),
            pl.BlockSpec((1, span, point_columns.shape[2]), lambda m, pat: (m, 0, 0)),
        ],
        out_specs=pl.BlockSpec((rows, span), lambda m, pat: (0, m)),
        scratch_shapes=[
            pltpu.VMEM((rows, span), jnp.float32),
            pltpu.VMEM((3, span, centre_all.shape[2]), jnp.float32),
        ],
    )
    return pl.pallas_call(
        functools.partial(evaluate_kernel, slots),
        out_shape=jax.ShapeDtypeStruct((rows, blocks * span), jnp.float32),
        grid_spec=grid_spec,
    )(pattern, coef_all, centre_all, point_columns)


def top_reduce_kernel(n, groups, span, term_ref, total_ref, parts_a, parts_b, gathered, local_sem, send_a, recv_a, send_b, recv_b, send_c, recv_c):
    me = lax.axis_index("grp")
    leaf = lax.axis_index("leaf")
    barrier = pltpu.get_barrier_semaphore()
    for r in range(n):
        @pl.when(me != r)
        def _():
            pl.semaphore_signal(barrier, inc=1, device_id=(leaf, r), device_id_type=MESH)
    for g in range(groups):
        @pl.when(leaf != g)
        def _():
            pl.semaphore_signal(barrier, inc=1, device_id=(g, me), device_id_type=MESH)
    pl.semaphore_wait(barrier, n - 1 + groups - 1)

    def column(q):
        return term_ref.at[:, pl.ds(pl.multiple_of(q * span, span), span)]

    def copy_a(k):
        dest = lax.rem(me + k, n)
        return pltpu.make_async_remote_copy(
            column(dest), parts_a.at[me], send_a.at[k], recv_a.at[me], device_id=(leaf, dest), device_id_type=MESH
        )

    def wait_a(k):
        src = lax.rem(me + n - k, n)
        pltpu.make_async_remote_copy(
            column(src), parts_a.at[src], send_a.at[0], recv_a.at[src], device_id=(leaf, src), device_id_type=MESH
        ).wait_recv()

    own = pltpu.make_async_copy(column(me), parts_a.at[me], local_sem.at[0])
    own.start()
    for k in range(1, n):
        copy_a(k).start()
    own.wait()
    for k in range(1, n):
        wait_a(k)
    for k in range(1, n):
        copy_a(k).wait_send()
    total = parts_a[0]
    for q in range(1, n):
        total = total + parts_a[q]
    parts_b[leaf] = total

    def copy_b(k):
        dest = lax.rem(leaf + k, groups)
        return pltpu.make_async_remote_copy(
            parts_b.at[leaf], parts_b.at[leaf], send_b.at[k], recv_b.at[leaf], device_id=(dest, me), device_id_type=MESH
        )

    for k in range(1, groups):
        copy_b(k).start()
    for k in range(1, groups):
        src = lax.rem(leaf + groups - k, groups)
        pltpu.make_async_remote_copy(
            parts_b.at[src], parts_b.at[src], send_b.at[0], recv_b.at[src], device_id=(src, me), device_id_type=MESH
        ).wait_recv()
    for k in range(1, groups):
        copy_b(k).wait_send()
    summed = parts_b[0]
    for g in range(1, groups):
        summed = summed + parts_b[g]
    gathered[me] = summed

    def copy_c(k):
        dest = lax.rem(me + k, n)
        return pltpu.make_async_remote_copy(
            gathered.at[me], gathered.at[me], send_c.at[k], recv_c.at[me], device_id=(leaf, dest), device_id_type=MESH
        )

    for k in range(1, n):
        copy_c(k).start()
    for k in range(1, n):
        src = lax.rem(me + n - k, n)
        pltpu.make_async_remote_copy(
            gathered.at[src], gathered.at[src], send_c.at[0], recv_c.at[src], device_id=(leaf, src), device_id_type=MESH
        ).wait_recv()
    for k in range(1, n):
        copy_c(k).wait_send()
    for q in range(n):
        total_ref[:, q * span : (q + 1) * span] = gathered[q]


def top_reduce(term, n, groups):
    rows, width = term.shape
    span = width // n
    vmem = pl.BlockSpec(memory_space=pltpu.VMEM)
    return pl.pallas_call(
        functools.partial(top_reduce_kernel, n, groups, span),
        out_shape=jax.ShapeDtypeStruct((rows, width), jnp.float32),
        in_specs=[vmem],
        out_specs=vmem,
        scratch_shapes=[
            pltpu.VMEM((n, rows, span), jnp.float32),
            pltpu.VMEM((groups, rows, span), jnp.float32),
            pltpu.VMEM((n, rows, span), jnp.float32),
            pltpu.SemaphoreType.DMA((1,)),
            pltpu.SemaphoreType.DMA((n,)),
            pltpu.SemaphoreType.DMA((n,)),
            pltpu.SemaphoreType.DMA((groups,)),
            pltpu.SemaphoreType.DMA((groups,)),
            pltpu.SemaphoreType.DMA((n,)),
            pltpu.SemaphoreType.DMA((n,)),
        ],
        compiler_params=pltpu.CompilerParams(collective_id=2, has_side_effects=True),
    )(term)


def slot_ranks(dest_rows, grp_size):
    onehot = (dest_rows[..., None] == jnp.arange(grp_size)).astype(jnp.int32)
    before = jnp.cumsum(onehot, axis=-2) - onehot
    return jnp.sum(before * onehot, axis=-1)


def evaluate(coef_all, centre_all, block_points, block_mask):
    dist = jnp.zeros((centre_all.shape[0], centre_all.shape[2], block_points.shape[1]), jnp.float32)
    for comp in range(3):
        delta = centre_all[:, comp, :, None] - block_points[None, comp, None, :]
        dist = dist + delta * delta
    weight = jnp.maximum(1.0 - dist / support_sq, 0.0) ** 3
    kernel = (weight * block_mask.astype(jnp.float32)[:, None, None]).astype(jnp.bfloat16)
    return jnp.einsum("krs,ksp->rp", coef_all, kernel, preferred_element_type=jnp.float32)


def on_device(
    rhs_leaf,
    rhs_sep,
    rhs_top,
    leaf_inverse,
    leaf_coupling,
    leaf_targets,
    sep_inverse,
    sep_blocks,
    top_coupling,
    top_inverse,
    top_lower,
    dest_map,
    centers,
    points,
    eval_pattern,
):
    grp_size = lax.axis_size("grp")
    my_index = lax.axis_index("grp")
    blocks_here = leaf_inverse.shape[0]
    snapshots = rhs_leaf.shape[0]
    span = leaf_inverse.shape[1]
    slot_count = CAP
    leaf_rhs = rhs_leaf.reshape(snapshots, blocks_here, span).transpose(1, 0, 2)
    leaf_sol = jnp.einsum("nrs,nts->nrt", leaf_rhs, leaf_inverse, precision=highest)
    leaf_half = leaf_sol.astype(jnp.bfloat16)
    partial_value = jnp.einsum(
        "nrs,ncbs->ncrb", leaf_half, leaf_coupling, preferred_element_type=jnp.float32
    )
    onehot = (leaf_targets[:, :, None] == jnp.arange(grp_size)[None, None, :]).astype(jnp.float32)
    picked = onehot
    parts = jnp.einsum("ncq,ncrb->qrb", picked, partial_value, precision=highest).astype(jnp.bfloat16)
    inverse_own = sep_inverse[0]
    own_blocks = sep_blocks[0]
    sep_sol = sep_solve("forward", (rhs_sep, parts), inverse_own, own_blocks, grp_size)
    sep_half = sep_sol.astype(jnp.bfloat16)
    top_term = jnp.dot(sep_half, top_coupling, preferred_element_type=jnp.float32)
    top_total = top_reduce(top_term, grp_size, lax.axis_size("leaf"))
    top_start = rhs_top - top_total
    coef_top, top_half = top_solve(top_start, top_inverse, top_lower)
    back_start = sep_sol - lax.dot_general(
        top_half, top_coupling, (((1,), (1,)), ((), ())), preferred_element_type=jnp.float32
    )

    coef_sep, known_table = sep_solve("backward", back_start, inverse_own, own_blocks, grp_size)
    picked = jnp.einsum(
        "ncq,qrb->ncrb",
        onehot.astype(jnp.bfloat16),
        known_table,
        preferred_element_type=jnp.float32,
    ).astype(jnp.bfloat16)
    reduced = jnp.einsum(
        "ncrb,ncbs->nrs", picked, leaf_coupling, preferred_element_type=jnp.float32
    )
    leaf_coef = jnp.einsum("nrs,nst->nrt", leaf_sol - reduced, leaf_inverse, precision=highest)
    coef_leaf = leaf_coef.transpose(1, 0, 2).reshape(snapshots, blocks_here * span)
    leaf_out = leaf_coef.astype(jnp.bfloat16)
    slot_ids = jnp.arange(slot_count)
    grp_ids = jnp.arange(grp_size)
    own_dest = dest_map[:, 0]
    slot_rank = slot_ranks(own_dest[None, :], grp_size)[0]
    selector = (own_dest[None, None, :] == grp_ids[:, None, None]) & (
        slot_rank[None, None, :] == slot_ids[None, :, None]
    )
    send_coef = jnp.einsum(
        "dkj,jrt->dkrt", selector.astype(jnp.bfloat16), leaf_out, preferred_element_type=jnp.float32
    ).astype(jnp.bfloat16)
    send_centre = jnp.einsum(
        "dkj,jct->dkct", selector.astype(jnp.float32), centers, precision=highest
    )
    received, recv_centre = (
        lax.all_to_all(send_coef, "grp", split_axis=0, concat_axis=0, tiled=True),
        lax.all_to_all(
            send_centre.astype(jnp.bfloat16), "grp", split_axis=0, concat_axis=0, tiled=True
        ).astype(send_centre.dtype),
    )
    slot_total = grp_size * slot_count
    coef_all = received.reshape(slot_total, snapshots, span)
    centre_all = recv_centre.reshape(slot_total, 3, span)
    point_blocks = eval_pattern.shape[0]
    point_columns = points[0].T.reshape(point_blocks, span, points.shape[1])
    values = evaluate_all(coef_all, centre_all, point_columns, eval_pattern)
    return (coef_leaf, coef_sep, coef_top, values)


def solution(mesh):
    in_specs = (
        P(None, ("leaf", "grp")),
        P(None, ("leaf", "grp")),
        P(),
        P(("leaf", "grp"), None, None),
        P(("leaf", "grp"), None, None, None),
        P(("leaf", "grp"), None),
        P(("leaf", "grp"), None, None),
        P(("leaf", "grp"), None, None, None),
        P(("leaf", "grp"), None),
        P(),
        P(),
        P(("leaf", "grp"), None),
        P(("leaf", "grp"), None, None),
        P(("leaf", "grp"), None, None),
        P(("leaf", "grp"), None),
    )
    out_specs = (P(None, ("leaf", "grp")), P(None, ("leaf", "grp")), P(), P(None, ("leaf", "grp")))
    return jax.shard_map(
        on_device, mesh=mesh, in_specs=in_specs, out_specs=out_specs, check_vma=False
    )
```

```python
import functools

import jax
import jax.numpy as jnp
from jax import lax
from jax.sharding import PartitionSpec as P
from jax.experimental import pallas as pl
from jax.experimental.pallas import tpu as pltpu

MESH = pl.DeviceIdType.MESH

CAP = 2


highest = lax.Precision.HIGHEST
support_sq = 0.25


def split_up(shard, dim, peers):
    dims = shard.shape
    pieces = shard.reshape(*dims[:dim], peers, dims[dim] // peers, *dims[dim + 1 :])
    return jnp.moveaxis(pieces, dim, 0)


def sum_at_owner(shard, axis, dim):
    pieces = split_up(shard, dim, lax.axis_size(axis))
    arrived = lax.all_to_all(pieces, axis, split_axis=0, concat_axis=0, tiled=True)
    return arrived.astype(jnp.float32).sum(axis=0)


def from_root(shard, axis, root):
    return lax.dynamic_index_in_dim(lax.all_gather(shard, axis), root, 0, keepdims=False)


def copy_for_each(shard, axis):
    copies = jnp.broadcast_to(shard, (lax.axis_size(axis), *shard.shape))
    return lax.all_to_all(copies, axis, split_axis=0, concat_axis=0, tiled=True)


def over_copies(shard, axis):
    return copy_for_each(shard, axis).astype(jnp.float32).sum(axis=0)


def joined_along(pieces, dim):
    dims = list(pieces.shape[1:])
    dims[dim] *= pieces.shape[0]
    return jnp.moveaxis(pieces, 0, dim).reshape(dims)


def gather_directly(shard, axis, dim):
    pieces = copy_for_each(shard, axis)
    return joined_along(pieces, dim)


def _nt(a, b):
    return lax.dot_general(a, b, (((1,), (1,)), ((), ())), preferred_element_type=jnp.float32)


def _nn(a, b):
    return lax.dot_general(a, b, (((1,), (0,)), ((), ())), preferred_element_type=jnp.float32)


def _nt_exact(a, b):
    return lax.dot_general(
        a, b, (((1,), (1,)), ((), ())), precision=highest, preferred_element_type=jnp.float32
    )


def _nn_exact(a, b):
    return lax.dot_general(
        a, b, (((1,), (0,)), ((), ())), precision=highest, preferred_element_type=jnp.float32
    )


def _greet_group(n, leaf, me):
    barrier = pltpu.get_barrier_semaphore()
    for r in range(n):
        @pl.when(me != r)
        def _():
            pl.semaphore_signal(barrier, inc=1, device_id=(leaf, r), device_id_type=MESH)
    pl.semaphore_wait(barrier, n - 1)


def _block_copy(halves, q, dest, send_sem, recv_sem, leaf):
    return pltpu.make_async_remote_copy(
        src_ref=halves.at[q],
        dst_ref=halves.at[q],
        send_sem=send_sem,
        recv_sem=recv_sem.at[q],
        device_id=(leaf, dest),
        device_id_type=MESH,
    )


def sep_forward_kernel(n, rhs_ref, part_ref, inv_ref, blocks_ref, sol_ref, halves, resid, send_sem, recv_sem, arrived, local_sem, give_sem, take_sem):
    me = lax.axis_index("grp")
    leaf = lax.axis_index("leaf")
    _greet_group(n, leaf, me)

    def give(dest):
        return pltpu.make_async_remote_copy(
            part_ref.at[dest], arrived.at[me], give_sem.at[dest], take_sem.at[me], device_id=(leaf, dest), device_id_type=MESH
        )

    own = pltpu.make_async_copy(part_ref.at[me], arrived.at[me], local_sem.at[0])
    own.start()
    for dest in range(n):
        @pl.when(me != dest)
        def _():
            give(dest).start()
    own.wait()
    for src in range(n):
        @pl.when(me != src)
        def _():
            pltpu.make_async_remote_copy(
                part_ref.at[src], arrived.at[src], give_sem.at[src], take_sem.at[src], device_id=(leaf, src), device_id_type=MESH
            ).wait_recv()
    total = arrived[0].astype(jnp.float32)
    for src in range(1, n):
        total = total + arrived[src].astype(jnp.float32)
    resid[...] = rhs_ref[...] - total
    for dest in range(n):
        @pl.when(me != dest)
        def _():
            give(dest).wait_send()

    def step(q, carry):
        @pl.when(me == q)
        def _():
            solved = _nt_exact(resid[...], inv_ref[...])
            sol_ref[...] = solved
            halves[q] = solved.astype(jnp.bfloat16)
            for k in range(1, n):
                @pl.when(q + k < n)
                def _():
                    _block_copy(halves, q, q + k, send_sem.at[k], recv_sem, leaf).start()
            for k in range(1, n):
                @pl.when(q + k < n)
                def _():
                    _block_copy(halves, q, q + k, send_sem.at[k], recv_sem, leaf).wait_send()

        @pl.when(me > q)
        def _():
            _block_copy(halves, q, q, send_sem.at[0], recv_sem, leaf).wait_recv()
            resid[...] = resid[...] - _nt(halves[q], blocks_ref[q])

        return carry

    lax.fori_loop(0, n, step, 0)


def sep_backward_kernel(n, start_ref, inv_ref, blocks_ref, sol_ref, table_ref, halves, resid, send_sem, recv_sem):
    me = lax.axis_index("grp")
    leaf = lax.axis_index("leaf")
    _greet_group(n, leaf, me)
    resid[...] = start_ref[...]

    def step(s, carry):
        q = n - 1 - s

        @pl.when(me == q)
        def _():
            solved = _nn_exact(resid[...], inv_ref[...])
            sol_ref[...] = solved
            halves[q] = solved.astype(jnp.bfloat16)
            for k in range(1, n):
                dest = lax.rem(q - k + n, n)
                _block_copy(halves, q, dest, send_sem.at[k], recv_sem, leaf).start()
            for k in range(1, n):
                dest = lax.rem(q - k + n, n)
                _block_copy(halves, q, dest, send_sem.at[k], recv_sem, leaf).wait_send()

        @pl.when(me != q)
        def _():
            _block_copy(halves, q, q, send_sem.at[0], recv_sem, leaf).wait_recv()

        @pl.when(me < q)
        def _():
            resid[...] = resid[...] - _nn(halves[q], blocks_ref[q])

        return carry

    lax.fori_loop(0, n, step, 0)
    table_ref[...] = halves[...]


def sep_solve(kind, start, inv, blocks, n):
    rows, width = (start[0] if kind == "forward" else start).shape
    vmem = pl.BlockSpec(memory_space=pltpu.VMEM)
    scratch = [
        pltpu.VMEM((n, rows, width), jnp.bfloat16),
        pltpu.VMEM((rows, width), jnp.float32),
        pltpu.SemaphoreType.DMA((n,)),
        pltpu.SemaphoreType.DMA((n,)),
    ]
    sol_shape = jax.ShapeDtypeStruct((rows, width), jnp.float32)
    params = dict(has_side_effects=True, vmem_limit_bytes=48 * 1024 * 1024)
    if kind == "forward":
        rhs, parts = start
        return pl.pallas_call(
            functools.partial(sep_forward_kernel, n),
            out_shape=sol_shape,
            in_specs=[vmem] * 4,
            out_specs=vmem,
            scratch_shapes=scratch
            + [
                pltpu.VMEM(parts.shape, parts.dtype),
                pltpu.SemaphoreType.DMA((1,)),
                pltpu.SemaphoreType.DMA((n,)),
                pltpu.SemaphoreType.DMA((n,)),
            ],
            compiler_params=pltpu.CompilerParams(collective_id=0, **params),
        )(rhs, parts, inv, blocks)
    return pl.pallas_call(
        functools.partial(sep_backward_kernel, n),
        out_shape=(sol_shape, jax.ShapeDtypeStruct((n, rows, width), jnp.bfloat16)),
        in_specs=[vmem] * 3,
        out_specs=(vmem, vmem),
        scratch_shapes=scratch,
        compiler_params=pltpu.CompilerParams(collective_id=1, **params),
    )(start, inv, blocks)


def top_solve_kernel(nt, span, start_ref, inv_ref, lower_ref, coef_ref, half_ref, fwd_half, fwd_full):
    for t in range(nt):
        cols = slice(t * span, (t + 1) * span)
        residue = start_ref[:, cols]
        if t > 0:
            residue = residue - _nt(fwd_half[:, : t * span], lower_ref[cols, : t * span])
        solved = _nt_exact(residue, inv_ref[t])
        fwd_full[:, cols] = solved
        fwd_half[:, cols] = solved.astype(jnp.bfloat16)
    for t in reversed(range(nt)):
        cols = slice(t * span, (t + 1) * span)
        residue = fwd_full[:, cols]
        if t < nt - 1:
            residue = residue - _nn(half_ref[:, (t + 1) * span :], lower_ref[(t + 1) * span :, cols])
        solved = _nn_exact(residue, inv_ref[t])
        coef_ref[:, cols] = solved
        half_ref[:, cols] = solved.astype(jnp.bfloat16)


def top_solve(top_start, top_inverse, top_lower):
    nt, span = top_inverse.shape[0], top_inverse.shape[1]
    rows, width = top_start.shape
    vmem = pl.BlockSpec(memory_space=pltpu.VMEM)
    return pl.pallas_call(
        functools.partial(top_solve_kernel, nt, span),
        out_shape=(
            jax.ShapeDtypeStruct((rows, width), jnp.float32),
            jax.ShapeDtypeStruct((rows, width), jnp.bfloat16),
        ),
        in_specs=[vmem] * 3,
        out_specs=(vmem, vmem),
        scratch_shapes=[
            pltpu.VMEM((rows, width), jnp.bfloat16),
            pltpu.VMEM((rows, width), jnp.float32),
        ],
        compiler_params=pltpu.CompilerParams(vmem_limit_bytes=48 * 1024 * 1024),
    )(top_start, top_inverse, top_lower)


def evaluate_kernel(slots, pattern_ref, coef_ref, centre_ref, column_ref, out_ref, acc, spread):
    m = pl.program_id(0)
    acc[...] = jnp.zeros_like(acc)
    column = column_ref[0]
    width = centre_ref.shape[2]
    for comp in range(3):
        spread[comp] = jnp.broadcast_to(column[:, comp : comp + 1], (column.shape[0], width))

    def one_slot(s, carry):
        @pl.when(pattern_ref[m, s] != 0)
        def _():
            centre = centre_ref[s]
            dist = None
            for comp in range(3):
                delta = centre[comp : comp + 1, :] - spread[comp]
                dist = delta * delta if dist is None else dist + delta * delta
            weight = jnp.maximum(1.0 - dist * (1.0 / support_sq), 0.0)
            kernel = (weight * weight * weight).astype(jnp.bfloat16)
            acc[...] += _nt(coef_ref[s], kernel)

        return carry

    lax.fori_loop(0, slots, one_slot, 0)
    out_ref[...] = acc[...]


def evaluate_all(coef_all, centre_all, point_columns, pattern):
    slots, rows, span = coef_all.shape
    blocks = point_columns.shape[0]
    full = lambda shape: pl.BlockSpec(shape, lambda m, pat: (0,) * len(shape))
    grid_spec = pltpu.PrefetchScalarGridSpec(
        num_scalar_prefetch=1,
        grid=(blocks,),
        in_specs=[
            full(coef_all.shape),
            full(centre_all.shape),
            pl.BlockSpec((1, span, point_columns.shape[2]), lambda m, pat: (m, 0, 0)),
        ],
        out_specs=pl.BlockSpec((rows, span), lambda m, pat: (0, m)),
        scratch_shapes=[
            pltpu.VMEM((rows, span), jnp.float32),
            pltpu.VMEM((3, span, centre_all.shape[2]), jnp.float32),
        ],
    )
    return pl.pallas_call(
        functools.partial(evaluate_kernel, slots),
        out_shape=jax.ShapeDtypeStruct((rows, blocks * span), jnp.float32),
        grid_spec=grid_spec,
    )(pattern, coef_all, centre_all, point_columns)


def top_reduce_kernel(n, groups, span, term_ref, total_ref, parts_a, parts_b, gathered, local_sem, send_a, recv_a, send_b, recv_b, send_c, recv_c):
    me = lax.axis_index("grp")
    leaf = lax.axis_index("leaf")
    barrier = pltpu.get_barrier_semaphore()
    for r in range(n):
        @pl.when(me != r)
        def _():
            pl.semaphore_signal(barrier, inc=1, device_id=(leaf, r), device_id_type=MESH)
    for g in range(groups):
        @pl.when(leaf != g)
        def _():
            pl.semaphore_signal(barrier, inc=1, device_id=(g, me), device_id_type=MESH)
    pl.semaphore_wait(barrier, n - 1 + groups - 1)

    def column(q):
        return term_ref.at[:, pl.ds(pl.multiple_of(q * span, span), span)]

    def copy_a(k):
        dest = lax.rem(me + k, n)
        return pltpu.make_async_remote_copy(
            column(dest), parts_a.at[me], send_a.at[k], recv_a.at[me], device_id=(leaf, dest), device_id_type=MESH
        )

    def wait_a(k):
        src = lax.rem(me + n - k, n)
        pltpu.make_async_remote_copy(
            column(src), parts_a.at[src], send_a.at[0], recv_a.at[src], device_id=(leaf, src), device_id_type=MESH
        ).wait_recv()

    own = pltpu.make_async_copy(column(me), parts_a.at[me], local_sem.at[0])
    own.start()
    for k in range(1, n):
        copy_a(k).start()
    own.wait()
    for k in range(1, n):
        wait_a(k)
    for k in range(1, n):
        copy_a(k).wait_send()
    total = parts_a[0]
    for q in range(1, n):
        total = total + parts_a[q]
    parts_b[leaf] = total

    def copy_b(k):
        dest = lax.rem(leaf + k, groups)
        return pltpu.make_async_remote_copy(
            parts_b.at[leaf], parts_b.at[leaf], send_b.at[k], recv_b.at[leaf], device_id=(dest, me), device_id_type=MESH
        )

    for k in range(1, groups):
        copy_b(k).start()
    for k in range(1, groups):
        src = lax.rem(leaf + groups - k, groups)
        pltpu.make_async_remote_copy(
            parts_b.at[src], parts_b.at[src], send_b.at[0], recv_b.at[src], device_id=(src, me), device_id_type=MESH
        ).wait_recv()
    for k in range(1, groups):
        copy_b(k).wait_send()
    summed = parts_b[0]
    for g in range(1, groups):
        summed = summed + parts_b[g]
    gathered[me] = summed

    def copy_c(k):
        dest = lax.rem(me + k, n)
        return pltpu.make_async_remote_copy(
            gathered.at[me], gathered.at[me], send_c.at[k], recv_c.at[me], device_id=(leaf, dest), device_id_type=MESH
        )

    for k in range(1, n):
        copy_c(k).start()
    for k in range(1, n):
        src = lax.rem(me + n - k, n)
        pltpu.make_async_remote_copy(
            gathered.at[src], gathered.at[src], send_c.at[0], recv_c.at[src], device_id=(leaf, src), device_id_type=MESH
        ).wait_recv()
    for k in range(1, n):
        copy_c(k).wait_send()
    for q in range(n):
        total_ref[:, q * span : (q + 1) * span] = gathered[q]


def top_reduce(term, n, groups):
    rows, width = term.shape
    span = width // n
    vmem = pl.BlockSpec(memory_space=pltpu.VMEM)
    return pl.pallas_call(
        functools.partial(top_reduce_kernel, n, groups, span),
        out_shape=jax.ShapeDtypeStruct((rows, width), jnp.float32),
        in_specs=[vmem],
        out_specs=vmem,
        scratch_shapes=[
            pltpu.VMEM((n, rows, span), jnp.float32),
            pltpu.VMEM((groups, rows, span), jnp.float32),
            pltpu.VMEM((n, rows, span), jnp.float32),
            pltpu.SemaphoreType.DMA((1,)),
            pltpu.SemaphoreType.DMA((n,)),
            pltpu.SemaphoreType.DMA((n,)),
            pltpu.SemaphoreType.DMA((groups,)),
            pltpu.SemaphoreType.DMA((groups,)),
            pltpu.SemaphoreType.DMA((n,)),
            pltpu.SemaphoreType.DMA((n,)),
        ],
        compiler_params=pltpu.CompilerParams(collective_id=2, has_side_effects=True),
    )(term)


def exchange_kernel(n, coef_ref, centre_ref, coef_out, centre_out, coef_buf, centre_buf, local_sem, send_sem, recv_sem):
    me = lax.axis_index("grp")
    leaf = lax.axis_index("leaf")
    _greet_group(n, leaf, me)
    pairs = ((coef_ref, coef_buf), (centre_ref, centre_buf))

    def push(kind, k):
        source, buf = pairs[kind]
        dest = lax.rem(me + k, n)
        return pltpu.make_async_remote_copy(
            source.at[dest], buf.at[me], send_sem.at[kind, k], recv_sem.at[kind, me], device_id=(leaf, dest), device_id_type=MESH
        )

    owns = [pltpu.make_async_copy(source.at[me], buf.at[me], local_sem.at[kind]) for kind, (source, buf) in enumerate(pairs)]
    for own in owns:
        own.start()
    for k in range(1, n):
        for kind in range(2):
            push(kind, k).start()
    for own in owns:
        own.wait()
    for k in range(1, n):
        src = lax.rem(me + n - k, n)
        for kind, (source, buf) in enumerate(pairs):
            pltpu.make_async_remote_copy(
                source.at[src], buf.at[src], send_sem.at[kind, 0], recv_sem.at[kind, src], device_id=(leaf, src), device_id_type=MESH
            ).wait_recv()
    for k in range(1, n):
        for kind in range(2):
            push(kind, k).wait_send()
    coef_out[...] = coef_buf[...]
    centre_out[...] = centre_buf[...]


def exchange(send_coef, send_centre, n):
    vmem = pl.BlockSpec(memory_space=pltpu.VMEM)
    return pl.pallas_call(
        functools.partial(exchange_kernel, n),
        out_shape=(
            jax.ShapeDtypeStruct(send_coef.shape, send_coef.dtype),
            jax.ShapeDtypeStruct(send_centre.shape, send_centre.dtype),
        ),
        in_specs=[vmem] * 2,
        out_specs=(vmem, vmem),
        scratch_shapes=[
            pltpu.VMEM(send_coef.shape, send_coef.dtype),
            pltpu.VMEM(send_centre.shape, send_centre.dtype),
            pltpu.SemaphoreType.DMA((2,)),
            pltpu.SemaphoreType.DMA((2, n)),
            pltpu.SemaphoreType.DMA((2, n)),
        ],
        compiler_params=pltpu.CompilerParams(collective_id=3, has_side_effects=True),
    )(send_coef, send_centre)


def slot_ranks(dest_rows, grp_size):
    onehot = (dest_rows[..., None] == jnp.arange(grp_size)).astype(jnp.int32)
    before = jnp.cumsum(onehot, axis=-2) - onehot
    return jnp.sum(before * onehot, axis=-1)


def evaluate(coef_all, centre_all, block_points, block_mask):
    dist = jnp.zeros((centre_all.shape[0], centre_all.shape[2], block_points.shape[1]), jnp.float32)
    for comp in range(3):
        delta = centre_all[:, comp, :, None] - block_points[None, comp, None, :]
        dist = dist + delta * delta
    weight = jnp.maximum(1.0 - dist / support_sq, 0.0) ** 3
    kernel = (weight * block_mask.astype(jnp.float32)[:, None, None]).astype(jnp.bfloat16)
    return jnp.einsum("krs,ksp->rp", coef_all, kernel, preferred_element_type=jnp.float32)


def on_device(
    rhs_leaf,
    rhs_sep,
    rhs_top,
    leaf_inverse,
    leaf_coupling,
    leaf_targets,
    sep_inverse,
    sep_blocks,
    top_coupling,
    top_inverse,
    top_lower,
    dest_map,
    centers,
    points,
    eval_pattern,
):
    grp_size = lax.axis_size("grp")
    my_index = lax.axis_index("grp")
    blocks_here = leaf_inverse.shape[0]
    snapshots = rhs_leaf.shape[0]
    span = leaf_inverse.shape[1]
    slot_count = CAP
    leaf_rhs = rhs_leaf.reshape(snapshots, blocks_here, span).transpose(1, 0, 2)
    leaf_sol = jnp.einsum("nrs,nts->nrt", leaf_rhs, leaf_inverse, precision=highest)
    leaf_half = leaf_sol.astype(jnp.bfloat16)
    partial_value = jnp.einsum(
        "nrs,ncbs->ncrb", leaf_half, leaf_coupling, preferred_element_type=jnp.float32
    )
    onehot = (leaf_targets[:, :, None] == jnp.arange(grp_size)[None, None, :]).astype(jnp.float32)
    picked = onehot
    parts = jnp.einsum("ncq,ncrb->qrb", picked, partial_value, precision=highest).astype(jnp.bfloat16)
    inverse_own = sep_inverse[0]
    own_blocks = sep_blocks[0]
    sep_sol = sep_solve("forward", (rhs_sep, parts), inverse_own, own_blocks, grp_size)
    sep_half = sep_sol.astype(jnp.bfloat16)
    top_term = jnp.dot(sep_half, top_coupling, preferred_element_type=jnp.float32)
    top_total = top_reduce(top_term, grp_size, lax.axis_size("leaf"))
    top_start = rhs_top - top_total
    coef_top, top_half = top_solve(top_start, top_inverse, top_lower)
    back_start = sep_sol - lax.dot_general(
        top_half, top_coupling, (((1,), (1,)), ((), ())), preferred_element_type=jnp.float32
    )

    coef_sep, known_table = sep_solve("backward", back_start, inverse_own, own_blocks, grp_size)
    picked = jnp.einsum(
        "ncq,qrb->ncrb",
        onehot.astype(jnp.bfloat16),
        known_table,
        preferred_element_type=jnp.float32,
    ).astype(jnp.bfloat16)
    reduced = jnp.einsum(
        "ncrb,ncbs->nrs", picked, leaf_coupling, preferred_element_type=jnp.float32
    )
    leaf_coef = jnp.einsum("nrs,nst->nrt", leaf_sol - reduced, leaf_inverse, precision=highest)
    coef_leaf = leaf_coef.transpose(1, 0, 2).reshape(snapshots, blocks_here * span)
    leaf_out = leaf_coef.astype(jnp.bfloat16)
    slot_ids = jnp.arange(slot_count)
    grp_ids = jnp.arange(grp_size)
    own_dest = dest_map[:, 0]
    slot_rank = slot_ranks(own_dest[None, :], grp_size)[0]
    selector = (own_dest[None, None, :] == grp_ids[:, None, None]) & (
        slot_rank[None, None, :] == slot_ids[None, :, None]
    )
    send_coef = jnp.einsum(
        "dkj,jrt->dkrt", selector.astype(jnp.bfloat16), leaf_out, preferred_element_type=jnp.float32
    ).astype(jnp.bfloat16)
    send_centre = jnp.einsum(
        "dkj,jct->dkct", selector.astype(jnp.float32), centers, precision=highest
    )
    received, recv_centre = exchange(send_coef, send_centre, grp_size)
    slot_total = grp_size * slot_count
    coef_all = received.reshape(slot_total, snapshots, span)
    centre_all = recv_centre.reshape(slot_total, 3, span)
    point_blocks = eval_pattern.shape[0]
    point_columns = points[0].T.reshape(point_blocks, span, points.shape[1])
    values = evaluate_all(coef_all, centre_all, point_columns, eval_pattern)
    return (coef_leaf, coef_sep, coef_top, values)


def solution(mesh):
    in_specs = (
        P(None, ("leaf", "grp")),
        P(None, ("leaf", "grp")),
        P(),
        P(("leaf", "grp"), None, None),
        P(("leaf", "grp"), None, None, None),
        P(("leaf", "grp"), None),
        P(("leaf", "grp"), None, None),
        P(("leaf", "grp"), None, None, None),
        P(("leaf", "grp"), None),
        P(),
        P(),
        P(("leaf", "grp"), None),
        P(("leaf", "grp"), None, None),
        P(("leaf", "grp"), None, None),
        P(("leaf", "grp"), None),
    )
    out_specs = (P(None, ("leaf", "grp")), P(None, ("leaf", "grp")), P(), P(None, ("leaf", "grp")))
    return jax.shard_map(
        on_device, mesh=mesh, in_specs=in_specs, out_specs=out_specs, check_vma=False
    )
```

```python
import functools

import jax
import jax.numpy as jnp
from jax import lax
from jax.sharding import PartitionSpec as P
from jax.experimental import pallas as pl
from jax.experimental.pallas import tpu as pltpu

MESH = pl.DeviceIdType.MESH

CAP = 2


highest = lax.Precision.HIGHEST
support_sq = 0.25


def split_up(shard, dim, peers):
    dims = shard.shape
    pieces = shard.reshape(*dims[:dim], peers, dims[dim] // peers, *dims[dim + 1 :])
    return jnp.moveaxis(pieces, dim, 0)


def sum_at_owner(shard, axis, dim):
    pieces = split_up(shard, dim, lax.axis_size(axis))
    arrived = lax.all_to_all(pieces, axis, split_axis=0, concat_axis=0, tiled=True)
    return arrived.astype(jnp.float32).sum(axis=0)


def from_root(shard, axis, root):
    return lax.dynamic_index_in_dim(lax.all_gather(shard, axis), root, 0, keepdims=False)


def copy_for_each(shard, axis):
    copies = jnp.broadcast_to(shard, (lax.axis_size(axis), *shard.shape))
    return lax.all_to_all(copies, axis, split_axis=0, concat_axis=0, tiled=True)


def over_copies(shard, axis):
    return copy_for_each(shard, axis).astype(jnp.float32).sum(axis=0)


def joined_along(pieces, dim):
    dims = list(pieces.shape[1:])
    dims[dim] *= pieces.shape[0]
    return jnp.moveaxis(pieces, 0, dim).reshape(dims)


def gather_directly(shard, axis, dim):
    pieces = copy_for_each(shard, axis)
    return joined_along(pieces, dim)


def _nt(a, b):
    return lax.dot_general(a, b, (((1,), (1,)), ((), ())), preferred_element_type=jnp.float32)


def _nn(a, b):
    return lax.dot_general(a, b, (((1,), (0,)), ((), ())), preferred_element_type=jnp.float32)


def _nt_exact(a, b):
    return lax.dot_general(
        a, b, (((1,), (1,)), ((), ())), precision=highest, preferred_element_type=jnp.float32
    )


def _nn_exact(a, b):
    return lax.dot_general(
        a, b, (((1,), (0,)), ((), ())), precision=highest, preferred_element_type=jnp.float32
    )


def _greet_group(n, leaf, me):
    barrier = pltpu.get_barrier_semaphore()
    for r in range(n):
        @pl.when(me != r)
        def _():
            pl.semaphore_signal(barrier, inc=1, device_id=(leaf, r), device_id_type=MESH)
    pl.semaphore_wait(barrier, n - 1)


def _block_copy(halves, q, dest, send_sem, recv_sem, leaf):
    return pltpu.make_async_remote_copy(
        src_ref=halves.at[q],
        dst_ref=halves.at[q],
        send_sem=send_sem,
        recv_sem=recv_sem.at[q],
        device_id=(leaf, dest),
        device_id_type=MESH,
    )


def _send_block(n, halves, s, solved, sol_ref, send_sem, recv_sem, leaf, dests):
    sol_ref[...] = solved
    halves[s] = solved.astype(jnp.bfloat16)
    for k in range(1, n):
        dest, live = dests(s, k)
        @pl.when(live)
        def _():
            _block_copy(halves, s, dest, send_sem.at[k], recv_sem, leaf).start()
    for k in range(1, n):
        dest, live = dests(s, k)
        @pl.when(live)
        def _():
            _block_copy(halves, s, dest, send_sem.at[k], recv_sem, leaf).wait_send()


def _through(y, hi_ref, lo_ref):
    return _nn(y, hi_ref[...]) + _nn(y, lo_ref[...])


def sep_forward_kernel(n, rhs_ref, part_ref, inv_ref, blocks_ref, hi_ref, lo_ref, sol_ref, halves, resid, base, send_sem, recv_sem, arrived, local_sem, give_sem, take_sem):
    me = lax.axis_index("grp")
    leaf = lax.axis_index("leaf")
    _greet_group(n, leaf, me)

    def give(dest):
        return pltpu.make_async_remote_copy(
            part_ref.at[dest], arrived.at[me], give_sem.at[dest], take_sem.at[me], device_id=(leaf, dest), device_id_type=MESH
        )

    own = pltpu.make_async_copy(part_ref.at[me], arrived.at[me], local_sem.at[0])
    own.start()
    for dest in range(n):
        @pl.when(me != dest)
        def _():
            give(dest).start()
    own.wait()
    for src in range(n):
        @pl.when(me != src)
        def _():
            pltpu.make_async_remote_copy(
                part_ref.at[src], arrived.at[src], give_sem.at[src], take_sem.at[src], device_id=(leaf, src), device_id_type=MESH
            ).wait_recv()
    total = arrived[0].astype(jnp.float32)
    for src in range(1, n):
        total = total + arrived[src].astype(jnp.float32)
    resid[...] = rhs_ref[...] - total
    for dest in range(n):
        @pl.when(me != dest)
        def _():
            give(dest).wait_send()

    dests = lambda s, k: (s + k, s + k < n)

    @pl.when(me == 0)
    def _():
        _send_block(n, halves, 0, _nt_exact(resid[...], inv_ref[...]), sol_ref, send_sem, recv_sem, leaf, dests)

    @pl.when(me == 1)
    def _():
        base[...] = _nt_exact(resid[...], inv_ref[...])

    def step(q, carry):
        @pl.when(me == q + 1)
        def _():
            _block_copy(halves, q, q, send_sem.at[0], recv_sem, leaf).wait_recv()
            solved = base[...] - _through(halves[q], hi_ref, lo_ref)
            _send_block(n, halves, q + 1, solved, sol_ref, send_sem, recv_sem, leaf, dests)

        @pl.when(me > q + 1)
        def _():
            _block_copy(halves, q, q, send_sem.at[0], recv_sem, leaf).wait_recv()
            resid[...] = resid[...] - _nt(halves[q], blocks_ref[q])

            @pl.when(me == q + 2)
            def _():
                base[...] = _nt_exact(resid[...], inv_ref[...])

        return carry

    lax.fori_loop(0, n - 1, step, 0)


def sep_backward_kernel(n, start_ref, inv_ref, blocks_ref, hi_ref, lo_ref, sol_ref, table_ref, halves, resid, base, send_sem, recv_sem):
    me = lax.axis_index("grp")
    leaf = lax.axis_index("leaf")
    _greet_group(n, leaf, me)
    resid[...] = start_ref[...]
    dests = lambda s, k: (lax.rem(s - k + n, n), True)

    @pl.when(me == n - 1)
    def _():
        _send_block(n, halves, n - 1, _nn_exact(resid[...], inv_ref[...]), sol_ref, send_sem, recv_sem, leaf, dests)

    @pl.when(me == n - 2)
    def _():
        base[...] = _nn_exact(resid[...], inv_ref[...])

    def step(s, carry):
        q = n - 1 - s

        @pl.when(me != q)
        def _():
            _block_copy(halves, q, q, send_sem.at[0], recv_sem, leaf).wait_recv()

        @pl.when(me == q - 1)
        def _():
            solved = base[...] - _through(halves[q], hi_ref, lo_ref)
            _send_block(n, halves, q - 1, solved, sol_ref, send_sem, recv_sem, leaf, dests)

        @pl.when(me < q - 1)
        def _():
            resid[...] = resid[...] - _nn(halves[q], blocks_ref[q])

            @pl.when(me == q - 2)
            def _():
                base[...] = _nn_exact(resid[...], inv_ref[...])

        return carry

    lax.fori_loop(0, n - 1, step, 0)
    @pl.when(me != 0)
    def _():
        _block_copy(halves, 0, 0, send_sem.at[0], recv_sem, leaf).wait_recv()
    table_ref[...] = halves[...]


def sep_solve(kind, start, inv, blocks, hi, lo, n):
    rows, width = (start[0] if kind == "forward" else start).shape
    vmem = pl.BlockSpec(memory_space=pltpu.VMEM)
    scratch = [
        pltpu.VMEM((n, rows, width), jnp.bfloat16),
        pltpu.VMEM((rows, width), jnp.float32),
        pltpu.VMEM((rows, width), jnp.float32),
        pltpu.SemaphoreType.DMA((n,)),
        pltpu.SemaphoreType.DMA((n,)),
    ]
    sol_shape = jax.ShapeDtypeStruct((rows, width), jnp.float32)
    params = dict(has_side_effects=True, vmem_limit_bytes=48 * 1024 * 1024)
    if kind == "forward":
        rhs, parts = start
        return pl.pallas_call(
            functools.partial(sep_forward_kernel, n),
            out_shape=sol_shape,
            in_specs=[vmem] * 6,
            out_specs=vmem,
            scratch_shapes=scratch
            + [
                pltpu.VMEM(parts.shape, parts.dtype),
                pltpu.SemaphoreType.DMA((1,)),
                pltpu.SemaphoreType.DMA((n,)),
                pltpu.SemaphoreType.DMA((n,)),
            ],
            compiler_params=pltpu.CompilerParams(collective_id=0, **params),
        )(rhs, parts, inv, blocks, hi, lo)
    return pl.pallas_call(
        functools.partial(sep_backward_kernel, n),
        out_shape=(sol_shape, jax.ShapeDtypeStruct((n, rows, width), jnp.bfloat16)),
        in_specs=[vmem] * 5,
        out_specs=(vmem, vmem),
        scratch_shapes=scratch,
        compiler_params=pltpu.CompilerParams(collective_id=1, **params),
    )(start, inv, blocks, hi, lo)


def split_pair(matrix):
    hi = matrix.astype(jnp.bfloat16)
    lo = (matrix - hi.astype(jnp.float32)).astype(jnp.bfloat16)
    return hi, lo


def top_solve_kernel(nt, span, start_ref, inv_ref, lower_ref, coef_ref, half_ref, fwd_half, fwd_full):
    for t in range(nt):
        cols = slice(t * span, (t + 1) * span)
        residue = start_ref[:, cols]
        if t > 0:
            residue = residue - _nt(fwd_half[:, : t * span], lower_ref[cols, : t * span])
        solved = _nt_exact(residue, inv_ref[t])
        fwd_full[:, cols] = solved
        fwd_half[:, cols] = solved.astype(jnp.bfloat16)
    for t in reversed(range(nt)):
        cols = slice(t * span, (t + 1) * span)
        residue = fwd_full[:, cols]
        if t < nt - 1:
            residue = residue - _nn(half_ref[:, (t + 1) * span :], lower_ref[(t + 1) * span :, cols])
        solved = _nn_exact(residue, inv_ref[t])
        coef_ref[:, cols] = solved
        half_ref[:, cols] = solved.astype(jnp.bfloat16)


def top_solve(top_start, top_inverse, top_lower):
    nt, span = top_inverse.shape[0], top_inverse.shape[1]
    rows, width = top_start.shape
    vmem = pl.BlockSpec(memory_space=pltpu.VMEM)
    return pl.pallas_call(
        functools.partial(top_solve_kernel, nt, span),
        out_shape=(
            jax.ShapeDtypeStruct((rows, width), jnp.float32),
            jax.ShapeDtypeStruct((rows, width), jnp.bfloat16),
        ),
        in_specs=[vmem] * 3,
        out_specs=(vmem, vmem),
        scratch_shapes=[
            pltpu.VMEM((rows, width), jnp.bfloat16),
            pltpu.VMEM((rows, width), jnp.float32),
        ],
        compiler_params=pltpu.CompilerParams(vmem_limit_bytes=48 * 1024 * 1024),
    )(top_start, top_inverse, top_lower)


def evaluate_kernel(slots, pattern_ref, coef_ref, centre_ref, column_ref, out_ref, acc, spread):
    m = pl.program_id(0)
    acc[...] = jnp.zeros_like(acc)
    column = column_ref[0]
    width = centre_ref.shape[2]
    for comp in range(3):
        spread[comp] = jnp.broadcast_to(column[:, comp : comp + 1], (column.shape[0], width))

    def one_slot(s, carry):
        @pl.when(pattern_ref[m, s] != 0)
        def _():
            centre = centre_ref[s]
            dist = None
            for comp in range(3):
                delta = centre[comp : comp + 1, :] - spread[comp]
                dist = delta * delta if dist is None else dist + delta * delta
            weight = jnp.maximum(1.0 - dist * (1.0 / support_sq), 0.0)
            kernel = (weight * weight * weight).astype(jnp.bfloat16)
            acc[...] += _nt(coef_ref[s], kernel)

        return carry

    lax.fori_loop(0, slots, one_slot, 0)
    out_ref[...] = acc[...]


def evaluate_all(coef_all, centre_all, point_columns, pattern):
    slots, rows, span = coef_all.shape
    blocks = point_columns.shape[0]
    full = lambda shape: pl.BlockSpec(shape, lambda m, pat: (0,) * len(shape))
    grid_spec = pltpu.PrefetchScalarGridSpec(
        num_scalar_prefetch=1,
        grid=(blocks,),
        in_specs=[
            full(coef_all.shape),
            full(centre_all.shape),
            pl.BlockSpec((1, span, point_columns.shape[2]), lambda m, pat: (m, 0, 0)),
        ],
        out_specs=pl.BlockSpec((rows, span), lambda m, pat: (0, m)),
        scratch_shapes=[
            pltpu.VMEM((rows, span), jnp.float32),
            pltpu.VMEM((3, span, centre_all.shape[2]), jnp.float32),
        ],
    )
    return pl.pallas_call(
        functools.partial(evaluate_kernel, slots),
        out_shape=jax.ShapeDtypeStruct((rows, blocks * span), jnp.float32),
        grid_spec=grid_spec,
    )(pattern, coef_all, centre_all, point_columns)


def top_reduce_kernel(n, groups, span, term_ref, total_ref, parts_a, parts_b, gathered, local_sem, send_a, recv_a, send_b, recv_b, send_c, recv_c):
    me = lax.axis_index("grp")
    leaf = lax.axis_index("leaf")
    barrier = pltpu.get_barrier_semaphore()
    for r in range(n):
        @pl.when(me != r)
        def _():
            pl.semaphore_signal(barrier, inc=1, device_id=(leaf, r), device_id_type=MESH)
    for g in range(groups):
        @pl.when(leaf != g)
        def _():
            pl.semaphore_signal(barrier, inc=1, device_id=(g, me), device_id_type=MESH)
    pl.semaphore_wait(barrier, n - 1 + groups - 1)

    def column(q):
        return term_ref.at[:, pl.ds(pl.multiple_of(q * span, span), span)]

    def copy_a(k):
        dest = lax.rem(me + k, n)
        return pltpu.make_async_remote_copy(
            column(dest), parts_a.at[me], send_a.at[k], recv_a.at[me], device_id=(leaf, dest), device_id_type=MESH
        )

    def wait_a(k):
        src = lax.rem(me + n - k, n)
        pltpu.make_async_remote_copy(
            column(src), parts_a.at[src], send_a.at[0], recv_a.at[src], device_id=(leaf, src), device_id_type=MESH
        ).wait_recv()

    own = pltpu.make_async_copy(column(me), parts_a.at[me], local_sem.at[0])
    own.start()
    for k in range(1, n):
        copy_a(k).start()
    own.wait()
    for k in range(1, n):
        wait_a(k)
    for k in range(1, n):
        copy_a(k).wait_send()
    total = parts_a[0]
    for q in range(1, n):
        total = total + parts_a[q]
    parts_b[leaf] = total

    def copy_b(k):
        dest = lax.rem(leaf + k, groups)
        return pltpu.make_async_remote_copy(
            parts_b.at[leaf], parts_b.at[leaf], send_b.at[k], recv_b.at[leaf], device_id=(dest, me), device_id_type=MESH
        )

    for k in range(1, groups):
        copy_b(k).start()
    for k in range(1, groups):
        src = lax.rem(leaf + groups - k, groups)
        pltpu.make_async_remote_copy(
            parts_b.at[src], parts_b.at[src], send_b.at[0], recv_b.at[src], device_id=(src, me), device_id_type=MESH
        ).wait_recv()
    for k in range(1, groups):
        copy_b(k).wait_send()
    summed = parts_b[0]
    for g in range(1, groups):
        summed = summed + parts_b[g]
    gathered[me] = summed

    def copy_c(k):
        dest = lax.rem(me + k, n)
        return pltpu.make_async_remote_copy(
            gathered.at[me], gathered.at[me], send_c.at[k], recv_c.at[me], device_id=(leaf, dest), device_id_type=MESH
        )

    for k in range(1, n):
        copy_c(k).start()
    for k in range(1, n):
        src = lax.rem(me + n - k, n)
        pltpu.make_async_remote_copy(
            gathered.at[src], gathered.at[src], send_c.at[0], recv_c.at[src], device_id=(leaf, src), device_id_type=MESH
        ).wait_recv()
    for k in range(1, n):
        copy_c(k).wait_send()
    for q in range(n):
        total_ref[:, q * span : (q + 1) * span] = gathered[q]


def top_reduce(term, n, groups):
    rows, width = term.shape
    span = width // n
    vmem = pl.BlockSpec(memory_space=pltpu.VMEM)
    return pl.pallas_call(
        functools.partial(top_reduce_kernel, n, groups, span),
        out_shape=jax.ShapeDtypeStruct((rows, width), jnp.float32),
        in_specs=[vmem],
        out_specs=vmem,
        scratch_shapes=[
            pltpu.VMEM((n, rows, span), jnp.float32),
            pltpu.VMEM((groups, rows, span), jnp.float32),
            pltpu.VMEM((n, rows, span), jnp.float32),
            pltpu.SemaphoreType.DMA((1,)),
            pltpu.SemaphoreType.DMA((n,)),
            pltpu.SemaphoreType.DMA((n,)),
            pltpu.SemaphoreType.DMA((groups,)),
            pltpu.SemaphoreType.DMA((groups,)),
            pltpu.SemaphoreType.DMA((n,)),
            pltpu.SemaphoreType.DMA((n,)),
        ],
        compiler_params=pltpu.CompilerParams(collective_id=2, has_side_effects=True),
    )(term)


def exchange_kernel(n, coef_ref, centre_ref, coef_out, centre_out, coef_buf, centre_buf, local_sem, send_sem, recv_sem):
    me = lax.axis_index("grp")
    leaf = lax.axis_index("leaf")
    _greet_group(n, leaf, me)
    pairs = ((coef_ref, coef_buf), (centre_ref, centre_buf))

    def push(kind, k):
        source, buf = pairs[kind]
        dest = lax.rem(me + k, n)
        return pltpu.make_async_remote_copy(
            source.at[dest], buf.at[me], send_sem.at[kind, k], recv_sem.at[kind, me], device_id=(leaf, dest), device_id_type=MESH
        )

    owns = [pltpu.make_async_copy(source.at[me], buf.at[me], local_sem.at[kind]) for kind, (source, buf) in enumerate(pairs)]
    for own in owns:
        own.start()
    for k in range(1, n):
        for kind in range(2):
            push(kind, k).start()
    for own in owns:
        own.wait()
    for k in range(1, n):
        src = lax.rem(me + n - k, n)
        for kind, (source, buf) in enumerate(pairs):
            pltpu.make_async_remote_copy(
                source.at[src], buf.at[src], send_sem.at[kind, 0], recv_sem.at[kind, src], device_id=(leaf, src), device_id_type=MESH
            ).wait_recv()
    for k in range(1, n):
        for kind in range(2):
            push(kind, k).wait_send()
    coef_out[...] = coef_buf[...]
    centre_out[...] = centre_buf[...]


def exchange(send_coef, send_centre, n):
    vmem = pl.BlockSpec(memory_space=pltpu.VMEM)
    return pl.pallas_call(
        functools.partial(exchange_kernel, n),
        out_shape=(
            jax.ShapeDtypeStruct(send_coef.shape, send_coef.dtype),
            jax.ShapeDtypeStruct(send_centre.shape, send_centre.dtype),
        ),
        in_specs=[vmem] * 2,
        out_specs=(vmem, vmem),
        scratch_shapes=[
            pltpu.VMEM(send_coef.shape, send_coef.dtype),
            pltpu.VMEM(send_centre.shape, send_centre.dtype),
            pltpu.SemaphoreType.DMA((2,)),
            pltpu.SemaphoreType.DMA((2, n)),
            pltpu.SemaphoreType.DMA((2, n)),
        ],
        compiler_params=pltpu.CompilerParams(collective_id=3, has_side_effects=True),
    )(send_coef, send_centre)


def slot_ranks(dest_rows, grp_size):
    onehot = (dest_rows[..., None] == jnp.arange(grp_size)).astype(jnp.int32)
    before = jnp.cumsum(onehot, axis=-2) - onehot
    return jnp.sum(before * onehot, axis=-1)


def evaluate(coef_all, centre_all, block_points, block_mask):
    dist = jnp.zeros((centre_all.shape[0], centre_all.shape[2], block_points.shape[1]), jnp.float32)
    for comp in range(3):
        delta = centre_all[:, comp, :, None] - block_points[None, comp, None, :]
        dist = dist + delta * delta
    weight = jnp.maximum(1.0 - dist / support_sq, 0.0) ** 3
    kernel = (weight * block_mask.astype(jnp.float32)[:, None, None]).astype(jnp.bfloat16)
    return jnp.einsum("krs,ksp->rp", coef_all, kernel, preferred_element_type=jnp.float32)


def on_device(
    rhs_leaf,
    rhs_sep,
    rhs_top,
    leaf_inverse,
    leaf_coupling,
    leaf_targets,
    sep_inverse,
    sep_blocks,
    top_coupling,
    top_inverse,
    top_lower,
    dest_map,
    centers,
    points,
    eval_pattern,
):
    grp_size = lax.axis_size("grp")
    my_index = lax.axis_index("grp")
    blocks_here = leaf_inverse.shape[0]
    snapshots = rhs_leaf.shape[0]
    span = leaf_inverse.shape[1]
    slot_count = CAP
    leaf_rhs = rhs_leaf.reshape(snapshots, blocks_here, span).transpose(1, 0, 2)
    leaf_sol = jnp.einsum("nrs,nts->nrt", leaf_rhs, leaf_inverse, precision=highest)
    leaf_half = leaf_sol.astype(jnp.bfloat16)
    partial_value = jnp.einsum(
        "nrs,ncbs->ncrb", leaf_half, leaf_coupling, preferred_element_type=jnp.float32
    )
    onehot = (leaf_targets[:, :, None] == jnp.arange(grp_size)[None, None, :]).astype(jnp.float32)
    picked = onehot
    parts = jnp.einsum("ncq,ncrb->qrb", picked, partial_value, precision=highest).astype(jnp.bfloat16)
    inverse_own = sep_inverse[0]
    own_blocks = sep_blocks[0]
    before = lax.dynamic_index_in_dim(own_blocks, jnp.maximum(my_index - 1, 0), 0, keepdims=False)
    fwd_hi, fwd_lo = split_pair(
        jnp.dot(before.astype(jnp.float32).T, inverse_own.T, precision=highest)
    )
    after = lax.dynamic_index_in_dim(own_blocks, jnp.minimum(my_index + 1, grp_size - 1), 0, keepdims=False)
    bwd_hi, bwd_lo = split_pair(jnp.dot(after.astype(jnp.float32), inverse_own, precision=highest))
    sep_sol = sep_solve("forward", (rhs_sep, parts), inverse_own, own_blocks, fwd_hi, fwd_lo, grp_size)
    sep_half = sep_sol.astype(jnp.bfloat16)
    top_term = jnp.dot(sep_half, top_coupling, preferred_element_type=jnp.float32)
    top_total = top_reduce(top_term, grp_size, lax.axis_size("leaf"))
    top_start = rhs_top - top_total
    coef_top, top_half = top_solve(top_start, top_inverse, top_lower)
    back_start = sep_sol - lax.dot_general(
        top_half, top_coupling, (((1,), (1,)), ((), ())), preferred_element_type=jnp.float32
    )

    coef_sep, known_table = sep_solve(
        "backward", back_start, inverse_own, own_blocks, bwd_hi, bwd_lo, grp_size
    )
    picked = jnp.einsum(
        "ncq,qrb->ncrb",
        onehot.astype(jnp.bfloat16),
        known_table,
        preferred_element_type=jnp.float32,
    ).astype(jnp.bfloat16)
    reduced = jnp.einsum(
        "ncrb,ncbs->nrs", picked, leaf_coupling, preferred_element_type=jnp.float32
    )
    leaf_coef = jnp.einsum("nrs,nst->nrt", leaf_sol - reduced, leaf_inverse, precision=highest)
    coef_leaf = leaf_coef.transpose(1, 0, 2).reshape(snapshots, blocks_here * span)
    leaf_out = leaf_coef.astype(jnp.bfloat16)
    slot_ids = jnp.arange(slot_count)
    grp_ids = jnp.arange(grp_size)
    own_dest = dest_map[:, 0]
    slot_rank = slot_ranks(own_dest[None, :], grp_size)[0]
    selector = (own_dest[None, None, :] == grp_ids[:, None, None]) & (
        slot_rank[None, None, :] == slot_ids[None, :, None]
    )
    send_coef = jnp.einsum(
        "dkj,jrt->dkrt", selector.astype(jnp.bfloat16), leaf_out, preferred_element_type=jnp.float32
    ).astype(jnp.bfloat16)
    send_centre = jnp.einsum(
        "dkj,jct->dkct", selector.astype(jnp.float32), centers, precision=highest
    )
    received, recv_centre = exchange(send_coef, send_centre, grp_size)
    slot_total = grp_size * slot_count
    coef_all = received.reshape(slot_total, snapshots, span)
    centre_all = recv_centre.reshape(slot_total, 3, span)
    point_blocks = eval_pattern.shape[0]
    point_columns = points[0].T.reshape(point_blocks, span, points.shape[1])
    values = evaluate_all(coef_all, centre_all, point_columns, eval_pattern)
    return (coef_leaf, coef_sep, coef_top, values)


def solution(mesh):
    in_specs = (
        P(None, ("leaf", "grp")),
        P(None, ("leaf", "grp")),
        P(),
        P(("leaf", "grp"), None, None),
        P(("leaf", "grp"), None, None, None),
        P(("leaf", "grp"), None),
        P(("leaf", "grp"), None, None),
        P(("leaf", "grp"), None, None, None),
        P(("leaf", "grp"), None),
        P(),
        P(),
        P(("leaf", "grp"), None),
        P(("leaf", "grp"), None, None),
        P(("leaf", "grp"), None, None),
        P(("leaf", "grp"), None),
    )
    out_specs = (P(None, ("leaf", "grp")), P(None, ("leaf", "grp")), P(), P(None, ("leaf", "grp")))
    return jax.shard_map(
        on_device, mesh=mesh, in_specs=in_specs, out_specs=out_specs, check_vma=False
    )
```

```python
import functools

import jax
import jax.numpy as jnp
from jax import lax
from jax.sharding import PartitionSpec as P
from jax.experimental import pallas as pl
from jax.experimental.pallas import tpu as pltpu

MESH = pl.DeviceIdType.MESH

CAP = 2


highest = lax.Precision.HIGHEST
support_sq = 0.25


def split_up(shard, dim, peers):
    dims = shard.shape
    pieces = shard.reshape(*dims[:dim], peers, dims[dim] // peers, *dims[dim + 1 :])
    return jnp.moveaxis(pieces, dim, 0)


def sum_at_owner(shard, axis, dim):
    pieces = split_up(shard, dim, lax.axis_size(axis))
    arrived = lax.all_to_all(pieces, axis, split_axis=0, concat_axis=0, tiled=True)
    return arrived.astype(jnp.float32).sum(axis=0)


def from_root(shard, axis, root):
    return lax.dynamic_index_in_dim(lax.all_gather(shard, axis), root, 0, keepdims=False)


def copy_for_each(shard, axis):
    copies = jnp.broadcast_to(shard, (lax.axis_size(axis), *shard.shape))
    return lax.all_to_all(copies, axis, split_axis=0, concat_axis=0, tiled=True)


def over_copies(shard, axis):
    return copy_for_each(shard, axis).astype(jnp.float32).sum(axis=0)


def joined_along(pieces, dim):
    dims = list(pieces.shape[1:])
    dims[dim] *= pieces.shape[0]
    return jnp.moveaxis(pieces, 0, dim).reshape(dims)


def gather_directly(shard, axis, dim):
    pieces = copy_for_each(shard, axis)
    return joined_along(pieces, dim)


def _nt(a, b):
    return lax.dot_general(a, b, (((1,), (1,)), ((), ())), preferred_element_type=jnp.float32)


def _nn(a, b):
    return lax.dot_general(a, b, (((1,), (0,)), ((), ())), preferred_element_type=jnp.float32)


def _nt_exact(a, b):
    return lax.dot_general(
        a, b, (((1,), (1,)), ((), ())), precision=highest, preferred_element_type=jnp.float32
    )


def _nn_exact(a, b):
    return lax.dot_general(
        a, b, (((1,), (0,)), ((), ())), precision=highest, preferred_element_type=jnp.float32
    )


def _greet_group(n, leaf, me):
    barrier = pltpu.get_barrier_semaphore()
    for r in range(n):
        @pl.when(me != r)
        def _():
            pl.semaphore_signal(barrier, inc=1, device_id=(leaf, r), device_id_type=MESH)
    pl.semaphore_wait(barrier, n - 1)


def _block_copy(halves, q, dest, send_sem, recv_sem, leaf):
    return pltpu.make_async_remote_copy(
        src_ref=halves.at[q],
        dst_ref=halves.at[q],
        send_sem=send_sem,
        recv_sem=recv_sem.at[q],
        device_id=(leaf, dest),
        device_id_type=MESH,
    )


def _send_block(n, halves, s, solved, sol_ref, send_sem, recv_sem, leaf, dests):
    sol_ref[...] = solved
    halves[s] = solved.astype(jnp.bfloat16)
    for k in range(1, n):
        dest, live = dests(s, k)
        @pl.when(live)
        def _():
            _block_copy(halves, s, dest, send_sem.at[k], recv_sem, leaf).start()
            if k == 1:
                _block_copy(halves, s, dest, send_sem.at[k], recv_sem, leaf).wait_send()
    for k in range(2, n):
        dest, live = dests(s, k)
        @pl.when(live)
        def _():
            _block_copy(halves, s, dest, send_sem.at[k], recv_sem, leaf).wait_send()


def _through(y, hi_ref, lo_ref):
    return _nn(y, hi_ref[...]) + _nn(y, lo_ref[...])


def sep_forward_kernel(n, rhs_ref, part_ref, inv_ref, blocks_ref, hi_ref, lo_ref, sol_ref, halves, resid, base, send_sem, recv_sem, arrived, local_sem, give_sem, take_sem):
    me = lax.axis_index("grp")
    leaf = lax.axis_index("leaf")
    _greet_group(n, leaf, me)

    def give(dest):
        return pltpu.make_async_remote_copy(
            part_ref.at[dest], arrived.at[me], give_sem.at[dest], take_sem.at[me], device_id=(leaf, dest), device_id_type=MESH
        )

    own = pltpu.make_async_copy(part_ref.at[me], arrived.at[me], local_sem.at[0])
    own.start()
    for dest in range(n):
        @pl.when(me != dest)
        def _():
            give(dest).start()
    own.wait()
    for src in range(n):
        @pl.when(me != src)
        def _():
            pltpu.make_async_remote_copy(
                part_ref.at[src], arrived.at[src], give_sem.at[src], take_sem.at[src], device_id=(leaf, src), device_id_type=MESH
            ).wait_recv()
    total = arrived[0].astype(jnp.float32)
    for src in range(1, n):
        total = total + arrived[src].astype(jnp.float32)
    resid[...] = rhs_ref[...] - total
    for dest in range(n):
        @pl.when(me != dest)
        def _():
            give(dest).wait_send()

    dests = lambda s, k: (s + k, s + k < n)

    @pl.when(me == 0)
    def _():
        _send_block(n, halves, 0, _nt_exact(resid[...], inv_ref[...]), sol_ref, send_sem, recv_sem, leaf, dests)

    @pl.when(me == 1)
    def _():
        base[...] = _nt_exact(resid[...], inv_ref[...])

    def step(q, carry):
        @pl.when(me == q + 1)
        def _():
            _block_copy(halves, q, q, send_sem.at[0], recv_sem, leaf).wait_recv()
            solved = base[...] - _through(halves[q], hi_ref, lo_ref)
            _send_block(n, halves, q + 1, solved, sol_ref, send_sem, recv_sem, leaf, dests)

        @pl.when(me > q + 1)
        def _():
            _block_copy(halves, q, q, send_sem.at[0], recv_sem, leaf).wait_recv()
            resid[...] = resid[...] - _nt(halves[q], blocks_ref[q])

            @pl.when(me == q + 2)
            def _():
                base[...] = _nt_exact(resid[...], inv_ref[...])

        return carry

    lax.fori_loop(0, n - 1, step, 0)


def sep_backward_kernel(n, start_ref, inv_ref, blocks_ref, hi_ref, lo_ref, sol_ref, table_ref, halves, resid, base, send_sem, recv_sem):
    me = lax.axis_index("grp")
    leaf = lax.axis_index("leaf")
    _greet_group(n, leaf, me)
    resid[...] = start_ref[...]
    dests = lambda s, k: (lax.rem(s - k + n, n), True)

    @pl.when(me == n - 1)
    def _():
        _send_block(n, halves, n - 1, _nn_exact(resid[...], inv_ref[...]), sol_ref, send_sem, recv_sem, leaf, dests)

    @pl.when(me == n - 2)
    def _():
        base[...] = _nn_exact(resid[...], inv_ref[...])

    def step(s, carry):
        q = n - 1 - s

        @pl.when(me != q)
        def _():
            _block_copy(halves, q, q, send_sem.at[0], recv_sem, leaf).wait_recv()

        @pl.when(me == q - 1)
        def _():
            solved = base[...] - _through(halves[q], hi_ref, lo_ref)
            _send_block(n, halves, q - 1, solved, sol_ref, send_sem, recv_sem, leaf, dests)

        @pl.when(me < q - 1)
        def _():
            resid[...] = resid[...] - _nn(halves[q], blocks_ref[q])

            @pl.when(me == q - 2)
            def _():
                base[...] = _nn_exact(resid[...], inv_ref[...])

        return carry

    lax.fori_loop(0, n - 1, step, 0)
    @pl.when(me != 0)
    def _():
        _block_copy(halves, 0, 0, send_sem.at[0], recv_sem, leaf).wait_recv()
    table_ref[...] = halves[...]


def sep_solve(kind, start, inv, blocks, hi, lo, n):
    rows, width = (start[0] if kind == "forward" else start).shape
    vmem = pl.BlockSpec(memory_space=pltpu.VMEM)
    scratch = [
        pltpu.VMEM((n, rows, width), jnp.bfloat16),
        pltpu.VMEM((rows, width), jnp.float32),
        pltpu.VMEM((rows, width), jnp.float32),
        pltpu.SemaphoreType.DMA((n,)),
        pltpu.SemaphoreType.DMA((n,)),
    ]
    sol_shape = jax.ShapeDtypeStruct((rows, width), jnp.float32)
    params = dict(has_side_effects=True, vmem_limit_bytes=48 * 1024 * 1024)
    if kind == "forward":
        rhs, parts = start
        return pl.pallas_call(
            functools.partial(sep_forward_kernel, n),
            out_shape=sol_shape,
            in_specs=[vmem] * 6,
            out_specs=vmem,
            scratch_shapes=scratch
            + [
                pltpu.VMEM(parts.shape, parts.dtype),
                pltpu.SemaphoreType.DMA((1,)),
                pltpu.SemaphoreType.DMA((n,)),
                pltpu.SemaphoreType.DMA((n,)),
            ],
            compiler_params=pltpu.CompilerParams(collective_id=0, **params),
        )(rhs, parts, inv, blocks, hi, lo)
    return pl.pallas_call(
        functools.partial(sep_backward_kernel, n),
        out_shape=(sol_shape, jax.ShapeDtypeStruct((n, rows, width), jnp.bfloat16)),
        in_specs=[vmem] * 5,
        out_specs=(vmem, vmem),
        scratch_shapes=scratch,
        compiler_params=pltpu.CompilerParams(collective_id=1, **params),
    )(start, inv, blocks, hi, lo)


def split_pair(matrix):
    hi = matrix.astype(jnp.bfloat16)
    lo = (matrix - hi.astype(jnp.float32)).astype(jnp.bfloat16)
    return hi, lo


def top_solve_kernel(nt, span, start_ref, inv_ref, lower_ref, coef_ref, half_ref, fwd_half, fwd_full):
    for t in range(nt):
        cols = slice(t * span, (t + 1) * span)
        residue = start_ref[:, cols]
        if t > 0:
            residue = residue - _nt(fwd_half[:, : t * span], lower_ref[cols, : t * span])
        solved = _nt_exact(residue, inv_ref[t])
        fwd_full[:, cols] = solved
        fwd_half[:, cols] = solved.astype(jnp.bfloat16)
    for t in reversed(range(nt)):
        cols = slice(t * span, (t + 1) * span)
        residue = fwd_full[:, cols]
        if t < nt - 1:
            residue = residue - _nn(half_ref[:, (t + 1) * span :], lower_ref[(t + 1) * span :, cols])
        solved = _nn_exact(residue, inv_ref[t])
        coef_ref[:, cols] = solved
        half_ref[:, cols] = solved.astype(jnp.bfloat16)


def top_solve(top_start, top_inverse, top_lower):
    nt, span = top_inverse.shape[0], top_inverse.shape[1]
    rows, width = top_start.shape
    vmem = pl.BlockSpec(memory_space=pltpu.VMEM)
    return pl.pallas_call(
        functools.partial(top_solve_kernel, nt, span),
        out_shape=(
            jax.ShapeDtypeStruct((rows, width), jnp.float32),
            jax.ShapeDtypeStruct((rows, width), jnp.bfloat16),
        ),
        in_specs=[vmem] * 3,
        out_specs=(vmem, vmem),
        scratch_shapes=[
            pltpu.VMEM((rows, width), jnp.bfloat16),
            pltpu.VMEM((rows, width), jnp.float32),
        ],
        compiler_params=pltpu.CompilerParams(vmem_limit_bytes=48 * 1024 * 1024),
    )(top_start, top_inverse, top_lower)


def evaluate_kernel(slots, pattern_ref, coef_ref, centre_ref, column_ref, out_ref, acc, spread):
    m = pl.program_id(0)
    acc[...] = jnp.zeros_like(acc)
    column = column_ref[0]
    width = centre_ref.shape[2]
    for comp in range(3):
        spread[comp] = jnp.broadcast_to(column[:, comp : comp + 1], (column.shape[0], width))

    def one_slot(s, carry):
        @pl.when(pattern_ref[m, s] != 0)
        def _():
            centre = centre_ref[s]
            dist = None
            for comp in range(3):
                delta = centre[comp : comp + 1, :] - spread[comp]
                dist = delta * delta if dist is None else dist + delta * delta
            weight = jnp.maximum(1.0 - dist * (1.0 / support_sq), 0.0)
            kernel = (weight * weight * weight).astype(jnp.bfloat16)
            acc[...] += _nt(coef_ref[s], kernel)

        return carry

    lax.fori_loop(0, slots, one_slot, 0)
    out_ref[...] = acc[...]


def evaluate_all(coef_all, centre_all, point_columns, pattern):
    slots, rows, span = coef_all.shape
    blocks = point_columns.shape[0]
    full = lambda shape: pl.BlockSpec(shape, lambda m, pat: (0,) * len(shape))
    grid_spec = pltpu.PrefetchScalarGridSpec(
        num_scalar_prefetch=1,
        grid=(blocks,),
        in_specs=[
            full(coef_all.shape),
            full(centre_all.shape),
            pl.BlockSpec((1, span, point_columns.shape[2]), lambda m, pat: (m, 0, 0)),
        ],
        out_specs=pl.BlockSpec((rows, span), lambda m, pat: (0, m)),
        scratch_shapes=[
            pltpu.VMEM((rows, span), jnp.float32),
            pltpu.VMEM((3, span, centre_all.shape[2]), jnp.float32),
        ],
    )
    return pl.pallas_call(
        functools.partial(evaluate_kernel, slots),
        out_shape=jax.ShapeDtypeStruct((rows, blocks * span), jnp.float32),
        grid_spec=grid_spec,
    )(pattern, coef_all, centre_all, point_columns)


def top_reduce_kernel(n, groups, span, term_ref, total_ref, parts_a, parts_b, gathered, local_sem, send_a, recv_a, send_b, recv_b, send_c, recv_c):
    me = lax.axis_index("grp")
    leaf = lax.axis_index("leaf")
    barrier = pltpu.get_barrier_semaphore()
    for r in range(n):
        @pl.when(me != r)
        def _():
            pl.semaphore_signal(barrier, inc=1, device_id=(leaf, r), device_id_type=MESH)
    for g in range(groups):
        @pl.when(leaf != g)
        def _():
            pl.semaphore_signal(barrier, inc=1, device_id=(g, me), device_id_type=MESH)
    pl.semaphore_wait(barrier, n - 1 + groups - 1)

    def column(q):
        return term_ref.at[:, pl.ds(pl.multiple_of(q * span, span), span)]

    def copy_a(k):
        dest = lax.rem(me + k, n)
        return pltpu.make_async_remote_copy(
            column(dest), parts_a.at[me], send_a.at[k], recv_a.at[me], device_id=(leaf, dest), device_id_type=MESH
        )

    def wait_a(k):
        src = lax.rem(me + n - k, n)
        pltpu.make_async_remote_copy(
            column(src), parts_a.at[src], send_a.at[0], recv_a.at[src], device_id=(leaf, src), device_id_type=MESH
        ).wait_recv()

    own = pltpu.make_async_copy(column(me), parts_a.at[me], local_sem.at[0])
    own.start()
    for k in range(1, n):
        copy_a(k).start()
    own.wait()
    for k in range(1, n):
        wait_a(k)
    for k in range(1, n):
        copy_a(k).wait_send()
    total = parts_a[0]
    for q in range(1, n):
        total = total + parts_a[q]
    parts_b[leaf] = total

    def copy_b(k):
        dest = lax.rem(leaf + k, groups)
        return pltpu.make_async_remote_copy(
            parts_b.at[leaf], parts_b.at[leaf], send_b.at[k], recv_b.at[leaf], device_id=(dest, me), device_id_type=MESH
        )

    for k in range(1, groups):
        copy_b(k).start()
    for k in range(1, groups):
        src = lax.rem(leaf + groups - k, groups)
        pltpu.make_async_remote_copy(
            parts_b.at[src], parts_b.at[src], send_b.at[0], recv_b.at[src], device_id=(src, me), device_id_type=MESH
        ).wait_recv()
    for k in range(1, groups):
        copy_b(k).wait_send()
    summed = parts_b[0]
    for g in range(1, groups):
        summed = summed + parts_b[g]
    gathered[me] = summed

    def copy_c(k):
        dest = lax.rem(me + k, n)
        return pltpu.make_async_remote_copy(
            gathered.at[me], gathered.at[me], send_c.at[k], recv_c.at[me], device_id=(leaf, dest), device_id_type=MESH
        )

    for k in range(1, n):
        copy_c(k).start()
    for k in range(1, n):
        src = lax.rem(me + n - k, n)
        pltpu.make_async_remote_copy(
            gathered.at[src], gathered.at[src], send_c.at[0], recv_c.at[src], device_id=(leaf, src), device_id_type=MESH
        ).wait_recv()
    for k in range(1, n):
        copy_c(k).wait_send()
    for q in range(n):
        total_ref[:, q * span : (q + 1) * span] = gathered[q]


def top_reduce(term, n, groups):
    rows, width = term.shape
    span = width // n
    vmem = pl.BlockSpec(memory_space=pltpu.VMEM)
    return pl.pallas_call(
        functools.partial(top_reduce_kernel, n, groups, span),
        out_shape=jax.ShapeDtypeStruct((rows, width), jnp.float32),
        in_specs=[vmem],
        out_specs=vmem,
        scratch_shapes=[
            pltpu.VMEM((n, rows, span), jnp.float32),
            pltpu.VMEM((groups, rows, span), jnp.float32),
            pltpu.VMEM((n, rows, span), jnp.float32),
            pltpu.SemaphoreType.DMA((1,)),
            pltpu.SemaphoreType.DMA((n,)),
            pltpu.SemaphoreType.DMA((n,)),
            pltpu.SemaphoreType.DMA((groups,)),
            pltpu.SemaphoreType.DMA((groups,)),
            pltpu.SemaphoreType.DMA((n,)),
            pltpu.SemaphoreType.DMA((n,)),
        ],
        compiler_params=pltpu.CompilerParams(collective_id=2, has_side_effects=True),
    )(term)


def exchange_kernel(n, coef_ref, centre_ref, coef_out, centre_out, coef_buf, centre_buf, local_sem, send_sem, recv_sem):
    me = lax.axis_index("grp")
    leaf = lax.axis_index("leaf")
    _greet_group(n, leaf, me)
    pairs = ((coef_ref, coef_buf), (centre_ref, centre_buf))

    def push(kind, k):
        source, buf = pairs[kind]
        dest = lax.rem(me + k, n)
        return pltpu.make_async_remote_copy(
            source.at[dest], buf.at[me], send_sem.at[kind, k], recv_sem.at[kind, me], device_id=(leaf, dest), device_id_type=MESH
        )

    owns = [pltpu.make_async_copy(source.at[me], buf.at[me], local_sem.at[kind]) for kind, (source, buf) in enumerate(pairs)]
    for own in owns:
        own.start()
    for k in range(1, n):
        for kind in range(2):
            push(kind, k).start()
    for own in owns:
        own.wait()
    for k in range(1, n):
        src = lax.rem(me + n - k, n)
        for kind, (source, buf) in enumerate(pairs):
            pltpu.make_async_remote_copy(
                source.at[src], buf.at[src], send_sem.at[kind, 0], recv_sem.at[kind, src], device_id=(leaf, src), device_id_type=MESH
            ).wait_recv()
    for k in range(1, n):
        for kind in range(2):
            push(kind, k).wait_send()
    coef_out[...] = coef_buf[...]
    centre_out[...] = centre_buf[...]


def exchange(send_coef, send_centre, n):
    vmem = pl.BlockSpec(memory_space=pltpu.VMEM)
    return pl.pallas_call(
        functools.partial(exchange_kernel, n),
        out_shape=(
            jax.ShapeDtypeStruct(send_coef.shape, send_coef.dtype),
            jax.ShapeDtypeStruct(send_centre.shape, send_centre.dtype),
        ),
        in_specs=[vmem] * 2,
        out_specs=(vmem, vmem),
        scratch_shapes=[
            pltpu.VMEM(send_coef.shape, send_coef.dtype),
            pltpu.VMEM(send_centre.shape, send_centre.dtype),
            pltpu.SemaphoreType.DMA((2,)),
            pltpu.SemaphoreType.DMA((2, n)),
            pltpu.SemaphoreType.DMA((2, n)),
        ],
        compiler_params=pltpu.CompilerParams(collective_id=3, has_side_effects=True),
    )(send_coef, send_centre)


def slot_ranks(dest_rows, grp_size):
    onehot = (dest_rows[..., None] == jnp.arange(grp_size)).astype(jnp.int32)
    before = jnp.cumsum(onehot, axis=-2) - onehot
    return jnp.sum(before * onehot, axis=-1)


def evaluate(coef_all, centre_all, block_points, block_mask):
    dist = jnp.zeros((centre_all.shape[0], centre_all.shape[2], block_points.shape[1]), jnp.float32)
    for comp in range(3):
        delta = centre_all[:, comp, :, None] - block_points[None, comp, None, :]
        dist = dist + delta * delta
    weight = jnp.maximum(1.0 - dist / support_sq, 0.0) ** 3
    kernel = (weight * block_mask.astype(jnp.float32)[:, None, None]).astype(jnp.bfloat16)
    return jnp.einsum("krs,ksp->rp", coef_all, kernel, preferred_element_type=jnp.float32)


def on_device(
    rhs_leaf,
    rhs_sep,
    rhs_top,
    leaf_inverse,
    leaf_coupling,
    leaf_targets,
    sep_inverse,
    sep_blocks,
    top_coupling,
    top_inverse,
    top_lower,
    dest_map,
    centers,
    points,
    eval_pattern,
):
    grp_size = lax.axis_size("grp")
    my_index = lax.axis_index("grp")
    blocks_here = leaf_inverse.shape[0]
    snapshots = rhs_leaf.shape[0]
    span = leaf_inverse.shape[1]
    slot_count = CAP
    leaf_rhs = rhs_leaf.reshape(snapshots, blocks_here, span).transpose(1, 0, 2)
    leaf_sol = jnp.einsum("nrs,nts->nrt", leaf_rhs, leaf_inverse, precision=highest)
    leaf_half = leaf_sol.astype(jnp.bfloat16)
    partial_value = jnp.einsum(
        "nrs,ncbs->ncrb", leaf_half, leaf_coupling, preferred_element_type=jnp.float32
    )
    onehot = (leaf_targets[:, :, None] == jnp.arange(grp_size)[None, None, :]).astype(jnp.float32)
    picked = onehot
    parts = jnp.einsum("ncq,ncrb->qrb", picked, partial_value, precision=highest).astype(jnp.bfloat16)
    inverse_own = sep_inverse[0]
    own_blocks = sep_blocks[0]
    before = lax.dynamic_index_in_dim(own_blocks, jnp.maximum(my_index - 1, 0), 0, keepdims=False)
    fwd_hi, fwd_lo = split_pair(
        jnp.dot(before.astype(jnp.float32).T, inverse_own.T, precision=highest)
    )
    after = lax.dynamic_index_in_dim(own_blocks, jnp.minimum(my_index + 1, grp_size - 1), 0, keepdims=False)
    bwd_hi, bwd_lo = split_pair(jnp.dot(after.astype(jnp.float32), inverse_own, precision=highest))
    sep_sol = sep_solve("forward", (rhs_sep, parts), inverse_own, own_blocks, fwd_hi, fwd_lo, grp_size)
    sep_half = sep_sol.astype(jnp.bfloat16)
    top_term = jnp.dot(sep_half, top_coupling, preferred_element_type=jnp.float32)
    top_total = top_reduce(top_term, grp_size, lax.axis_size("leaf"))
    top_start = rhs_top - top_total
    coef_top, top_half = top_solve(top_start, top_inverse, top_lower)
    back_start = sep_sol - lax.dot_general(
        top_half, top_coupling, (((1,), (1,)), ((), ())), preferred_element_type=jnp.float32
    )

    coef_sep, known_table = sep_solve(
        "backward", back_start, inverse_own, own_blocks, bwd_hi, bwd_lo, grp_size
    )
    picked = jnp.einsum(
        "ncq,qrb->ncrb",
        onehot.astype(jnp.bfloat16),
        known_table,
        preferred_element_type=jnp.float32,
    ).astype(jnp.bfloat16)
    reduced = jnp.einsum(
        "ncrb,ncbs->nrs", picked, leaf_coupling, preferred_element_type=jnp.float32
    )
    leaf_coef = jnp.einsum("nrs,nst->nrt", leaf_sol - reduced, leaf_inverse, precision=highest)
    coef_leaf = leaf_coef.transpose(1, 0, 2).reshape(snapshots, blocks_here * span)
    leaf_out = leaf_coef.astype(jnp.bfloat16)
    slot_ids = jnp.arange(slot_count)
    grp_ids = jnp.arange(grp_size)
    own_dest = dest_map[:, 0]
    slot_rank = slot_ranks(own_dest[None, :], grp_size)[0]
    selector = (own_dest[None, None, :] == grp_ids[:, None, None]) & (
        slot_rank[None, None, :] == slot_ids[None, :, None]
    )
    send_coef = jnp.einsum(
        "dkj,jrt->dkrt", selector.astype(jnp.bfloat16), leaf_out, preferred_element_type=jnp.float32
    ).astype(jnp.bfloat16)
    send_centre = jnp.einsum(
        "dkj,jct->dkct", selector.astype(jnp.float32), centers, precision=highest
    )
    received, recv_centre = exchange(send_coef, send_centre, grp_size)
    slot_total = grp_size * slot_count
    coef_all = received.reshape(slot_total, snapshots, span)
    centre_all = recv_centre.reshape(slot_total, 3, span)
    point_blocks = eval_pattern.shape[0]
    point_columns = points[0].T.reshape(point_blocks, span, points.shape[1])
    values = evaluate_all(coef_all, centre_all, point_columns, eval_pattern)
    return (coef_leaf, coef_sep, coef_top, values)


def solution(mesh):
    in_specs = (
        P(None, ("leaf", "grp")),
        P(None, ("leaf", "grp")),
        P(),
        P(("leaf", "grp"), None, None),
        P(("leaf", "grp"), None, None, None),
        P(("leaf", "grp"), None),
        P(("leaf", "grp"), None, None),
        P(("leaf", "grp"), None, None, None),
        P(("leaf", "grp"), None),
        P(),
        P(),
        P(("leaf", "grp"), None),
        P(("leaf", "grp"), None, None),
        P(("leaf", "grp"), None, None),
        P(("leaf", "grp"), None),
    )
    out_specs = (P(None, ("leaf", "grp")), P(None, ("leaf", "grp")), P(), P(None, ("leaf", "grp")))
    return jax.shard_map(
        on_device, mesh=mesh, in_specs=in_specs, out_specs=out_specs, check_vma=False
    )
```

```python
import functools

import jax
import jax.numpy as jnp
from jax import lax
from jax.sharding import PartitionSpec as P
from jax.experimental import pallas as pl
from jax.experimental.pallas import tpu as pltpu

MESH = pl.DeviceIdType.MESH

CAP = 2


highest = lax.Precision.HIGHEST
support_sq = 0.25


def split_up(shard, dim, peers):
    dims = shard.shape
    pieces = shard.reshape(*dims[:dim], peers, dims[dim] // peers, *dims[dim + 1 :])
    return jnp.moveaxis(pieces, dim, 0)


def sum_at_owner(shard, axis, dim):
    pieces = split_up(shard, dim, lax.axis_size(axis))
    arrived = lax.all_to_all(pieces, axis, split_axis=0, concat_axis=0, tiled=True)
    return arrived.astype(jnp.float32).sum(axis=0)


def from_root(shard, axis, root):
    return lax.dynamic_index_in_dim(lax.all_gather(shard, axis), root, 0, keepdims=False)


def copy_for_each(shard, axis):
    copies = jnp.broadcast_to(shard, (lax.axis_size(axis), *shard.shape))
    return lax.all_to_all(copies, axis, split_axis=0, concat_axis=0, tiled=True)


def over_copies(shard, axis):
    return copy_for_each(shard, axis).astype(jnp.float32).sum(axis=0)


def joined_along(pieces, dim):
    dims = list(pieces.shape[1:])
    dims[dim] *= pieces.shape[0]
    return jnp.moveaxis(pieces, 0, dim).reshape(dims)


def gather_directly(shard, axis, dim):
    pieces = copy_for_each(shard, axis)
    return joined_along(pieces, dim)


def _nt(a, b):
    return lax.dot_general(a, b, (((1,), (1,)), ((), ())), preferred_element_type=jnp.float32)


def _nn(a, b):
    return lax.dot_general(a, b, (((1,), (0,)), ((), ())), preferred_element_type=jnp.float32)


def _nt_exact(a, b):
    return lax.dot_general(
        a, b, (((1,), (1,)), ((), ())), precision=highest, preferred_element_type=jnp.float32
    )


def _nn_exact(a, b):
    return lax.dot_general(
        a, b, (((1,), (0,)), ((), ())), precision=highest, preferred_element_type=jnp.float32
    )


def _greet_group(n, leaf, me):
    barrier = pltpu.get_barrier_semaphore()
    for r in range(n):
        @pl.when(me != r)
        def _():
            pl.semaphore_signal(barrier, inc=1, device_id=(leaf, r), device_id_type=MESH)
    pl.semaphore_wait(barrier, n - 1)


def _block_copy(halves, q, dest, send_sem, recv_sem, leaf):
    return pltpu.make_async_remote_copy(
        src_ref=halves.at[q],
        dst_ref=halves.at[q],
        send_sem=send_sem,
        recv_sem=recv_sem.at[q],
        device_id=(leaf, dest),
        device_id_type=MESH,
    )


def _send_block(n, halves, s, solved, sol_ref, send_sem, recv_sem, leaf, dests):
    sol_ref[...] = solved
    halves[s] = solved.astype(jnp.bfloat16)
    for k in range(1, n):
        dest, live = dests(s, k)
        @pl.when(live)
        def _():
            _block_copy(halves, s, dest, send_sem.at[k], recv_sem, leaf).start()
            if k == 1:
                _block_copy(halves, s, dest, send_sem.at[k], recv_sem, leaf).wait_send()
    for k in range(2, n):
        dest, live = dests(s, k)
        @pl.when(live)
        def _():
            _block_copy(halves, s, dest, send_sem.at[k], recv_sem, leaf).wait_send()


def _through(y, hi_ref, lo_ref):
    return _nn(y, hi_ref[...]) + _nn(y, lo_ref[...])


def sep_forward_kernel(n, rhs_ref, part_ref, inv_ref, blocks_ref, hi_ref, lo_ref, sol_ref, halves, resid, base, send_sem, recv_sem, arrived, local_sem, give_sem, take_sem):
    me = lax.axis_index("grp")
    leaf = lax.axis_index("leaf")
    _greet_group(n, leaf, me)

    def give(dest):
        return pltpu.make_async_remote_copy(
            part_ref.at[dest], arrived.at[me], give_sem.at[dest], take_sem.at[me], device_id=(leaf, dest), device_id_type=MESH
        )

    own = pltpu.make_async_copy(part_ref.at[me], arrived.at[me], local_sem.at[0])
    own.start()
    for dest in range(n):
        @pl.when(me != dest)
        def _():
            give(dest).start()
    own.wait()
    for src in range(n):
        @pl.when(me != src)
        def _():
            pltpu.make_async_remote_copy(
                part_ref.at[src], arrived.at[src], give_sem.at[src], take_sem.at[src], device_id=(leaf, src), device_id_type=MESH
            ).wait_recv()
    total = arrived[0].astype(jnp.float32)
    for src in range(1, n):
        total = total + arrived[src].astype(jnp.float32)
    resid[...] = rhs_ref[...] - total
    for dest in range(n):
        @pl.when(me != dest)
        def _():
            give(dest).wait_send()

    dests = lambda s, k: (s + k, s + k < n)

    @pl.when(me == 0)
    def _():
        _send_block(n, halves, 0, _nt_exact(resid[...], inv_ref[...]), sol_ref, send_sem, recv_sem, leaf, dests)

    @pl.when(me == 1)
    def _():
        base[...] = _nt_exact(resid[...], inv_ref[...])

    def step(q, carry):
        @pl.when(me == q + 1)
        def _():
            _block_copy(halves, q, q, send_sem.at[0], recv_sem, leaf).wait_recv()
            solved = base[...] - _through(halves[q], hi_ref, lo_ref)
            _send_block(n, halves, q + 1, solved, sol_ref, send_sem, recv_sem, leaf, dests)

        @pl.when(me > q + 1)
        def _():
            _block_copy(halves, q, q, send_sem.at[0], recv_sem, leaf).wait_recv()
            resid[...] = resid[...] - _nt(halves[q], blocks_ref[q])

            @pl.when(me == q + 2)
            def _():
                base[...] = _nt_exact(resid[...], inv_ref[...])

        return carry

    lax.fori_loop(0, n - 1, step, 0)


def sep_backward_kernel(n, start_ref, inv_ref, blocks_ref, hi_ref, lo_ref, sol_ref, table_ref, halves, resid, base, send_sem, recv_sem):
    me = lax.axis_index("grp")
    leaf = lax.axis_index("leaf")
    _greet_group(n, leaf, me)
    resid[...] = start_ref[...]
    dests = lambda s, k: (s - k, s - k >= 0)

    @pl.when(me == n - 1)
    def _():
        _send_block(n, halves, n - 1, _nn_exact(resid[...], inv_ref[...]), sol_ref, send_sem, recv_sem, leaf, dests)

    @pl.when(me == n - 2)
    def _():
        base[...] = _nn_exact(resid[...], inv_ref[...])

    def step(s, carry):
        q = n - 1 - s

        @pl.when(me < q)
        def _():
            _block_copy(halves, q, q, send_sem.at[0], recv_sem, leaf).wait_recv()

        @pl.when(me == q - 1)
        def _():
            solved = base[...] - _through(halves[q], hi_ref, lo_ref)
            _send_block(n, halves, q - 1, solved, sol_ref, send_sem, recv_sem, leaf, dests)

        @pl.when(me < q - 1)
        def _():
            resid[...] = resid[...] - _nn(halves[q], blocks_ref[q])

            @pl.when(me == q - 2)
            def _():
                base[...] = _nn_exact(resid[...], inv_ref[...])

        return carry

    lax.fori_loop(0, n - 1, step, 0)
    for k in range(1, n):
        @pl.when(me + k < n)
        def _():
            _block_copy(halves, me, me + k, send_sem.at[k], recv_sem, leaf).start()
    for q in range(n):
        @pl.when(q < me)
        def _():
            _block_copy(halves, q, q, send_sem.at[0], recv_sem, leaf).wait_recv()
    for k in range(1, n):
        @pl.when(me + k < n)
        def _():
            _block_copy(halves, me, me + k, send_sem.at[k], recv_sem, leaf).wait_send()
    table_ref[...] = halves[...]


def sep_solve(kind, start, inv, blocks, hi, lo, n):
    rows, width = (start[0] if kind == "forward" else start).shape
    vmem = pl.BlockSpec(memory_space=pltpu.VMEM)
    scratch = [
        pltpu.VMEM((n, rows, width), jnp.bfloat16),
        pltpu.VMEM((rows, width), jnp.float32),
        pltpu.VMEM((rows, width), jnp.float32),
        pltpu.SemaphoreType.DMA((n,)),
        pltpu.SemaphoreType.DMA((n,)),
    ]
    sol_shape = jax.ShapeDtypeStruct((rows, width), jnp.float32)
    params = dict(has_side_effects=True, vmem_limit_bytes=48 * 1024 * 1024)
    if kind == "forward":
        rhs, parts = start
        return pl.pallas_call(
            functools.partial(sep_forward_kernel, n),
            out_shape=sol_shape,
            in_specs=[vmem] * 6,
            out_specs=vmem,
            scratch_shapes=scratch
            + [
                pltpu.VMEM(parts.shape, parts.dtype),
                pltpu.SemaphoreType.DMA((1,)),
                pltpu.SemaphoreType.DMA((n,)),
                pltpu.SemaphoreType.DMA((n,)),
            ],
            compiler_params=pltpu.CompilerParams(collective_id=0, **params),
        )(rhs, parts, inv, blocks, hi, lo)
    return pl.pallas_call(
        functools.partial(sep_backward_kernel, n),
        out_shape=(sol_shape, jax.ShapeDtypeStruct((n, rows, width), jnp.bfloat16)),
        in_specs=[vmem] * 5,
        out_specs=(vmem, vmem),
        scratch_shapes=scratch,
        compiler_params=pltpu.CompilerParams(collective_id=1, **params),
    )(start, inv, blocks, hi, lo)


def split_pair(matrix):
    hi = matrix.astype(jnp.bfloat16)
    lo = (matrix - hi.astype(jnp.float32)).astype(jnp.bfloat16)
    return hi, lo


def top_solve_kernel(nt, span, start_ref, inv_ref, lower_ref, coef_ref, half_ref, fwd_half, fwd_full):
    for t in range(nt):
        cols = slice(t * span, (t + 1) * span)
        residue = start_ref[:, cols]
        if t > 0:
            residue = residue - _nt(fwd_half[:, : t * span], lower_ref[cols, : t * span])
        solved = _nt_exact(residue, inv_ref[t])
        fwd_full[:, cols] = solved
        fwd_half[:, cols] = solved.astype(jnp.bfloat16)
    for t in reversed(range(nt)):
        cols = slice(t * span, (t + 1) * span)
        residue = fwd_full[:, cols]
        if t < nt - 1:
            residue = residue - _nn(half_ref[:, (t + 1) * span :], lower_ref[(t + 1) * span :, cols])
        solved = _nn_exact(residue, inv_ref[t])
        coef_ref[:, cols] = solved
        half_ref[:, cols] = solved.astype(jnp.bfloat16)


def top_solve(top_start, top_inverse, top_lower):
    nt, span = top_inverse.shape[0], top_inverse.shape[1]
    rows, width = top_start.shape
    vmem = pl.BlockSpec(memory_space=pltpu.VMEM)
    return pl.pallas_call(
        functools.partial(top_solve_kernel, nt, span),
        out_shape=(
            jax.ShapeDtypeStruct((rows, width), jnp.float32),
            jax.ShapeDtypeStruct((rows, width), jnp.bfloat16),
        ),
        in_specs=[vmem] * 3,
        out_specs=(vmem, vmem),
        scratch_shapes=[
            pltpu.VMEM((rows, width), jnp.bfloat16),
            pltpu.VMEM((rows, width), jnp.float32),
        ],
        compiler_params=pltpu.CompilerParams(vmem_limit_bytes=48 * 1024 * 1024),
    )(top_start, top_inverse, top_lower)


def evaluate_kernel(slots, pattern_ref, coef_ref, centre_ref, column_ref, out_ref, acc, spread):
    m = pl.program_id(0)
    acc[...] = jnp.zeros_like(acc)
    column = column_ref[0]
    width = centre_ref.shape[2]
    for comp in range(3):
        spread[comp] = jnp.broadcast_to(column[:, comp : comp + 1], (column.shape[0], width))

    def one_slot(s, carry):
        @pl.when(pattern_ref[m, s] != 0)
        def _():
            centre = centre_ref[s]
            dist = None
            for comp in range(3):
                delta = centre[comp : comp + 1, :] - spread[comp]
                dist = delta * delta if dist is None else dist + delta * delta
            weight = jnp.maximum(1.0 - dist * (1.0 / support_sq), 0.0)
            kernel = (weight * weight * weight).astype(jnp.bfloat16)
            acc[...] += _nt(coef_ref[s], kernel)

        return carry

    lax.fori_loop(0, slots, one_slot, 0)
    out_ref[...] = acc[...]


def evaluate_all(coef_all, centre_all, point_columns, pattern):
    slots, rows, span = coef_all.shape
    blocks = point_columns.shape[0]
    full = lambda shape: pl.BlockSpec(shape, lambda m, pat: (0,) * len(shape))
    grid_spec = pltpu.PrefetchScalarGridSpec(
        num_scalar_prefetch=1,
        grid=(blocks,),
        in_specs=[
            full(coef_all.shape),
            full(centre_all.shape),
            pl.BlockSpec((1, span, point_columns.shape[2]), lambda m, pat: (m, 0, 0)),
        ],
        out_specs=pl.BlockSpec((rows, span), lambda m, pat: (0, m)),
        scratch_shapes=[
            pltpu.VMEM((rows, span), jnp.float32),
            pltpu.VMEM((3, span, centre_all.shape[2]), jnp.float32),
        ],
    )
    return pl.pallas_call(
        functools.partial(evaluate_kernel, slots),
        out_shape=jax.ShapeDtypeStruct((rows, blocks * span), jnp.float32),
        grid_spec=grid_spec,
    )(pattern, coef_all, centre_all, point_columns)


def top_reduce_kernel(n, groups, span, term_ref, total_ref, parts_a, parts_b, gathered, local_sem, send_a, recv_a, send_b, recv_b, send_c, recv_c):
    me = lax.axis_index("grp")
    leaf = lax.axis_index("leaf")
    barrier = pltpu.get_barrier_semaphore()
    for r in range(n):
        @pl.when(me != r)
        def _():
            pl.semaphore_signal(barrier, inc=1, device_id=(leaf, r), device_id_type=MESH)
    for g in range(groups):
        @pl.when(leaf != g)
        def _():
            pl.semaphore_signal(barrier, inc=1, device_id=(g, me), device_id_type=MESH)
    pl.semaphore_wait(barrier, n - 1 + groups - 1)

    def column(q):
        return term_ref.at[:, pl.ds(pl.multiple_of(q * span, span), span)]

    def copy_a(k):
        dest = lax.rem(me + k, n)
        return pltpu.make_async_remote_copy(
            column(dest), parts_a.at[me], send_a.at[k], recv_a.at[me], device_id=(leaf, dest), device_id_type=MESH
        )

    def wait_a(k):
        src = lax.rem(me + n - k, n)
        pltpu.make_async_remote_copy(
            column(src), parts_a.at[src], send_a.at[0], recv_a.at[src], device_id=(leaf, src), device_id_type=MESH
        ).wait_recv()

    own = pltpu.make_async_copy(column(me), parts_a.at[me], local_sem.at[0])
    own.start()
    for k in range(1, n):
        copy_a(k).start()
    own.wait()
    for k in range(1, n):
        wait_a(k)
    for k in range(1, n):
        copy_a(k).wait_send()
    total = parts_a[0]
    for q in range(1, n):
        total = total + parts_a[q]
    parts_b[leaf] = total

    def copy_b(k):
        dest = lax.rem(leaf + k, groups)
        return pltpu.make_async_remote_copy(
            parts_b.at[leaf], parts_b.at[leaf], send_b.at[k], recv_b.at[leaf], device_id=(dest, me), device_id_type=MESH
        )

    for k in range(1, groups):
        copy_b(k).start()
    for k in range(1, groups):
        src = lax.rem(leaf + groups - k, groups)
        pltpu.make_async_remote_copy(
            parts_b.at[src], parts_b.at[src], send_b.at[0], recv_b.at[src], device_id=(src, me), device_id_type=MESH
        ).wait_recv()
    for k in range(1, groups):
        copy_b(k).wait_send()
    summed = parts_b[0]
    for g in range(1, groups):
        summed = summed + parts_b[g]
    gathered[me] = summed

    def copy_c(k):
        dest = lax.rem(me + k, n)
        return pltpu.make_async_remote_copy(
            gathered.at[me], gathered.at[me], send_c.at[k], recv_c.at[me], device_id=(leaf, dest), device_id_type=MESH
        )

    for k in range(1, n):
        copy_c(k).start()
    for k in range(1, n):
        src = lax.rem(me + n - k, n)
        pltpu.make_async_remote_copy(
            gathered.at[src], gathered.at[src], send_c.at[0], recv_c.at[src], device_id=(leaf, src), device_id_type=MESH
        ).wait_recv()
    for k in range(1, n):
        copy_c(k).wait_send()
    for q in range(n):
        total_ref[:, q * span : (q + 1) * span] = gathered[q]


def top_reduce(term, n, groups):
    rows, width = term.shape
    span = width // n
    vmem = pl.BlockSpec(memory_space=pltpu.VMEM)
    return pl.pallas_call(
        functools.partial(top_reduce_kernel, n, groups, span),
        out_shape=jax.ShapeDtypeStruct((rows, width), jnp.float32),
        in_specs=[vmem],
        out_specs=vmem,
        scratch_shapes=[
            pltpu.VMEM((n, rows, span), jnp.float32),
            pltpu.VMEM((groups, rows, span), jnp.float32),
            pltpu.VMEM((n, rows, span), jnp.float32),
            pltpu.SemaphoreType.DMA((1,)),
            pltpu.SemaphoreType.DMA((n,)),
            pltpu.SemaphoreType.DMA((n,)),
            pltpu.SemaphoreType.DMA((groups,)),
            pltpu.SemaphoreType.DMA((groups,)),
            pltpu.SemaphoreType.DMA((n,)),
            pltpu.SemaphoreType.DMA((n,)),
        ],
        compiler_params=pltpu.CompilerParams(collective_id=2, has_side_effects=True),
    )(term)


def exchange_kernel(n, coef_ref, centre_ref, coef_out, centre_out, coef_buf, centre_buf, local_sem, send_sem, recv_sem):
    me = lax.axis_index("grp")
    leaf = lax.axis_index("leaf")
    _greet_group(n, leaf, me)
    pairs = ((coef_ref, coef_buf), (centre_ref, centre_buf))

    def push(kind, k):
        source, buf = pairs[kind]
        dest = lax.rem(me + k, n)
        return pltpu.make_async_remote_copy(
            source.at[dest], buf.at[me], send_sem.at[kind, k], recv_sem.at[kind, me], device_id=(leaf, dest), device_id_type=MESH
        )

    owns = [pltpu.make_async_copy(source.at[me], buf.at[me], local_sem.at[kind]) for kind, (source, buf) in enumerate(pairs)]
    for own in owns:
        own.start()
    for k in range(1, n):
        for kind in range(2):
            push(kind, k).start()
    for own in owns:
        own.wait()
    for k in range(1, n):
        src = lax.rem(me + n - k, n)
        for kind, (source, buf) in enumerate(pairs):
            pltpu.make_async_remote_copy(
                source.at[src], buf.at[src], send_sem.at[kind, 0], recv_sem.at[kind, src], device_id=(leaf, src), device_id_type=MESH
            ).wait_recv()
    for k in range(1, n):
        for kind in range(2):
            push(kind, k).wait_send()
    coef_out[...] = coef_buf[...]
    centre_out[...] = centre_buf[...]


def exchange(send_coef, send_centre, n):
    vmem = pl.BlockSpec(memory_space=pltpu.VMEM)
    return pl.pallas_call(
        functools.partial(exchange_kernel, n),
        out_shape=(
            jax.ShapeDtypeStruct(send_coef.shape, send_coef.dtype),
            jax.ShapeDtypeStruct(send_centre.shape, send_centre.dtype),
        ),
        in_specs=[vmem] * 2,
        out_specs=(vmem, vmem),
        scratch_shapes=[
            pltpu.VMEM(send_coef.shape, send_coef.dtype),
            pltpu.VMEM(send_centre.shape, send_centre.dtype),
            pltpu.SemaphoreType.DMA((2,)),
            pltpu.SemaphoreType.DMA((2, n)),
            pltpu.SemaphoreType.DMA((2, n)),
        ],
        compiler_params=pltpu.CompilerParams(collective_id=3, has_side_effects=True),
    )(send_coef, send_centre)


def slot_ranks(dest_rows, grp_size):
    onehot = (dest_rows[..., None] == jnp.arange(grp_size)).astype(jnp.int32)
    before = jnp.cumsum(onehot, axis=-2) - onehot
    return jnp.sum(before * onehot, axis=-1)


def evaluate(coef_all, centre_all, block_points, block_mask):
    dist = jnp.zeros((centre_all.shape[0], centre_all.shape[2], block_points.shape[1]), jnp.float32)
    for comp in range(3):
        delta = centre_all[:, comp, :, None] - block_points[None, comp, None, :]
        dist = dist + delta * delta
    weight = jnp.maximum(1.0 - dist / support_sq, 0.0) ** 3
    kernel = (weight * block_mask.astype(jnp.float32)[:, None, None]).astype(jnp.bfloat16)
    return jnp.einsum("krs,ksp->rp", coef_all, kernel, preferred_element_type=jnp.float32)


def on_device(
    rhs_leaf,
    rhs_sep,
    rhs_top,
    leaf_inverse,
    leaf_coupling,
    leaf_targets,
    sep_inverse,
    sep_blocks,
    top_coupling,
    top_inverse,
    top_lower,
    dest_map,
    centers,
    points,
    eval_pattern,
):
    grp_size = lax.axis_size("grp")
    my_index = lax.axis_index("grp")
    blocks_here = leaf_inverse.shape[0]
    snapshots = rhs_leaf.shape[0]
    span = leaf_inverse.shape[1]
    slot_count = CAP
    leaf_rhs = rhs_leaf.reshape(snapshots, blocks_here, span).transpose(1, 0, 2)
    leaf_sol = jnp.einsum("nrs,nts->nrt", leaf_rhs, leaf_inverse, precision=highest)
    leaf_half = leaf_sol.astype(jnp.bfloat16)
    partial_value = jnp.einsum(
        "nrs,ncbs->ncrb", leaf_half, leaf_coupling, preferred_element_type=jnp.float32
    )
    onehot = (leaf_targets[:, :, None] == jnp.arange(grp_size)[None, None, :]).astype(jnp.float32)
    picked = onehot
    parts = jnp.einsum("ncq,ncrb->qrb", picked, partial_value, precision=highest).astype(jnp.bfloat16)
    inverse_own = sep_inverse[0]
    own_blocks = sep_blocks[0]
    before = lax.dynamic_index_in_dim(own_blocks, jnp.maximum(my_index - 1, 0), 0, keepdims=False)
    fwd_hi, fwd_lo = split_pair(
        jnp.dot(before.astype(jnp.float32).T, inverse_own.T, precision=highest)
    )
    after = lax.dynamic_index_in_dim(own_blocks, jnp.minimum(my_index + 1, grp_size - 1), 0, keepdims=False)
    bwd_hi, bwd_lo = split_pair(jnp.dot(after.astype(jnp.float32), inverse_own, precision=highest))
    sep_sol = sep_solve("forward", (rhs_sep, parts), inverse_own, own_blocks, fwd_hi, fwd_lo, grp_size)
    sep_half = sep_sol.astype(jnp.bfloat16)
    top_term = jnp.dot(sep_half, top_coupling, preferred_element_type=jnp.float32)
    top_total = top_reduce(top_term, grp_size, lax.axis_size("leaf"))
    top_start = rhs_top - top_total
    coef_top, top_half = top_solve(top_start, top_inverse, top_lower)
    back_start = sep_sol - lax.dot_general(
        top_half, top_coupling, (((1,), (1,)), ((), ())), preferred_element_type=jnp.float32
    )

    coef_sep, known_table = sep_solve(
        "backward", back_start, inverse_own, own_blocks, bwd_hi, bwd_lo, grp_size
    )
    picked = jnp.einsum(
        "ncq,qrb->ncrb",
        onehot.astype(jnp.bfloat16),
        known_table,
        preferred_element_type=jnp.float32,
    ).astype(jnp.bfloat16)
    reduced = jnp.einsum(
        "ncrb,ncbs->nrs", picked, leaf_coupling, preferred_element_type=jnp.float32
    )
    leaf_coef = jnp.einsum("nrs,nst->nrt", leaf_sol - reduced, leaf_inverse, precision=highest)
    coef_leaf = leaf_coef.transpose(1, 0, 2).reshape(snapshots, blocks_here * span)
    leaf_out = leaf_coef.astype(jnp.bfloat16)
    slot_ids = jnp.arange(slot_count)
    grp_ids = jnp.arange(grp_size)
    own_dest = dest_map[:, 0]
    slot_rank = slot_ranks(own_dest[None, :], grp_size)[0]
    selector = (own_dest[None, None, :] == grp_ids[:, None, None]) & (
        slot_rank[None, None, :] == slot_ids[None, :, None]
    )
    send_coef = jnp.einsum(
        "dkj,jrt->dkrt", selector.astype(jnp.bfloat16), leaf_out, preferred_element_type=jnp.float32
    ).astype(jnp.bfloat16)
    send_centre = jnp.einsum(
        "dkj,jct->dkct", selector.astype(jnp.float32), centers, precision=highest
    )
    received, recv_centre = exchange(send_coef, send_centre, grp_size)
    slot_total = grp_size * slot_count
    coef_all = received.reshape(slot_total, snapshots, span)
    centre_all = recv_centre.reshape(slot_total, 3, span)
    point_blocks = eval_pattern.shape[0]
    point_columns = points[0].T.reshape(point_blocks, span, points.shape[1])
    values = evaluate_all(coef_all, centre_all, point_columns, eval_pattern)
    return (coef_leaf, coef_sep, coef_top, values)


def solution(mesh):
    in_specs = (
        P(None, ("leaf", "grp")),
        P(None, ("leaf", "grp")),
        P(),
        P(("leaf", "grp"), None, None),
        P(("leaf", "grp"), None, None, None),
        P(("leaf", "grp"), None),
        P(("leaf", "grp"), None, None),
        P(("leaf", "grp"), None, None, None),
        P(("leaf", "grp"), None),
        P(),
        P(),
        P(("leaf", "grp"), None),
        P(("leaf", "grp"), None, None),
        P(("leaf", "grp"), None, None),
        P(("leaf", "grp"), None),
    )
    out_specs = (P(None, ("leaf", "grp")), P(None, ("leaf", "grp")), P(), P(None, ("leaf", "grp")))
    return jax.shard_map(
        on_device, mesh=mesh, in_specs=in_specs, out_specs=out_specs, check_vma=False
    )
```

```python
import functools

import jax
import jax.numpy as jnp
from jax import lax
from jax.sharding import PartitionSpec as P
from jax.experimental import pallas as pl
from jax.experimental.pallas import tpu as pltpu

MESH = pl.DeviceIdType.MESH

CAP = 2


highest = lax.Precision.HIGHEST
support_sq = 0.25


def split_up(shard, dim, peers):
    dims = shard.shape
    pieces = shard.reshape(*dims[:dim], peers, dims[dim] // peers, *dims[dim + 1 :])
    return jnp.moveaxis(pieces, dim, 0)


def sum_at_owner(shard, axis, dim):
    pieces = split_up(shard, dim, lax.axis_size(axis))
    arrived = lax.all_to_all(pieces, axis, split_axis=0, concat_axis=0, tiled=True)
    return arrived.astype(jnp.float32).sum(axis=0)


def from_root(shard, axis, root):
    return lax.dynamic_index_in_dim(lax.all_gather(shard, axis), root, 0, keepdims=False)


def copy_for_each(shard, axis):
    copies = jnp.broadcast_to(shard, (lax.axis_size(axis), *shard.shape))
    return lax.all_to_all(copies, axis, split_axis=0, concat_axis=0, tiled=True)


def over_copies(shard, axis):
    return copy_for_each(shard, axis).astype(jnp.float32).sum(axis=0)


def joined_along(pieces, dim):
    dims = list(pieces.shape[1:])
    dims[dim] *= pieces.shape[0]
    return jnp.moveaxis(pieces, 0, dim).reshape(dims)


def gather_directly(shard, axis, dim):
    pieces = copy_for_each(shard, axis)
    return joined_along(pieces, dim)


def _nt(a, b):
    return lax.dot_general(a, b, (((1,), (1,)), ((), ())), preferred_element_type=jnp.float32)


def _nn(a, b):
    return lax.dot_general(a, b, (((1,), (0,)), ((), ())), preferred_element_type=jnp.float32)


def _nt_exact(a, b):
    return lax.dot_general(
        a, b, (((1,), (1,)), ((), ())), precision=highest, preferred_element_type=jnp.float32
    )


def _nn_exact(a, b):
    return lax.dot_general(
        a, b, (((1,), (0,)), ((), ())), precision=highest, preferred_element_type=jnp.float32
    )


def _greet_group(n, leaf, me):
    barrier = pltpu.get_barrier_semaphore()
    for r in range(n):
        @pl.when(me != r)
        def _():
            pl.semaphore_signal(barrier, inc=1, device_id=(leaf, r), device_id_type=MESH)
    pl.semaphore_wait(barrier, n - 1)


def _block_copy(halves, q, dest, send_sem, recv_sem, leaf):
    return pltpu.make_async_remote_copy(
        src_ref=halves.at[q],
        dst_ref=halves.at[q],
        send_sem=send_sem,
        recv_sem=recv_sem.at[q],
        device_id=(leaf, dest),
        device_id_type=MESH,
    )


def _send_block(n, halves, s, solved, sol_ref, send_sem, recv_sem, leaf, dests):
    sol_ref[...] = solved
    halves[s] = solved.astype(jnp.bfloat16)
    for k in range(1, n):
        dest, live = dests(s, k)
        @pl.when(live)
        def _():
            _block_copy(halves, s, dest, send_sem.at[k], recv_sem, leaf).start()
            if k == 1:
                _block_copy(halves, s, dest, send_sem.at[k], recv_sem, leaf).wait_send()
    for k in range(2, n):
        dest, live = dests(s, k)
        @pl.when(live)
        def _():
            _block_copy(halves, s, dest, send_sem.at[k], recv_sem, leaf).wait_send()


def _through(y, hi_ref, lo_ref):
    return _nn(y, hi_ref[...]) + _nn(y, lo_ref[...])


def sep_forward_kernel(n, rhs_ref, part_ref, inv_ref, blocks_ref, hi_ref, lo_ref, sol_ref, halves, resid, base, send_sem, recv_sem, arrived, local_sem, give_sem, take_sem):
    me = lax.axis_index("grp")
    leaf = lax.axis_index("leaf")
    _greet_group(n, leaf, me)

    def give(dest):
        return pltpu.make_async_remote_copy(
            part_ref.at[dest], arrived.at[me], give_sem.at[dest], take_sem.at[me], device_id=(leaf, dest), device_id_type=MESH
        )

    own = pltpu.make_async_copy(part_ref.at[me], arrived.at[me], local_sem.at[0])
    own.start()
    for dest in range(n):
        @pl.when(me != dest)
        def _():
            give(dest).start()
    own.wait()
    for src in range(n):
        @pl.when(me != src)
        def _():
            pltpu.make_async_remote_copy(
                part_ref.at[src], arrived.at[src], give_sem.at[src], take_sem.at[src], device_id=(leaf, src), device_id_type=MESH
            ).wait_recv()
    total = arrived[0].astype(jnp.float32)
    for src in range(1, n):
        total = total + arrived[src].astype(jnp.float32)
    resid[...] = rhs_ref[...] - total
    for dest in range(n):
        @pl.when(me != dest)
        def _():
            give(dest).wait_send()

    dests = lambda s, k: (s + k, s + k < n)

    @pl.when(me == 0)
    def _():
        _send_block(n, halves, 0, _nt_exact(resid[...], inv_ref[...]), sol_ref, send_sem, recv_sem, leaf, dests)

    @pl.when(me == 1)
    def _():
        base[...] = _nt_exact(resid[...], inv_ref[...])

    def step(q, carry):
        @pl.when(me == q + 1)
        def _():
            _block_copy(halves, q, q, send_sem.at[0], recv_sem, leaf).wait_recv()
            solved = base[...] - _through(halves[q], hi_ref, lo_ref)
            _send_block(n, halves, q + 1, solved, sol_ref, send_sem, recv_sem, leaf, dests)

        @pl.when(me > q + 1)
        def _():
            _block_copy(halves, q, q, send_sem.at[0], recv_sem, leaf).wait_recv()
            resid[...] = resid[...] - _nt(halves[q], blocks_ref[q])

            @pl.when(me == q + 2)
            def _():
                base[...] = _nt_exact(resid[...], inv_ref[...])

        return carry

    lax.fori_loop(0, n - 1, step, 0)


def sep_backward_kernel(n, start_ref, inv_ref, blocks_ref, hi_ref, lo_ref, sol_ref, table_ref, halves, resid, base, send_sem, recv_sem):
    me = lax.axis_index("grp")
    leaf = lax.axis_index("leaf")
    _greet_group(n, leaf, me)
    resid[...] = start_ref[...]
    dests = lambda s, k: (s - k, s - k >= 0)

    @pl.when(me == n - 1)
    def _():
        _send_block(n, halves, n - 1, _nn_exact(resid[...], inv_ref[...]), sol_ref, send_sem, recv_sem, leaf, dests)

    @pl.when(me == n - 2)
    def _():
        base[...] = _nn_exact(resid[...], inv_ref[...])

    def step(s, carry):
        q = n - 1 - s

        @pl.when(me < q)
        def _():
            _block_copy(halves, q, q, send_sem.at[0], recv_sem, leaf).wait_recv()

        @pl.when(me == q - 1)
        def _():
            solved = base[...] - _through(halves[q], hi_ref, lo_ref)
            _send_block(n, halves, q - 1, solved, sol_ref, send_sem, recv_sem, leaf, dests)

        @pl.when(me < q - 1)
        def _():
            resid[...] = resid[...] - _nn(halves[q], blocks_ref[q])

            @pl.when(me == q - 2)
            def _():
                base[...] = _nn_exact(resid[...], inv_ref[...])

        return carry

    lax.fori_loop(0, n - 1, step, 0)
    for k in range(1, n):
        @pl.when(me + k < n)
        def _():
            _block_copy(halves, me, me + k, send_sem.at[k], recv_sem, leaf).start()
    for q in range(n):
        @pl.when(q < me)
        def _():
            _block_copy(halves, q, q, send_sem.at[0], recv_sem, leaf).wait_recv()
    for k in range(1, n):
        @pl.when(me + k < n)
        def _():
            _block_copy(halves, me, me + k, send_sem.at[k], recv_sem, leaf).wait_send()
    table_ref[...] = halves[...]


def sep_solve(kind, start, inv, blocks, hi, lo, n):
    rows, width = (start[0] if kind == "forward" else start).shape
    vmem = pl.BlockSpec(memory_space=pltpu.VMEM)
    scratch = [
        pltpu.VMEM((n, rows, width), jnp.bfloat16),
        pltpu.VMEM((rows, width), jnp.float32),
        pltpu.VMEM((rows, width), jnp.float32),
        pltpu.SemaphoreType.DMA((n,)),
        pltpu.SemaphoreType.DMA((n,)),
    ]
    sol_shape = jax.ShapeDtypeStruct((rows, width), jnp.float32)
    params = dict(has_side_effects=True, vmem_limit_bytes=48 * 1024 * 1024)
    if kind == "forward":
        rhs, parts = start
        return pl.pallas_call(
            functools.partial(sep_forward_kernel, n),
            out_shape=sol_shape,
            in_specs=[vmem] * 6,
            out_specs=vmem,
            scratch_shapes=scratch
            + [
                pltpu.VMEM(parts.shape, parts.dtype),
                pltpu.SemaphoreType.DMA((1,)),
                pltpu.SemaphoreType.DMA((n,)),
                pltpu.SemaphoreType.DMA((n,)),
            ],
            compiler_params=pltpu.CompilerParams(collective_id=0, **params),
        )(rhs, parts, inv, blocks, hi, lo)
    return pl.pallas_call(
        functools.partial(sep_backward_kernel, n),
        out_shape=(sol_shape, jax.ShapeDtypeStruct((n, rows, width), jnp.bfloat16)),
        in_specs=[vmem] * 5,
        out_specs=(vmem, vmem),
        scratch_shapes=scratch,
        compiler_params=pltpu.CompilerParams(collective_id=1, **params),
    )(start, inv, blocks, hi, lo)


def split_pair(matrix):
    hi = matrix.astype(jnp.bfloat16)
    lo = (matrix - hi.astype(jnp.float32)).astype(jnp.bfloat16)
    return hi, lo


def top_solve_kernel(nt, span, start_ref, inv_ref, lower_ref, coef_ref, half_ref, fwd_half, fwd_full):
    for t in range(nt):
        cols = slice(t * span, (t + 1) * span)
        residue = start_ref[:, cols]
        if t > 0:
            residue = residue - _nt(fwd_half[:, : t * span], lower_ref[cols, : t * span])
        solved = _nt_exact(residue, inv_ref[t])
        fwd_full[:, cols] = solved
        fwd_half[:, cols] = solved.astype(jnp.bfloat16)
    for t in reversed(range(nt)):
        cols = slice(t * span, (t + 1) * span)
        residue = fwd_full[:, cols]
        if t < nt - 1:
            residue = residue - _nn(half_ref[:, (t + 1) * span :], lower_ref[(t + 1) * span :, cols])
        solved = _nn_exact(residue, inv_ref[t])
        coef_ref[:, cols] = solved
        half_ref[:, cols] = solved.astype(jnp.bfloat16)


def top_solve(top_start, top_inverse, top_lower):
    nt, span = top_inverse.shape[0], top_inverse.shape[1]
    rows, width = top_start.shape
    vmem = pl.BlockSpec(memory_space=pltpu.VMEM)
    return pl.pallas_call(
        functools.partial(top_solve_kernel, nt, span),
        out_shape=(
            jax.ShapeDtypeStruct((rows, width), jnp.float32),
            jax.ShapeDtypeStruct((rows, width), jnp.bfloat16),
        ),
        in_specs=[vmem] * 3,
        out_specs=(vmem, vmem),
        scratch_shapes=[
            pltpu.VMEM((rows, width), jnp.bfloat16),
            pltpu.VMEM((rows, width), jnp.float32),
        ],
        compiler_params=pltpu.CompilerParams(vmem_limit_bytes=48 * 1024 * 1024),
    )(top_start, top_inverse, top_lower)


def evaluate_kernel(slots, pattern_ref, coef_ref, centre_ref, point_ref, out_ref, acc):
    m = pl.program_id(0)
    acc[...] = jnp.zeros_like(acc)
    points_here = point_ref[0]

    def one_slot(s, carry):
        @pl.when(pattern_ref[m, s] != 0)
        def _():
            dist = _nn_exact(centre_ref[s], points_here)
            weight = jnp.maximum(1.0 - dist * (1.0 / support_sq), 0.0)
            kernel = (weight * weight * weight).astype(jnp.bfloat16)
            acc[...] += _nn(coef_ref[s], kernel)

        return carry

    lax.fori_loop(0, slots, one_slot, 0)
    out_ref[...] = acc[...]


def evaluate_all(coef_all, centre_all, point_rows, pattern):
    slots, rows, span = coef_all.shape
    blocks = point_rows.shape[0]
    full = lambda shape: pl.BlockSpec(shape, lambda m, pat: (0,) * len(shape))
    grid_spec = pltpu.PrefetchScalarGridSpec(
        num_scalar_prefetch=1,
        grid=(blocks,),
        in_specs=[
            full(coef_all.shape),
            full(centre_all.shape),
            pl.BlockSpec((1,) + point_rows.shape[1:], lambda m, pat: (m, 0, 0)),
        ],
        out_specs=pl.BlockSpec((rows, span), lambda m, pat: (0, m)),
        scratch_shapes=[pltpu.VMEM((rows, span), jnp.float32)],
    )
    return pl.pallas_call(
        functools.partial(evaluate_kernel, slots),
        out_shape=jax.ShapeDtypeStruct((rows, blocks * span), jnp.float32),
        grid_spec=grid_spec,
    )(pattern, coef_all, centre_all, point_rows)


def augmented(coords, scale, axis):
    squares = jnp.sum(coords * coords, axis=axis, keepdims=True)
    ones = jnp.ones_like(squares)
    zeros = jnp.zeros_like(jnp.concatenate([squares] * 3, axis=axis))
    if scale == 1:
        return jnp.concatenate([coords, squares, ones, zeros], axis=axis)
    return jnp.concatenate([coords * scale, ones, squares, zeros], axis=axis)


def top_reduce_kernel(n, groups, span, term_ref, total_ref, parts_a, parts_b, gathered, local_sem, send_a, recv_a, send_b, recv_b, send_c, recv_c):
    me = lax.axis_index("grp")
    leaf = lax.axis_index("leaf")
    barrier = pltpu.get_barrier_semaphore()
    for r in range(n):
        @pl.when(me != r)
        def _():
            pl.semaphore_signal(barrier, inc=1, device_id=(leaf, r), device_id_type=MESH)
    for g in range(groups):
        @pl.when(leaf != g)
        def _():
            pl.semaphore_signal(barrier, inc=1, device_id=(g, me), device_id_type=MESH)
    pl.semaphore_wait(barrier, n - 1 + groups - 1)

    def column(q):
        return term_ref.at[:, pl.ds(pl.multiple_of(q * span, span), span)]

    def copy_a(k):
        dest = lax.rem(me + k, n)
        return pltpu.make_async_remote_copy(
            column(dest), parts_a.at[me], send_a.at[k], recv_a.at[me], device_id=(leaf, dest), device_id_type=MESH
        )

    def wait_a(k):
        src = lax.rem(me + n - k, n)
        pltpu.make_async_remote_copy(
            column(src), parts_a.at[src], send_a.at[0], recv_a.at[src], device_id=(leaf, src), device_id_type=MESH
        ).wait_recv()

    own = pltpu.make_async_copy(column(me), parts_a.at[me], local_sem.at[0])
    own.start()
    for k in range(1, n):
        copy_a(k).start()
    own.wait()
    for k in range(1, n):
        wait_a(k)
    for k in range(1, n):
        copy_a(k).wait_send()
    total = parts_a[0]
    for q in range(1, n):
        total = total + parts_a[q]
    parts_b[leaf] = total

    def copy_b(k):
        dest = lax.rem(leaf + k, groups)
        return pltpu.make_async_remote_copy(
            parts_b.at[leaf], parts_b.at[leaf], send_b.at[k], recv_b.at[leaf], device_id=(dest, me), device_id_type=MESH
        )

    for k in range(1, groups):
        copy_b(k).start()
    for k in range(1, groups):
        src = lax.rem(leaf + groups - k, groups)
        pltpu.make_async_remote_copy(
            parts_b.at[src], parts_b.at[src], send_b.at[0], recv_b.at[src], device_id=(src, me), device_id_type=MESH
        ).wait_recv()
    for k in range(1, groups):
        copy_b(k).wait_send()
    summed = parts_b[0]
    for g in range(1, groups):
        summed = summed + parts_b[g]
    gathered[me] = summed

    def copy_c(k):
        dest = lax.rem(me + k, n)
        return pltpu.make_async_remote_copy(
            gathered.at[me], gathered.at[me], send_c.at[k], recv_c.at[me], device_id=(leaf, dest), device_id_type=MESH
        )

    for k in range(1, n):
        copy_c(k).start()
    for k in range(1, n):
        src = lax.rem(me + n - k, n)
        pltpu.make_async_remote_copy(
            gathered.at[src], gathered.at[src], send_c.at[0], recv_c.at[src], device_id=(leaf, src), device_id_type=MESH
        ).wait_recv()
    for k in range(1, n):
        copy_c(k).wait_send()
    for q in range(n):
        total_ref[:, q * span : (q + 1) * span] = gathered[q]


def top_reduce(term, n, groups):
    rows, width = term.shape
    span = width // n
    vmem = pl.BlockSpec(memory_space=pltpu.VMEM)
    return pl.pallas_call(
        functools.partial(top_reduce_kernel, n, groups, span),
        out_shape=jax.ShapeDtypeStruct((rows, width), jnp.float32),
        in_specs=[vmem],
        out_specs=vmem,
        scratch_shapes=[
            pltpu.VMEM((n, rows, span), jnp.float32),
            pltpu.VMEM((groups, rows, span), jnp.float32),
            pltpu.VMEM((n, rows, span), jnp.float32),
            pltpu.SemaphoreType.DMA((1,)),
            pltpu.SemaphoreType.DMA((n,)),
            pltpu.SemaphoreType.DMA((n,)),
            pltpu.SemaphoreType.DMA((groups,)),
            pltpu.SemaphoreType.DMA((groups,)),
            pltpu.SemaphoreType.DMA((n,)),
            pltpu.SemaphoreType.DMA((n,)),
        ],
        compiler_params=pltpu.CompilerParams(collective_id=2, has_side_effects=True),
    )(term)


def exchange_kernel(n, coef_ref, centre_ref, coef_out, centre_out, coef_buf, centre_buf, local_sem, send_sem, recv_sem):
    me = lax.axis_index("grp")
    leaf = lax.axis_index("leaf")
    _greet_group(n, leaf, me)
    pairs = ((coef_ref, coef_buf), (centre_ref, centre_buf))

    def push(kind, k):
        source, buf = pairs[kind]
        dest = lax.rem(me + k, n)
        return pltpu.make_async_remote_copy(
            source.at[dest], buf.at[me], send_sem.at[kind, k], recv_sem.at[kind, me], device_id=(leaf, dest), device_id_type=MESH
        )

    owns = [pltpu.make_async_copy(source.at[me], buf.at[me], local_sem.at[kind]) for kind, (source, buf) in enumerate(pairs)]
    for own in owns:
        own.start()
    for k in range(1, n):
        for kind in range(2):
            push(kind, k).start()
    for own in owns:
        own.wait()
    for k in range(1, n):
        src = lax.rem(me + n - k, n)
        for kind, (source, buf) in enumerate(pairs):
            pltpu.make_async_remote_copy(
                source.at[src], buf.at[src], send_sem.at[kind, 0], recv_sem.at[kind, src], device_id=(leaf, src), device_id_type=MESH
            ).wait_recv()
    for k in range(1, n):
        for kind in range(2):
            push(kind, k).wait_send()
    coef_out[...] = coef_buf[...]
    centre_out[...] = centre_buf[...]


def exchange(send_coef, send_centre, n):
    vmem = pl.BlockSpec(memory_space=pltpu.VMEM)
    return pl.pallas_call(
        functools.partial(exchange_kernel, n),
        out_shape=(
            jax.ShapeDtypeStruct(send_coef.shape, send_coef.dtype),
            jax.ShapeDtypeStruct(send_centre.shape, send_centre.dtype),
        ),
        in_specs=[vmem] * 2,
        out_specs=(vmem, vmem),
        scratch_shapes=[
            pltpu.VMEM(send_coef.shape, send_coef.dtype),
            pltpu.VMEM(send_centre.shape, send_centre.dtype),
            pltpu.SemaphoreType.DMA((2,)),
            pltpu.SemaphoreType.DMA((2, n)),
            pltpu.SemaphoreType.DMA((2, n)),
        ],
        compiler_params=pltpu.CompilerParams(collective_id=3, has_side_effects=True),
    )(send_coef, send_centre)


def slot_ranks(dest_rows, grp_size):
    onehot = (dest_rows[..., None] == jnp.arange(grp_size)).astype(jnp.int32)
    before = jnp.cumsum(onehot, axis=-2) - onehot
    return jnp.sum(before * onehot, axis=-1)


def evaluate(coef_all, centre_all, block_points, block_mask):
    dist = jnp.zeros((centre_all.shape[0], centre_all.shape[2], block_points.shape[1]), jnp.float32)
    for comp in range(3):
        delta = centre_all[:, comp, :, None] - block_points[None, comp, None, :]
        dist = dist + delta * delta
    weight = jnp.maximum(1.0 - dist / support_sq, 0.0) ** 3
    kernel = (weight * block_mask.astype(jnp.float32)[:, None, None]).astype(jnp.bfloat16)
    return jnp.einsum("krs,ksp->rp", coef_all, kernel, preferred_element_type=jnp.float32)


def on_device(
    rhs_leaf,
    rhs_sep,
    rhs_top,
    leaf_inverse,
    leaf_coupling,
    leaf_targets,
    sep_inverse,
    sep_blocks,
    top_coupling,
    top_inverse,
    top_lower,
    dest_map,
    centers,
    points,
    eval_pattern,
):
    grp_size = lax.axis_size("grp")
    my_index = lax.axis_index("grp")
    blocks_here = leaf_inverse.shape[0]
    snapshots = rhs_leaf.shape[0]
    span = leaf_inverse.shape[1]
    slot_count = CAP
    leaf_rhs = rhs_leaf.reshape(snapshots, blocks_here, span).transpose(1, 0, 2)
    leaf_sol = jnp.einsum("nrs,nts->nrt", leaf_rhs, leaf_inverse, precision=highest)
    leaf_half = leaf_sol.astype(jnp.bfloat16)
    partial_value = jnp.einsum(
        "nrs,ncbs->ncrb", leaf_half, leaf_coupling, preferred_element_type=jnp.float32
    )
    onehot = (leaf_targets[:, :, None] == jnp.arange(grp_size)[None, None, :]).astype(jnp.float32)
    picked = onehot
    parts = jnp.einsum("ncq,ncrb->qrb", picked, partial_value, precision=highest).astype(jnp.bfloat16)
    inverse_own = sep_inverse[0]
    own_blocks = sep_blocks[0]
    before = lax.dynamic_index_in_dim(own_blocks, jnp.maximum(my_index - 1, 0), 0, keepdims=False)
    fwd_hi, fwd_lo = split_pair(
        jnp.dot(before.astype(jnp.float32).T, inverse_own.T, precision=highest)
    )
    after = lax.dynamic_index_in_dim(own_blocks, jnp.minimum(my_index + 1, grp_size - 1), 0, keepdims=False)
    bwd_hi, bwd_lo = split_pair(jnp.dot(after.astype(jnp.float32), inverse_own, precision=highest))
    sep_sol = sep_solve("forward", (rhs_sep, parts), inverse_own, own_blocks, fwd_hi, fwd_lo, grp_size)
    sep_half = sep_sol.astype(jnp.bfloat16)
    top_term = jnp.dot(sep_half, top_coupling, preferred_element_type=jnp.float32)
    top_total = top_reduce(top_term, grp_size, lax.axis_size("leaf"))
    top_start = rhs_top - top_total
    coef_top, top_half = top_solve(top_start, top_inverse, top_lower)
    back_start = sep_sol - lax.dot_general(
        top_half, top_coupling, (((1,), (1,)), ((), ())), preferred_element_type=jnp.float32
    )

    coef_sep, known_table = sep_solve(
        "backward", back_start, inverse_own, own_blocks, bwd_hi, bwd_lo, grp_size
    )
    picked = jnp.einsum(
        "ncq,qrb->ncrb",
        onehot.astype(jnp.bfloat16),
        known_table,
        preferred_element_type=jnp.float32,
    ).astype(jnp.bfloat16)
    reduced = jnp.einsum(
        "ncrb,ncbs->nrs", picked, leaf_coupling, preferred_element_type=jnp.float32
    )
    leaf_coef = jnp.einsum("nrs,nst->nrt", leaf_sol - reduced, leaf_inverse, precision=highest)
    coef_leaf = leaf_coef.transpose(1, 0, 2).reshape(snapshots, blocks_here * span)
    leaf_out = leaf_coef.astype(jnp.bfloat16)
    slot_ids = jnp.arange(slot_count)
    grp_ids = jnp.arange(grp_size)
    own_dest = dest_map[:, 0]
    slot_rank = slot_ranks(own_dest[None, :], grp_size)[0]
    selector = (own_dest[None, None, :] == grp_ids[:, None, None]) & (
        slot_rank[None, None, :] == slot_ids[None, :, None]
    )
    send_coef = jnp.einsum(
        "dkj,jrt->dkrt", selector.astype(jnp.bfloat16), leaf_out, preferred_element_type=jnp.float32
    ).astype(jnp.bfloat16)
    send_centre = jnp.einsum(
        "dkj,jct->dkct", selector.astype(jnp.float32), centers, precision=highest
    )
    received, recv_centre = exchange(send_coef, send_centre, grp_size)
    slot_total = grp_size * slot_count
    coef_all = received.reshape(slot_total, snapshots, span)
    centre_all = recv_centre.reshape(slot_total, 3, span)
    point_blocks = eval_pattern.shape[0]
    centre_rows = augmented(jnp.swapaxes(centre_all, 1, 2), 1, 2)
    point_rows = augmented(points[0].reshape(3, point_blocks, span).transpose(1, 0, 2), -2.0, 1)
    values = evaluate_all(coef_all, centre_rows, point_rows, eval_pattern)
    return (coef_leaf, coef_sep, coef_top, values)


def solution(mesh):
    in_specs = (
        P(None, ("leaf", "grp")),
        P(None, ("leaf", "grp")),
        P(),
        P(("leaf", "grp"), None, None),
        P(("leaf", "grp"), None, None, None),
        P(("leaf", "grp"), None),
        P(("leaf", "grp"), None, None),
        P(("leaf", "grp"), None, None, None),
        P(("leaf", "grp"), None),
        P(),
        P(),
        P(("leaf", "grp"), None),
        P(("leaf", "grp"), None, None),
        P(("leaf", "grp"), None, None),
        P(("leaf", "grp"), None),
    )
    out_specs = (P(None, ("leaf", "grp")), P(None, ("leaf", "grp")), P(), P(None, ("leaf", "grp")))
    return jax.shard_map(
        on_device, mesh=mesh, in_specs=in_specs, out_specs=out_specs, check_vma=False
    )
```

```python
import functools

import jax
import jax.numpy as jnp
from jax import lax
from jax.sharding import PartitionSpec as P
from jax.experimental import pallas as pl
from jax.experimental.pallas import tpu as pltpu

MESH = pl.DeviceIdType.MESH

CAP = 2


highest = lax.Precision.HIGHEST
support_sq = 0.25


def split_up(shard, dim, peers):
    dims = shard.shape
    pieces = shard.reshape(*dims[:dim], peers, dims[dim] // peers, *dims[dim + 1 :])
    return jnp.moveaxis(pieces, dim, 0)


def sum_at_owner(shard, axis, dim):
    pieces = split_up(shard, dim, lax.axis_size(axis))
    arrived = lax.all_to_all(pieces, axis, split_axis=0, concat_axis=0, tiled=True)
    return arrived.astype(jnp.float32).sum(axis=0)


def from_root(shard, axis, root):
    return lax.dynamic_index_in_dim(lax.all_gather(shard, axis), root, 0, keepdims=False)


def copy_for_each(shard, axis):
    copies = jnp.broadcast_to(shard, (lax.axis_size(axis), *shard.shape))
    return lax.all_to_all(copies, axis, split_axis=0, concat_axis=0, tiled=True)


def over_copies(shard, axis):
    return copy_for_each(shard, axis).astype(jnp.float32).sum(axis=0)


def joined_along(pieces, dim):
    dims = list(pieces.shape[1:])
    dims[dim] *= pieces.shape[0]
    return jnp.moveaxis(pieces, 0, dim).reshape(dims)


def gather_directly(shard, axis, dim):
    pieces = copy_for_each(shard, axis)
    return joined_along(pieces, dim)


def _nt(a, b):
    return lax.dot_general(a, b, (((1,), (1,)), ((), ())), preferred_element_type=jnp.float32)


def _nn(a, b):
    return lax.dot_general(a, b, (((1,), (0,)), ((), ())), preferred_element_type=jnp.float32)


def _nt_exact(a, b):
    return lax.dot_general(
        a, b, (((1,), (1,)), ((), ())), precision=highest, preferred_element_type=jnp.float32
    )


def _nn_exact(a, b):
    return lax.dot_general(
        a, b, (((1,), (0,)), ((), ())), precision=highest, preferred_element_type=jnp.float32
    )


def _greet_group(n, leaf, me):
    barrier = pltpu.get_barrier_semaphore()
    for r in range(n):
        @pl.when(me != r)
        def _():
            pl.semaphore_signal(barrier, inc=1, device_id=(leaf, r), device_id_type=MESH)
    pl.semaphore_wait(barrier, n - 1)


def _block_copy(halves, q, dest, send_sem, recv_sem, leaf):
    return pltpu.make_async_remote_copy(
        src_ref=halves.at[q],
        dst_ref=halves.at[q],
        send_sem=send_sem,
        recv_sem=recv_sem.at[q],
        device_id=(leaf, dest),
        device_id_type=MESH,
    )


def _send_block(n, halves, s, solved, sol_ref, send_sem, recv_sem, leaf, dests):
    sol_ref[...] = solved
    halves[s] = solved.astype(jnp.bfloat16)
    for k in range(1, n):
        dest, live = dests(s, k)
        @pl.when(live)
        def _():
            _block_copy(halves, s, dest, send_sem.at[k], recv_sem, leaf).start()
            if k == 1:
                _block_copy(halves, s, dest, send_sem.at[k], recv_sem, leaf).wait_send()
    for k in range(2, n):
        dest, live = dests(s, k)
        @pl.when(live)
        def _():
            _block_copy(halves, s, dest, send_sem.at[k], recv_sem, leaf).wait_send()


def _through(y, hi_ref, lo_ref):
    return _nn(y, hi_ref[...]) + _nn(y, lo_ref[...])


def sep_forward_kernel(n, rhs_ref, part_ref, inv_ref, blocks_ref, hi_ref, lo_ref, sol_ref, halves, resid, base, send_sem, recv_sem, arrived, local_sem, give_sem, take_sem):
    me = lax.axis_index("grp")
    leaf = lax.axis_index("leaf")
    _greet_group(n, leaf, me)

    def give(dest):
        return pltpu.make_async_remote_copy(
            part_ref.at[dest], arrived.at[me], give_sem.at[dest], take_sem.at[me], device_id=(leaf, dest), device_id_type=MESH
        )

    own = pltpu.make_async_copy(part_ref.at[me], arrived.at[me], local_sem.at[0])
    own.start()
    for dest in range(n):
        @pl.when(me != dest)
        def _():
            give(dest).start()
    own.wait()
    for src in range(n):
        @pl.when(me != src)
        def _():
            pltpu.make_async_remote_copy(
                part_ref.at[src], arrived.at[src], give_sem.at[src], take_sem.at[src], device_id=(leaf, src), device_id_type=MESH
            ).wait_recv()
    total = arrived[0].astype(jnp.float32)
    for src in range(1, n):
        total = total + arrived[src].astype(jnp.float32)
    resid[...] = rhs_ref[...] - total
    for dest in range(n):
        @pl.when(me != dest)
        def _():
            give(dest).wait_send()

    dests = lambda s, k: (s + k, s + k < n)

    @pl.when(me == 0)
    def _():
        _send_block(n, halves, 0, _nt_exact(resid[...], inv_ref[...]), sol_ref, send_sem, recv_sem, leaf, dests)

    @pl.when(me == 1)
    def _():
        base[...] = _nt_exact(resid[...], inv_ref[...])

    def step(q, carry):
        @pl.when(me == q + 1)
        def _():
            _block_copy(halves, q, q, send_sem.at[0], recv_sem, leaf).wait_recv()
            solved = base[...] - _through(halves[q], hi_ref, lo_ref)
            _send_block(n, halves, q + 1, solved, sol_ref, send_sem, recv_sem, leaf, dests)

        @pl.when(me > q + 1)
        def _():
            _block_copy(halves, q, q, send_sem.at[0], recv_sem, leaf).wait_recv()
            resid[...] = resid[...] - _nt(halves[q], blocks_ref[q])

            @pl.when(me == q + 2)
            def _():
                base[...] = _nt_exact(resid[...], inv_ref[...])

        return carry

    lax.fori_loop(0, n - 1, step, 0)


def sep_backward_kernel(n, start_ref, inv_ref, blocks_ref, hi_ref, lo_ref, sol_ref, table_ref, halves, resid, base, send_sem, recv_sem):
    me = lax.axis_index("grp")
    leaf = lax.axis_index("leaf")
    _greet_group(n, leaf, me)
    resid[...] = start_ref[...]
    dests = lambda s, k: (s - k, s - k >= 0)

    @pl.when(me == n - 1)
    def _():
        _send_block(n, halves, n - 1, _nn_exact(resid[...], inv_ref[...]), sol_ref, send_sem, recv_sem, leaf, dests)

    @pl.when(me == n - 2)
    def _():
        base[...] = _nn_exact(resid[...], inv_ref[...])

    def step(s, carry):
        q = n - 1 - s

        @pl.when(me < q)
        def _():
            _block_copy(halves, q, q, send_sem.at[0], recv_sem, leaf).wait_recv()

        @pl.when(me == q - 1)
        def _():
            solved = base[...] - _through(halves[q], hi_ref, lo_ref)
            _send_block(n, halves, q - 1, solved, sol_ref, send_sem, recv_sem, leaf, dests)

        @pl.when(me < q - 1)
        def _():
            resid[...] = resid[...] - _nn(halves[q], blocks_ref[q])

            @pl.when(me == q - 2)
            def _():
                base[...] = _nn_exact(resid[...], inv_ref[...])

        return carry

    lax.fori_loop(0, n - 1, step, 0)
    for k in range(1, n):
        @pl.when(me + k < n)
        def _():
            _block_copy(halves, me, me + k, send_sem.at[k], recv_sem, leaf).start()
    for q in range(n):
        @pl.when(q < me)
        def _():
            _block_copy(halves, q, q, send_sem.at[0], recv_sem, leaf).wait_recv()
    for k in range(1, n):
        @pl.when(me + k < n)
        def _():
            _block_copy(halves, me, me + k, send_sem.at[k], recv_sem, leaf).wait_send()
    table_ref[...] = halves[...]


def sep_solve(kind, start, inv, blocks, hi, lo, n):
    rows, width = (start[0] if kind == "forward" else start).shape
    vmem = pl.BlockSpec(memory_space=pltpu.VMEM)
    scratch = [
        pltpu.VMEM((n, rows, width), jnp.bfloat16),
        pltpu.VMEM((rows, width), jnp.float32),
        pltpu.VMEM((rows, width), jnp.float32),
        pltpu.SemaphoreType.DMA((n,)),
        pltpu.SemaphoreType.DMA((n,)),
    ]
    sol_shape = jax.ShapeDtypeStruct((rows, width), jnp.float32)
    params = dict(has_side_effects=True, vmem_limit_bytes=48 * 1024 * 1024)
    if kind == "forward":
        rhs, parts = start
        return pl.pallas_call(
            functools.partial(sep_forward_kernel, n),
            out_shape=sol_shape,
            in_specs=[vmem] * 6,
            out_specs=vmem,
            scratch_shapes=scratch
            + [
                pltpu.VMEM(parts.shape, parts.dtype),
                pltpu.SemaphoreType.DMA((1,)),
                pltpu.SemaphoreType.DMA((n,)),
                pltpu.SemaphoreType.DMA((n,)),
            ],
            compiler_params=pltpu.CompilerParams(collective_id=0, **params),
        )(rhs, parts, inv, blocks, hi, lo)
    return pl.pallas_call(
        functools.partial(sep_backward_kernel, n),
        out_shape=(sol_shape, jax.ShapeDtypeStruct((n, rows, width), jnp.bfloat16)),
        in_specs=[vmem] * 5,
        out_specs=(vmem, vmem),
        scratch_shapes=scratch,
        compiler_params=pltpu.CompilerParams(collective_id=1, **params),
    )(start, inv, blocks, hi, lo)


def split_pair(matrix):
    hi = matrix.astype(jnp.bfloat16)
    lo = (matrix - hi.astype(jnp.float32)).astype(jnp.bfloat16)
    return hi, lo


def top_solve_kernel(nt, span, start_ref, inv_ref, lower_ref, coef_ref, half_ref, fwd_half, fwd_full):
    for t in range(nt):
        cols = slice(t * span, (t + 1) * span)
        residue = start_ref[:, cols]
        if t > 0:
            residue = residue - _nt(fwd_half[:, : t * span], lower_ref[cols, : t * span])
        solved = _nt_exact(residue, inv_ref[t])
        fwd_full[:, cols] = solved
        fwd_half[:, cols] = solved.astype(jnp.bfloat16)
    for t in reversed(range(nt)):
        cols = slice(t * span, (t + 1) * span)
        residue = fwd_full[:, cols]
        if t < nt - 1:
            residue = residue - _nn(half_ref[:, (t + 1) * span :], lower_ref[(t + 1) * span :, cols])
        solved = _nn_exact(residue, inv_ref[t])
        coef_ref[:, cols] = solved
        half_ref[:, cols] = solved.astype(jnp.bfloat16)


def top_solve(top_start, top_inverse, top_lower):
    nt, span = top_inverse.shape[0], top_inverse.shape[1]
    rows, width = top_start.shape
    vmem = pl.BlockSpec(memory_space=pltpu.VMEM)
    return pl.pallas_call(
        functools.partial(top_solve_kernel, nt, span),
        out_shape=(
            jax.ShapeDtypeStruct((rows, width), jnp.float32),
            jax.ShapeDtypeStruct((rows, width), jnp.bfloat16),
        ),
        in_specs=[vmem] * 3,
        out_specs=(vmem, vmem),
        scratch_shapes=[
            pltpu.VMEM((rows, width), jnp.bfloat16),
            pltpu.VMEM((rows, width), jnp.float32),
        ],
        compiler_params=pltpu.CompilerParams(vmem_limit_bytes=48 * 1024 * 1024),
    )(top_start, top_inverse, top_lower)


def evaluate_kernel(slots, pattern_ref, coef_ref, centre_ref, column_ref, out_ref, acc, spread):
    m = pl.program_id(0)
    acc[...] = jnp.zeros_like(acc)
    column = column_ref[0]
    width = centre_ref.shape[2]
    for comp in range(3):
        spread[comp] = jnp.broadcast_to(column[:, comp : comp + 1], (column.shape[0], width))

    def one_slot(s, carry):
        @pl.when(pattern_ref[m, s] != 0)
        def _():
            centre = centre_ref[s]
            dist = None
            for comp in range(3):
                delta = centre[comp : comp + 1, :] - spread[comp]
                dist = delta * delta if dist is None else dist + delta * delta
            weight = jnp.maximum(1.0 - dist * (1.0 / support_sq), 0.0)
            kernel = (weight * weight * weight).astype(jnp.bfloat16)
            acc[...] += _nt(coef_ref[s], kernel)

        return carry

    lax.fori_loop(0, slots, one_slot, 0)
    out_ref[...] = acc[...]


def evaluate_all(coef_all, centre_all, point_columns, pattern):
    slots, rows, span = coef_all.shape
    blocks = point_columns.shape[0]
    full = lambda shape: pl.BlockSpec(shape, lambda m, pat: (0,) * len(shape))
    grid_spec = pltpu.PrefetchScalarGridSpec(
        num_scalar_prefetch=1,
        grid=(blocks,),
        in_specs=[
            full(coef_all.shape),
            full(centre_all.shape),
            pl.BlockSpec((1, span, point_columns.shape[2]), lambda m, pat: (m, 0, 0)),
        ],
        out_specs=pl.BlockSpec((rows, span), lambda m, pat: (0, m)),
        scratch_shapes=[
            pltpu.VMEM((rows, span), jnp.float32),
            pltpu.VMEM((3, span, centre_all.shape[2]), jnp.float32),
        ],
    )
    return pl.pallas_call(
        functools.partial(evaluate_kernel, slots),
        out_shape=jax.ShapeDtypeStruct((rows, blocks * span), jnp.float32),
        grid_spec=grid_spec,
    )(pattern, coef_all, centre_all, point_columns)


def top_reduce_kernel(n, groups, span, term_ref, total_ref, parts_a, parts_b, gathered, local_sem, send_a, recv_a, send_b, recv_b, send_c, recv_c):
    me = lax.axis_index("grp")
    leaf = lax.axis_index("leaf")
    barrier = pltpu.get_barrier_semaphore()
    for r in range(n):
        @pl.when(me != r)
        def _():
            pl.semaphore_signal(barrier, inc=1, device_id=(leaf, r), device_id_type=MESH)
    for g in range(groups):
        @pl.when(leaf != g)
        def _():
            pl.semaphore_signal(barrier, inc=1, device_id=(g, me), device_id_type=MESH)
    pl.semaphore_wait(barrier, n - 1 + groups - 1)

    def column(q):
        return term_ref.at[:, pl.ds(pl.multiple_of(q * span, span), span)]

    def copy_a(k):
        dest = lax.rem(me + k, n)
        return pltpu.make_async_remote_copy(
            column(dest), parts_a.at[me], send_a.at[k], recv_a.at[me], device_id=(leaf, dest), device_id_type=MESH
        )

    def wait_a(k):
        src = lax.rem(me + n - k, n)
        pltpu.make_async_remote_copy(
            column(src), parts_a.at[src], send_a.at[0], recv_a.at[src], device_id=(leaf, src), device_id_type=MESH
        ).wait_recv()

    own = pltpu.make_async_copy(column(me), parts_a.at[me], local_sem.at[0])
    own.start()
    for k in range(1, n):
        copy_a(k).start()
    own.wait()
    for k in range(1, n):
        wait_a(k)
    for k in range(1, n):
        copy_a(k).wait_send()
    total = parts_a[0]
    for q in range(1, n):
        total = total + parts_a[q]
    parts_b[leaf] = total

    def copy_b(k):
        dest = lax.rem(leaf + k, groups)
        return pltpu.make_async_remote_copy(
            parts_b.at[leaf], parts_b.at[leaf], send_b.at[k], recv_b.at[leaf], device_id=(dest, me), device_id_type=MESH
        )

    for k in range(1, groups):
        copy_b(k).start()
    for k in range(1, groups):
        src = lax.rem(leaf + groups - k, groups)
        pltpu.make_async_remote_copy(
            parts_b.at[src], parts_b.at[src], send_b.at[0], recv_b.at[src], device_id=(src, me), device_id_type=MESH
        ).wait_recv()
    for k in range(1, groups):
        copy_b(k).wait_send()
    summed = parts_b[0]
    for g in range(1, groups):
        summed = summed + parts_b[g]
    gathered[me] = summed

    def copy_c(k):
        dest = lax.rem(me + k, n)
        return pltpu.make_async_remote_copy(
            gathered.at[me], gathered.at[me], send_c.at[k], recv_c.at[me], device_id=(leaf, dest), device_id_type=MESH
        )

    for k in range(1, n):
        copy_c(k).start()
    for k in range(1, n):
        src = lax.rem(me + n - k, n)
        pltpu.make_async_remote_copy(
            gathered.at[src], gathered.at[src], send_c.at[0], recv_c.at[src], device_id=(leaf, src), device_id_type=MESH
        ).wait_recv()
    for k in range(1, n):
        copy_c(k).wait_send()
    for q in range(n):
        total_ref[:, q * span : (q + 1) * span] = gathered[q]


def top_reduce(term, n, groups):
    rows, width = term.shape
    span = width // n
    vmem = pl.BlockSpec(memory_space=pltpu.VMEM)
    return pl.pallas_call(
        functools.partial(top_reduce_kernel, n, groups, span),
        out_shape=jax.ShapeDtypeStruct((rows, width), jnp.float32),
        in_specs=[vmem],
        out_specs=vmem,
        scratch_shapes=[
            pltpu.VMEM((n, rows, span), jnp.float32),
            pltpu.VMEM((groups, rows, span), jnp.float32),
            pltpu.VMEM((n, rows, span), jnp.float32),
            pltpu.SemaphoreType.DMA((1,)),
            pltpu.SemaphoreType.DMA((n,)),
            pltpu.SemaphoreType.DMA((n,)),
            pltpu.SemaphoreType.DMA((groups,)),
            pltpu.SemaphoreType.DMA((groups,)),
            pltpu.SemaphoreType.DMA((n,)),
            pltpu.SemaphoreType.DMA((n,)),
        ],
        compiler_params=pltpu.CompilerParams(collective_id=2, has_side_effects=True),
    )(term)


def exchange_kernel(n, coef_ref, centre_ref, coef_out, centre_out, coef_buf, centre_buf, local_sem, send_sem, recv_sem):
    me = lax.axis_index("grp")
    leaf = lax.axis_index("leaf")
    _greet_group(n, leaf, me)
    pairs = ((coef_ref, coef_buf), (centre_ref, centre_buf))

    def push(kind, k):
        source, buf = pairs[kind]
        dest = lax.rem(me + k, n)
        return pltpu.make_async_remote_copy(
            source.at[dest], buf.at[me], send_sem.at[kind, k], recv_sem.at[kind, me], device_id=(leaf, dest), device_id_type=MESH
        )

    owns = [pltpu.make_async_copy(source.at[me], buf.at[me], local_sem.at[kind]) for kind, (source, buf) in enumerate(pairs)]
    for own in owns:
        own.start()
    for k in range(1, n):
        for kind in range(2):
            push(kind, k).start()
    for own in owns:
        own.wait()
    for k in range(1, n):
        src = lax.rem(me + n - k, n)
        for kind, (source, buf) in enumerate(pairs):
            pltpu.make_async_remote_copy(
                source.at[src], buf.at[src], send_sem.at[kind, 0], recv_sem.at[kind, src], device_id=(leaf, src), device_id_type=MESH
            ).wait_recv()
    for k in range(1, n):
        for kind in range(2):
            push(kind, k).wait_send()
    coef_out[...] = coef_buf[...]
    centre_out[...] = centre_buf[...]


def exchange(send_coef, send_centre, n):
    vmem = pl.BlockSpec(memory_space=pltpu.VMEM)
    return pl.pallas_call(
        functools.partial(exchange_kernel, n),
        out_shape=(
            jax.ShapeDtypeStruct(send_coef.shape, send_coef.dtype),
            jax.ShapeDtypeStruct(send_centre.shape, send_centre.dtype),
        ),
        in_specs=[vmem] * 2,
        out_specs=(vmem, vmem),
        scratch_shapes=[
            pltpu.VMEM(send_coef.shape, send_coef.dtype),
            pltpu.VMEM(send_centre.shape, send_centre.dtype),
            pltpu.SemaphoreType.DMA((2,)),
            pltpu.SemaphoreType.DMA((2, n)),
            pltpu.SemaphoreType.DMA((2, n)),
        ],
        compiler_params=pltpu.CompilerParams(collective_id=3, has_side_effects=True),
    )(send_coef, send_centre)


def slot_ranks(dest_rows, grp_size):
    onehot = (dest_rows[..., None] == jnp.arange(grp_size)).astype(jnp.int32)
    before = jnp.cumsum(onehot, axis=-2) - onehot
    return jnp.sum(before * onehot, axis=-1)


def evaluate(coef_all, centre_all, block_points, block_mask):
    dist = jnp.zeros((centre_all.shape[0], centre_all.shape[2], block_points.shape[1]), jnp.float32)
    for comp in range(3):
        delta = centre_all[:, comp, :, None] - block_points[None, comp, None, :]
        dist = dist + delta * delta
    weight = jnp.maximum(1.0 - dist / support_sq, 0.0) ** 3
    kernel = (weight * block_mask.astype(jnp.float32)[:, None, None]).astype(jnp.bfloat16)
    return jnp.einsum("krs,ksp->rp", coef_all, kernel, preferred_element_type=jnp.float32)


def on_device(
    rhs_leaf,
    rhs_sep,
    rhs_top,
    leaf_inverse,
    leaf_coupling,
    leaf_targets,
    sep_inverse,
    sep_blocks,
    top_coupling,
    top_inverse,
    top_lower,
    dest_map,
    centers,
    points,
    eval_pattern,
):
    grp_size = lax.axis_size("grp")
    my_index = lax.axis_index("grp")
    blocks_here = leaf_inverse.shape[0]
    snapshots = rhs_leaf.shape[0]
    span = leaf_inverse.shape[1]
    slot_count = CAP
    leaf_rhs = rhs_leaf.reshape(snapshots, blocks_here, span).transpose(1, 0, 2)
    leaf_sol = jnp.einsum("nrs,nts->nrt", leaf_rhs, leaf_inverse, precision=highest)
    leaf_half = leaf_sol.astype(jnp.bfloat16)
    partial_value = jnp.einsum(
        "nrs,ncbs->ncrb", leaf_half, leaf_coupling, preferred_element_type=jnp.float32
    )
    onehot = (leaf_targets[:, :, None] == jnp.arange(grp_size)[None, None, :]).astype(jnp.float32)
    picked = onehot
    parts = jnp.einsum("ncq,ncrb->qrb", picked, partial_value, precision=highest).astype(jnp.bfloat16)
    inverse_own = sep_inverse[0]
    own_blocks = sep_blocks[0]
    before = lax.dynamic_index_in_dim(own_blocks, jnp.maximum(my_index - 1, 0), 0, keepdims=False)
    fwd_hi, fwd_lo = split_pair(
        jnp.dot(before.astype(jnp.float32).T, inverse_own.T, precision=highest)
    )
    after = lax.dynamic_index_in_dim(own_blocks, jnp.minimum(my_index + 1, grp_size - 1), 0, keepdims=False)
    bwd_hi, bwd_lo = split_pair(jnp.dot(after.astype(jnp.float32), inverse_own, precision=highest))
    sep_sol = sep_solve("forward", (rhs_sep, parts), inverse_own, own_blocks, fwd_hi, fwd_lo, grp_size)
    sep_half = sep_sol.astype(jnp.bfloat16)
    top_term = jnp.dot(sep_half, top_coupling, preferred_element_type=jnp.float32)
    top_total = top_reduce(top_term, grp_size, lax.axis_size("leaf"))
    top_start = rhs_top - top_total
    coef_top, top_half = top_solve(top_start, top_inverse, top_lower)
    back_start = sep_sol - lax.dot_general(
        top_half, top_coupling, (((1,), (1,)), ((), ())), preferred_element_type=jnp.float32
    )

    coef_sep, known_table = sep_solve(
        "backward", back_start, inverse_own, own_blocks, bwd_hi, bwd_lo, grp_size
    )
    picked = jnp.einsum(
        "ncq,qrb->ncrb",
        onehot.astype(jnp.bfloat16),
        known_table,
        preferred_element_type=jnp.float32,
    ).astype(jnp.bfloat16)
    reduced = jnp.einsum(
        "ncrb,ncbs->nrs", picked, leaf_coupling, preferred_element_type=jnp.float32
    )
    leaf_coef = jnp.einsum("nrs,nst->nrt", leaf_sol - reduced, leaf_inverse, precision=highest)
    coef_leaf = leaf_coef.transpose(1, 0, 2).reshape(snapshots, blocks_here * span)
    leaf_out = leaf_coef.astype(jnp.bfloat16)
    slot_ids = jnp.arange(slot_count)
    grp_ids = jnp.arange(grp_size)
    own_dest = dest_map[:, 0]
    slot_rank = slot_ranks(own_dest[None, :], grp_size)[0]
    selector = (own_dest[None, None, :] == grp_ids[:, None, None]) & (
        slot_rank[None, None, :] == slot_ids[None, :, None]
    )
    send_coef = jnp.einsum(
        "dkj,jrt->dkrt", selector.astype(jnp.bfloat16), leaf_out, preferred_element_type=jnp.float32
    ).astype(jnp.bfloat16)
    send_centre = jnp.einsum(
        "dkj,jct->dkct", selector.astype(jnp.float32), centers, precision=highest
    )
    received, recv_centre = exchange(send_coef, send_centre, grp_size)
    slot_total = grp_size * slot_count
    coef_all = received.reshape(slot_total, snapshots, span)
    centre_all = recv_centre.reshape(slot_total, 3, span)
    point_blocks = eval_pattern.shape[0]
    point_columns = points[0].T.reshape(point_blocks, span, points.shape[1])
    filled = jnp.any(coef_all != 0, axis=(1, 2))
    flags = ((eval_pattern != 0) & filled[None, :]).astype(jnp.int32)
    values = evaluate_all(coef_all, centre_all, point_columns, flags)
    return (coef_leaf, coef_sep, coef_top, values)


def solution(mesh):
    in_specs = (
        P(None, ("leaf", "grp")),
        P(None, ("leaf", "grp")),
        P(),
        P(("leaf", "grp"), None, None),
        P(("leaf", "grp"), None, None, None),
        P(("leaf", "grp"), None),
        P(("leaf", "grp"), None, None),
        P(("leaf", "grp"), None, None, None),
        P(("leaf", "grp"), None),
        P(),
        P(),
        P(("leaf", "grp"), None),
        P(("leaf", "grp"), None, None),
        P(("leaf", "grp"), None, None),
        P(("leaf", "grp"), None),
    )
    out_specs = (P(None, ("leaf", "grp")), P(None, ("leaf", "grp")), P(), P(None, ("leaf", "grp")))
    return jax.shard_map(
        on_device, mesh=mesh, in_specs=in_specs, out_specs=out_specs, check_vma=False
    )
```

```python
import functools

import jax
import jax.numpy as jnp
from jax import lax
from jax.sharding import PartitionSpec as P
from jax.experimental import pallas as pl
from jax.experimental.pallas import tpu as pltpu

MESH = pl.DeviceIdType.MESH

CAP = 2


highest = lax.Precision.HIGHEST
support_sq = 0.25


def split_up(shard, dim, peers):
    dims = shard.shape
    pieces = shard.reshape(*dims[:dim], peers, dims[dim] // peers, *dims[dim + 1 :])
    return jnp.moveaxis(pieces, dim, 0)


def sum_at_owner(shard, axis, dim):
    pieces = split_up(shard, dim, lax.axis_size(axis))
    arrived = lax.all_to_all(pieces, axis, split_axis=0, concat_axis=0, tiled=True)
    return arrived.astype(jnp.float32).sum(axis=0)


def from_root(shard, axis, root):
    return lax.dynamic_index_in_dim(lax.all_gather(shard, axis), root, 0, keepdims=False)


def copy_for_each(shard, axis):
    copies = jnp.broadcast_to(shard, (lax.axis_size(axis), *shard.shape))
    return lax.all_to_all(copies, axis, split_axis=0, concat_axis=0, tiled=True)


def over_copies(shard, axis):
    return copy_for_each(shard, axis).astype(jnp.float32).sum(axis=0)


def joined_along(pieces, dim):
    dims = list(pieces.shape[1:])
    dims[dim] *= pieces.shape[0]
    return jnp.moveaxis(pieces, 0, dim).reshape(dims)


def gather_directly(shard, axis, dim):
    pieces = copy_for_each(shard, axis)
    return joined_along(pieces, dim)


def _nt(a, b):
    return lax.dot_general(a, b, (((1,), (1,)), ((), ())), preferred_element_type=jnp.float32)


def _nn(a, b):
    return lax.dot_general(a, b, (((1,), (0,)), ((), ())), preferred_element_type=jnp.float32)


def _nt_exact(a, b):
    return lax.dot_general(
        a, b, (((1,), (1,)), ((), ())), precision=highest, preferred_element_type=jnp.float32
    )


def _nn_exact(a, b):
    return lax.dot_general(
        a, b, (((1,), (0,)), ((), ())), precision=highest, preferred_element_type=jnp.float32
    )


def _greet_group(n, leaf, me):
    barrier = pltpu.get_barrier_semaphore()
    for r in range(n):
        @pl.when(me != r)
        def _():
            pl.semaphore_signal(barrier, inc=1, device_id=(leaf, r), device_id_type=MESH)
    pl.semaphore_wait(barrier, n - 1)


def _block_copy(halves, q, dest, send_sem, recv_sem, leaf):
    return pltpu.make_async_remote_copy(
        src_ref=halves.at[q],
        dst_ref=halves.at[q],
        send_sem=send_sem,
        recv_sem=recv_sem.at[q],
        device_id=(leaf, dest),
        device_id_type=MESH,
    )


def _send_block(n, halves, s, solved, sol_ref, send_sem, recv_sem, leaf, dests):
    sol_ref[...] = solved
    halves[s] = solved.astype(jnp.bfloat16)
    for k in range(1, n):
        dest, live = dests(s, k)
        @pl.when(live)
        def _():
            _block_copy(halves, s, dest, send_sem.at[k], recv_sem, leaf).start()
            if k == 1:
                _block_copy(halves, s, dest, send_sem.at[k], recv_sem, leaf).wait_send()
    for k in range(2, n):
        dest, live = dests(s, k)
        @pl.when(live)
        def _():
            _block_copy(halves, s, dest, send_sem.at[k], recv_sem, leaf).wait_send()


def _through(y, hi_ref, lo_ref):
    return _nn(y, hi_ref[...]) + _nn(y, lo_ref[...])


def sep_forward_kernel(n, rhs_ref, part_ref, inv_ref, blocks_ref, hi_ref, lo_ref, sol_ref, halves, resid, base, send_sem, recv_sem, arrived, local_sem, give_sem, take_sem):
    me = lax.axis_index("grp")
    leaf = lax.axis_index("leaf")
    _greet_group(n, leaf, me)

    def give(dest):
        return pltpu.make_async_remote_copy(
            part_ref.at[dest], arrived.at[me], give_sem.at[dest], take_sem.at[me], device_id=(leaf, dest), device_id_type=MESH
        )

    own = pltpu.make_async_copy(part_ref.at[me], arrived.at[me], local_sem.at[0])
    own.start()
    for dest in range(n):
        @pl.when(me != dest)
        def _():
            give(dest).start()
    own.wait()
    for src in range(n):
        @pl.when(me != src)
        def _():
            pltpu.make_async_remote_copy(
                part_ref.at[src], arrived.at[src], give_sem.at[src], take_sem.at[src], device_id=(leaf, src), device_id_type=MESH
            ).wait_recv()
    total = arrived[0].astype(jnp.float32)
    for src in range(1, n):
        total = total + arrived[src].astype(jnp.float32)
    resid[...] = rhs_ref[...] - total
    for dest in range(n):
        @pl.when(me != dest)
        def _():
            give(dest).wait_send()

    dests = lambda s, k: (s + k, s + k < n)

    @pl.when(me == 0)
    def _():
        _send_block(n, halves, 0, _nt_exact(resid[...], inv_ref[...]), sol_ref, send_sem, recv_sem, leaf, dests)

    @pl.when(me == 1)
    def _():
        base[...] = _nt_exact(resid[...], inv_ref[...])

    def step(q, carry):
        @pl.when(me == q + 1)
        def _():
            _block_copy(halves, q, q, send_sem.at[0], recv_sem, leaf).wait_recv()
            solved = base[...] - _through(halves[q], hi_ref, lo_ref)
            _send_block(n, halves, q + 1, solved, sol_ref, send_sem, recv_sem, leaf, dests)

        @pl.when(me > q + 1)
        def _():
            _block_copy(halves, q, q, send_sem.at[0], recv_sem, leaf).wait_recv()
            resid[...] = resid[...] - _nt(halves[q], blocks_ref[q])

            @pl.when(me == q + 2)
            def _():
                base[...] = _nt_exact(resid[...], inv_ref[...])

        return carry

    lax.fori_loop(0, n - 1, step, 0)


def sep_backward_kernel(n, start_ref, inv_ref, blocks_ref, hi_ref, lo_ref, sol_ref, table_ref, halves, resid, base, send_sem, recv_sem):
    me = lax.axis_index("grp")
    leaf = lax.axis_index("leaf")
    _greet_group(n, leaf, me)
    resid[...] = start_ref[...]
    dests = lambda s, k: (s - k, s - k >= 0)

    @pl.when(me == n - 1)
    def _():
        _send_block(n, halves, n - 1, _nn_exact(resid[...], inv_ref[...]), sol_ref, send_sem, recv_sem, leaf, dests)

    @pl.when(me == n - 2)
    def _():
        base[...] = _nn_exact(resid[...], inv_ref[...])

    def step(s, carry):
        q = n - 1 - s

        @pl.when(me < q)
        def _():
            _block_copy(halves, q, q, send_sem.at[0], recv_sem, leaf).wait_recv()

        @pl.when(me == q - 1)
        def _():
            solved = base[...] - _through(halves[q], hi_ref, lo_ref)
            _send_block(n, halves, q - 1, solved, sol_ref, send_sem, recv_sem, leaf, dests)

        @pl.when(me < q - 1)
        def _():
            resid[...] = resid[...] - _nn(halves[q], blocks_ref[q])

            @pl.when(me == q - 2)
            def _():
                base[...] = _nn_exact(resid[...], inv_ref[...])

        return carry

    lax.fori_loop(0, n - 1, step, 0)
    for k in range(1, n):
        @pl.when(me + k < n)
        def _():
            _block_copy(halves, me, me + k, send_sem.at[k], recv_sem, leaf).start()
    for q in range(n):
        @pl.when(q < me)
        def _():
            _block_copy(halves, q, q, send_sem.at[0], recv_sem, leaf).wait_recv()
    for k in range(1, n):
        @pl.when(me + k < n)
        def _():
            _block_copy(halves, me, me + k, send_sem.at[k], recv_sem, leaf).wait_send()
    table_ref[...] = halves[...]


def sep_solve(kind, start, inv, blocks, hi, lo, n):
    rows, width = (start[0] if kind == "forward" else start).shape
    vmem = pl.BlockSpec(memory_space=pltpu.VMEM)
    scratch = [
        pltpu.VMEM((n, rows, width), jnp.bfloat16),
        pltpu.VMEM((rows, width), jnp.float32),
        pltpu.VMEM((rows, width), jnp.float32),
        pltpu.SemaphoreType.DMA((n,)),
        pltpu.SemaphoreType.DMA((n,)),
    ]
    sol_shape = jax.ShapeDtypeStruct((rows, width), jnp.float32)
    params = dict(has_side_effects=True, vmem_limit_bytes=48 * 1024 * 1024)
    if kind == "forward":
        rhs, parts = start
        return pl.pallas_call(
            functools.partial(sep_forward_kernel, n),
            out_shape=sol_shape,
            in_specs=[vmem] * 6,
            out_specs=vmem,
            scratch_shapes=scratch
            + [
                pltpu.VMEM(parts.shape, parts.dtype),
                pltpu.SemaphoreType.DMA((1,)),
                pltpu.SemaphoreType.DMA((n,)),
                pltpu.SemaphoreType.DMA((n,)),
            ],
            compiler_params=pltpu.CompilerParams(collective_id=0, **params),
        )(rhs, parts, inv, blocks, hi, lo)
    return pl.pallas_call(
        functools.partial(sep_backward_kernel, n),
        out_shape=(sol_shape, jax.ShapeDtypeStruct((n, rows, width), jnp.bfloat16)),
        in_specs=[vmem] * 5,
        out_specs=(vmem, vmem),
        scratch_shapes=scratch,
        compiler_params=pltpu.CompilerParams(collective_id=1, **params),
    )(start, inv, blocks, hi, lo)


def split_pair(matrix):
    hi = matrix.astype(jnp.bfloat16)
    lo = (matrix - hi.astype(jnp.float32)).astype(jnp.bfloat16)
    return hi, lo


def top_solve_kernel(nt, span, start_ref, inv_ref, lower_ref, coef_ref, half_ref, fwd_half, fwd_full):
    for t in range(nt):
        cols = slice(t * span, (t + 1) * span)
        residue = start_ref[:, cols]
        if t > 0:
            residue = residue - _nt(fwd_half[:, : t * span], lower_ref[cols, : t * span])
        solved = _nt_exact(residue, inv_ref[t])
        fwd_full[:, cols] = solved
        fwd_half[:, cols] = solved.astype(jnp.bfloat16)
    for t in reversed(range(nt)):
        cols = slice(t * span, (t + 1) * span)
        residue = fwd_full[:, cols]
        if t < nt - 1:
            residue = residue - _nn(half_ref[:, (t + 1) * span :], lower_ref[(t + 1) * span :, cols])
        solved = _nn_exact(residue, inv_ref[t])
        coef_ref[:, cols] = solved
        half_ref[:, cols] = solved.astype(jnp.bfloat16)


def top_solve(top_start, top_inverse, top_lower):
    nt, span = top_inverse.shape[0], top_inverse.shape[1]
    rows, width = top_start.shape
    vmem = pl.BlockSpec(memory_space=pltpu.VMEM)
    return pl.pallas_call(
        functools.partial(top_solve_kernel, nt, span),
        out_shape=(
            jax.ShapeDtypeStruct((rows, width), jnp.float32),
            jax.ShapeDtypeStruct((rows, width), jnp.bfloat16),
        ),
        in_specs=[vmem] * 3,
        out_specs=(vmem, vmem),
        scratch_shapes=[
            pltpu.VMEM((rows, width), jnp.bfloat16),
            pltpu.VMEM((rows, width), jnp.float32),
        ],
        compiler_params=pltpu.CompilerParams(vmem_limit_bytes=48 * 1024 * 1024),
    )(top_start, top_inverse, top_lower)


def evaluate_kernel(slots, pattern_ref, coef_ref, centre_ref, point_ref, out_ref, acc, spread):
    m = pl.program_id(0)
    width = point_ref.shape[2]

    @pl.when(m == 0)
    def _():
        for s in range(slots):
            column = centre_ref[s]
            for comp in range(3):
                spread[s, comp] = jnp.broadcast_to(column[:, comp : comp + 1], (column.shape[0], width))

    acc[...] = jnp.zeros_like(acc)
    row = point_ref[0]

    def one_slot(s, carry):
        @pl.when(pattern_ref[m, s] != 0)
        def _():
            dist = None
            for comp in range(3):
                delta = spread[s, comp] - row[comp : comp + 1, :]
                dist = delta * delta if dist is None else dist + delta * delta
            weight = jnp.maximum(1.0 - dist, 0.0)
            kernel = (weight * weight * weight).astype(jnp.bfloat16)
            acc[...] += _nn(coef_ref[s], kernel)

        return carry

    lax.fori_loop(0, slots, one_slot, 0)
    out_ref[...] = acc[...]


def evaluate_all(coef_all, centre_columns, point_rows, pattern):
    slots, rows, span = coef_all.shape
    blocks = point_rows.shape[0]
    full = lambda shape: pl.BlockSpec(shape, lambda m, pat: (0,) * len(shape))
    grid_spec = pltpu.PrefetchScalarGridSpec(
        num_scalar_prefetch=1,
        grid=(blocks,),
        in_specs=[
            full(coef_all.shape),
            full(centre_columns.shape),
            pl.BlockSpec((1,) + point_rows.shape[1:], lambda m, pat: (m, 0, 0)),
        ],
        out_specs=pl.BlockSpec((rows, span), lambda m, pat: (0, m)),
        scratch_shapes=[
            pltpu.VMEM((rows, span), jnp.float32),
            pltpu.VMEM((slots, 3, centre_columns.shape[1], point_rows.shape[2]), jnp.float32),
        ],
    )
    return pl.pallas_call(
        functools.partial(evaluate_kernel, slots),
        out_shape=jax.ShapeDtypeStruct((rows, blocks * span), jnp.float32),
        grid_spec=grid_spec,
        compiler_params=pltpu.CompilerParams(vmem_limit_bytes=48 * 1024 * 1024),
    )(pattern, coef_all, centre_columns, point_rows)


def top_reduce_kernel(n, groups, span, term_ref, total_ref, parts_a, parts_b, gathered, local_sem, send_a, recv_a, send_b, recv_b, send_c, recv_c):
    me = lax.axis_index("grp")
    leaf = lax.axis_index("leaf")
    barrier = pltpu.get_barrier_semaphore()
    for r in range(n):
        @pl.when(me != r)
        def _():
            pl.semaphore_signal(barrier, inc=1, device_id=(leaf, r), device_id_type=MESH)
    for g in range(groups):
        @pl.when(leaf != g)
        def _():
            pl.semaphore_signal(barrier, inc=1, device_id=(g, me), device_id_type=MESH)
    pl.semaphore_wait(barrier, n - 1 + groups - 1)

    def column(q):
        return term_ref.at[:, pl.ds(pl.multiple_of(q * span, span), span)]

    def copy_a(k):
        dest = lax.rem(me + k, n)
        return pltpu.make_async_remote_copy(
            column(dest), parts_a.at[me], send_a.at[k], recv_a.at[me], device_id=(leaf, dest), device_id_type=MESH
        )

    def wait_a(k):
        src = lax.rem(me + n - k, n)
        pltpu.make_async_remote_copy(
            column(src), parts_a.at[src], send_a.at[0], recv_a.at[src], device_id=(leaf, src), device_id_type=MESH
        ).wait_recv()

    own = pltpu.make_async_copy(column(me), parts_a.at[me], local_sem.at[0])
    own.start()
    for k in range(1, n):
        copy_a(k).start()
    own.wait()
    for k in range(1, n):
        wait_a(k)
    for k in range(1, n):
        copy_a(k).wait_send()
    total = parts_a[0]
    for q in range(1, n):
        total = total + parts_a[q]
    parts_b[leaf] = total

    def copy_b(k):
        dest = lax.rem(leaf + k, groups)
        return pltpu.make_async_remote_copy(
            parts_b.at[leaf], parts_b.at[leaf], send_b.at[k], recv_b.at[leaf], device_id=(dest, me), device_id_type=MESH
        )

    for k in range(1, groups):
        copy_b(k).start()
    for k in range(1, groups):
        src = lax.rem(leaf + groups - k, groups)
        pltpu.make_async_remote_copy(
            parts_b.at[src], parts_b.at[src], send_b.at[0], recv_b.at[src], device_id=(src, me), device_id_type=MESH
        ).wait_recv()
    for k in range(1, groups):
        copy_b(k).wait_send()
    summed = parts_b[0]
    for g in range(1, groups):
        summed = summed + parts_b[g]
    gathered[me] = summed

    def copy_c(k):
        dest = lax.rem(me + k, n)
        return pltpu.make_async_remote_copy(
            gathered.at[me], gathered.at[me], send_c.at[k], recv_c.at[me], device_id=(leaf, dest), device_id_type=MESH
        )

    for k in range(1, n):
        copy_c(k).start()
    for k in range(1, n):
        src = lax.rem(me + n - k, n)
        pltpu.make_async_remote_copy(
            gathered.at[src], gathered.at[src], send_c.at[0], recv_c.at[src], device_id=(leaf, src), device_id_type=MESH
        ).wait_recv()
    for k in range(1, n):
        copy_c(k).wait_send()
    for q in range(n):
        total_ref[:, q * span : (q + 1) * span] = gathered[q]


def top_reduce(term, n, groups):
    rows, width = term.shape
    span = width // n
    vmem = pl.BlockSpec(memory_space=pltpu.VMEM)
    return pl.pallas_call(
        functools.partial(top_reduce_kernel, n, groups, span),
        out_shape=jax.ShapeDtypeStruct((rows, width), jnp.float32),
        in_specs=[vmem],
        out_specs=vmem,
        scratch_shapes=[
            pltpu.VMEM((n, rows, span), jnp.float32),
            pltpu.VMEM((groups, rows, span), jnp.float32),
            pltpu.VMEM((n, rows, span), jnp.float32),
            pltpu.SemaphoreType.DMA((1,)),
            pltpu.SemaphoreType.DMA((n,)),
            pltpu.SemaphoreType.DMA((n,)),
            pltpu.SemaphoreType.DMA((groups,)),
            pltpu.SemaphoreType.DMA((groups,)),
            pltpu.SemaphoreType.DMA((n,)),
            pltpu.SemaphoreType.DMA((n,)),
        ],
        compiler_params=pltpu.CompilerParams(collective_id=2, has_side_effects=True),
    )(term)


def exchange_kernel(n, coef_ref, centre_ref, coef_out, centre_out, coef_buf, centre_buf, local_sem, send_sem, recv_sem):
    me = lax.axis_index("grp")
    leaf = lax.axis_index("leaf")
    _greet_group(n, leaf, me)
    pairs = ((coef_ref, coef_buf), (centre_ref, centre_buf))

    def push(kind, k):
        source, buf = pairs[kind]
        dest = lax.rem(me + k, n)
        return pltpu.make_async_remote_copy(
            source.at[dest], buf.at[me], send_sem.at[kind, k], recv_sem.at[kind, me], device_id=(leaf, dest), device_id_type=MESH
        )

    owns = [pltpu.make_async_copy(source.at[me], buf.at[me], local_sem.at[kind]) for kind, (source, buf) in enumerate(pairs)]
    for own in owns:
        own.start()
    for k in range(1, n):
        for kind in range(2):
            push(kind, k).start()
    for own in owns:
        own.wait()
    for k in range(1, n):
        src = lax.rem(me + n - k, n)
        for kind, (source, buf) in enumerate(pairs):
            pltpu.make_async_remote_copy(
                source.at[src], buf.at[src], send_sem.at[kind, 0], recv_sem.at[kind, src], device_id=(leaf, src), device_id_type=MESH
            ).wait_recv()
    for k in range(1, n):
        for kind in range(2):
            push(kind, k).wait_send()
    coef_out[...] = coef_buf[...]
    centre_out[...] = centre_buf[...]


def exchange(send_coef, send_centre, n):
    vmem = pl.BlockSpec(memory_space=pltpu.VMEM)
    return pl.pallas_call(
        functools.partial(exchange_kernel, n),
        out_shape=(
            jax.ShapeDtypeStruct(send_coef.shape, send_coef.dtype),
            jax.ShapeDtypeStruct(send_centre.shape, send_centre.dtype),
        ),
        in_specs=[vmem] * 2,
        out_specs=(vmem, vmem),
        scratch_shapes=[
            pltpu.VMEM(send_coef.shape, send_coef.dtype),
            pltpu.VMEM(send_centre.shape, send_centre.dtype),
            pltpu.SemaphoreType.DMA((2,)),
            pltpu.SemaphoreType.DMA((2, n)),
            pltpu.SemaphoreType.DMA((2, n)),
        ],
        compiler_params=pltpu.CompilerParams(collective_id=3, has_side_effects=True),
    )(send_coef, send_centre)


def slot_ranks(dest_rows, grp_size):
    onehot = (dest_rows[..., None] == jnp.arange(grp_size)).astype(jnp.int32)
    before = jnp.cumsum(onehot, axis=-2) - onehot
    return jnp.sum(before * onehot, axis=-1)


def evaluate(coef_all, centre_all, block_points, block_mask):
    dist = jnp.zeros((centre_all.shape[0], centre_all.shape[2], block_points.shape[1]), jnp.float32)
    for comp in range(3):
        delta = centre_all[:, comp, :, None] - block_points[None, comp, None, :]
        dist = dist + delta * delta
    weight = jnp.maximum(1.0 - dist / support_sq, 0.0) ** 3
    kernel = (weight * block_mask.astype(jnp.float32)[:, None, None]).astype(jnp.bfloat16)
    return jnp.einsum("krs,ksp->rp", coef_all, kernel, preferred_element_type=jnp.float32)


def on_device(
    rhs_leaf,
    rhs_sep,
    rhs_top,
    leaf_inverse,
    leaf_coupling,
    leaf_targets,
    sep_inverse,
    sep_blocks,
    top_coupling,
    top_inverse,
    top_lower,
    dest_map,
    centers,
    points,
    eval_pattern,
):
    grp_size = lax.axis_size("grp")
    my_index = lax.axis_index("grp")
    blocks_here = leaf_inverse.shape[0]
    snapshots = rhs_leaf.shape[0]
    span = leaf_inverse.shape[1]
    slot_count = CAP
    leaf_rhs = rhs_leaf.reshape(snapshots, blocks_here, span).transpose(1, 0, 2)
    leaf_sol = jnp.einsum("nrs,nts->nrt", leaf_rhs, leaf_inverse, precision=highest)
    leaf_half = leaf_sol.astype(jnp.bfloat16)
    partial_value = jnp.einsum(
        "nrs,ncbs->ncrb", leaf_half, leaf_coupling, preferred_element_type=jnp.float32
    )
    onehot = (leaf_targets[:, :, None] == jnp.arange(grp_size)[None, None, :]).astype(jnp.float32)
    picked = onehot
    parts = jnp.einsum("ncq,ncrb->qrb", picked, partial_value, precision=highest).astype(jnp.bfloat16)
    inverse_own = sep_inverse[0]
    own_blocks = sep_blocks[0]
    before = lax.dynamic_index_in_dim(own_blocks, jnp.maximum(my_index - 1, 0), 0, keepdims=False)
    fwd_hi, fwd_lo = split_pair(
        jnp.dot(before.astype(jnp.float32).T, inverse_own.T, precision=highest)
    )
    after = lax.dynamic_index_in_dim(own_blocks, jnp.minimum(my_index + 1, grp_size - 1), 0, keepdims=False)
    bwd_hi, bwd_lo = split_pair(jnp.dot(after.astype(jnp.float32), inverse_own, precision=highest))
    sep_sol = sep_solve("forward", (rhs_sep, parts), inverse_own, own_blocks, fwd_hi, fwd_lo, grp_size)
    sep_half = sep_sol.astype(jnp.bfloat16)
    top_term = jnp.dot(sep_half, top_coupling, preferred_element_type=jnp.float32)
    top_total = top_reduce(top_term, grp_size, lax.axis_size("leaf"))
    top_start = rhs_top - top_total
    coef_top, top_half = top_solve(top_start, top_inverse, top_lower)
    back_start = sep_sol - lax.dot_general(
        top_half, top_coupling, (((1,), (1,)), ((), ())), preferred_element_type=jnp.float32
    )

    coef_sep, known_table = sep_solve(
        "backward", back_start, inverse_own, own_blocks, bwd_hi, bwd_lo, grp_size
    )
    picked = jnp.einsum(
        "ncq,qrb->ncrb",
        onehot.astype(jnp.bfloat16),
        known_table,
        preferred_element_type=jnp.float32,
    ).astype(jnp.bfloat16)
    reduced = jnp.einsum(
        "ncrb,ncbs->nrs", picked, leaf_coupling, preferred_element_type=jnp.float32
    )
    leaf_coef = jnp.einsum("nrs,nst->nrt", leaf_sol - reduced, leaf_inverse, precision=highest)
    coef_leaf = leaf_coef.transpose(1, 0, 2).reshape(snapshots, blocks_here * span)
    leaf_out = leaf_coef.astype(jnp.bfloat16)
    slot_ids = jnp.arange(slot_count)
    grp_ids = jnp.arange(grp_size)
    own_dest = dest_map[:, 0]
    slot_rank = slot_ranks(own_dest[None, :], grp_size)[0]
    selector = (own_dest[None, None, :] == grp_ids[:, None, None]) & (
        slot_rank[None, None, :] == slot_ids[None, :, None]
    )
    send_coef = jnp.einsum(
        "dkj,jrt->dkrt", selector.astype(jnp.bfloat16), leaf_out, preferred_element_type=jnp.float32
    ).astype(jnp.bfloat16)
    send_centre = jnp.einsum(
        "dkj,jct->dkct", selector.astype(jnp.float32), centers, precision=highest
    )
    received, recv_centre = exchange(send_coef, send_centre, grp_size)
    slot_total = grp_size * slot_count
    coef_all = received.reshape(slot_total, snapshots, span)
    centre_all = recv_centre.reshape(slot_total, 3, span)
    point_blocks = eval_pattern.shape[0]
    scale = support_sq**-0.5
    centre_columns = jnp.swapaxes(centre_all * scale, 1, 2)
    point_rows = (points[0] * scale).reshape(3, point_blocks, span).transpose(1, 0, 2)
    filled = jnp.any(coef_all != 0, axis=(1, 2))
    flags = ((eval_pattern != 0) & filled[None, :]).astype(jnp.int32)
    values = evaluate_all(coef_all, centre_columns, point_rows, flags)
    return (coef_leaf, coef_sep, coef_top, values)


def solution(mesh):
    in_specs = (
        P(None, ("leaf", "grp")),
        P(None, ("leaf", "grp")),
        P(),
        P(("leaf", "grp"), None, None),
        P(("leaf", "grp"), None, None, None),
        P(("leaf", "grp"), None),
        P(("leaf", "grp"), None, None),
        P(("leaf", "grp"), None, None, None),
        P(("leaf", "grp"), None),
        P(),
        P(),
        P(("leaf", "grp"), None),
        P(("leaf", "grp"), None, None),
        P(("leaf", "grp"), None, None),
        P(("leaf", "grp"), None),
    )
    out_specs = (P(None, ("leaf", "grp")), P(None, ("leaf", "grp")), P(), P(None, ("leaf", "grp")))
    return jax.shard_map(
        on_device, mesh=mesh, in_specs=in_specs, out_specs=out_specs, check_vma=False
    )
```

```python
import functools

import jax
import jax.numpy as jnp
from jax import lax
from jax.sharding import PartitionSpec as P
from jax.experimental import pallas as pl
from jax.experimental.pallas import tpu as pltpu

MESH = pl.DeviceIdType.MESH

CAP = 2


highest = lax.Precision.HIGHEST
support_sq = 0.25


def split_up(shard, dim, peers):
    dims = shard.shape
    pieces = shard.reshape(*dims[:dim], peers, dims[dim] // peers, *dims[dim + 1 :])
    return jnp.moveaxis(pieces, dim, 0)


def sum_at_owner(shard, axis, dim):
    pieces = split_up(shard, dim, lax.axis_size(axis))
    arrived = lax.all_to_all(pieces, axis, split_axis=0, concat_axis=0, tiled=True)
    return arrived.astype(jnp.float32).sum(axis=0)


def from_root(shard, axis, root):
    return lax.dynamic_index_in_dim(lax.all_gather(shard, axis), root, 0, keepdims=False)


def copy_for_each(shard, axis):
    copies = jnp.broadcast_to(shard, (lax.axis_size(axis), *shard.shape))
    return lax.all_to_all(copies, axis, split_axis=0, concat_axis=0, tiled=True)


def over_copies(shard, axis):
    return copy_for_each(shard, axis).astype(jnp.float32).sum(axis=0)


def joined_along(pieces, dim):
    dims = list(pieces.shape[1:])
    dims[dim] *= pieces.shape[0]
    return jnp.moveaxis(pieces, 0, dim).reshape(dims)


def gather_directly(shard, axis, dim):
    pieces = copy_for_each(shard, axis)
    return joined_along(pieces, dim)


def _nt(a, b):
    return lax.dot_general(a, b, (((1,), (1,)), ((), ())), preferred_element_type=jnp.float32)


def _nn(a, b):
    return lax.dot_general(a, b, (((1,), (0,)), ((), ())), preferred_element_type=jnp.float32)


def _nt_exact(a, b):
    return lax.dot_general(
        a, b, (((1,), (1,)), ((), ())), precision=highest, preferred_element_type=jnp.float32
    )


def _nn_exact(a, b):
    return lax.dot_general(
        a, b, (((1,), (0,)), ((), ())), precision=highest, preferred_element_type=jnp.float32
    )


def _greet_group(n, leaf, me):
    barrier = pltpu.get_barrier_semaphore()
    for r in range(n):
        @pl.when(me != r)
        def _():
            pl.semaphore_signal(barrier, inc=1, device_id=(leaf, r), device_id_type=MESH)
    pl.semaphore_wait(barrier, n - 1)


def _block_copy(halves, q, dest, send_sem, recv_sem, leaf):
    return pltpu.make_async_remote_copy(
        src_ref=halves.at[q],
        dst_ref=halves.at[q],
        send_sem=send_sem,
        recv_sem=recv_sem.at[q],
        device_id=(leaf, dest),
        device_id_type=MESH,
    )


def _send_block(n, halves, s, solved, sol_ref, send_sem, recv_sem, leaf, dests):
    sol_ref[...] = solved
    halves[s] = solved.astype(jnp.bfloat16)
    for k in range(1, n):
        dest, live = dests(s, k)
        @pl.when(live)
        def _():
            _block_copy(halves, s, dest, send_sem.at[k], recv_sem, leaf).start()
            if k == 1:
                _block_copy(halves, s, dest, send_sem.at[k], recv_sem, leaf).wait_send()
    for k in range(2, n):
        dest, live = dests(s, k)
        @pl.when(live)
        def _():
            _block_copy(halves, s, dest, send_sem.at[k], recv_sem, leaf).wait_send()


def _through(y, hi_ref, lo_ref):
    return _nn(y, hi_ref[...]) + _nn(y, lo_ref[...])


def sep_forward_kernel(n, rhs_ref, part_ref, inv_ref, blocks_ref, hi_ref, lo_ref, sol_ref, halves, resid, base, send_sem, recv_sem, arrived, local_sem, give_sem, take_sem):
    me = lax.axis_index("grp")
    leaf = lax.axis_index("leaf")
    _greet_group(n, leaf, me)

    def give(dest):
        return pltpu.make_async_remote_copy(
            part_ref.at[dest], arrived.at[me], give_sem.at[dest], take_sem.at[me], device_id=(leaf, dest), device_id_type=MESH
        )

    own = pltpu.make_async_copy(part_ref.at[me], arrived.at[me], local_sem.at[0])
    own.start()
    for dest in range(n):
        @pl.when(me != dest)
        def _():
            give(dest).start()
    own.wait()
    for src in range(n):
        @pl.when(me != src)
        def _():
            pltpu.make_async_remote_copy(
                part_ref.at[src], arrived.at[src], give_sem.at[src], take_sem.at[src], device_id=(leaf, src), device_id_type=MESH
            ).wait_recv()
    total = arrived[0].astype(jnp.float32)
    for src in range(1, n):
        total = total + arrived[src].astype(jnp.float32)
    resid[...] = rhs_ref[...] - total
    for dest in range(n):
        @pl.when(me != dest)
        def _():
            give(dest).wait_send()

    dests = lambda s, k: (s + k, s + k < n)

    @pl.when(me == 0)
    def _():
        _send_block(n, halves, 0, _nt_exact(resid[...], inv_ref[...]), sol_ref, send_sem, recv_sem, leaf, dests)

    @pl.when(me == 1)
    def _():
        base[...] = _nt_exact(resid[...], inv_ref[...])

    def step(q, carry):
        @pl.when(me == q + 1)
        def _():
            _block_copy(halves, q, q, send_sem.at[0], recv_sem, leaf).wait_recv()
            solved = base[...] - _through(halves[q], hi_ref, lo_ref)
            _send_block(n, halves, q + 1, solved, sol_ref, send_sem, recv_sem, leaf, dests)

        @pl.when(me > q + 1)
        def _():
            _block_copy(halves, q, q, send_sem.at[0], recv_sem, leaf).wait_recv()
            resid[...] = resid[...] - _nt(halves[q], blocks_ref[q])

            @pl.when(me == q + 2)
            def _():
                base[...] = _nt_exact(resid[...], inv_ref[...])

        return carry

    lax.fori_loop(0, n - 1, step, 0)


def sep_backward_kernel(n, start_ref, inv_ref, blocks_ref, hi_ref, lo_ref, sol_ref, table_ref, halves, resid, base, send_sem, recv_sem):
    me = lax.axis_index("grp")
    leaf = lax.axis_index("leaf")
    _greet_group(n, leaf, me)
    resid[...] = start_ref[...]
    dests = lambda s, k: (s - k, s - k >= 0)

    @pl.when(me == n - 1)
    def _():
        _send_block(n, halves, n - 1, _nn_exact(resid[...], inv_ref[...]), sol_ref, send_sem, recv_sem, leaf, dests)

    @pl.when(me == n - 2)
    def _():
        base[...] = _nn_exact(resid[...], inv_ref[...])

    def step(s, carry):
        q = n - 1 - s

        @pl.when(me < q)
        def _():
            _block_copy(halves, q, q, send_sem.at[0], recv_sem, leaf).wait_recv()

        @pl.when(me == q - 1)
        def _():
            solved = base[...] - _through(halves[q], hi_ref, lo_ref)
            _send_block(n, halves, q - 1, solved, sol_ref, send_sem, recv_sem, leaf, dests)

        @pl.when(me < q - 1)
        def _():
            resid[...] = resid[...] - _nn(halves[q], blocks_ref[q])

            @pl.when(me == q - 2)
            def _():
                base[...] = _nn_exact(resid[...], inv_ref[...])

        return carry

    lax.fori_loop(0, n - 1, step, 0)
    for k in range(1, n):
        @pl.when(me + k < n)
        def _():
            _block_copy(halves, me, me + k, send_sem.at[k], recv_sem, leaf).start()
    for q in range(n):
        @pl.when(q < me)
        def _():
            _block_copy(halves, q, q, send_sem.at[0], recv_sem, leaf).wait_recv()
    for k in range(1, n):
        @pl.when(me + k < n)
        def _():
            _block_copy(halves, me, me + k, send_sem.at[k], recv_sem, leaf).wait_send()
    table_ref[...] = halves[...]


def sep_solve(kind, start, inv, blocks, hi, lo, n):
    rows, width = (start[0] if kind == "forward" else start).shape
    vmem = pl.BlockSpec(memory_space=pltpu.VMEM)
    scratch = [
        pltpu.VMEM((n, rows, width), jnp.bfloat16),
        pltpu.VMEM((rows, width), jnp.float32),
        pltpu.VMEM((rows, width), jnp.float32),
        pltpu.SemaphoreType.DMA((n,)),
        pltpu.SemaphoreType.DMA((n,)),
    ]
    sol_shape = jax.ShapeDtypeStruct((rows, width), jnp.float32)
    params = dict(has_side_effects=True, vmem_limit_bytes=48 * 1024 * 1024)
    if kind == "forward":
        rhs, parts = start
        return pl.pallas_call(
            functools.partial(sep_forward_kernel, n),
            out_shape=sol_shape,
            in_specs=[vmem] * 6,
            out_specs=vmem,
            scratch_shapes=scratch
            + [
                pltpu.VMEM(parts.shape, parts.dtype),
                pltpu.SemaphoreType.DMA((1,)),
                pltpu.SemaphoreType.DMA((n,)),
                pltpu.SemaphoreType.DMA((n,)),
            ],
            compiler_params=pltpu.CompilerParams(collective_id=0, **params),
        )(rhs, parts, inv, blocks, hi, lo)
    return pl.pallas_call(
        functools.partial(sep_backward_kernel, n),
        out_shape=(sol_shape, jax.ShapeDtypeStruct((n, rows, width), jnp.bfloat16)),
        in_specs=[vmem] * 5,
        out_specs=(vmem, vmem),
        scratch_shapes=scratch,
        compiler_params=pltpu.CompilerParams(collective_id=1, **params),
    )(start, inv, blocks, hi, lo)


def split_pair(matrix):
    hi = matrix.astype(jnp.bfloat16)
    lo = (matrix - hi.astype(jnp.float32)).astype(jnp.bfloat16)
    return hi, lo


def top_solve_kernel(nt, span, start_ref, inv_ref, lower_ref, coef_ref, half_ref, fwd_half, fwd_full):
    for t in range(nt):
        cols = slice(t * span, (t + 1) * span)
        residue = start_ref[:, cols]
        if t > 0:
            residue = residue - _nt(fwd_half[:, : t * span], lower_ref[cols, : t * span])
        solved = _nt_exact(residue, inv_ref[t])
        fwd_full[:, cols] = solved
        fwd_half[:, cols] = solved.astype(jnp.bfloat16)
    for t in reversed(range(nt)):
        cols = slice(t * span, (t + 1) * span)
        residue = fwd_full[:, cols]
        if t < nt - 1:
            residue = residue - _nn(half_ref[:, (t + 1) * span :], lower_ref[(t + 1) * span :, cols])
        solved = _nn_exact(residue, inv_ref[t])
        coef_ref[:, cols] = solved
        half_ref[:, cols] = solved.astype(jnp.bfloat16)


def top_solve(top_start, top_inverse, top_lower):
    nt, span = top_inverse.shape[0], top_inverse.shape[1]
    rows, width = top_start.shape
    vmem = pl.BlockSpec(memory_space=pltpu.VMEM)
    return pl.pallas_call(
        functools.partial(top_solve_kernel, nt, span),
        out_shape=(
            jax.ShapeDtypeStruct((rows, width), jnp.float32),
            jax.ShapeDtypeStruct((rows, width), jnp.bfloat16),
        ),
        in_specs=[vmem] * 3,
        out_specs=(vmem, vmem),
        scratch_shapes=[
            pltpu.VMEM((rows, width), jnp.bfloat16),
            pltpu.VMEM((rows, width), jnp.float32),
        ],
        compiler_params=pltpu.CompilerParams(vmem_limit_bytes=48 * 1024 * 1024),
    )(top_start, top_inverse, top_lower)


def evaluate_kernel(slots, pattern_ref, coef_ref, centre_ref, point_ref, out_ref, acc, spread):
    m = pl.program_id(0)
    width = point_ref.shape[2]

    @pl.when(m == 0)
    def _():
        for s in range(slots):
            column = centre_ref[s]
            for comp in range(3):
                spread[s, comp] = jnp.broadcast_to(column[:, comp : comp + 1], (column.shape[0], width))

    acc[...] = jnp.zeros_like(acc)
    row = point_ref[0]

    def one_slot(s, carry):
        @pl.when(pattern_ref[m, s] != 0)
        def _():
            dist = None
            for comp in range(3):
                delta = spread[s, comp] - row[comp : comp + 1, :]
                dist = delta * delta if dist is None else dist + delta * delta
            weight = jnp.maximum(1.0 - dist, 0.0)
            kernel = (weight * weight * weight).astype(jnp.bfloat16)
            acc[...] += _nn(coef_ref[s], kernel)

        return carry

    lax.fori_loop(0, slots, one_slot, 0)
    out_ref[...] = acc[...]


def evaluate_all(coef_all, centre_columns, point_rows, pattern):
    slots, rows, span = coef_all.shape
    blocks = point_rows.shape[0]
    full = lambda shape: pl.BlockSpec(shape, lambda m, pat: (0,) * len(shape))
    grid_spec = pltpu.PrefetchScalarGridSpec(
        num_scalar_prefetch=1,
        grid=(blocks,),
        in_specs=[
            full(coef_all.shape),
            full(centre_columns.shape),
            pl.BlockSpec((1,) + point_rows.shape[1:], lambda m, pat: (m, 0, 0)),
        ],
        out_specs=pl.BlockSpec((rows, span), lambda m, pat: (0, m)),
        scratch_shapes=[
            pltpu.VMEM((rows, span), jnp.float32),
            pltpu.VMEM((slots, 3, centre_columns.shape[1], point_rows.shape[2]), jnp.float32),
        ],
    )
    return pl.pallas_call(
        functools.partial(evaluate_kernel, slots),
        out_shape=jax.ShapeDtypeStruct((rows, blocks * span), jnp.float32),
        grid_spec=grid_spec,
        compiler_params=pltpu.CompilerParams(vmem_limit_bytes=48 * 1024 * 1024),
    )(pattern, coef_all, centre_columns, point_rows)


def top_reduce_kernel(n, groups, span, term_ref, total_ref, parts_a, parts_b, gathered, local_sem, send_a, recv_a, send_b, recv_b, send_c, recv_c):
    me = lax.axis_index("grp")
    leaf = lax.axis_index("leaf")
    barrier = pltpu.get_barrier_semaphore()
    for r in range(n):
        @pl.when(me != r)
        def _():
            pl.semaphore_signal(barrier, inc=1, device_id=(leaf, r), device_id_type=MESH)
    for g in range(groups):
        @pl.when(leaf != g)
        def _():
            pl.semaphore_signal(barrier, inc=1, device_id=(g, me), device_id_type=MESH)
    pl.semaphore_wait(barrier, n - 1 + groups - 1)

    def column(q):
        return term_ref.at[:, pl.ds(pl.multiple_of(q * span, span), span)]

    def copy_a(k):
        dest = lax.rem(me + k, n)
        return pltpu.make_async_remote_copy(
            column(dest), parts_a.at[me], send_a.at[k], recv_a.at[me], device_id=(leaf, dest), device_id_type=MESH
        )

    def wait_a(k):
        src = lax.rem(me + n - k, n)
        pltpu.make_async_remote_copy(
            column(src), parts_a.at[src], send_a.at[0], recv_a.at[src], device_id=(leaf, src), device_id_type=MESH
        ).wait_recv()

    own = pltpu.make_async_copy(column(me), parts_a.at[me], local_sem.at[0])
    own.start()
    for k in range(1, n):
        copy_a(k).start()
    own.wait()
    for k in range(1, n):
        wait_a(k)
    for k in range(1, n):
        copy_a(k).wait_send()
    total = parts_a[0]
    for q in range(1, n):
        total = total + parts_a[q]
    parts_b[leaf] = total

    def copy_b(k):
        dest = lax.rem(leaf + k, groups)
        return pltpu.make_async_remote_copy(
            parts_b.at[leaf], parts_b.at[leaf], send_b.at[k], recv_b.at[leaf], device_id=(dest, me), device_id_type=MESH
        )

    for k in range(1, groups):
        copy_b(k).start()
    for k in range(1, groups):
        src = lax.rem(leaf + groups - k, groups)
        pltpu.make_async_remote_copy(
            parts_b.at[src], parts_b.at[src], send_b.at[0], recv_b.at[src], device_id=(src, me), device_id_type=MESH
        ).wait_recv()
    for k in range(1, groups):
        copy_b(k).wait_send()
    summed = parts_b[0]
    for g in range(1, groups):
        summed = summed + parts_b[g]
    gathered[me] = summed

    def copy_c(k):
        dest = lax.rem(me + k, n)
        return pltpu.make_async_remote_copy(
            gathered.at[me], gathered.at[me], send_c.at[k], recv_c.at[me], device_id=(leaf, dest), device_id_type=MESH
        )

    for k in range(1, n):
        copy_c(k).start()
    for k in range(1, n):
        src = lax.rem(me + n - k, n)
        pltpu.make_async_remote_copy(
            gathered.at[src], gathered.at[src], send_c.at[0], recv_c.at[src], device_id=(leaf, src), device_id_type=MESH
        ).wait_recv()
    for k in range(1, n):
        copy_c(k).wait_send()
    for q in range(n):
        total_ref[:, q * span : (q + 1) * span] = gathered[q]


def top_reduce(term, n, groups):
    rows, width = term.shape
    span = width // n
    vmem = pl.BlockSpec(memory_space=pltpu.VMEM)
    return pl.pallas_call(
        functools.partial(top_reduce_kernel, n, groups, span),
        out_shape=jax.ShapeDtypeStruct((rows, width), jnp.float32),
        in_specs=[vmem],
        out_specs=vmem,
        scratch_shapes=[
            pltpu.VMEM((n, rows, span), jnp.float32),
            pltpu.VMEM((groups, rows, span), jnp.float32),
            pltpu.VMEM((n, rows, span), jnp.float32),
            pltpu.SemaphoreType.DMA((1,)),
            pltpu.SemaphoreType.DMA((n,)),
            pltpu.SemaphoreType.DMA((n,)),
            pltpu.SemaphoreType.DMA((groups,)),
            pltpu.SemaphoreType.DMA((groups,)),
            pltpu.SemaphoreType.DMA((n,)),
            pltpu.SemaphoreType.DMA((n,)),
        ],
        compiler_params=pltpu.CompilerParams(collective_id=2, has_side_effects=True),
    )(term)


def exchange_kernel(n, coef_ref, centre_ref, coef_out, centre_out, coef_buf, centre_buf, local_sem, send_sem, recv_sem):
    me = lax.axis_index("grp")
    leaf = lax.axis_index("leaf")
    _greet_group(n, leaf, me)
    pairs = ((coef_ref, coef_buf), (centre_ref, centre_buf))

    def push(kind, k):
        source, buf = pairs[kind]
        dest = lax.rem(me + k, n)
        return pltpu.make_async_remote_copy(
            source.at[dest], buf.at[me], send_sem.at[kind, k], recv_sem.at[kind, me], device_id=(leaf, dest), device_id_type=MESH
        )

    owns = [pltpu.make_async_copy(source.at[me], buf.at[me], local_sem.at[kind]) for kind, (source, buf) in enumerate(pairs)]
    for own in owns:
        own.start()
    for k in range(1, n):
        for kind in range(2):
            push(kind, k).start()
    for own in owns:
        own.wait()
    for k in range(1, n):
        src = lax.rem(me + n - k, n)
        for kind, (source, buf) in enumerate(pairs):
            pltpu.make_async_remote_copy(
                source.at[src], buf.at[src], send_sem.at[kind, 0], recv_sem.at[kind, src], device_id=(leaf, src), device_id_type=MESH
            ).wait_recv()
    for k in range(1, n):
        for kind in range(2):
            push(kind, k).wait_send()
    coef_out[...] = coef_buf[...]
    centre_out[...] = centre_buf[...]


def exchange(send_coef, send_centre, n):
    vmem = pl.BlockSpec(memory_space=pltpu.VMEM)
    return pl.pallas_call(
        functools.partial(exchange_kernel, n),
        out_shape=(
            jax.ShapeDtypeStruct(send_coef.shape, send_coef.dtype),
            jax.ShapeDtypeStruct(send_centre.shape, send_centre.dtype),
        ),
        in_specs=[vmem] * 2,
        out_specs=(vmem, vmem),
        scratch_shapes=[
            pltpu.VMEM(send_coef.shape, send_coef.dtype),
            pltpu.VMEM(send_centre.shape, send_centre.dtype),
            pltpu.SemaphoreType.DMA((2,)),
            pltpu.SemaphoreType.DMA((2, n)),
            pltpu.SemaphoreType.DMA((2, n)),
        ],
        compiler_params=pltpu.CompilerParams(collective_id=3, has_side_effects=True),
    )(send_coef, send_centre)


def slot_ranks(dest_rows, grp_size):
    onehot = (dest_rows[..., None] == jnp.arange(grp_size)).astype(jnp.int32)
    before = jnp.cumsum(onehot, axis=-2) - onehot
    return jnp.sum(before * onehot, axis=-1)


def evaluate(coef_all, centre_all, block_points, block_mask):
    dist = jnp.zeros((centre_all.shape[0], centre_all.shape[2], block_points.shape[1]), jnp.float32)
    for comp in range(3):
        delta = centre_all[:, comp, :, None] - block_points[None, comp, None, :]
        dist = dist + delta * delta
    weight = jnp.maximum(1.0 - dist / support_sq, 0.0) ** 3
    kernel = (weight * block_mask.astype(jnp.float32)[:, None, None]).astype(jnp.bfloat16)
    return jnp.einsum("krs,ksp->rp", coef_all, kernel, preferred_element_type=jnp.float32)


def on_device(
    rhs_leaf,
    rhs_sep,
    rhs_top,
    leaf_inverse,
    leaf_coupling,
    leaf_targets,
    sep_inverse,
    sep_blocks,
    top_coupling,
    top_inverse,
    top_lower,
    dest_map,
    centers,
    points,
    eval_pattern,
):
    grp_size = lax.axis_size("grp")
    my_index = lax.axis_index("grp")
    blocks_here = leaf_inverse.shape[0]
    snapshots = rhs_leaf.shape[0]
    span = leaf_inverse.shape[1]
    slot_count = CAP
    leaf_rhs = rhs_leaf.reshape(snapshots, blocks_here, span).transpose(1, 0, 2)
    leaf_sol = jnp.einsum("nrs,nts->nrt", leaf_rhs, leaf_inverse, precision=highest)
    leaf_half = leaf_sol.astype(jnp.bfloat16)
    partial_value = jnp.einsum(
        "nrs,ncbs->ncrb", leaf_half, leaf_coupling, preferred_element_type=jnp.float32
    )
    onehot = (leaf_targets[:, :, None] == jnp.arange(grp_size)[None, None, :]).astype(jnp.float32)
    picked = onehot
    parts = jnp.einsum("ncq,ncrb->qrb", picked, partial_value, precision=highest).astype(jnp.bfloat16)
    inverse_own = sep_inverse[0]
    own_blocks = sep_blocks[0]
    before = lax.dynamic_index_in_dim(own_blocks, jnp.maximum(my_index - 1, 0), 0, keepdims=False)
    fwd_hi, fwd_lo = split_pair(
        jnp.dot(before.astype(jnp.float32).T, inverse_own.T, precision=highest)
    )
    after = lax.dynamic_index_in_dim(own_blocks, jnp.minimum(my_index + 1, grp_size - 1), 0, keepdims=False)
    bwd_hi, bwd_lo = split_pair(jnp.dot(after.astype(jnp.float32), inverse_own, precision=highest))
    sep_sol = sep_solve("forward", (rhs_sep, parts), inverse_own, own_blocks, fwd_hi, fwd_lo, grp_size)
    sep_half = sep_sol.astype(jnp.bfloat16)
    top_term = jnp.dot(sep_half, top_coupling, preferred_element_type=jnp.float32)
    top_total = top_reduce(top_term, grp_size, lax.axis_size("leaf"))
    top_start = rhs_top - top_total
    coef_top, top_half = top_solve(top_start, top_inverse, top_lower)
    back_start = sep_sol - lax.dot_general(
        top_half, top_coupling, (((1,), (1,)), ((), ())), preferred_element_type=jnp.float32
    )

    coef_sep, known_table = sep_solve(
        "backward", back_start, inverse_own, own_blocks, bwd_hi, bwd_lo, grp_size
    )
    picked = jnp.einsum(
        "ncq,qrb->ncrb",
        onehot.astype(jnp.bfloat16),
        known_table,
        preferred_element_type=jnp.float32,
    ).astype(jnp.bfloat16)
    reduced = jnp.einsum(
        "ncrb,ncbs->nrs", picked, leaf_coupling, preferred_element_type=jnp.float32
    )
    leaf_coef = jnp.einsum("nrs,nst->nrt", leaf_sol - reduced, leaf_inverse, precision=highest)
    coef_leaf = leaf_coef.transpose(1, 0, 2).reshape(snapshots, blocks_here * span)
    leaf_out = leaf_coef.astype(jnp.bfloat16)
    slot_ids = jnp.arange(slot_count)
    grp_ids = jnp.arange(grp_size)
    own_dest = dest_map[:, 0]
    slot_rank = slot_ranks(own_dest[None, :], grp_size)[0]
    selector = (own_dest[None, None, :] == grp_ids[:, None, None]) & (
        slot_rank[None, None, :] == slot_ids[None, :, None]
    )
    send_coef = jnp.einsum(
        "dkj,jrt->dkrt", selector.astype(jnp.bfloat16), leaf_out, preferred_element_type=jnp.float32
    ).astype(jnp.bfloat16)
    send_centre = jnp.einsum(
        "dkj,jct->dkct", selector.astype(jnp.float32), centers, precision=highest
    )
    received, recv_centre = exchange(send_coef, send_centre, grp_size)
    slot_total = grp_size * slot_count
    coef_all = received.reshape(slot_total, snapshots, span)
    centre_all = recv_centre.reshape(slot_total, 3, span)
    point_blocks = eval_pattern.shape[0]
    scale = support_sq**-0.5
    centre_columns = jnp.swapaxes(centre_all * scale, 1, 2)
    point_rows = (points[0] * scale).reshape(3, point_blocks, span).transpose(1, 0, 2)
    values = evaluate_all(coef_all, centre_columns, point_rows, eval_pattern)
    return (coef_leaf, coef_sep, coef_top, values)


def solution(mesh):
    in_specs = (
        P(None, ("leaf", "grp")),
        P(None, ("leaf", "grp")),
        P(),
        P(("leaf", "grp"), None, None),
        P(("leaf", "grp"), None, None, None),
        P(("leaf", "grp"), None),
        P(("leaf", "grp"), None, None),
        P(("leaf", "grp"), None, None, None),
        P(("leaf", "grp"), None),
        P(),
        P(),
        P(("leaf", "grp"), None),
        P(("leaf", "grp"), None, None),
        P(("leaf", "grp"), None, None),
        P(("leaf", "grp"), None),
    )
    out_specs = (P(None, ("leaf", "grp")), P(None, ("leaf", "grp")), P(), P(None, ("leaf", "grp")))
    return jax.shard_map(
        on_device, mesh=mesh, in_specs=in_specs, out_specs=out_specs, check_vma=False
    )
```

```python
import functools

import jax
import jax.numpy as jnp
from jax import lax
from jax.sharding import PartitionSpec as P
from jax.experimental import pallas as pl
from jax.experimental.pallas import tpu as pltpu

MESH = pl.DeviceIdType.MESH

CAP = 2


highest = lax.Precision.HIGHEST
support_sq = 0.25


def split_up(shard, dim, peers):
    dims = shard.shape
    pieces = shard.reshape(*dims[:dim], peers, dims[dim] // peers, *dims[dim + 1 :])
    return jnp.moveaxis(pieces, dim, 0)


def sum_at_owner(shard, axis, dim):
    pieces = split_up(shard, dim, lax.axis_size(axis))
    arrived = lax.all_to_all(pieces, axis, split_axis=0, concat_axis=0, tiled=True)
    return arrived.astype(jnp.float32).sum(axis=0)


def from_root(shard, axis, root):
    return lax.dynamic_index_in_dim(lax.all_gather(shard, axis), root, 0, keepdims=False)


def copy_for_each(shard, axis):
    copies = jnp.broadcast_to(shard, (lax.axis_size(axis), *shard.shape))
    return lax.all_to_all(copies, axis, split_axis=0, concat_axis=0, tiled=True)


def over_copies(shard, axis):
    return copy_for_each(shard, axis).astype(jnp.float32).sum(axis=0)


def joined_along(pieces, dim):
    dims = list(pieces.shape[1:])
    dims[dim] *= pieces.shape[0]
    return jnp.moveaxis(pieces, 0, dim).reshape(dims)


def gather_directly(shard, axis, dim):
    pieces = copy_for_each(shard, axis)
    return joined_along(pieces, dim)


def _nt(a, b):
    return lax.dot_general(a, b, (((1,), (1,)), ((), ())), preferred_element_type=jnp.float32)


def _nn(a, b):
    return lax.dot_general(a, b, (((1,), (0,)), ((), ())), preferred_element_type=jnp.float32)


def _nt_exact(a, b):
    return lax.dot_general(
        a, b, (((1,), (1,)), ((), ())), precision=highest, preferred_element_type=jnp.float32
    )


def _nn_exact(a, b):
    return lax.dot_general(
        a, b, (((1,), (0,)), ((), ())), precision=highest, preferred_element_type=jnp.float32
    )


def _greet_group(n, leaf, me):
    barrier = pltpu.get_barrier_semaphore()
    for r in range(n):
        @pl.when(me != r)
        def _():
            pl.semaphore_signal(barrier, inc=1, device_id=(leaf, r), device_id_type=MESH)
    pl.semaphore_wait(barrier, n - 1)


def _block_copy(halves, q, dest, send_sem, recv_sem, leaf):
    return pltpu.make_async_remote_copy(
        src_ref=halves.at[q],
        dst_ref=halves.at[q],
        send_sem=send_sem,
        recv_sem=recv_sem.at[q],
        device_id=(leaf, dest),
        device_id_type=MESH,
    )


def _send_block(n, halves, s, solved, sol_ref, send_sem, recv_sem, leaf, dests):
    sol_ref[...] = solved
    halves[s] = solved.astype(jnp.bfloat16)
    for k in range(1, n):
        dest, live = dests(s, k)
        @pl.when(live)
        def _():
            _block_copy(halves, s, dest, send_sem.at[k], recv_sem, leaf).start()
            if k == 1:
                _block_copy(halves, s, dest, send_sem.at[k], recv_sem, leaf).wait_send()
    for k in range(2, n):
        dest, live = dests(s, k)
        @pl.when(live)
        def _():
            _block_copy(halves, s, dest, send_sem.at[k], recv_sem, leaf).wait_send()


def _through(y, hi_ref, lo_ref):
    return _nn(y, hi_ref[...]) + _nn(y, lo_ref[...])


def sep_forward_kernel(n, rhs_ref, part_ref, inv_ref, blocks_ref, hi_ref, lo_ref, sol_ref, halves, resid, base, send_sem, recv_sem, arrived, local_sem, give_sem, take_sem):
    me = lax.axis_index("grp")
    leaf = lax.axis_index("leaf")
    _greet_group(n, leaf, me)

    def give(dest):
        return pltpu.make_async_remote_copy(
            part_ref.at[dest], arrived.at[me], give_sem.at[dest], take_sem.at[me], device_id=(leaf, dest), device_id_type=MESH
        )

    own = pltpu.make_async_copy(part_ref.at[me], arrived.at[me], local_sem.at[0])
    own.start()
    for dest in range(n):
        @pl.when(me != dest)
        def _():
            give(dest).start()
    own.wait()
    for src in range(n):
        @pl.when(me != src)
        def _():
            pltpu.make_async_remote_copy(
                part_ref.at[src], arrived.at[src], give_sem.at[src], take_sem.at[src], device_id=(leaf, src), device_id_type=MESH
            ).wait_recv()
    total = arrived[0].astype(jnp.float32)
    for src in range(1, n):
        total = total + arrived[src].astype(jnp.float32)
    resid[...] = rhs_ref[...] - total
    for dest in range(n):
        @pl.when(me != dest)
        def _():
            give(dest).wait_send()

    dests = lambda s, k: (s + k, s + k < n)

    @pl.when(me == 0)
    def _():
        _send_block(n, halves, 0, _nt_exact(resid[...], inv_ref[...]), sol_ref, send_sem, recv_sem, leaf, dests)

    @pl.when(me == 1)
    def _():
        base[...] = _nt_exact(resid[...], inv_ref[...])

    def step(q, carry):
        @pl.when(me == q + 1)
        def _():
            _block_copy(halves, q, q, send_sem.at[0], recv_sem, leaf).wait_recv()
            solved = base[...] - _through(halves[q], hi_ref, lo_ref)
            _send_block(n, halves, q + 1, solved, sol_ref, send_sem, recv_sem, leaf, dests)

        @pl.when(me > q + 1)
        def _():
            _block_copy(halves, q, q, send_sem.at[0], recv_sem, leaf).wait_recv()
            resid[...] = resid[...] - _nt(halves[q], blocks_ref[q])

            @pl.when(me == q + 2)
            def _():
                base[...] = _nt_exact(resid[...], inv_ref[...])

        return carry

    lax.fori_loop(0, n - 1, step, 0)


def sep_backward_kernel(n, start_ref, inv_ref, blocks_ref, hi_ref, lo_ref, sol_ref, table_ref, halves, resid, base, send_sem, recv_sem):
    me = lax.axis_index("grp")
    leaf = lax.axis_index("leaf")
    _greet_group(n, leaf, me)
    resid[...] = start_ref[...]
    dests = lambda s, k: (s - k, s - k >= 0)

    @pl.when(me == n - 1)
    def _():
        _send_block(n, halves, n - 1, _nn_exact(resid[...], inv_ref[...]), sol_ref, send_sem, recv_sem, leaf, dests)

    @pl.when(me == n - 2)
    def _():
        base[...] = _nn_exact(resid[...], inv_ref[...])

    def step(s, carry):
        q = n - 1 - s

        @pl.when(me < q)
        def _():
            _block_copy(halves, q, q, send_sem.at[0], recv_sem, leaf).wait_recv()

        @pl.when(me == q - 1)
        def _():
            solved = base[...] - _through(halves[q], hi_ref, lo_ref)
            _send_block(n, halves, q - 1, solved, sol_ref, send_sem, recv_sem, leaf, dests)

        @pl.when(me < q - 1)
        def _():
            resid[...] = resid[...] - _nn(halves[q], blocks_ref[q])

            @pl.when(me == q - 2)
            def _():
                base[...] = _nn_exact(resid[...], inv_ref[...])

        return carry

    lax.fori_loop(0, n - 1, step, 0)
    for k in range(1, n):
        @pl.when(me + k < n)
        def _():
            _block_copy(halves, me, me + k, send_sem.at[k], recv_sem, leaf).start()
    for q in range(n):
        @pl.when(q < me)
        def _():
            _block_copy(halves, q, q, send_sem.at[0], recv_sem, leaf).wait_recv()
    for k in range(1, n):
        @pl.when(me + k < n)
        def _():
            _block_copy(halves, me, me + k, send_sem.at[k], recv_sem, leaf).wait_send()
    table_ref[...] = halves[...]


def sep_solve(kind, start, inv, blocks, hi, lo, n):
    rows, width = (start[0] if kind == "forward" else start).shape
    vmem = pl.BlockSpec(memory_space=pltpu.VMEM)
    scratch = [
        pltpu.VMEM((n, rows, width), jnp.bfloat16),
        pltpu.VMEM((rows, width), jnp.float32),
        pltpu.VMEM((rows, width), jnp.float32),
        pltpu.SemaphoreType.DMA((n,)),
        pltpu.SemaphoreType.DMA((n,)),
    ]
    sol_shape = jax.ShapeDtypeStruct((rows, width), jnp.float32)
    params = dict(has_side_effects=True, vmem_limit_bytes=48 * 1024 * 1024)
    if kind == "forward":
        rhs, parts = start
        return pl.pallas_call(
            functools.partial(sep_forward_kernel, n),
            out_shape=sol_shape,
            in_specs=[vmem] * 6,
            out_specs=vmem,
            scratch_shapes=scratch
            + [
                pltpu.VMEM(parts.shape, parts.dtype),
                pltpu.SemaphoreType.DMA((1,)),
                pltpu.SemaphoreType.DMA((n,)),
                pltpu.SemaphoreType.DMA((n,)),
            ],
            compiler_params=pltpu.CompilerParams(collective_id=0, **params),
        )(rhs, parts, inv, blocks, hi, lo)
    return pl.pallas_call(
        functools.partial(sep_backward_kernel, n),
        out_shape=(sol_shape, jax.ShapeDtypeStruct((n, rows, width), jnp.bfloat16)),
        in_specs=[vmem] * 5,
        out_specs=(vmem, vmem),
        scratch_shapes=scratch,
        compiler_params=pltpu.CompilerParams(collective_id=1, **params),
    )(start, inv, blocks, hi, lo)


def split_pair(matrix):
    hi = matrix.astype(jnp.bfloat16)
    lo = (matrix - hi.astype(jnp.float32)).astype(jnp.bfloat16)
    return hi, lo


def _three_pass(x, hi, lo, dims):
    x_hi = x.astype(jnp.bfloat16)
    x_lo = (x - x_hi.astype(jnp.float32)).astype(jnp.bfloat16)
    dot = lambda u, v: lax.dot_general(u, v, (dims, ((), ())), preferred_element_type=jnp.float32)
    return dot(x_hi, hi) + (dot(x_hi, lo) + dot(x_lo, hi))


def top_solve_kernel(nt, span, start_ref, hi_ref, lo_ref, lower_ref, coef_ref, half_ref, fwd_half, fwd_full):
    for t in range(nt):
        cols = slice(t * span, (t + 1) * span)
        residue = start_ref[:, cols]
        if t > 0:
            residue = residue - _nt(fwd_half[:, : t * span], lower_ref[cols, : t * span])
        solved = _three_pass(residue, hi_ref[t], lo_ref[t], ((1,), (1,)))
        fwd_full[:, cols] = solved
        fwd_half[:, cols] = solved.astype(jnp.bfloat16)
    for t in reversed(range(nt)):
        cols = slice(t * span, (t + 1) * span)
        residue = fwd_full[:, cols]
        if t < nt - 1:
            residue = residue - _nn(half_ref[:, (t + 1) * span :], lower_ref[(t + 1) * span :, cols])
        solved = _three_pass(residue, hi_ref[t], lo_ref[t], ((1,), (0,)))
        coef_ref[:, cols] = solved
        half_ref[:, cols] = solved.astype(jnp.bfloat16)


def top_solve(top_start, top_inverse, top_lower):
    nt, span = top_inverse.shape[0], top_inverse.shape[1]
    rows, width = top_start.shape
    vmem = pl.BlockSpec(memory_space=pltpu.VMEM)
    return pl.pallas_call(
        functools.partial(top_solve_kernel, nt, span),
        out_shape=(
            jax.ShapeDtypeStruct((rows, width), jnp.float32),
            jax.ShapeDtypeStruct((rows, width), jnp.bfloat16),
        ),
        in_specs=[vmem] * 4,
        out_specs=(vmem, vmem),
        scratch_shapes=[
            pltpu.VMEM((rows, width), jnp.bfloat16),
            pltpu.VMEM((rows, width), jnp.float32),
        ],
        compiler_params=pltpu.CompilerParams(vmem_limit_bytes=48 * 1024 * 1024),
    )(top_start, *split_pair(top_inverse), top_lower)


def evaluate_kernel(slots, pattern_ref, coef_ref, centre_ref, column_ref, out_ref, acc, spread):
    m = pl.program_id(0)
    acc[...] = jnp.zeros_like(acc)
    column = column_ref[0]
    width = centre_ref.shape[2]
    for comp in range(3):
        spread[comp] = jnp.broadcast_to(column[:, comp : comp + 1], (column.shape[0], width))

    def one_slot(s, carry):
        @pl.when(pattern_ref[m, s] != 0)
        def _():
            centre = centre_ref[s]
            dist = None
            for comp in range(3):
                delta = centre[comp : comp + 1, :] - spread[comp]
                dist = delta * delta if dist is None else dist + delta * delta
            weight = jnp.maximum(1.0 - dist * (1.0 / support_sq), 0.0)
            kernel = (weight * weight * weight).astype(jnp.bfloat16)
            acc[...] += _nt(coef_ref[s], kernel)

        return carry

    lax.fori_loop(0, slots, one_slot, 0)
    out_ref[...] = acc[...]


def evaluate_all(coef_all, centre_all, point_columns, pattern):
    slots, rows, span = coef_all.shape
    blocks = point_columns.shape[0]
    full = lambda shape: pl.BlockSpec(shape, lambda m, pat: (0,) * len(shape))
    grid_spec = pltpu.PrefetchScalarGridSpec(
        num_scalar_prefetch=1,
        grid=(blocks,),
        in_specs=[
            full(coef_all.shape),
            full(centre_all.shape),
            pl.BlockSpec((1, span, point_columns.shape[2]), lambda m, pat: (m, 0, 0)),
        ],
        out_specs=pl.BlockSpec((rows, span), lambda m, pat: (0, m)),
        scratch_shapes=[
            pltpu.VMEM((rows, span), jnp.float32),
            pltpu.VMEM((3, span, centre_all.shape[2]), jnp.float32),
        ],
    )
    return pl.pallas_call(
        functools.partial(evaluate_kernel, slots),
        out_shape=jax.ShapeDtypeStruct((rows, blocks * span), jnp.float32),
        grid_spec=grid_spec,
    )(pattern, coef_all, centre_all, point_columns)


def top_reduce_kernel(n, groups, span, term_ref, total_ref, parts_a, parts_b, gathered, local_sem, send_a, recv_a, send_b, recv_b, send_c, recv_c):
    me = lax.axis_index("grp")
    leaf = lax.axis_index("leaf")
    barrier = pltpu.get_barrier_semaphore()
    for r in range(n):
        @pl.when(me != r)
        def _():
            pl.semaphore_signal(barrier, inc=1, device_id=(leaf, r), device_id_type=MESH)
    for g in range(groups):
        @pl.when(leaf != g)
        def _():
            pl.semaphore_signal(barrier, inc=1, device_id=(g, me), device_id_type=MESH)
    pl.semaphore_wait(barrier, n - 1 + groups - 1)

    def column(q):
        return term_ref.at[:, pl.ds(pl.multiple_of(q * span, span), span)]

    def copy_a(k):
        dest = lax.rem(me + k, n)
        return pltpu.make_async_remote_copy(
            column(dest), parts_a.at[me], send_a.at[k], recv_a.at[me], device_id=(leaf, dest), device_id_type=MESH
        )

    def wait_a(k):
        src = lax.rem(me + n - k, n)
        pltpu.make_async_remote_copy(
            column(src), parts_a.at[src], send_a.at[0], recv_a.at[src], device_id=(leaf, src), device_id_type=MESH
        ).wait_recv()

    own = pltpu.make_async_copy(column(me), parts_a.at[me], local_sem.at[0])
    own.start()
    for k in range(1, n):
        copy_a(k).start()
    own.wait()
    for k in range(1, n):
        wait_a(k)
    for k in range(1, n):
        copy_a(k).wait_send()
    total = parts_a[0]
    for q in range(1, n):
        total = total + parts_a[q]
    parts_b[leaf] = total

    def copy_b(k):
        dest = lax.rem(leaf + k, groups)
        return pltpu.make_async_remote_copy(
            parts_b.at[leaf], parts_b.at[leaf], send_b.at[k], recv_b.at[leaf], device_id=(dest, me), device_id_type=MESH
        )

    for k in range(1, groups):
        copy_b(k).start()
    for k in range(1, groups):
        src = lax.rem(leaf + groups - k, groups)
        pltpu.make_async_remote_copy(
            parts_b.at[src], parts_b.at[src], send_b.at[0], recv_b.at[src], device_id=(src, me), device_id_type=MESH
        ).wait_recv()
    for k in range(1, groups):
        copy_b(k).wait_send()
    summed = parts_b[0]
    for g in range(1, groups):
        summed = summed + parts_b[g]
    gathered[me] = summed

    def copy_c(k):
        dest = lax.rem(me + k, n)
        return pltpu.make_async_remote_copy(
            gathered.at[me], gathered.at[me], send_c.at[k], recv_c.at[me], device_id=(leaf, dest), device_id_type=MESH
        )

    for k in range(1, n):
        copy_c(k).start()
    for k in range(1, n):
        src = lax.rem(me + n - k, n)
        pltpu.make_async_remote_copy(
            gathered.at[src], gathered.at[src], send_c.at[0], recv_c.at[src], device_id=(leaf, src), device_id_type=MESH
        ).wait_recv()
    for k in range(1, n):
        copy_c(k).wait_send()
    for q in range(n):
        total_ref[:, q * span : (q + 1) * span] = gathered[q]


def top_reduce(term, n, groups):
    rows, width = term.shape
    span = width // n
    vmem = pl.BlockSpec(memory_space=pltpu.VMEM)
    return pl.pallas_call(
        functools.partial(top_reduce_kernel, n, groups, span),
        out_shape=jax.ShapeDtypeStruct((rows, width), jnp.float32),
        in_specs=[vmem],
        out_specs=vmem,
        scratch_shapes=[
            pltpu.VMEM((n, rows, span), jnp.float32),
            pltpu.VMEM((groups, rows, span), jnp.float32),
            pltpu.VMEM((n, rows, span), jnp.float32),
            pltpu.SemaphoreType.DMA((1,)),
            pltpu.SemaphoreType.DMA((n,)),
            pltpu.SemaphoreType.DMA((n,)),
            pltpu.SemaphoreType.DMA((groups,)),
            pltpu.SemaphoreType.DMA((groups,)),
            pltpu.SemaphoreType.DMA((n,)),
            pltpu.SemaphoreType.DMA((n,)),
        ],
        compiler_params=pltpu.CompilerParams(collective_id=2, has_side_effects=True),
    )(term)


def exchange_kernel(n, coef_ref, centre_ref, coef_out, centre_out, coef_buf, centre_buf, local_sem, send_sem, recv_sem):
    me = lax.axis_index("grp")
    leaf = lax.axis_index("leaf")
    _greet_group(n, leaf, me)
    pairs = ((coef_ref, coef_buf), (centre_ref, centre_buf))

    def push(kind, k):
        source, buf = pairs[kind]
        dest = lax.rem(me + k, n)
        return pltpu.make_async_remote_copy(
            source.at[dest], buf.at[me], send_sem.at[kind, k], recv_sem.at[kind, me], device_id=(leaf, dest), device_id_type=MESH
        )

    owns = [pltpu.make_async_copy(source.at[me], buf.at[me], local_sem.at[kind]) for kind, (source, buf) in enumerate(pairs)]
    for own in owns:
        own.start()
    for k in range(1, n):
        for kind in range(2):
            push(kind, k).start()
    for own in owns:
        own.wait()
    for k in range(1, n):
        src = lax.rem(me + n - k, n)
        for kind, (source, buf) in enumerate(pairs):
            pltpu.make_async_remote_copy(
                source.at[src], buf.at[src], send_sem.at[kind, 0], recv_sem.at[kind, src], device_id=(leaf, src), device_id_type=MESH
            ).wait_recv()
    for k in range(1, n):
        for kind in range(2):
            push(kind, k).wait_send()
    coef_out[...] = coef_buf[...]
    centre_out[...] = centre_buf[...]


def exchange(send_coef, send_centre, n):
    vmem = pl.BlockSpec(memory_space=pltpu.VMEM)
    return pl.pallas_call(
        functools.partial(exchange_kernel, n),
        out_shape=(
            jax.ShapeDtypeStruct(send_coef.shape, send_coef.dtype),
            jax.ShapeDtypeStruct(send_centre.shape, send_centre.dtype),
        ),
        in_specs=[vmem] * 2,
        out_specs=(vmem, vmem),
        scratch_shapes=[
            pltpu.VMEM(send_coef.shape, send_coef.dtype),
            pltpu.VMEM(send_centre.shape, send_centre.dtype),
            pltpu.SemaphoreType.DMA((2,)),
            pltpu.SemaphoreType.DMA((2, n)),
            pltpu.SemaphoreType.DMA((2, n)),
        ],
        compiler_params=pltpu.CompilerParams(collective_id=3, has_side_effects=True),
    )(send_coef, send_centre)


def slot_ranks(dest_rows, grp_size):
    onehot = (dest_rows[..., None] == jnp.arange(grp_size)).astype(jnp.int32)
    before = jnp.cumsum(onehot, axis=-2) - onehot
    return jnp.sum(before * onehot, axis=-1)


def evaluate(coef_all, centre_all, block_points, block_mask):
    dist = jnp.zeros((centre_all.shape[0], centre_all.shape[2], block_points.shape[1]), jnp.float32)
    for comp in range(3):
        delta = centre_all[:, comp, :, None] - block_points[None, comp, None, :]
        dist = dist + delta * delta
    weight = jnp.maximum(1.0 - dist / support_sq, 0.0) ** 3
    kernel = (weight * block_mask.astype(jnp.float32)[:, None, None]).astype(jnp.bfloat16)
    return jnp.einsum("krs,ksp->rp", coef_all, kernel, preferred_element_type=jnp.float32)


def on_device(
    rhs_leaf,
    rhs_sep,
    rhs_top,
    leaf_inverse,
    leaf_coupling,
    leaf_targets,
    sep_inverse,
    sep_blocks,
    top_coupling,
    top_inverse,
    top_lower,
    dest_map,
    centers,
    points,
    eval_pattern,
):
    grp_size = lax.axis_size("grp")
    my_index = lax.axis_index("grp")
    blocks_here = leaf_inverse.shape[0]
    snapshots = rhs_leaf.shape[0]
    span = leaf_inverse.shape[1]
    slot_count = CAP
    leaf_rhs = rhs_leaf.reshape(snapshots, blocks_here, span).transpose(1, 0, 2)
    leaf_sol = jnp.einsum("nrs,nts->nrt", leaf_rhs, leaf_inverse, precision=highest)
    leaf_half = leaf_sol.astype(jnp.bfloat16)
    partial_value = jnp.einsum(
        "nrs,ncbs->ncrb", leaf_half, leaf_coupling, preferred_element_type=jnp.float32
    )
    onehot = (leaf_targets[:, :, None] == jnp.arange(grp_size)[None, None, :]).astype(jnp.float32)
    picked = onehot
    parts = jnp.einsum("ncq,ncrb->qrb", picked, partial_value, precision=highest).astype(jnp.bfloat16)
    inverse_own = sep_inverse[0]
    own_blocks = sep_blocks[0]
    before = lax.dynamic_index_in_dim(own_blocks, jnp.maximum(my_index - 1, 0), 0, keepdims=False)
    fwd_hi, fwd_lo = split_pair(
        jnp.dot(before.astype(jnp.float32).T, inverse_own.T, precision=highest)
    )
    after = lax.dynamic_index_in_dim(own_blocks, jnp.minimum(my_index + 1, grp_size - 1), 0, keepdims=False)
    bwd_hi, bwd_lo = split_pair(jnp.dot(after.astype(jnp.float32), inverse_own, precision=highest))
    sep_sol = sep_solve("forward", (rhs_sep, parts), inverse_own, own_blocks, fwd_hi, fwd_lo, grp_size)
    sep_half = sep_sol.astype(jnp.bfloat16)
    top_term = jnp.dot(sep_half, top_coupling, preferred_element_type=jnp.float32)
    top_total = top_reduce(top_term, grp_size, lax.axis_size("leaf"))
    top_start = rhs_top - top_total
    coef_top, top_half = top_solve(top_start, top_inverse, top_lower)
    back_start = sep_sol - lax.dot_general(
        top_half, top_coupling, (((1,), (1,)), ((), ())), preferred_element_type=jnp.float32
    )

    coef_sep, known_table = sep_solve(
        "backward", back_start, inverse_own, own_blocks, bwd_hi, bwd_lo, grp_size
    )
    picked = jnp.einsum(
        "ncq,qrb->ncrb",
        onehot.astype(jnp.bfloat16),
        known_table,
        preferred_element_type=jnp.float32,
    ).astype(jnp.bfloat16)
    reduced = jnp.einsum(
        "ncrb,ncbs->nrs", picked, leaf_coupling, preferred_element_type=jnp.float32
    )
    leaf_coef = jnp.einsum("nrs,nst->nrt", leaf_sol - reduced, leaf_inverse, precision=highest)
    coef_leaf = leaf_coef.transpose(1, 0, 2).reshape(snapshots, blocks_here * span)
    leaf_out = leaf_coef.astype(jnp.bfloat16)
    slot_ids = jnp.arange(slot_count)
    grp_ids = jnp.arange(grp_size)
    own_dest = dest_map[:, 0]
    slot_rank = slot_ranks(own_dest[None, :], grp_size)[0]
    selector = (own_dest[None, None, :] == grp_ids[:, None, None]) & (
        slot_rank[None, None, :] == slot_ids[None, :, None]
    )
    send_coef = jnp.einsum(
        "dkj,jrt->dkrt", selector.astype(jnp.bfloat16), leaf_out, preferred_element_type=jnp.float32
    ).astype(jnp.bfloat16)
    send_centre = jnp.einsum(
        "dkj,jct->dkct", selector.astype(jnp.float32), centers, precision=highest
    )
    received, recv_centre = exchange(send_coef, send_centre, grp_size)
    slot_total = grp_size * slot_count
    coef_all = received.reshape(slot_total, snapshots, span)
    centre_all = recv_centre.reshape(slot_total, 3, span)
    point_blocks = eval_pattern.shape[0]
    point_columns = points[0].T.reshape(point_blocks, span, points.shape[1])
    values = evaluate_all(coef_all, centre_all, point_columns, eval_pattern)
    return (coef_leaf, coef_sep, coef_top, values)


def solution(mesh):
    in_specs = (
        P(None, ("leaf", "grp")),
        P(None, ("leaf", "grp")),
        P(),
        P(("leaf", "grp"), None, None),
        P(("leaf", "grp"), None, None, None),
        P(("leaf", "grp"), None),
        P(("leaf", "grp"), None, None),
        P(("leaf", "grp"), None, None, None),
        P(("leaf", "grp"), None),
        P(),
        P(),
        P(("leaf", "grp"), None),
        P(("leaf", "grp"), None, None),
        P(("leaf", "grp"), None, None),
        P(("leaf", "grp"), None),
    )
    out_specs = (P(None, ("leaf", "grp")), P(None, ("leaf", "grp")), P(), P(None, ("leaf", "grp")))
    return jax.shard_map(
        on_device, mesh=mesh, in_specs=in_specs, out_specs=out_specs, check_vma=False
    )
```

```python
import functools

import jax
import jax.numpy as jnp
from jax import lax
from jax.sharding import PartitionSpec as P
from jax.experimental import pallas as pl
from jax.experimental.pallas import tpu as pltpu

MESH = pl.DeviceIdType.MESH

CAP = 2


highest = lax.Precision.HIGHEST
three_pass = lax.Precision.HIGH
support_sq = 0.25


def split_up(shard, dim, peers):
    dims = shard.shape
    pieces = shard.reshape(*dims[:dim], peers, dims[dim] // peers, *dims[dim + 1 :])
    return jnp.moveaxis(pieces, dim, 0)


def sum_at_owner(shard, axis, dim):
    pieces = split_up(shard, dim, lax.axis_size(axis))
    arrived = lax.all_to_all(pieces, axis, split_axis=0, concat_axis=0, tiled=True)
    return arrived.astype(jnp.float32).sum(axis=0)


def from_root(shard, axis, root):
    return lax.dynamic_index_in_dim(lax.all_gather(shard, axis), root, 0, keepdims=False)


def copy_for_each(shard, axis):
    copies = jnp.broadcast_to(shard, (lax.axis_size(axis), *shard.shape))
    return lax.all_to_all(copies, axis, split_axis=0, concat_axis=0, tiled=True)


def over_copies(shard, axis):
    return copy_for_each(shard, axis).astype(jnp.float32).sum(axis=0)


def joined_along(pieces, dim):
    dims = list(pieces.shape[1:])
    dims[dim] *= pieces.shape[0]
    return jnp.moveaxis(pieces, 0, dim).reshape(dims)


def gather_directly(shard, axis, dim):
    pieces = copy_for_each(shard, axis)
    return joined_along(pieces, dim)


def _nt(a, b):
    return lax.dot_general(a, b, (((1,), (1,)), ((), ())), preferred_element_type=jnp.float32)


def _nn(a, b):
    return lax.dot_general(a, b, (((1,), (0,)), ((), ())), preferred_element_type=jnp.float32)


def _nt_exact(a, b):
    return lax.dot_general(
        a, b, (((1,), (1,)), ((), ())), precision=highest, preferred_element_type=jnp.float32
    )


def _nn_exact(a, b):
    return lax.dot_general(
        a, b, (((1,), (0,)), ((), ())), precision=highest, preferred_element_type=jnp.float32
    )


def _greet_group(n, leaf, me):
    barrier = pltpu.get_barrier_semaphore()
    for r in range(n):
        @pl.when(me != r)
        def _():
            pl.semaphore_signal(barrier, inc=1, device_id=(leaf, r), device_id_type=MESH)
    pl.semaphore_wait(barrier, n - 1)


def _block_copy(halves, q, dest, send_sem, recv_sem, leaf):
    return pltpu.make_async_remote_copy(
        src_ref=halves.at[q],
        dst_ref=halves.at[q],
        send_sem=send_sem,
        recv_sem=recv_sem.at[q],
        device_id=(leaf, dest),
        device_id_type=MESH,
    )


def _send_block(n, halves, s, solved, sol_ref, send_sem, recv_sem, leaf, dests):
    sol_ref[...] = solved
    halves[s] = solved.astype(jnp.bfloat16)
    for k in range(1, n):
        dest, live = dests(s, k)
        @pl.when(live)
        def _():
            _block_copy(halves, s, dest, send_sem.at[k], recv_sem, leaf).start()
            if k == 1:
                _block_copy(halves, s, dest, send_sem.at[k], recv_sem, leaf).wait_send()
    for k in range(2, n):
        dest, live = dests(s, k)
        @pl.when(live)
        def _():
            _block_copy(halves, s, dest, send_sem.at[k], recv_sem, leaf).wait_send()


def _through(y, hi_ref, lo_ref):
    return _nn(y, hi_ref[...]) + _nn(y, lo_ref[...])


def sep_forward_kernel(n, rhs_ref, part_ref, inv_ref, blocks_ref, hi_ref, lo_ref, sol_ref, halves, resid, base, send_sem, recv_sem, arrived, local_sem, give_sem, take_sem):
    me = lax.axis_index("grp")
    leaf = lax.axis_index("leaf")
    _greet_group(n, leaf, me)

    def give(dest):
        return pltpu.make_async_remote_copy(
            part_ref.at[dest], arrived.at[me], give_sem.at[dest], take_sem.at[me], device_id=(leaf, dest), device_id_type=MESH
        )

    own = pltpu.make_async_copy(part_ref.at[me], arrived.at[me], local_sem.at[0])
    own.start()
    for dest in range(n):
        @pl.when(me != dest)
        def _():
            give(dest).start()
    own.wait()
    for src in range(n):
        @pl.when(me != src)
        def _():
            pltpu.make_async_remote_copy(
                part_ref.at[src], arrived.at[src], give_sem.at[src], take_sem.at[src], device_id=(leaf, src), device_id_type=MESH
            ).wait_recv()
    total = arrived[0].astype(jnp.float32)
    for src in range(1, n):
        total = total + arrived[src].astype(jnp.float32)
    resid[...] = rhs_ref[...] - total
    for dest in range(n):
        @pl.when(me != dest)
        def _():
            give(dest).wait_send()

    dests = lambda s, k: (s + k, s + k < n)

    @pl.when(me == 0)
    def _():
        _send_block(n, halves, 0, _nt_exact(resid[...], inv_ref[...]), sol_ref, send_sem, recv_sem, leaf, dests)

    @pl.when(me == 1)
    def _():
        base[...] = _nt_exact(resid[...], inv_ref[...])

    def step(q, carry):
        @pl.when(me == q + 1)
        def _():
            _block_copy(halves, q, q, send_sem.at[0], recv_sem, leaf).wait_recv()
            solved = base[...] - _through(halves[q], hi_ref, lo_ref)
            _send_block(n, halves, q + 1, solved, sol_ref, send_sem, recv_sem, leaf, dests)

        @pl.when(me > q + 1)
        def _():
            _block_copy(halves, q, q, send_sem.at[0], recv_sem, leaf).wait_recv()
            resid[...] = resid[...] - _nt(halves[q], blocks_ref[q])

            @pl.when(me == q + 2)
            def _():
                base[...] = _nt_exact(resid[...], inv_ref[...])

        return carry

    lax.fori_loop(0, n - 1, step, 0)


def sep_backward_kernel(n, start_ref, inv_ref, blocks_ref, hi_ref, lo_ref, sol_ref, table_ref, halves, resid, base, send_sem, recv_sem):
    me = lax.axis_index("grp")
    leaf = lax.axis_index("leaf")
    _greet_group(n, leaf, me)
    resid[...] = start_ref[...]
    dests = lambda s, k: (s - k, s - k >= 0)

    @pl.when(me == n - 1)
    def _():
        _send_block(n, halves, n - 1, _nn_exact(resid[...], inv_ref[...]), sol_ref, send_sem, recv_sem, leaf, dests)

    @pl.when(me == n - 2)
    def _():
        base[...] = _nn_exact(resid[...], inv_ref[...])

    def step(s, carry):
        q = n - 1 - s

        @pl.when(me < q)
        def _():
            _block_copy(halves, q, q, send_sem.at[0], recv_sem, leaf).wait_recv()

        @pl.when(me == q - 1)
        def _():
            solved = base[...] - _through(halves[q], hi_ref, lo_ref)
            _send_block(n, halves, q - 1, solved, sol_ref, send_sem, recv_sem, leaf, dests)

        @pl.when(me < q - 1)
        def _():
            resid[...] = resid[...] - _nn(halves[q], blocks_ref[q])

            @pl.when(me == q - 2)
            def _():
                base[...] = _nn_exact(resid[...], inv_ref[...])

        return carry

    lax.fori_loop(0, n - 1, step, 0)
    for k in range(1, n):
        @pl.when(me + k < n)
        def _():
            _block_copy(halves, me, me + k, send_sem.at[k], recv_sem, leaf).start()
    for q in range(n):
        @pl.when(q < me)
        def _():
            _block_copy(halves, q, q, send_sem.at[0], recv_sem, leaf).wait_recv()
    for k in range(1, n):
        @pl.when(me + k < n)
        def _():
            _block_copy(halves, me, me + k, send_sem.at[k], recv_sem, leaf).wait_send()
    table_ref[...] = halves[...]


def sep_solve(kind, start, inv, blocks, hi, lo, n):
    rows, width = (start[0] if kind == "forward" else start).shape
    vmem = pl.BlockSpec(memory_space=pltpu.VMEM)
    scratch = [
        pltpu.VMEM((n, rows, width), jnp.bfloat16),
        pltpu.VMEM((rows, width), jnp.float32),
        pltpu.VMEM((rows, width), jnp.float32),
        pltpu.SemaphoreType.DMA((n,)),
        pltpu.SemaphoreType.DMA((n,)),
    ]
    sol_shape = jax.ShapeDtypeStruct((rows, width), jnp.float32)
    params = dict(has_side_effects=True, vmem_limit_bytes=48 * 1024 * 1024)
    if kind == "forward":
        rhs, parts = start
        return pl.pallas_call(
            functools.partial(sep_forward_kernel, n),
            out_shape=sol_shape,
            in_specs=[vmem] * 6,
            out_specs=vmem,
            scratch_shapes=scratch
            + [
                pltpu.VMEM(parts.shape, parts.dtype),
                pltpu.SemaphoreType.DMA((1,)),
                pltpu.SemaphoreType.DMA((n,)),
                pltpu.SemaphoreType.DMA((n,)),
            ],
            compiler_params=pltpu.CompilerParams(collective_id=0, **params),
        )(rhs, parts, inv, blocks, hi, lo)
    return pl.pallas_call(
        functools.partial(sep_backward_kernel, n),
        out_shape=(sol_shape, jax.ShapeDtypeStruct((n, rows, width), jnp.bfloat16)),
        in_specs=[vmem] * 5,
        out_specs=(vmem, vmem),
        scratch_shapes=scratch,
        compiler_params=pltpu.CompilerParams(collective_id=1, **params),
    )(start, inv, blocks, hi, lo)


def split_pair(matrix):
    hi = matrix.astype(jnp.bfloat16)
    lo = (matrix - hi.astype(jnp.float32)).astype(jnp.bfloat16)
    return hi, lo


def _three_pass(x, hi, lo, dims):
    x_hi = x.astype(jnp.bfloat16)
    x_lo = (x - x_hi.astype(jnp.float32)).astype(jnp.bfloat16)
    dot = lambda u, v: lax.dot_general(u, v, (dims, ((), ())), preferred_element_type=jnp.float32)
    return dot(x_hi, hi) + (dot(x_hi, lo) + dot(x_lo, hi))


def top_solve_kernel(nt, span, start_ref, hi_ref, lo_ref, lower_ref, coef_ref, half_ref, fwd_half, fwd_full):
    for t in range(nt):
        cols = slice(t * span, (t + 1) * span)
        residue = start_ref[:, cols]
        if t > 0:
            residue = residue - _nt(fwd_half[:, : t * span], lower_ref[cols, : t * span])
        solved = _three_pass(residue, hi_ref[t], lo_ref[t], ((1,), (1,)))
        fwd_full[:, cols] = solved
        fwd_half[:, cols] = solved.astype(jnp.bfloat16)
    for t in reversed(range(nt)):
        cols = slice(t * span, (t + 1) * span)
        residue = fwd_full[:, cols]
        if t < nt - 1:
            residue = residue - _nn(half_ref[:, (t + 1) * span :], lower_ref[(t + 1) * span :, cols])
        solved = _three_pass(residue, hi_ref[t], lo_ref[t], ((1,), (0,)))
        coef_ref[:, cols] = solved
        half_ref[:, cols] = solved.astype(jnp.bfloat16)


def top_solve(top_start, top_inverse, top_lower):
    nt, span = top_inverse.shape[0], top_inverse.shape[1]
    rows, width = top_start.shape
    vmem = pl.BlockSpec(memory_space=pltpu.VMEM)
    return pl.pallas_call(
        functools.partial(top_solve_kernel, nt, span),
        out_shape=(
            jax.ShapeDtypeStruct((rows, width), jnp.float32),
            jax.ShapeDtypeStruct((rows, width), jnp.bfloat16),
        ),
        in_specs=[vmem] * 4,
        out_specs=(vmem, vmem),
        scratch_shapes=[
            pltpu.VMEM((rows, width), jnp.bfloat16),
            pltpu.VMEM((rows, width), jnp.float32),
        ],
        compiler_params=pltpu.CompilerParams(vmem_limit_bytes=48 * 1024 * 1024),
    )(top_start, *split_pair(top_inverse), top_lower)


def evaluate_kernel(slots, pattern_ref, coef_ref, centre_ref, column_ref, out_ref, acc, spread):
    m = pl.program_id(0)
    acc[...] = jnp.zeros_like(acc)
    column = column_ref[0]
    width = centre_ref.shape[2]
    for comp in range(3):
        spread[comp] = jnp.broadcast_to(column[:, comp : comp + 1], (column.shape[0], width))

    def one_slot(s, carry):
        @pl.when(pattern_ref[m, s] != 0)
        def _():
            centre = centre_ref[s]
            dist = None
            for comp in range(3):
                delta = centre[comp : comp + 1, :] - spread[comp]
                dist = delta * delta if dist is None else dist + delta * delta
            weight = jnp.maximum(1.0 - dist * (1.0 / support_sq), 0.0)
            kernel = (weight * weight * weight).astype(jnp.bfloat16)
            acc[...] += _nt(coef_ref[s], kernel)

        return carry

    lax.fori_loop(0, slots, one_slot, 0)
    out_ref[...] = acc[...]


def evaluate_all(coef_all, centre_all, point_columns, pattern):
    slots, rows, span = coef_all.shape
    blocks = point_columns.shape[0]
    full = lambda shape: pl.BlockSpec(shape, lambda m, pat: (0,) * len(shape))
    grid_spec = pltpu.PrefetchScalarGridSpec(
        num_scalar_prefetch=1,
        grid=(blocks,),
        in_specs=[
            full(coef_all.shape),
            full(centre_all.shape),
            pl.BlockSpec((1, span, point_columns.shape[2]), lambda m, pat: (m, 0, 0)),
        ],
        out_specs=pl.BlockSpec((rows, span), lambda m, pat: (0, m)),
        scratch_shapes=[
            pltpu.VMEM((rows, span), jnp.float32),
            pltpu.VMEM((3, span, centre_all.shape[2]), jnp.float32),
        ],
    )
    return pl.pallas_call(
        functools.partial(evaluate_kernel, slots),
        out_shape=jax.ShapeDtypeStruct((rows, blocks * span), jnp.float32),
        grid_spec=grid_spec,
    )(pattern, coef_all, centre_all, point_columns)


def top_reduce_kernel(n, groups, span, term_ref, total_ref, parts_a, parts_b, gathered, local_sem, send_a, recv_a, send_b, recv_b, send_c, recv_c):
    me = lax.axis_index("grp")
    leaf = lax.axis_index("leaf")
    barrier = pltpu.get_barrier_semaphore()
    for r in range(n):
        @pl.when(me != r)
        def _():
            pl.semaphore_signal(barrier, inc=1, device_id=(leaf, r), device_id_type=MESH)
    for g in range(groups):
        @pl.when(leaf != g)
        def _():
            pl.semaphore_signal(barrier, inc=1, device_id=(g, me), device_id_type=MESH)
    pl.semaphore_wait(barrier, n - 1 + groups - 1)

    def column(q):
        return term_ref.at[:, pl.ds(pl.multiple_of(q * span, span), span)]

    def copy_a(k):
        dest = lax.rem(me + k, n)
        return pltpu.make_async_remote_copy(
            column(dest), parts_a.at[me], send_a.at[k], recv_a.at[me], device_id=(leaf, dest), device_id_type=MESH
        )

    def wait_a(k):
        src = lax.rem(me + n - k, n)
        pltpu.make_async_remote_copy(
            column(src), parts_a.at[src], send_a.at[0], recv_a.at[src], device_id=(leaf, src), device_id_type=MESH
        ).wait_recv()

    own = pltpu.make_async_copy(column(me), parts_a.at[me], local_sem.at[0])
    own.start()
    for k in range(1, n):
        copy_a(k).start()
    own.wait()
    for k in range(1, n):
        wait_a(k)
    for k in range(1, n):
        copy_a(k).wait_send()
    total = parts_a[0]
    for q in range(1, n):
        total = total + parts_a[q]
    parts_b[leaf] = total

    def copy_b(k):
        dest = lax.rem(leaf + k, groups)
        return pltpu.make_async_remote_copy(
            parts_b.at[leaf], parts_b.at[leaf], send_b.at[k], recv_b.at[leaf], device_id=(dest, me), device_id_type=MESH
        )

    for k in range(1, groups):
        copy_b(k).start()
    for k in range(1, groups):
        src = lax.rem(leaf + groups - k, groups)
        pltpu.make_async_remote_copy(
            parts_b.at[src], parts_b.at[src], send_b.at[0], recv_b.at[src], device_id=(src, me), device_id_type=MESH
        ).wait_recv()
    for k in range(1, groups):
        copy_b(k).wait_send()
    summed = parts_b[0]
    for g in range(1, groups):
        summed = summed + parts_b[g]
    gathered[me] = summed

    def copy_c(k):
        dest = lax.rem(me + k, n)
        return pltpu.make_async_remote_copy(
            gathered.at[me], gathered.at[me], send_c.at[k], recv_c.at[me], device_id=(leaf, dest), device_id_type=MESH
        )

    for k in range(1, n):
        copy_c(k).start()
    for k in range(1, n):
        src = lax.rem(me + n - k, n)
        pltpu.make_async_remote_copy(
            gathered.at[src], gathered.at[src], send_c.at[0], recv_c.at[src], device_id=(leaf, src), device_id_type=MESH
        ).wait_recv()
    for k in range(1, n):
        copy_c(k).wait_send()
    for q in range(n):
        total_ref[:, q * span : (q + 1) * span] = gathered[q]


def top_reduce(term, n, groups):
    rows, width = term.shape
    span = width // n
    vmem = pl.BlockSpec(memory_space=pltpu.VMEM)
    return pl.pallas_call(
        functools.partial(top_reduce_kernel, n, groups, span),
        out_shape=jax.ShapeDtypeStruct((rows, width), jnp.float32),
        in_specs=[vmem],
        out_specs=vmem,
        scratch_shapes=[
            pltpu.VMEM((n, rows, span), jnp.float32),
            pltpu.VMEM((groups, rows, span), jnp.float32),
            pltpu.VMEM((n, rows, span), jnp.float32),
            pltpu.SemaphoreType.DMA((1,)),
            pltpu.SemaphoreType.DMA((n,)),
            pltpu.SemaphoreType.DMA((n,)),
            pltpu.SemaphoreType.DMA((groups,)),
            pltpu.SemaphoreType.DMA((groups,)),
            pltpu.SemaphoreType.DMA((n,)),
            pltpu.SemaphoreType.DMA((n,)),
        ],
        compiler_params=pltpu.CompilerParams(collective_id=2, has_side_effects=True),
    )(term)


def exchange_kernel(n, coef_ref, centre_ref, coef_out, centre_out, coef_buf, centre_buf, local_sem, send_sem, recv_sem):
    me = lax.axis_index("grp")
    leaf = lax.axis_index("leaf")
    _greet_group(n, leaf, me)
    pairs = ((coef_ref, coef_buf), (centre_ref, centre_buf))

    def push(kind, k):
        source, buf = pairs[kind]
        dest = lax.rem(me + k, n)
        return pltpu.make_async_remote_copy(
            source.at[dest], buf.at[me], send_sem.at[kind, k], recv_sem.at[kind, me], device_id=(leaf, dest), device_id_type=MESH
        )

    owns = [pltpu.make_async_copy(source.at[me], buf.at[me], local_sem.at[kind]) for kind, (source, buf) in enumerate(pairs)]
    for own in owns:
        own.start()
    for k in range(1, n):
        for kind in range(2):
            push(kind, k).start()
    for own in owns:
        own.wait()
    for k in range(1, n):
        src = lax.rem(me + n - k, n)
        for kind, (source, buf) in enumerate(pairs):
            pltpu.make_async_remote_copy(
                source.at[src], buf.at[src], send_sem.at[kind, 0], recv_sem.at[kind, src], device_id=(leaf, src), device_id_type=MESH
            ).wait_recv()
    for k in range(1, n):
        for kind in range(2):
            push(kind, k).wait_send()
    coef_out[...] = coef_buf[...]
    centre_out[...] = centre_buf[...]


def exchange(send_coef, send_centre, n):
    vmem = pl.BlockSpec(memory_space=pltpu.VMEM)
    return pl.pallas_call(
        functools.partial(exchange_kernel, n),
        out_shape=(
            jax.ShapeDtypeStruct(send_coef.shape, send_coef.dtype),
            jax.ShapeDtypeStruct(send_centre.shape, send_centre.dtype),
        ),
        in_specs=[vmem] * 2,
        out_specs=(vmem, vmem),
        scratch_shapes=[
            pltpu.VMEM(send_coef.shape, send_coef.dtype),
            pltpu.VMEM(send_centre.shape, send_centre.dtype),
            pltpu.SemaphoreType.DMA((2,)),
            pltpu.SemaphoreType.DMA((2, n)),
            pltpu.SemaphoreType.DMA((2, n)),
        ],
        compiler_params=pltpu.CompilerParams(collective_id=3, has_side_effects=True),
    )(send_coef, send_centre)


def slot_ranks(dest_rows, grp_size):
    onehot = (dest_rows[..., None] == jnp.arange(grp_size)).astype(jnp.int32)
    before = jnp.cumsum(onehot, axis=-2) - onehot
    return jnp.sum(before * onehot, axis=-1)


def evaluate(coef_all, centre_all, block_points, block_mask):
    dist = jnp.zeros((centre_all.shape[0], centre_all.shape[2], block_points.shape[1]), jnp.float32)
    for comp in range(3):
        delta = centre_all[:, comp, :, None] - block_points[None, comp, None, :]
        dist = dist + delta * delta
    weight = jnp.maximum(1.0 - dist / support_sq, 0.0) ** 3
    kernel = (weight * block_mask.astype(jnp.float32)[:, None, None]).astype(jnp.bfloat16)
    return jnp.einsum("krs,ksp->rp", coef_all, kernel, preferred_element_type=jnp.float32)


def on_device(
    rhs_leaf,
    rhs_sep,
    rhs_top,
    leaf_inverse,
    leaf_coupling,
    leaf_targets,
    sep_inverse,
    sep_blocks,
    top_coupling,
    top_inverse,
    top_lower,
    dest_map,
    centers,
    points,
    eval_pattern,
):
    grp_size = lax.axis_size("grp")
    my_index = lax.axis_index("grp")
    blocks_here = leaf_inverse.shape[0]
    snapshots = rhs_leaf.shape[0]
    span = leaf_inverse.shape[1]
    slot_count = CAP
    leaf_rhs = rhs_leaf.reshape(snapshots, blocks_here, span).transpose(1, 0, 2)
    leaf_sol = jnp.einsum("nrs,nts->nrt", leaf_rhs, leaf_inverse, precision=three_pass)
    leaf_half = leaf_sol.astype(jnp.bfloat16)
    partial_value = jnp.einsum(
        "nrs,ncbs->ncrb", leaf_half, leaf_coupling, preferred_element_type=jnp.float32
    )
    onehot = (leaf_targets[:, :, None] == jnp.arange(grp_size)[None, None, :]).astype(jnp.float32)
    picked = onehot
    parts = jnp.einsum("ncq,ncrb->qrb", picked, partial_value, precision=three_pass).astype(jnp.bfloat16)
    inverse_own = sep_inverse[0]
    own_blocks = sep_blocks[0]
    before = lax.dynamic_index_in_dim(own_blocks, jnp.maximum(my_index - 1, 0), 0, keepdims=False)
    fwd_hi, fwd_lo = split_pair(
        jnp.dot(before.astype(jnp.float32).T, inverse_own.T, precision=three_pass)
    )
    after = lax.dynamic_index_in_dim(own_blocks, jnp.minimum(my_index + 1, grp_size - 1), 0, keepdims=False)
    bwd_hi, bwd_lo = split_pair(jnp.dot(after.astype(jnp.float32), inverse_own, precision=three_pass))
    sep_sol = sep_solve("forward", (rhs_sep, parts), inverse_own, own_blocks, fwd_hi, fwd_lo, grp_size)
    sep_half = sep_sol.astype(jnp.bfloat16)
    top_term = jnp.dot(sep_half, top_coupling, preferred_element_type=jnp.float32)
    top_total = top_reduce(top_term, grp_size, lax.axis_size("leaf"))
    top_start = rhs_top - top_total
    coef_top, top_half = top_solve(top_start, top_inverse, top_lower)
    back_start = sep_sol - lax.dot_general(
        top_half, top_coupling, (((1,), (1,)), ((), ())), preferred_element_type=jnp.float32
    )

    coef_sep, known_table = sep_solve(
        "backward", back_start, inverse_own, own_blocks, bwd_hi, bwd_lo, grp_size
    )
    picked = jnp.einsum(
        "ncq,qrb->ncrb",
        onehot.astype(jnp.bfloat16),
        known_table,
        preferred_element_type=jnp.float32,
    ).astype(jnp.bfloat16)
    reduced = jnp.einsum(
        "ncrb,ncbs->nrs", picked, leaf_coupling, preferred_element_type=jnp.float32
    )
    leaf_coef = jnp.einsum("nrs,nst->nrt", leaf_sol - reduced, leaf_inverse, precision=three_pass)
    coef_leaf = leaf_coef.transpose(1, 0, 2).reshape(snapshots, blocks_here * span)
    leaf_out = leaf_coef.astype(jnp.bfloat16)
    slot_ids = jnp.arange(slot_count)
    grp_ids = jnp.arange(grp_size)
    own_dest = dest_map[:, 0]
    slot_rank = slot_ranks(own_dest[None, :], grp_size)[0]
    selector = (own_dest[None, None, :] == grp_ids[:, None, None]) & (
        slot_rank[None, None, :] == slot_ids[None, :, None]
    )
    send_coef = jnp.einsum(
        "dkj,jrt->dkrt", selector.astype(jnp.bfloat16), leaf_out, preferred_element_type=jnp.float32
    ).astype(jnp.bfloat16)
    send_centre = jnp.einsum(
        "dkj,jct->dkct", selector.astype(jnp.float32), centers, precision=highest
    )
    received, recv_centre = exchange(send_coef, send_centre, grp_size)
    slot_total = grp_size * slot_count
    coef_all = received.reshape(slot_total, snapshots, span)
    centre_all = recv_centre.reshape(slot_total, 3, span)
    point_blocks = eval_pattern.shape[0]
    point_columns = points[0].T.reshape(point_blocks, span, points.shape[1])
    values = evaluate_all(coef_all, centre_all, point_columns, eval_pattern)
    return (coef_leaf, coef_sep, coef_top, values)


def solution(mesh):
    in_specs = (
        P(None, ("leaf", "grp")),
        P(None, ("leaf", "grp")),
        P(),
        P(("leaf", "grp"), None, None),
        P(("leaf", "grp"), None, None, None),
        P(("leaf", "grp"), None),
        P(("leaf", "grp"), None, None),
        P(("leaf", "grp"), None, None, None),
        P(("leaf", "grp"), None),
        P(),
        P(),
        P(("leaf", "grp"), None),
        P(("leaf", "grp"), None, None),
        P(("leaf", "grp"), None, None),
        P(("leaf", "grp"), None),
    )
    out_specs = (P(None, ("leaf", "grp")), P(None, ("leaf", "grp")), P(), P(None, ("leaf", "grp")))
    return jax.shard_map(
        on_device, mesh=mesh, in_specs=in_specs, out_specs=out_specs, check_vma=False
    )
```

```python
import functools

import jax
import jax.numpy as jnp
from jax import lax
from jax.sharding import PartitionSpec as P
from jax.experimental import pallas as pl
from jax.experimental.pallas import tpu as pltpu

MESH = pl.DeviceIdType.MESH

CAP = 2


highest = lax.Precision.HIGHEST
three_pass = lax.Precision.HIGH
support_sq = 0.25


def split_up(shard, dim, peers):
    dims = shard.shape
    pieces = shard.reshape(*dims[:dim], peers, dims[dim] // peers, *dims[dim + 1 :])
    return jnp.moveaxis(pieces, dim, 0)


def sum_at_owner(shard, axis, dim):
    pieces = split_up(shard, dim, lax.axis_size(axis))
    arrived = lax.all_to_all(pieces, axis, split_axis=0, concat_axis=0, tiled=True)
    return arrived.astype(jnp.float32).sum(axis=0)


def from_root(shard, axis, root):
    return lax.dynamic_index_in_dim(lax.all_gather(shard, axis), root, 0, keepdims=False)


def copy_for_each(shard, axis):
    copies = jnp.broadcast_to(shard, (lax.axis_size(axis), *shard.shape))
    return lax.all_to_all(copies, axis, split_axis=0, concat_axis=0, tiled=True)


def over_copies(shard, axis):
    return copy_for_each(shard, axis).astype(jnp.float32).sum(axis=0)


def joined_along(pieces, dim):
    dims = list(pieces.shape[1:])
    dims[dim] *= pieces.shape[0]
    return jnp.moveaxis(pieces, 0, dim).reshape(dims)


def gather_directly(shard, axis, dim):
    pieces = copy_for_each(shard, axis)
    return joined_along(pieces, dim)


def _nt(a, b):
    return lax.dot_general(a, b, (((1,), (1,)), ((), ())), preferred_element_type=jnp.float32)


def _nn(a, b):
    return lax.dot_general(a, b, (((1,), (0,)), ((), ())), preferred_element_type=jnp.float32)


def _split(x):
    hi = x.astype(jnp.bfloat16)
    return hi, (x - hi.astype(jnp.float32)).astype(jnp.bfloat16)


def _three_products(a, b, dims):
    a_hi, a_lo = _split(a)
    b_hi, b_lo = _split(b)
    dot = lambda u, v: lax.dot_general(u, v, (dims, ((), ())), preferred_element_type=jnp.float32)
    return dot(a_hi, b_hi) + (dot(a_hi, b_lo) + dot(a_lo, b_hi))


def _nt_exact(a, b):
    return _three_products(a, b, ((1,), (1,)))


def _nn_exact(a, b):
    return _three_products(a, b, ((1,), (0,)))


def _greet_group(n, leaf, me):
    barrier = pltpu.get_barrier_semaphore()
    for r in range(n):
        @pl.when(me != r)
        def _():
            pl.semaphore_signal(barrier, inc=1, device_id=(leaf, r), device_id_type=MESH)
    pl.semaphore_wait(barrier, n - 1)


def _block_copy(halves, q, dest, send_sem, recv_sem, leaf):
    return pltpu.make_async_remote_copy(
        src_ref=halves.at[q],
        dst_ref=halves.at[q],
        send_sem=send_sem,
        recv_sem=recv_sem.at[q],
        device_id=(leaf, dest),
        device_id_type=MESH,
    )


def _send_block(n, halves, s, solved, sol_ref, send_sem, recv_sem, leaf, dests):
    sol_ref[...] = solved
    halves[s] = solved.astype(jnp.bfloat16)
    for k in range(1, n):
        dest, live = dests(s, k)
        @pl.when(live)
        def _():
            _block_copy(halves, s, dest, send_sem.at[k], recv_sem, leaf).start()
            if k == 1:
                _block_copy(halves, s, dest, send_sem.at[k], recv_sem, leaf).wait_send()
    for k in range(2, n):
        dest, live = dests(s, k)
        @pl.when(live)
        def _():
            _block_copy(halves, s, dest, send_sem.at[k], recv_sem, leaf).wait_send()


def _through(y, hi_ref, lo_ref):
    return _nn(y, hi_ref[...]) + _nn(y, lo_ref[...])


def sep_forward_kernel(n, rhs_ref, part_ref, inv_ref, blocks_ref, hi_ref, lo_ref, sol_ref, halves, resid, base, send_sem, recv_sem, arrived, local_sem, give_sem, take_sem):
    me = lax.axis_index("grp")
    leaf = lax.axis_index("leaf")
    _greet_group(n, leaf, me)

    def give(dest):
        return pltpu.make_async_remote_copy(
            part_ref.at[dest], arrived.at[me], give_sem.at[dest], take_sem.at[me], device_id=(leaf, dest), device_id_type=MESH
        )

    own = pltpu.make_async_copy(part_ref.at[me], arrived.at[me], local_sem.at[0])
    own.start()
    for dest in range(n):
        @pl.when(me != dest)
        def _():
            give(dest).start()
    own.wait()
    for src in range(n):
        @pl.when(me != src)
        def _():
            pltpu.make_async_remote_copy(
                part_ref.at[src], arrived.at[src], give_sem.at[src], take_sem.at[src], device_id=(leaf, src), device_id_type=MESH
            ).wait_recv()
    total = arrived[0].astype(jnp.float32)
    for src in range(1, n):
        total = total + arrived[src].astype(jnp.float32)
    resid[...] = rhs_ref[...] - total
    for dest in range(n):
        @pl.when(me != dest)
        def _():
            give(dest).wait_send()

    dests = lambda s, k: (s + k, s + k < n)

    @pl.when(me == 0)
    def _():
        _send_block(n, halves, 0, _nt_exact(resid[...], inv_ref[...]), sol_ref, send_sem, recv_sem, leaf, dests)

    @pl.when(me == 1)
    def _():
        base[...] = _nt_exact(resid[...], inv_ref[...])

    def step(q, carry):
        @pl.when(me == q + 1)
        def _():
            _block_copy(halves, q, q, send_sem.at[0], recv_sem, leaf).wait_recv()
            solved = base[...] - _through(halves[q], hi_ref, lo_ref)
            _send_block(n, halves, q + 1, solved, sol_ref, send_sem, recv_sem, leaf, dests)

        @pl.when(me > q + 1)
        def _():
            _block_copy(halves, q, q, send_sem.at[0], recv_sem, leaf).wait_recv()
            resid[...] = resid[...] - _nt(halves[q], blocks_ref[q])

            @pl.when(me == q + 2)
            def _():
                base[...] = _nt_exact(resid[...], inv_ref[...])

        return carry

    lax.fori_loop(0, n - 1, step, 0)


def sep_backward_kernel(n, start_ref, inv_ref, blocks_ref, hi_ref, lo_ref, sol_ref, table_ref, halves, resid, base, send_sem, recv_sem):
    me = lax.axis_index("grp")
    leaf = lax.axis_index("leaf")
    _greet_group(n, leaf, me)
    resid[...] = start_ref[...]
    dests = lambda s, k: (s - k, s - k >= 0)

    @pl.when(me == n - 1)
    def _():
        _send_block(n, halves, n - 1, _nn_exact(resid[...], inv_ref[...]), sol_ref, send_sem, recv_sem, leaf, dests)

    @pl.when(me == n - 2)
    def _():
        base[...] = _nn_exact(resid[...], inv_ref[...])

    def step(s, carry):
        q = n - 1 - s

        @pl.when(me < q)
        def _():
            _block_copy(halves, q, q, send_sem.at[0], recv_sem, leaf).wait_recv()

        @pl.when(me == q - 1)
        def _():
            solved = base[...] - _through(halves[q], hi_ref, lo_ref)
            _send_block(n, halves, q - 1, solved, sol_ref, send_sem, recv_sem, leaf, dests)

        @pl.when(me < q - 1)
        def _():
            resid[...] = resid[...] - _nn(halves[q], blocks_ref[q])

            @pl.when(me == q - 2)
            def _():
                base[...] = _nn_exact(resid[...], inv_ref[...])

        return carry

    lax.fori_loop(0, n - 1, step, 0)
    for k in range(1, n):
        @pl.when(me + k < n)
        def _():
            _block_copy(halves, me, me + k, send_sem.at[k], recv_sem, leaf).start()
    for q in range(n):
        @pl.when(q < me)
        def _():
            _block_copy(halves, q, q, send_sem.at[0], recv_sem, leaf).wait_recv()
    for k in range(1, n):
        @pl.when(me + k < n)
        def _():
            _block_copy(halves, me, me + k, send_sem.at[k], recv_sem, leaf).wait_send()
    table_ref[...] = halves[...]


def sep_solve(kind, start, inv, blocks, hi, lo, n):
    rows, width = (start[0] if kind == "forward" else start).shape
    vmem = pl.BlockSpec(memory_space=pltpu.VMEM)
    scratch = [
        pltpu.VMEM((n, rows, width), jnp.bfloat16),
        pltpu.VMEM((rows, width), jnp.float32),
        pltpu.VMEM((rows, width), jnp.float32),
        pltpu.SemaphoreType.DMA((n,)),
        pltpu.SemaphoreType.DMA((n,)),
    ]
    sol_shape = jax.ShapeDtypeStruct((rows, width), jnp.float32)
    params = dict(has_side_effects=True, vmem_limit_bytes=48 * 1024 * 1024)
    if kind == "forward":
        rhs, parts = start
        return pl.pallas_call(
            functools.partial(sep_forward_kernel, n),
            out_shape=sol_shape,
            in_specs=[vmem] * 6,
            out_specs=vmem,
            scratch_shapes=scratch
            + [
                pltpu.VMEM(parts.shape, parts.dtype),
                pltpu.SemaphoreType.DMA((1,)),
                pltpu.SemaphoreType.DMA((n,)),
                pltpu.SemaphoreType.DMA((n,)),
            ],
            compiler_params=pltpu.CompilerParams(collective_id=0, **params),
        )(rhs, parts, inv, blocks, hi, lo)
    return pl.pallas_call(
        functools.partial(sep_backward_kernel, n),
        out_shape=(sol_shape, jax.ShapeDtypeStruct((n, rows, width), jnp.bfloat16)),
        in_specs=[vmem] * 5,
        out_specs=(vmem, vmem),
        scratch_shapes=scratch,
        compiler_params=pltpu.CompilerParams(collective_id=1, **params),
    )(start, inv, blocks, hi, lo)


def split_pair(matrix):
    hi = matrix.astype(jnp.bfloat16)
    lo = (matrix - hi.astype(jnp.float32)).astype(jnp.bfloat16)
    return hi, lo


def _three_pass(x, hi, lo, dims):
    x_hi = x.astype(jnp.bfloat16)
    x_lo = (x - x_hi.astype(jnp.float32)).astype(jnp.bfloat16)
    dot = lambda u, v: lax.dot_general(u, v, (dims, ((), ())), preferred_element_type=jnp.float32)
    return dot(x_hi, hi) + (dot(x_hi, lo) + dot(x_lo, hi))


def top_solve_kernel(nt, span, start_ref, hi_ref, lo_ref, lower_ref, coef_ref, half_ref, fwd_half, fwd_full):
    for t in range(nt):
        cols = slice(t * span, (t + 1) * span)
        residue = start_ref[:, cols]
        if t > 0:
            residue = residue - _nt(fwd_half[:, : t * span], lower_ref[cols, : t * span])
        solved = _three_pass(residue, hi_ref[t], lo_ref[t], ((1,), (1,)))
        fwd_full[:, cols] = solved
        fwd_half[:, cols] = solved.astype(jnp.bfloat16)
    for t in reversed(range(nt)):
        cols = slice(t * span, (t + 1) * span)
        residue = fwd_full[:, cols]
        if t < nt - 1:
            residue = residue - _nn(half_ref[:, (t + 1) * span :], lower_ref[(t + 1) * span :, cols])
        solved = _three_pass(residue, hi_ref[t], lo_ref[t], ((1,), (0,)))
        coef_ref[:, cols] = solved
        half_ref[:, cols] = solved.astype(jnp.bfloat16)


def top_solve(top_start, top_inverse, top_lower):
    nt, span = top_inverse.shape[0], top_inverse.shape[1]
    rows, width = top_start.shape
    vmem = pl.BlockSpec(memory_space=pltpu.VMEM)
    return pl.pallas_call(
        functools.partial(top_solve_kernel, nt, span),
        out_shape=(
            jax.ShapeDtypeStruct((rows, width), jnp.float32),
            jax.ShapeDtypeStruct((rows, width), jnp.bfloat16),
        ),
        in_specs=[vmem] * 4,
        out_specs=(vmem, vmem),
        scratch_shapes=[
            pltpu.VMEM((rows, width), jnp.bfloat16),
            pltpu.VMEM((rows, width), jnp.float32),
        ],
        compiler_params=pltpu.CompilerParams(vmem_limit_bytes=48 * 1024 * 1024),
    )(top_start, *split_pair(top_inverse), top_lower)


def evaluate_kernel(slots, pattern_ref, coef_ref, centre_ref, column_ref, out_ref, acc, spread):
    m = pl.program_id(0)
    acc[...] = jnp.zeros_like(acc)
    column = column_ref[0]
    width = centre_ref.shape[2]
    for comp in range(3):
        spread[comp] = jnp.broadcast_to(column[:, comp : comp + 1], (column.shape[0], width))

    def one_slot(s, carry):
        @pl.when(pattern_ref[m, s] != 0)
        def _():
            centre = centre_ref[s]
            dist = None
            for comp in range(3):
                delta = centre[comp : comp + 1, :] - spread[comp]
                dist = delta * delta if dist is None else dist + delta * delta
            weight = jnp.maximum(1.0 - dist * (1.0 / support_sq), 0.0)
            kernel = (weight * weight * weight).astype(jnp.bfloat16)
            acc[...] += _nt(coef_ref[s], kernel)

        return carry

    lax.fori_loop(0, slots, one_slot, 0)
    out_ref[...] = acc[...]


def evaluate_all(coef_all, centre_all, point_columns, pattern):
    slots, rows, span = coef_all.shape
    blocks = point_columns.shape[0]
    full = lambda shape: pl.BlockSpec(shape, lambda m, pat: (0,) * len(shape))
    grid_spec = pltpu.PrefetchScalarGridSpec(
        num_scalar_prefetch=1,
        grid=(blocks,),
        in_specs=[
            full(coef_all.shape),
            full(centre_all.shape),
            pl.BlockSpec((1, span, point_columns.shape[2]), lambda m, pat: (m, 0, 0)),
        ],
        out_specs=pl.BlockSpec((rows, span), lambda m, pat: (0, m)),
        scratch_shapes=[
            pltpu.VMEM((rows, span), jnp.float32),
            pltpu.VMEM((3, span, centre_all.shape[2]), jnp.float32),
        ],
    )
    return pl.pallas_call(
        functools.partial(evaluate_kernel, slots),
        out_shape=jax.ShapeDtypeStruct((rows, blocks * span), jnp.float32),
        grid_spec=grid_spec,
    )(pattern, coef_all, centre_all, point_columns)


def top_reduce_kernel(n, groups, span, term_ref, total_ref, parts_a, parts_b, gathered, local_sem, send_a, recv_a, send_b, recv_b, send_c, recv_c):
    me = lax.axis_index("grp")
    leaf = lax.axis_index("leaf")
    barrier = pltpu.get_barrier_semaphore()
    for r in range(n):
        @pl.when(me != r)
        def _():
            pl.semaphore_signal(barrier, inc=1, device_id=(leaf, r), device_id_type=MESH)
    for g in range(groups):
        @pl.when(leaf != g)
        def _():
            pl.semaphore_signal(barrier, inc=1, device_id=(g, me), device_id_type=MESH)
    pl.semaphore_wait(barrier, n - 1 + groups - 1)

    def column(q):
        return term_ref.at[:, pl.ds(pl.multiple_of(q * span, span), span)]

    def copy_a(k):
        dest = lax.rem(me + k, n)
        return pltpu.make_async_remote_copy(
            column(dest), parts_a.at[me], send_a.at[k], recv_a.at[me], device_id=(leaf, dest), device_id_type=MESH
        )

    def wait_a(k):
        src = lax.rem(me + n - k, n)
        pltpu.make_async_remote_copy(
            column(src), parts_a.at[src], send_a.at[0], recv_a.at[src], device_id=(leaf, src), device_id_type=MESH
        ).wait_recv()

    own = pltpu.make_async_copy(column(me), parts_a.at[me], local_sem.at[0])
    own.start()
    for k in range(1, n):
        copy_a(k).start()
    own.wait()
    for k in range(1, n):
        wait_a(k)
    for k in range(1, n):
        copy_a(k).wait_send()
    total = parts_a[0]
    for q in range(1, n):
        total = total + parts_a[q]
    parts_b[leaf] = total

    def copy_b(k):
        dest = lax.rem(leaf + k, groups)
        return pltpu.make_async_remote_copy(
            parts_b.at[leaf], parts_b.at[leaf], send_b.at[k], recv_b.at[leaf], device_id=(dest, me), device_id_type=MESH
        )

    for k in range(1, groups):
        copy_b(k).start()
    for k in range(1, groups):
        src = lax.rem(leaf + groups - k, groups)
        pltpu.make_async_remote_copy(
            parts_b.at[src], parts_b.at[src], send_b.at[0], recv_b.at[src], device_id=(src, me), device_id_type=MESH
        ).wait_recv()
    for k in range(1, groups):
        copy_b(k).wait_send()
    summed = parts_b[0]
    for g in range(1, groups):
        summed = summed + parts_b[g]
    gathered[me] = summed

    def copy_c(k):
        dest = lax.rem(me + k, n)
        return pltpu.make_async_remote_copy(
            gathered.at[me], gathered.at[me], send_c.at[k], recv_c.at[me], device_id=(leaf, dest), device_id_type=MESH
        )

    for k in range(1, n):
        copy_c(k).start()
    for k in range(1, n):
        src = lax.rem(me + n - k, n)
        pltpu.make_async_remote_copy(
            gathered.at[src], gathered.at[src], send_c.at[0], recv_c.at[src], device_id=(leaf, src), device_id_type=MESH
        ).wait_recv()
    for k in range(1, n):
        copy_c(k).wait_send()
    for q in range(n):
        total_ref[:, q * span : (q + 1) * span] = gathered[q]


def top_reduce(term, n, groups):
    rows, width = term.shape
    span = width // n
    vmem = pl.BlockSpec(memory_space=pltpu.VMEM)
    return pl.pallas_call(
        functools.partial(top_reduce_kernel, n, groups, span),
        out_shape=jax.ShapeDtypeStruct((rows, width), jnp.float32),
        in_specs=[vmem],
        out_specs=vmem,
        scratch_shapes=[
            pltpu.VMEM((n, rows, span), jnp.float32),
            pltpu.VMEM((groups, rows, span), jnp.float32),
            pltpu.VMEM((n, rows, span), jnp.float32),
            pltpu.SemaphoreType.DMA((1,)),
            pltpu.SemaphoreType.DMA((n,)),
            pltpu.SemaphoreType.DMA((n,)),
            pltpu.SemaphoreType.DMA((groups,)),
            pltpu.SemaphoreType.DMA((groups,)),
            pltpu.SemaphoreType.DMA((n,)),
            pltpu.SemaphoreType.DMA((n,)),
        ],
        compiler_params=pltpu.CompilerParams(collective_id=2, has_side_effects=True),
    )(term)


def exchange_kernel(n, coef_ref, centre_ref, coef_out, centre_out, coef_buf, centre_buf, local_sem, send_sem, recv_sem):
    me = lax.axis_index("grp")
    leaf = lax.axis_index("leaf")
    _greet_group(n, leaf, me)
    pairs = ((coef_ref, coef_buf), (centre_ref, centre_buf))

    def push(kind, k):
        source, buf = pairs[kind]
        dest = lax.rem(me + k, n)
        return pltpu.make_async_remote_copy(
            source.at[dest], buf.at[me], send_sem.at[kind, k], recv_sem.at[kind, me], device_id=(leaf, dest), device_id_type=MESH
        )

    owns = [pltpu.make_async_copy(source.at[me], buf.at[me], local_sem.at[kind]) for kind, (source, buf) in enumerate(pairs)]
    for own in owns:
        own.start()
    for k in range(1, n):
        for kind in range(2):
            push(kind, k).start()
    for own in owns:
        own.wait()
    for k in range(1, n):
        src = lax.rem(me + n - k, n)
        for kind, (source, buf) in enumerate(pairs):
            pltpu.make_async_remote_copy(
                source.at[src], buf.at[src], send_sem.at[kind, 0], recv_sem.at[kind, src], device_id=(leaf, src), device_id_type=MESH
            ).wait_recv()
    for k in range(1, n):
        for kind in range(2):
            push(kind, k).wait_send()
    coef_out[...] = coef_buf[...]
    centre_out[...] = centre_buf[...]


def exchange(send_coef, send_centre, n):
    vmem = pl.BlockSpec(memory_space=pltpu.VMEM)
    return pl.pallas_call(
        functools.partial(exchange_kernel, n),
        out_shape=(
            jax.ShapeDtypeStruct(send_coef.shape, send_coef.dtype),
            jax.ShapeDtypeStruct(send_centre.shape, send_centre.dtype),
        ),
        in_specs=[vmem] * 2,
        out_specs=(vmem, vmem),
        scratch_shapes=[
            pltpu.VMEM(send_coef.shape, send_coef.dtype),
            pltpu.VMEM(send_centre.shape, send_centre.dtype),
            pltpu.SemaphoreType.DMA((2,)),
            pltpu.SemaphoreType.DMA((2, n)),
            pltpu.SemaphoreType.DMA((2, n)),
        ],
        compiler_params=pltpu.CompilerParams(collective_id=3, has_side_effects=True),
    )(send_coef, send_centre)


def slot_ranks(dest_rows, grp_size):
    onehot = (dest_rows[..., None] == jnp.arange(grp_size)).astype(jnp.int32)
    before = jnp.cumsum(onehot, axis=-2) - onehot
    return jnp.sum(before * onehot, axis=-1)


def evaluate(coef_all, centre_all, block_points, block_mask):
    dist = jnp.zeros((centre_all.shape[0], centre_all.shape[2], block_points.shape[1]), jnp.float32)
    for comp in range(3):
        delta = centre_all[:, comp, :, None] - block_points[None, comp, None, :]
        dist = dist + delta * delta
    weight = jnp.maximum(1.0 - dist / support_sq, 0.0) ** 3
    kernel = (weight * block_mask.astype(jnp.float32)[:, None, None]).astype(jnp.bfloat16)
    return jnp.einsum("krs,ksp->rp", coef_all, kernel, preferred_element_type=jnp.float32)


def on_device(
    rhs_leaf,
    rhs_sep,
    rhs_top,
    leaf_inverse,
    leaf_coupling,
    leaf_targets,
    sep_inverse,
    sep_blocks,
    top_coupling,
    top_inverse,
    top_lower,
    dest_map,
    centers,
    points,
    eval_pattern,
):
    grp_size = lax.axis_size("grp")
    my_index = lax.axis_index("grp")
    blocks_here = leaf_inverse.shape[0]
    snapshots = rhs_leaf.shape[0]
    span = leaf_inverse.shape[1]
    slot_count = CAP
    leaf_rhs = rhs_leaf.reshape(snapshots, blocks_here, span).transpose(1, 0, 2)
    leaf_sol = jnp.einsum("nrs,nts->nrt", leaf_rhs, leaf_inverse, precision=three_pass)
    leaf_half = leaf_sol.astype(jnp.bfloat16)
    partial_value = jnp.einsum(
        "nrs,ncbs->ncrb", leaf_half, leaf_coupling, preferred_element_type=jnp.float32
    )
    onehot = (leaf_targets[:, :, None] == jnp.arange(grp_size)[None, None, :]).astype(jnp.float32)
    picked = onehot
    parts = jnp.einsum("ncq,ncrb->qrb", picked, partial_value, precision=three_pass).astype(jnp.bfloat16)
    inverse_own = sep_inverse[0]
    own_blocks = sep_blocks[0]
    before = lax.dynamic_index_in_dim(own_blocks, jnp.maximum(my_index - 1, 0), 0, keepdims=False)
    fwd_hi, fwd_lo = split_pair(
        jnp.dot(before.astype(jnp.float32).T, inverse_own.T, precision=three_pass)
    )
    after = lax.dynamic_index_in_dim(own_blocks, jnp.minimum(my_index + 1, grp_size - 1), 0, keepdims=False)
    bwd_hi, bwd_lo = split_pair(jnp.dot(after.astype(jnp.float32), inverse_own, precision=three_pass))
    sep_sol = sep_solve("forward", (rhs_sep, parts), inverse_own, own_blocks, fwd_hi, fwd_lo, grp_size)
    sep_half = sep_sol.astype(jnp.bfloat16)
    top_term = jnp.dot(sep_half, top_coupling, preferred_element_type=jnp.float32)
    top_total = top_reduce(top_term, grp_size, lax.axis_size("leaf"))
    top_start = rhs_top - top_total
    coef_top, top_half = top_solve(top_start, top_inverse, top_lower)
    back_start = sep_sol - lax.dot_general(
        top_half, top_coupling, (((1,), (1,)), ((), ())), preferred_element_type=jnp.float32
    )

    coef_sep, known_table = sep_solve(
        "backward", back_start, inverse_own, own_blocks, bwd_hi, bwd_lo, grp_size
    )
    picked = jnp.einsum(
        "ncq,qrb->ncrb",
        onehot.astype(jnp.bfloat16),
        known_table,
        preferred_element_type=jnp.float32,
    ).astype(jnp.bfloat16)
    reduced = jnp.einsum(
        "ncrb,ncbs->nrs", picked, leaf_coupling, preferred_element_type=jnp.float32
    )
    leaf_coef = jnp.einsum("nrs,nst->nrt", leaf_sol - reduced, leaf_inverse, precision=three_pass)
    coef_leaf = leaf_coef.transpose(1, 0, 2).reshape(snapshots, blocks_here * span)
    leaf_out = leaf_coef.astype(jnp.bfloat16)
    slot_ids = jnp.arange(slot_count)
    grp_ids = jnp.arange(grp_size)
    own_dest = dest_map[:, 0]
    slot_rank = slot_ranks(own_dest[None, :], grp_size)[0]
    selector = (own_dest[None, None, :] == grp_ids[:, None, None]) & (
        slot_rank[None, None, :] == slot_ids[None, :, None]
    )
    send_coef = jnp.einsum(
        "dkj,jrt->dkrt", selector.astype(jnp.bfloat16), leaf_out, preferred_element_type=jnp.float32
    ).astype(jnp.bfloat16)
    send_centre = jnp.einsum(
        "dkj,jct->dkct", selector.astype(jnp.float32), centers, precision=highest
    )
    received, recv_centre = exchange(send_coef, send_centre, grp_size)
    slot_total = grp_size * slot_count
    coef_all = received.reshape(slot_total, snapshots, span)
    centre_all = recv_centre.reshape(slot_total, 3, span)
    point_blocks = eval_pattern.shape[0]
    point_columns = points[0].T.reshape(point_blocks, span, points.shape[1])
    values = evaluate_all(coef_all, centre_all, point_columns, eval_pattern)
    return (coef_leaf, coef_sep, coef_top, values)


def solution(mesh):
    in_specs = (
        P(None, ("leaf", "grp")),
        P(None, ("leaf", "grp")),
        P(),
        P(("leaf", "grp"), None, None),
        P(("leaf", "grp"), None, None, None),
        P(("leaf", "grp"), None),
        P(("leaf", "grp"), None, None),
        P(("leaf", "grp"), None, None, None),
        P(("leaf", "grp"), None),
        P(),
        P(),
        P(("leaf", "grp"), None),
        P(("leaf", "grp"), None, None),
        P(("leaf", "grp"), None, None),
        P(("leaf", "grp"), None),
    )
    out_specs = (P(None, ("leaf", "grp")), P(None, ("leaf", "grp")), P(), P(None, ("leaf", "grp")))
    return jax.shard_map(
        on_device, mesh=mesh, in_specs=in_specs, out_specs=out_specs, check_vma=False
    )
```

```python
import functools

import jax
import jax.numpy as jnp
from jax import lax
from jax.sharding import PartitionSpec as P
from jax.experimental import pallas as pl
from jax.experimental.pallas import tpu as pltpu

MESH = pl.DeviceIdType.MESH

CAP = 2


highest = lax.Precision.HIGHEST
three_pass = lax.Precision.HIGH
support_sq = 0.25


def split_up(shard, dim, peers):
    dims = shard.shape
    pieces = shard.reshape(*dims[:dim], peers, dims[dim] // peers, *dims[dim + 1 :])
    return jnp.moveaxis(pieces, dim, 0)


def sum_at_owner(shard, axis, dim):
    pieces = split_up(shard, dim, lax.axis_size(axis))
    arrived = lax.all_to_all(pieces, axis, split_axis=0, concat_axis=0, tiled=True)
    return arrived.astype(jnp.float32).sum(axis=0)


def from_root(shard, axis, root):
    return lax.dynamic_index_in_dim(lax.all_gather(shard, axis), root, 0, keepdims=False)


def copy_for_each(shard, axis):
    copies = jnp.broadcast_to(shard, (lax.axis_size(axis), *shard.shape))
    return lax.all_to_all(copies, axis, split_axis=0, concat_axis=0, tiled=True)


def over_copies(shard, axis):
    return copy_for_each(shard, axis).astype(jnp.float32).sum(axis=0)


def joined_along(pieces, dim):
    dims = list(pieces.shape[1:])
    dims[dim] *= pieces.shape[0]
    return jnp.moveaxis(pieces, 0, dim).reshape(dims)


def gather_directly(shard, axis, dim):
    pieces = copy_for_each(shard, axis)
    return joined_along(pieces, dim)


def _nt(a, b):
    return lax.dot_general(a, b, (((1,), (1,)), ((), ())), preferred_element_type=jnp.float32)


def _nn(a, b):
    return lax.dot_general(a, b, (((1,), (0,)), ((), ())), preferred_element_type=jnp.float32)


def _split(x):
    hi = x.astype(jnp.bfloat16)
    return hi, (x - hi.astype(jnp.float32)).astype(jnp.bfloat16)


def _three_products(a, b, dims):
    a_hi, a_lo = _split(a)
    b_hi, b_lo = _split(b)
    dot = lambda u, v: lax.dot_general(u, v, (dims, ((), ())), preferred_element_type=jnp.float32)
    return dot(a_hi, b_hi) + (dot(a_hi, b_lo) + dot(a_lo, b_hi))


def _nt_exact(a, b):
    return _three_products(a, b, ((1,), (1,)))


def _nn_exact(a, b):
    return _three_products(a, b, ((1,), (0,)))


def _greet_group(n, leaf, me):
    barrier = pltpu.get_barrier_semaphore()
    for r in range(n):
        @pl.when(me != r)
        def _():
            pl.semaphore_signal(barrier, inc=1, device_id=(leaf, r), device_id_type=MESH)
    pl.semaphore_wait(barrier, n - 1)


def _block_copy(halves, q, dest, send_sem, recv_sem, leaf):
    return pltpu.make_async_remote_copy(
        src_ref=halves.at[q],
        dst_ref=halves.at[q],
        send_sem=send_sem,
        recv_sem=recv_sem.at[q],
        device_id=(leaf, dest),
        device_id_type=MESH,
    )


def _send_block(n, halves, s, solved, sol_ref, send_sem, recv_sem, leaf, dests):
    sol_ref[...] = solved
    halves[s] = solved.astype(jnp.bfloat16)
    for k in range(1, n):
        dest, live = dests(s, k)
        @pl.when(live)
        def _():
            _block_copy(halves, s, dest, send_sem.at[k], recv_sem, leaf).start()
            if k == 1:
                _block_copy(halves, s, dest, send_sem.at[k], recv_sem, leaf).wait_send()
    for k in range(2, n):
        dest, live = dests(s, k)
        @pl.when(live)
        def _():
            _block_copy(halves, s, dest, send_sem.at[k], recv_sem, leaf).wait_send()


def _through(y, hi_ref, lo_ref):
    return _nn(y, hi_ref[...]) + _nn(y, lo_ref[...])


def sep_forward_kernel(n, rhs_ref, part_ref, inv_ref, blocks_hbm, hi_ref, lo_ref, sol_ref, halves, resid, base, send_sem, recv_sem, blocks_ref, block_sem, arrived, local_sem, give_sem, take_sem):
    me = lax.axis_index("grp")
    leaf = lax.axis_index("leaf")
    fetch = pltpu.make_async_copy(blocks_hbm, blocks_ref, block_sem.at[0])
    fetch.start()
    _greet_group(n, leaf, me)

    def give(dest):
        return pltpu.make_async_remote_copy(
            part_ref.at[dest], arrived.at[me], give_sem.at[dest], take_sem.at[me], device_id=(leaf, dest), device_id_type=MESH
        )

    own = pltpu.make_async_copy(part_ref.at[me], arrived.at[me], local_sem.at[0])
    own.start()
    for dest in range(n):
        @pl.when(me != dest)
        def _():
            give(dest).start()
    own.wait()
    for src in range(n):
        @pl.when(me != src)
        def _():
            pltpu.make_async_remote_copy(
                part_ref.at[src], arrived.at[src], give_sem.at[src], take_sem.at[src], device_id=(leaf, src), device_id_type=MESH
            ).wait_recv()
    total = arrived[0].astype(jnp.float32)
    for src in range(1, n):
        total = total + arrived[src].astype(jnp.float32)
    resid[...] = rhs_ref[...] - total
    for dest in range(n):
        @pl.when(me != dest)
        def _():
            give(dest).wait_send()

    dests = lambda s, k: (s + k, s + k < n)
    fetch.wait()

    @pl.when(me == 0)
    def _():
        _send_block(n, halves, 0, _nt_exact(resid[...], inv_ref[...]), sol_ref, send_sem, recv_sem, leaf, dests)

    @pl.when(me == 1)
    def _():
        base[...] = _nt_exact(resid[...], inv_ref[...])

    def step(q, carry):
        @pl.when(me == q + 1)
        def _():
            _block_copy(halves, q, q, send_sem.at[0], recv_sem, leaf).wait_recv()
            solved = base[...] - _through(halves[q], hi_ref, lo_ref)
            _send_block(n, halves, q + 1, solved, sol_ref, send_sem, recv_sem, leaf, dests)

        @pl.when(me > q + 1)
        def _():
            _block_copy(halves, q, q, send_sem.at[0], recv_sem, leaf).wait_recv()
            resid[...] = resid[...] - _nt(halves[q], blocks_ref[q])

            @pl.when(me == q + 2)
            def _():
                base[...] = _nt_exact(resid[...], inv_ref[...])

        return carry

    lax.fori_loop(0, n - 1, step, 0)


def sep_backward_kernel(n, start_ref, inv_ref, blocks_hbm, hi_ref, lo_ref, sol_ref, table_ref, halves, resid, base, send_sem, recv_sem, blocks_ref, block_sem):
    me = lax.axis_index("grp")
    leaf = lax.axis_index("leaf")
    fetch = pltpu.make_async_copy(blocks_hbm, blocks_ref, block_sem.at[0])
    fetch.start()
    _greet_group(n, leaf, me)
    resid[...] = start_ref[...]
    dests = lambda s, k: (s - k, s - k >= 0)
    fetch.wait()

    @pl.when(me == n - 1)
    def _():
        _send_block(n, halves, n - 1, _nn_exact(resid[...], inv_ref[...]), sol_ref, send_sem, recv_sem, leaf, dests)

    @pl.when(me == n - 2)
    def _():
        base[...] = _nn_exact(resid[...], inv_ref[...])

    def step(s, carry):
        q = n - 1 - s

        @pl.when(me < q)
        def _():
            _block_copy(halves, q, q, send_sem.at[0], recv_sem, leaf).wait_recv()

        @pl.when(me == q - 1)
        def _():
            solved = base[...] - _through(halves[q], hi_ref, lo_ref)
            _send_block(n, halves, q - 1, solved, sol_ref, send_sem, recv_sem, leaf, dests)

        @pl.when(me < q - 1)
        def _():
            resid[...] = resid[...] - _nn(halves[q], blocks_ref[q])

            @pl.when(me == q - 2)
            def _():
                base[...] = _nn_exact(resid[...], inv_ref[...])

        return carry

    lax.fori_loop(0, n - 1, step, 0)
    for k in range(1, n):
        @pl.when(me + k < n)
        def _():
            _block_copy(halves, me, me + k, send_sem.at[k], recv_sem, leaf).start()
    for q in range(n):
        @pl.when(q < me)
        def _():
            _block_copy(halves, q, q, send_sem.at[0], recv_sem, leaf).wait_recv()
    for k in range(1, n):
        @pl.when(me + k < n)
        def _():
            _block_copy(halves, me, me + k, send_sem.at[k], recv_sem, leaf).wait_send()
    table_ref[...] = halves[...]


def sep_solve(kind, start, inv, blocks, hi, lo, n):
    rows, width = (start[0] if kind == "forward" else start).shape
    vmem = pl.BlockSpec(memory_space=pltpu.VMEM)
    scratch = [
        pltpu.VMEM((n, rows, width), jnp.bfloat16),
        pltpu.VMEM((rows, width), jnp.float32),
        pltpu.VMEM((rows, width), jnp.float32),
        pltpu.SemaphoreType.DMA((n,)),
        pltpu.SemaphoreType.DMA((n,)),
        pltpu.VMEM(blocks.shape, blocks.dtype),
        pltpu.SemaphoreType.DMA((1,)),
    ]
    anywhere = pl.BlockSpec(memory_space=pl.ANY)
    sol_shape = jax.ShapeDtypeStruct((rows, width), jnp.float32)
    params = dict(has_side_effects=True, vmem_limit_bytes=48 * 1024 * 1024)
    if kind == "forward":
        rhs, parts = start
        return pl.pallas_call(
            functools.partial(sep_forward_kernel, n),
            out_shape=sol_shape,
            in_specs=[vmem, vmem, vmem, anywhere, vmem, vmem],
            out_specs=vmem,
            scratch_shapes=scratch
            + [
                pltpu.VMEM(parts.shape, parts.dtype),
                pltpu.SemaphoreType.DMA((1,)),
                pltpu.SemaphoreType.DMA((n,)),
                pltpu.SemaphoreType.DMA((n,)),
            ],
            compiler_params=pltpu.CompilerParams(collective_id=0, **params),
        )(rhs, parts, inv, blocks, hi, lo)
    return pl.pallas_call(
        functools.partial(sep_backward_kernel, n),
        out_shape=(sol_shape, jax.ShapeDtypeStruct((n, rows, width), jnp.bfloat16)),
        in_specs=[vmem, vmem, anywhere, vmem, vmem],
        out_specs=(vmem, vmem),
        scratch_shapes=scratch,
        compiler_params=pltpu.CompilerParams(collective_id=1, **params),
    )(start, inv, blocks, hi, lo)


def split_pair(matrix):
    hi = matrix.astype(jnp.bfloat16)
    lo = (matrix - hi.astype(jnp.float32)).astype(jnp.bfloat16)
    return hi, lo


def _three_pass(x, hi, lo, dims):
    x_hi = x.astype(jnp.bfloat16)
    x_lo = (x - x_hi.astype(jnp.float32)).astype(jnp.bfloat16)
    dot = lambda u, v: lax.dot_general(u, v, (dims, ((), ())), preferred_element_type=jnp.float32)
    return dot(x_hi, hi) + (dot(x_hi, lo) + dot(x_lo, hi))


def top_solve_kernel(nt, span, start_ref, hi_ref, lo_ref, lower_ref, coef_ref, half_ref, fwd_half, fwd_full):
    for t in range(nt):
        cols = slice(t * span, (t + 1) * span)
        residue = start_ref[:, cols]
        if t > 0:
            residue = residue - _nt(fwd_half[:, : t * span], lower_ref[cols, : t * span])
        solved = _three_pass(residue, hi_ref[t], lo_ref[t], ((1,), (1,)))
        fwd_full[:, cols] = solved
        fwd_half[:, cols] = solved.astype(jnp.bfloat16)
    for t in reversed(range(nt)):
        cols = slice(t * span, (t + 1) * span)
        residue = fwd_full[:, cols]
        if t < nt - 1:
            residue = residue - _nn(half_ref[:, (t + 1) * span :], lower_ref[(t + 1) * span :, cols])
        solved = _three_pass(residue, hi_ref[t], lo_ref[t], ((1,), (0,)))
        coef_ref[:, cols] = solved
        half_ref[:, cols] = solved.astype(jnp.bfloat16)


def top_solve(top_start, top_inverse, top_lower):
    nt, span = top_inverse.shape[0], top_inverse.shape[1]
    rows, width = top_start.shape
    vmem = pl.BlockSpec(memory_space=pltpu.VMEM)
    return pl.pallas_call(
        functools.partial(top_solve_kernel, nt, span),
        out_shape=(
            jax.ShapeDtypeStruct((rows, width), jnp.float32),
            jax.ShapeDtypeStruct((rows, width), jnp.bfloat16),
        ),
        in_specs=[vmem] * 4,
        out_specs=(vmem, vmem),
        scratch_shapes=[
            pltpu.VMEM((rows, width), jnp.bfloat16),
            pltpu.VMEM((rows, width), jnp.float32),
        ],
        compiler_params=pltpu.CompilerParams(vmem_limit_bytes=48 * 1024 * 1024),
    )(top_start, *split_pair(top_inverse), top_lower)


def evaluate_kernel(slots, pattern_ref, coef_ref, centre_ref, column_ref, out_ref, acc, spread):
    m = pl.program_id(0)
    acc[...] = jnp.zeros_like(acc)
    column = column_ref[0]
    width = centre_ref.shape[2]
    for comp in range(3):
        spread[comp] = jnp.broadcast_to(column[:, comp : comp + 1], (column.shape[0], width))

    def one_slot(s, carry):
        @pl.when(pattern_ref[m, s] != 0)
        def _():
            centre = centre_ref[s]
            dist = None
            for comp in range(3):
                delta = centre[comp : comp + 1, :] - spread[comp]
                dist = delta * delta if dist is None else dist + delta * delta
            weight = jnp.maximum(1.0 - dist * (1.0 / support_sq), 0.0)
            kernel = (weight * weight * weight).astype(jnp.bfloat16)
            acc[...] += _nt(coef_ref[s], kernel)

        return carry

    lax.fori_loop(0, slots, one_slot, 0)
    out_ref[...] = acc[...]


def evaluate_all(coef_all, centre_all, point_columns, pattern):
    slots, rows, span = coef_all.shape
    blocks = point_columns.shape[0]
    full = lambda shape: pl.BlockSpec(shape, lambda m, pat: (0,) * len(shape))
    grid_spec = pltpu.PrefetchScalarGridSpec(
        num_scalar_prefetch=1,
        grid=(blocks,),
        in_specs=[
            full(coef_all.shape),
            full(centre_all.shape),
            pl.BlockSpec((1, span, point_columns.shape[2]), lambda m, pat: (m, 0, 0)),
        ],
        out_specs=pl.BlockSpec((rows, span), lambda m, pat: (0, m)),
        scratch_shapes=[
            pltpu.VMEM((rows, span), jnp.float32),
            pltpu.VMEM((3, span, centre_all.shape[2]), jnp.float32),
        ],
    )
    return pl.pallas_call(
        functools.partial(evaluate_kernel, slots),
        out_shape=jax.ShapeDtypeStruct((rows, blocks * span), jnp.float32),
        grid_spec=grid_spec,
    )(pattern, coef_all, centre_all, point_columns)


def top_reduce_kernel(n, groups, span, term_ref, total_ref, parts_a, parts_b, gathered, local_sem, send_a, recv_a, send_b, recv_b, send_c, recv_c):
    me = lax.axis_index("grp")
    leaf = lax.axis_index("leaf")
    barrier = pltpu.get_barrier_semaphore()
    for r in range(n):
        @pl.when(me != r)
        def _():
            pl.semaphore_signal(barrier, inc=1, device_id=(leaf, r), device_id_type=MESH)
    for g in range(groups):
        @pl.when(leaf != g)
        def _():
            pl.semaphore_signal(barrier, inc=1, device_id=(g, me), device_id_type=MESH)
    pl.semaphore_wait(barrier, n - 1 + groups - 1)

    def column(q):
        return term_ref.at[:, pl.ds(pl.multiple_of(q * span, span), span)]

    def copy_a(k):
        dest = lax.rem(me + k, n)
        return pltpu.make_async_remote_copy(
            column(dest), parts_a.at[me], send_a.at[k], recv_a.at[me], device_id=(leaf, dest), device_id_type=MESH
        )

    def wait_a(k):
        src = lax.rem(me + n - k, n)
        pltpu.make_async_remote_copy(
            column(src), parts_a.at[src], send_a.at[0], recv_a.at[src], device_id=(leaf, src), device_id_type=MESH
        ).wait_recv()

    own = pltpu.make_async_copy(column(me), parts_a.at[me], local_sem.at[0])
    own.start()
    for k in range(1, n):
        copy_a(k).start()
    own.wait()
    for k in range(1, n):
        wait_a(k)
    for k in range(1, n):
        copy_a(k).wait_send()
    total = parts_a[0]
    for q in range(1, n):
        total = total + parts_a[q]
    parts_b[leaf] = total

    def copy_b(k):
        dest = lax.rem(leaf + k, groups)
        return pltpu.make_async_remote_copy(
            parts_b.at[leaf], parts_b.at[leaf], send_b.at[k], recv_b.at[leaf], device_id=(dest, me), device_id_type=MESH
        )

    for k in range(1, groups):
        copy_b(k).start()
    for k in range(1, groups):
        src = lax.rem(leaf + groups - k, groups)
        pltpu.make_async_remote_copy(
            parts_b.at[src], parts_b.at[src], send_b.at[0], recv_b.at[src], device_id=(src, me), device_id_type=MESH
        ).wait_recv()
    for k in range(1, groups):
        copy_b(k).wait_send()
    summed = parts_b[0]
    for g in range(1, groups):
        summed = summed + parts_b[g]
    gathered[me] = summed

    def copy_c(k):
        dest = lax.rem(me + k, n)
        return pltpu.make_async_remote_copy(
            gathered.at[me], gathered.at[me], send_c.at[k], recv_c.at[me], device_id=(leaf, dest), device_id_type=MESH
        )

    for k in range(1, n):
        copy_c(k).start()
    for k in range(1, n):
        src = lax.rem(me + n - k, n)
        pltpu.make_async_remote_copy(
            gathered.at[src], gathered.at[src], send_c.at[0], recv_c.at[src], device_id=(leaf, src), device_id_type=MESH
        ).wait_recv()
    for k in range(1, n):
        copy_c(k).wait_send()
    for q in range(n):
        total_ref[:, q * span : (q + 1) * span] = gathered[q]


def top_reduce(term, n, groups):
    rows, width = term.shape
    span = width // n
    vmem = pl.BlockSpec(memory_space=pltpu.VMEM)
    return pl.pallas_call(
        functools.partial(top_reduce_kernel, n, groups, span),
        out_shape=jax.ShapeDtypeStruct((rows, width), jnp.float32),
        in_specs=[vmem],
        out_specs=vmem,
        scratch_shapes=[
            pltpu.VMEM((n, rows, span), jnp.float32),
            pltpu.VMEM((groups, rows, span), jnp.float32),
            pltpu.VMEM((n, rows, span), jnp.float32),
            pltpu.SemaphoreType.DMA((1,)),
            pltpu.SemaphoreType.DMA((n,)),
            pltpu.SemaphoreType.DMA((n,)),
            pltpu.SemaphoreType.DMA((groups,)),
            pltpu.SemaphoreType.DMA((groups,)),
            pltpu.SemaphoreType.DMA((n,)),
            pltpu.SemaphoreType.DMA((n,)),
        ],
        compiler_params=pltpu.CompilerParams(collective_id=2, has_side_effects=True),
    )(term)


def exchange_kernel(n, coef_ref, centre_ref, coef_out, centre_out, coef_buf, centre_buf, local_sem, send_sem, recv_sem):
    me = lax.axis_index("grp")
    leaf = lax.axis_index("leaf")
    _greet_group(n, leaf, me)
    pairs = ((coef_ref, coef_buf), (centre_ref, centre_buf))

    def push(kind, k):
        source, buf = pairs[kind]
        dest = lax.rem(me + k, n)
        return pltpu.make_async_remote_copy(
            source.at[dest], buf.at[me], send_sem.at[kind, k], recv_sem.at[kind, me], device_id=(leaf, dest), device_id_type=MESH
        )

    owns = [pltpu.make_async_copy(source.at[me], buf.at[me], local_sem.at[kind]) for kind, (source, buf) in enumerate(pairs)]
    for own in owns:
        own.start()
    for k in range(1, n):
        for kind in range(2):
            push(kind, k).start()
    for own in owns:
        own.wait()
    for k in range(1, n):
        src = lax.rem(me + n - k, n)
        for kind, (source, buf) in enumerate(pairs):
            pltpu.make_async_remote_copy(
                source.at[src], buf.at[src], send_sem.at[kind, 0], recv_sem.at[kind, src], device_id=(leaf, src), device_id_type=MESH
            ).wait_recv()
    for k in range(1, n):
        for kind in range(2):
            push(kind, k).wait_send()
    coef_out[...] = coef_buf[...]
    centre_out[...] = centre_buf[...]


def exchange(send_coef, send_centre, n):
    vmem = pl.BlockSpec(memory_space=pltpu.VMEM)
    return pl.pallas_call(
        functools.partial(exchange_kernel, n),
        out_shape=(
            jax.ShapeDtypeStruct(send_coef.shape, send_coef.dtype),
            jax.ShapeDtypeStruct(send_centre.shape, send_centre.dtype),
        ),
        in_specs=[vmem] * 2,
        out_specs=(vmem, vmem),
        scratch_shapes=[
            pltpu.VMEM(send_coef.shape, send_coef.dtype),
            pltpu.VMEM(send_centre.shape, send_centre.dtype),
            pltpu.SemaphoreType.DMA((2,)),
            pltpu.SemaphoreType.DMA((2, n)),
            pltpu.SemaphoreType.DMA((2, n)),
        ],
        compiler_params=pltpu.CompilerParams(collective_id=3, has_side_effects=True),
    )(send_coef, send_centre)


def slot_ranks(dest_rows, grp_size):
    onehot = (dest_rows[..., None] == jnp.arange(grp_size)).astype(jnp.int32)
    before = jnp.cumsum(onehot, axis=-2) - onehot
    return jnp.sum(before * onehot, axis=-1)


def evaluate(coef_all, centre_all, block_points, block_mask):
    dist = jnp.zeros((centre_all.shape[0], centre_all.shape[2], block_points.shape[1]), jnp.float32)
    for comp in range(3):
        delta = centre_all[:, comp, :, None] - block_points[None, comp, None, :]
        dist = dist + delta * delta
    weight = jnp.maximum(1.0 - dist / support_sq, 0.0) ** 3
    kernel = (weight * block_mask.astype(jnp.float32)[:, None, None]).astype(jnp.bfloat16)
    return jnp.einsum("krs,ksp->rp", coef_all, kernel, preferred_element_type=jnp.float32)


def on_device(
    rhs_leaf,
    rhs_sep,
    rhs_top,
    leaf_inverse,
    leaf_coupling,
    leaf_targets,
    sep_inverse,
    sep_blocks,
    top_coupling,
    top_inverse,
    top_lower,
    dest_map,
    centers,
    points,
    eval_pattern,
):
    grp_size = lax.axis_size("grp")
    my_index = lax.axis_index("grp")
    blocks_here = leaf_inverse.shape[0]
    snapshots = rhs_leaf.shape[0]
    span = leaf_inverse.shape[1]
    slot_count = CAP
    leaf_rhs = rhs_leaf.reshape(snapshots, blocks_here, span).transpose(1, 0, 2)
    leaf_sol = jnp.einsum("nrs,nts->nrt", leaf_rhs, leaf_inverse, precision=three_pass)
    leaf_half = leaf_sol.astype(jnp.bfloat16)
    partial_value = jnp.einsum(
        "nrs,ncbs->ncrb", leaf_half, leaf_coupling, preferred_element_type=jnp.float32
    )
    onehot = (leaf_targets[:, :, None] == jnp.arange(grp_size)[None, None, :]).astype(jnp.float32)
    picked = onehot
    parts = jnp.einsum("ncq,ncrb->qrb", picked, partial_value, precision=three_pass).astype(jnp.bfloat16)
    inverse_own = sep_inverse[0]
    own_blocks = sep_blocks[0]
    before = lax.dynamic_index_in_dim(own_blocks, jnp.maximum(my_index - 1, 0), 0, keepdims=False)
    fwd_hi, fwd_lo = split_pair(
        jnp.dot(before.astype(jnp.float32).T, inverse_own.T, precision=three_pass)
    )
    after = lax.dynamic_index_in_dim(own_blocks, jnp.minimum(my_index + 1, grp_size - 1), 0, keepdims=False)
    bwd_hi, bwd_lo = split_pair(jnp.dot(after.astype(jnp.float32), inverse_own, precision=three_pass))
    sep_sol = sep_solve("forward", (rhs_sep, parts), inverse_own, own_blocks, fwd_hi, fwd_lo, grp_size)
    sep_half = sep_sol.astype(jnp.bfloat16)
    top_term = jnp.dot(sep_half, top_coupling, preferred_element_type=jnp.float32)
    top_total = top_reduce(top_term, grp_size, lax.axis_size("leaf"))
    top_start = rhs_top - top_total
    coef_top, top_half = top_solve(top_start, top_inverse, top_lower)
    back_start = sep_sol - lax.dot_general(
        top_half, top_coupling, (((1,), (1,)), ((), ())), preferred_element_type=jnp.float32
    )

    coef_sep, known_table = sep_solve(
        "backward", back_start, inverse_own, own_blocks, bwd_hi, bwd_lo, grp_size
    )
    picked = jnp.einsum(
        "ncq,qrb->ncrb",
        onehot.astype(jnp.bfloat16),
        known_table,
        preferred_element_type=jnp.float32,
    ).astype(jnp.bfloat16)
    reduced = jnp.einsum(
        "ncrb,ncbs->nrs", picked, leaf_coupling, preferred_element_type=jnp.float32
    )
    leaf_coef = jnp.einsum("nrs,nst->nrt", leaf_sol - reduced, leaf_inverse, precision=three_pass)
    coef_leaf = leaf_coef.transpose(1, 0, 2).reshape(snapshots, blocks_here * span)
    leaf_out = leaf_coef.astype(jnp.bfloat16)
    slot_ids = jnp.arange(slot_count)
    grp_ids = jnp.arange(grp_size)
    own_dest = dest_map[:, 0]
    slot_rank = slot_ranks(own_dest[None, :], grp_size)[0]
    selector = (own_dest[None, None, :] == grp_ids[:, None, None]) & (
        slot_rank[None, None, :] == slot_ids[None, :, None]
    )
    send_coef = jnp.einsum(
        "dkj,jrt->dkrt", selector.astype(jnp.bfloat16), leaf_out, preferred_element_type=jnp.float32
    ).astype(jnp.bfloat16)
    send_centre = jnp.einsum(
        "dkj,jct->dkct", selector.astype(jnp.float32), centers, precision=highest
    )
    received, recv_centre = exchange(send_coef, send_centre, grp_size)
    slot_total = grp_size * slot_count
    coef_all = received.reshape(slot_total, snapshots, span)
    centre_all = recv_centre.reshape(slot_total, 3, span)
    point_blocks = eval_pattern.shape[0]
    point_columns = points[0].T.reshape(point_blocks, span, points.shape[1])
    values = evaluate_all(coef_all, centre_all, point_columns, eval_pattern)
    return (coef_leaf, coef_sep, coef_top, values)


def solution(mesh):
    in_specs = (
        P(None, ("leaf", "grp")),
        P(None, ("leaf", "grp")),
        P(),
        P(("leaf", "grp"), None, None),
        P(("leaf", "grp"), None, None, None),
        P(("leaf", "grp"), None),
        P(("leaf", "grp"), None, None),
        P(("leaf", "grp"), None, None, None),
        P(("leaf", "grp"), None),
        P(),
        P(),
        P(("leaf", "grp"), None),
        P(("leaf", "grp"), None, None),
        P(("leaf", "grp"), None, None),
        P(("leaf", "grp"), None),
    )
    out_specs = (P(None, ("leaf", "grp")), P(None, ("leaf", "grp")), P(), P(None, ("leaf", "grp")))
    return jax.shard_map(
        on_device, mesh=mesh, in_specs=in_specs, out_specs=out_specs, check_vma=False
    )
```
